32 devices in a mesh: dp: 8 (over z, x), tensor: 4 (over y, core).
Axes of the slice: x: 2, y: 2, z: 4, core: 2. Of those that a mesh axis runs over, the one named last changes fastest.
Arguments:
- tokens: bfloat16 [2, 2048, 1024], P(None, 'dp'), may hold values from -6 to 6
- ln1_gain: bfloat16 [1024], replicated, may hold values from 0.5 to 1.5
- ln1_bias: bfloat16 [1024], replicated, may hold values from -0.625 to 0.625
- w_qkv: bfloat16 [1024, 3, 1024], P(None, None, 'tensor'), may hold values from -0.1875 to 0.1875
- qv_bias: bfloat16 [2, 1024], P(None, 'tensor'), may hold values from -0.625 to 0.625
- w_out: bfloat16 [1024, 1024], P('tensor'), may hold values from -2 to 2
- out_bias: bfloat16 [1024], replicated, may hold values from -0.625 to 0.625
- ln2_gain: bfloat16 [1024], replicated, may hold values from 0.5 to 1.5
- ln2_bias: bfloat16 [1024], replicated, may hold values from -0.625 to 0.625
- router: bfloat16 [1024, 2], replicated, may hold values from -0.125 to 0.125
- w_in: bfloat16 [2, 1024, 4096], P(None, None, 'tensor'), may hold values from -0.1875 to 0.1875
- in_bias: bfloat16 [2, 4096], P(None, 'tensor'), may hold values from -0.625 to 0.625
- w_back: bfloat16 [2, 4096, 1024], P(None, 'tensor'), may hold values from -0.1875 to 0.1875
- back_bias: bfloat16 [2, 1024], replicated, may hold values from -0.875 to 0.875
- routes: int32 [2, 2048, 1], P(None, 'dp'), may hold values from 0 to 1, as said below
- prefix: int32 [2], replicated, may hold values from 204 to 1024
- cotangent: bfloat16 [2, 2048, 1024], P(None, 'dp'), may hold values from -6 to 6
Outputs:
- result: float32 [2, 2048, 1024], P(None, 'dp')
- input_grad: float32 [2, 2048, 1024], P(None, 'dp')
- grad_ln1_gain: float32 [1024], replicated
- grad_ln1_bias: float32 [1024], replicated
- grad_w_qkv: float32 [1024, 3, 1024], P(None, None, 'tensor')
- grad_qv_bias: float32 [2, 1024], P(None, 'tensor')
- grad_w_out: float32 [1024, 1024], P('tensor')
- grad_out_bias: float32 [1024], replicated
- grad_ln2_gain: float32 [1024], replicated
- grad_ln2_bias: float32 [1024], replicated
- grad_router: float32 [1024, 2], replicated
- grad_w_in: float32 [2, 1024, 4096], P(None, None, 'tensor')
- grad_in_bias: float32 [2, 4096], P(None, 'tensor')
- grad_w_back: float32 [2, 4096, 1024], P(None, 'tensor')
- grad_back_bias: float32 [2, 1024], replicated
The draws below stay inside these ranges and needn't reach their ends.
Inputs may be any that keep to these rules, and one draw needn't show every extreme that they name: `routes`: each token names one expert; every expert is named by some token.
All inputs are finite; a program needn't handle non-finite values.
Results may differ from the reference program's by a relative error of at most 0.04.
Values may be sent and summed in bfloat16 or wider, within the bound.
A program may use at most 192 MiB of HBM per device.

```python
import math
import jax
import jax.numpy as jnp
from jax import lax

D = 1024
HEADS = 16
HEAD_DIM = 64
FFE = 4096
EXPERTS = 2
SPAN = 256
SEQS = 2
TOK_DEV = 512
SEQ = 2048
CAP = 320
N_DP = 8


def draw_routes(key, part):
    key_heavy, key_level, key_token, key_other = jax.random.split(jax.random.fold_in(key, 17), 4)
    block_count = SEQ // SPAN
    heavy = jax.random.randint(key_heavy, (block_count,), 0, EXPERTS, dtype=jnp.int32)
    level = jax.random.randint(key_level, (block_count,), 0, 4, dtype=jnp.int32)
    block_of = jnp.arange(SEQ, dtype=jnp.int32) // SPAN
    threshold = (60 + 10 * level)[block_of]
    heavy_tok = heavy[block_of]
    roll = jax.random.randint(key_token, (SEQS, SEQ), 0, 100, dtype=jnp.int32)
    other = jax.random.randint(key_other, (SEQS, SEQ), 0, EXPERTS - 1, dtype=jnp.int32)
    light = (heavy_tok[None, :] + 1 + other) % EXPERTS
    chosen = jnp.where(roll < threshold[None, :], heavy_tok[None, :], light)
    chosen = chosen.at[0, :EXPERTS].set(jnp.arange(EXPERTS, dtype=jnp.int32))
    return chosen[:, :, None].astype(jnp.int32)


def levels(stream_key, dims, cuts, low, largest):
    def one(position, shards_of):
        steps = jax.random.uniform(jax.random.fold_in(jax.random.fold_in(stream_key, 6), position), (shards_of,), jnp.float32, low / len(cuts), largest / len(cuts))
        return jnp.repeat(jnp.exp(steps), dims[position] // shards_of).reshape((-1,) + (1,) * (len(dims) - position - 1))

    gain = one(*cuts[0])
    for cut in cuts[1:]:
        gain = gain * one(*cut)
    return gain


def normal_values(own_key, dims, deviation, reach, cuts=(), held_as=jnp.bfloat16):
    array = jax.random.normal(own_key, dims, jnp.float32) * deviation
    if len(cuts) > 0:
        array = levels(own_key, dims, cuts, -0.22, 0.18) * array
    return jnp.clip(array, min=-reach, max=reach).astype(held_as)


def setup_inputs(seed: int = 0) -> dict:
    streams_of = jax.random.split(jax.random.key(seed), 18)
    return {
        "tokens": normal_values(streams_of[0], (SEQS, SEQ, D), 1.0, 6.0, ((1, 8),)),
        "ln1_gain": jnp.clip(1.0 + 0.1 * jax.random.normal(streams_of[1], (D,), jnp.float32), 0.5, 1.5).astype(jnp.bfloat16),
        "ln1_bias": normal_values(streams_of[2], (D,), 0.1, 0.625),
        "w_qkv": normal_values(streams_of[3], (D, 3, D), D ** -0.5, 0.1875, ((2, 4),)),
        "qv_bias": normal_values(streams_of[4], (2, D), 0.1, 0.625, ((1, 4),)),
        "w_out": normal_values(streams_of[5], (D, D), (max(D // 128, 1)) ** -0.5, 2.0, ((0, 4),)),
        "out_bias": normal_values(streams_of[6], (D,), 0.1, 0.625),
        "ln2_gain": jnp.clip(1.0 + 0.1 * jax.random.normal(streams_of[7], (D,), jnp.float32), 0.5, 1.5).astype(jnp.bfloat16),
        "ln2_bias": normal_values(streams_of[8], (D,), 0.1, 0.625),
        "router": normal_values(streams_of[9], (D, EXPERTS), (2 * D) ** -0.5, 0.125),
        "w_in": normal_values(streams_of[10], (EXPERTS, D, FFE), D ** -0.5, 0.1875, ((2, 4),)),
        "in_bias": normal_values(streams_of[11], (EXPERTS, FFE), 0.1, 0.625, ((1, 4),)),
        "w_back": normal_values(streams_of[12], (EXPERTS, FFE, D), (FFE // 4) ** -0.5, 0.1875, ((1, 4),)),
        "back_bias": normal_values(streams_of[13], (EXPERTS, D), 0.15, 0.875),
        "routes": draw_routes(jax.random.fold_in(streams_of[17], 71), 0),
        "prefix": jax.random.randint(streams_of[15], (SEQS,), SEQ // 10, SEQ // 2 + 1).astype(jnp.int32),
        "cotangent": normal_values(streams_of[16], (SEQS, SEQ, D), 1.0, 6.0, ((1, 8),)),
    }


@jax.custom_vjp
def low(v):
    return lax.optimization_barrier(v.astype(jnp.bfloat16)).astype(jnp.float32)

@jax.custom_vjp
def low_back(v):
    return v

def low_keep(v):
    return (low(v), None)

def low_pass(kept, grad):
    return (grad,)

def back_keep(v):
    return (v, None)

def back_low(kept, grad):
    return (low(grad),)
low.defvjp(low_keep, low_pass)
low_back.defvjp(back_keep, back_low)
HIGHEST = lax.Precision.HIGHEST
SCALE = 0.125
EPSILON = 1e-05
MASKED = -1e+30

def layer_norm(values, norm_gain, norm_bias):
    centred = values - lax.optimization_barrier(jnp.mean(values, axis=-1, keepdims=True))
    spread = lax.optimization_barrier(jnp.mean(centred * centred, axis=-1, keepdims=True))
    return centred * lax.rsqrt(spread + EPSILON) * norm_gain + norm_bias

def query_block(query_rows, row_start, key_all, value_all, prefix_len):
    block_width = query_rows.shape[0]
    scores = low_back(jnp.einsum('qhd,khd->hqk', query_rows, key_all, precision=HIGHEST) * SCALE)
    query_pos = row_start + jnp.arange(block_width, dtype=jnp.int32)
    key_pos = jnp.arange(key_all.shape[0], dtype=jnp.int32)
    visible_mask = (key_pos[None, :] <= query_pos[:, None]) | (key_pos[None, :] < prefix_len)
    scores = jnp.where(visible_mask[None], scores, MASKED)
    weights = jax.nn.softmax(scores, axis=-1)
    return jnp.einsum('hqk,khd->qhd', weights, value_all, precision=HIGHEST)

def sequence_attend(packed):
    query_all, key_all, value_all, prefix_len = packed
    block_width = math.gcd(SEQ, 512)
    blocks = query_all.reshape(SEQ // block_width, block_width, HEADS, HEAD_DIM)
    starts = jnp.arange(SEQ // block_width, dtype=jnp.int32) * block_width
    checked = jax.checkpoint(query_block)
    mixed_out = lax.map(lambda block_item: checked(block_item[0], block_item[1], key_all, value_all, prefix_len), (blocks, starts))
    return mixed_out.reshape(SEQ, HEADS, HEAD_DIM)

def expert_device(hidden_dev, route_dev, in_weight, in_shift, back_weight, back_shift):
    expert_ids = jnp.arange(EXPERTS, dtype=jnp.int32)
    expert_hot = (route_dev[:, None] == expert_ids[None, :]).astype(jnp.int32)
    earlier = jnp.cumsum(expert_hot, axis=0, dtype=jnp.int32) - expert_hot
    slot_place = lax.optimization_barrier(jnp.sum(earlier * expert_hot, axis=1, dtype=jnp.int32))
    slot_ids = jnp.arange(CAP, dtype=jnp.int32)
    select = ((expert_hot[:, :, None] == 1) & (slot_place[:, None, None] == slot_ids[None, None, :])).astype(jnp.float32)
    slot_inputs = jnp.einsum('tec,td->ecd', select, hidden_dev, precision=HIGHEST)
    pre_act = low_back(jnp.einsum('ecd,edf->ecf', slot_inputs, in_weight, precision=HIGHEST) + in_shift[:, None, :])
    active = low(jax.nn.gelu(pre_act, approximate=False))
    slot_out = low_back(jnp.einsum('ecf,efd->ecd', active, back_weight, precision=HIGHEST) + back_shift[:, None, :])
    return jnp.einsum('tec,ecd->td', select, slot_out, precision=HIGHEST)

def reference(tokens, ln1_gain, ln1_bias, w_qkv, qv_bias, w_out, out_bias, ln2_gain, ln2_bias, router, w_in, in_bias, w_back, back_bias, routes, prefix, cotangent):
    params = tuple((weight_arg.astype(jnp.float32) for weight_arg in (ln1_gain, ln1_bias, w_qkv, qv_bias, w_out, out_bias, ln2_gain, ln2_bias, router, w_in, in_bias, w_back, back_bias)))
    chosen = routes[:, :, 0]
    expert_ids = jnp.arange(EXPERTS, dtype=jnp.int32)
    hot_float = (chosen[:, :, None] == expert_ids[None, None, :]).astype(jnp.float32)
    route_dev = chosen.reshape(SEQS, N_DP, SPAN).transpose(1, 0, 2).reshape(N_DP, TOK_DEV)
    expert_run = jax.checkpoint(expert_device)

    def forward(source, weights_all):
        gain_one, bias_one, qkv_weight, qkv_shift, out_weight, out_shift, gain_two, bias_two, router_weight, in_weight, in_shift, back_weight, back_shift = weights_all
        hidden_one = low(layer_norm(source, gain_one, bias_one))
        projected = jnp.einsum('sti,icf->stcf', hidden_one, qkv_weight, precision=HIGHEST)
        query = low(low_back(projected[:, :, 0] + qkv_shift[0]))
        key_val = low(low_back(projected[:, :, 1]))
        value = low(low_back(projected[:, :, 2] + qkv_shift[1]))
        split = (SEQS, SEQ, HEADS, HEAD_DIM)
        mixed_out = lax.map(sequence_attend, (query.reshape(split), key_val.reshape(split), value.reshape(split), prefix))
        mixed_out = low(low_back(mixed_out.reshape(SEQS, SEQ, D)))
        attn_out = low_back(jnp.einsum('stf,fd->std', mixed_out, out_weight, precision=HIGHEST) + out_shift)
        residual = source + attn_out
        hidden_two = low(layer_norm(residual, gain_two, bias_two))
        logits = low_back(jnp.einsum('std,de->ste', hidden_two, router_weight, precision=HIGHEST))
        probs = jax.nn.softmax(logits, axis=-1)
        gate_value = lax.optimization_barrier(jnp.sum(probs * hot_float, axis=-1))
        by_dev = hidden_two.reshape(SEQS, N_DP, SPAN, D).transpose(1, 0, 2, 3).reshape(N_DP, TOK_DEV, D)
        expert_out = lax.map(lambda pair_item: expert_run(pair_item[0], pair_item[1], in_weight, in_shift, back_weight, back_shift), (by_dev, route_dev))
        expert_out = expert_out.reshape(N_DP, SEQS, SPAN, D).transpose(1, 0, 2, 3).reshape(SEQS, SEQ, D)
        return residual + gate_value[:, :, None] * expert_out
    result, pullback = jax.vjp(forward, tokens.astype(jnp.float32), params)
    input_grad, grads = pullback(cotangent.astype(jnp.float32))
    return (result, input_grad, grads[0], grads[1], grads[2], grads[3], grads[4], grads[5], grads[6], grads[7], grads[8], grads[9], grads[10], grads[11], grads[12])
```

```python
import functools
import math

import jax
import jax.numpy as jnp
from jax import lax
from jax.experimental import pallas as pl
from jax.experimental.pallas import tpu as pltpu
from jax.sharding import PartitionSpec as P

F32 = jnp.float32
BF = jnp.bfloat16
MESH = pl.DeviceIdType.MESH
EPS = 1e-05
CAP = 320
HEAD_DIM = 64
NEG = -1e30
CH = 128


def mm(a, b):
    return lax.dot_general(a, b, (((1,), (0,)), ((), ())), preferred_element_type=F32)


def mm_bt(a, b):
    return lax.dot_general(a, b, (((1,), (1,)), ((), ())), preferred_element_type=F32)


def mm_at(a, b):
    return lax.dot_general(a, b, (((0,), (0,)), ((), ())), preferred_element_type=F32)


def loop(n, body):
    def step(i, carry):
        body(i)
        return carry

    lax.fori_loop(0, n, step, 0)


def al(v, m):
    return pl.multiple_of(v, m)


def lanes(rows):
    return lax.broadcasted_iota(jnp.int32, (rows, 128), 1)


def roll64(v):
    return pltpu.roll(v, 64, 1)


class Ctx:
    def __init__(self, ssem, rsem, lsem):
        self.ssem, self.rsem, self.lsem = ssem, rsem, lsem
        self.next = 0
        self.pending = []
        dp = lax.axis_index("dp")
        t = lax.axis_index("tensor")
        self.dp, self.t = dp, t
        self.z, self.x = dp // 2, lax.rem(dp, 2)
        self.y, self.c = t // 2, lax.rem(t, 2)
        x1 = 1 - self.x
        dpx = self.z * 2 + x1
        tm = self.y * 2 + 1 - self.c
        ty = (1 - self.y) * 2 + self.c
        self.mate = (dp, tm)
        self.yp = (dp, ty)
        self.xp = (dpx, t)
        self.dg = (dpx, ty)
        self.t_mate, self.t_y = tm, ty

    def sems(self, n):
        k = self.next
        self.next += n
        return k

    def rc(self, src, dst, k, dev, kr=None):
        return pltpu.make_async_remote_copy(
            src_ref=src,
            dst_ref=dst,
            send_sem=self.ssem.at[k],
            recv_sem=self.rsem.at[k if kr is None else kr],
            device_id=dev,
            device_id_type=MESH,
        )

    def send(self, src, dst, k, dev):
        cp = self.rc(src, dst, k, dev)
        cp.start()
        self.pending.append(cp)
        return cp

    def drain(self):
        for cp in self.pending:
            cp.wait_send()
        self.pending = []


def barrier_start(C, n_dp):
    sem = pltpu.get_barrier_semaphore()
    devs = [(lax.rem(C.dp + o, n_dp), C.t) for o in range(1, n_dp)]
    devs += [C.mate, C.yp, C.dg, (C.dp, 3 - C.t)]
    for d in devs:
        pl.semaphore_signal(sem, inc=1, device_id=d, device_id_type=MESH)
    return sem, len(devs)


def norm_parts(v):
    mean = jnp.mean(v, axis=-1, keepdims=True)
    cent = v - mean
    var = jnp.mean(cent * cent, axis=-1, keepdims=True)
    r = lax.rsqrt(var + EPS)
    return cent * r, r


def stage_qkv(R, C):
    rows = R.tok.shape[0]
    gain, bias = R.par[0:1, :], R.par[1:2, :]

    def ln(i):
        at = pl.ds(al(i * 32, 32), 32)
        n, _ = norm_parts(R.tok[at, :].astype(F32))
        R.h1[at, :] = (n * gain + bias).astype(BF)

    loop(rows // 32, ln)
    hp = R.wqkv.shape[2] // HEAD_DIM

    def seq(s):
        at = pl.ds(al(s * 256, 256), 256)
        h = R.h1[at, :]
        lo = lanes(256) < 64
        lo2 = lanes(128) < 64
        for pr in range(hp // 2):
            cut = slice(pr * 128, pr * 128 + 128)
            tq = (mm(h, R.wqkv[0, :, cut]) + R.qvb[0:1, cut].astype(F32)) * 0.125
            tk = mm(h, R.wqkv[1, :, cut])
            tv = mm(h, R.wqkv[2, :, cut]) + R.qvb[1:2, cut].astype(F32)
            p = s * hp + 2 * pr
            R.asend[p, 0:256, :] = jnp.where(lo, tq, roll64(tk)).astype(BF)
            R.asend[p + 1, 0:256, :] = jnp.where(lo, roll64(tq), tk).astype(BF)
            a, b = tv[0:128], tv[128:256]
            R.asend[p, 256:384, :] = jnp.where(lo2, a, roll64(b)).astype(BF)
            R.asend[p + 1, 256:384, :] = jnp.where(lo2, roll64(a), b).astype(BF)

    loop(rows // 256, seq)


def all_to_all(R, C, src, dst, n):
    k = C.sems(n)
    cps = [
        C.send(src.at[lax.rem(C.dp + o, n)], dst.at[C.dp], k + o, (lax.rem(C.dp + o, n), C.t))
        for o in range(1, n)
    ]
    mine = pltpu.make_async_copy(src.at[C.dp], dst.at[C.dp], C.lsem.at[0])
    mine.start()

    def wait():
        mine.wait()
        for cp in cps:
            cp.wait_recv()

    return wait


def stage_attend(R, C, n):
    lo = lanes(256) < 64
    lo2 = lanes(128) < 64
    one = jnp.where((lanes(256) == 64) | (lanes(256) == 65), 1.0, 0.0)
    one2 = one[0:128]

    def unpack(b):
        qk = R.arecv[b, 0:256, :].astype(F32)
        vf = R.arecv[b, 256:384, :].astype(F32)
        at = pl.ds(al(b * 256, 256), 256)
        R.Q[at, :] = jnp.where(lo, qk, 0.0).astype(BF)
        R.K[at, :] = jnp.where(lo, roll64(qk), one).astype(BF)
        R.V[pl.ds(al(b * 256, 128), 128), :] = jnp.where(lo2, vf, one2).astype(BF)
        R.V[pl.ds(al(b * 256 + 128, 128), 128), :] = jnp.where(lo2, roll64(vf), one2).astype(BF)

    loop(n, unpack)
    T = 512
    half = R.Q.shape[0] // 2 // T - 1
    seqs = R.prefix.shape[0]
    prefix = R.prefix[C.dp // (n // seqs)]
    k = C.sems(n)

    def rows_of(i):
        at = pl.ds(al(i * T, T), T)
        q = R.Q[at, :]
        qpos = i * T + lax.broadcasted_iota(jnp.int32, (T, 1), 0)
        lim = jnp.maximum(qpos, prefix - 1)

        def tile(j, carry):
            m, acc = carry
            kat = pl.ds(al(j * T, T), T)
            s = mm_bt(q, R.K[kat, :])
            kpos = j * T + lax.broadcasted_iota(jnp.int32, (T, T), 1)
            s = jnp.where(kpos <= lim, s, NEG)
            m2 = jnp.maximum(m, jnp.max(s, axis=1, keepdims=True))
            p = jnp.exp(s - m2).astype(BF)
            acc = acc * jnp.exp(m - m2) + mm(p, R.V[kat, :])
            return m2, acc

        m, acc = lax.fori_loop(
            0,
            jnp.maximum(i, half) + 1,
            tile,
            (jnp.full((T, 1), NEG, F32), jnp.zeros((T, 128), F32)),
        )
        total = acc[:, 64:65]
        o = acc / total
        lse = m + jnp.log(total)
        R.of[at, :] = jnp.where(lanes(T) < 64, o, lse)
        for u in range(2):
            b = i * 2 + u
            top, bot = o[u * 256 : u * 256 + 128], o[u * 256 + 128 : u * 256 + 256]
            R.osend[b] = jnp.where(lo2, top, roll64(bot)).astype(BF)

            @pl.when(b != C.dp)
            def _():
                C.rc(R.osend.at[b], R.orecv.at[C.dp], k + b, (b, C.t), k + C.dp).start()

    loop(R.Q.shape[0] // T, rows_of)
    mine = pltpu.make_async_copy(R.osend.at[C.dp], R.orecv.at[C.dp], C.lsem.at[0])
    mine.start()
    mine.wait()
    for b in range(n):

        @pl.when(b != C.dp)
        def _():
            cp = C.rc(R.osend.at[b], R.orecv.at[b], k + b, (b, C.t), k + b)
            cp.wait_send()
            cp.wait_recv()

    unfold_heads(R.orecv, R.otok, n, seqs)


def unfold_heads(src, dst, n, seqs):
    hp = n // seqs
    lo2 = lanes(128) < 64
    for s in range(seqs):
        for pr in range(hp // 2):
            e = src[s * hp + 2 * pr].astype(F32)
            d = src[s * hp + 2 * pr + 1].astype(F32)
            cut = slice(pr * 128, pr * 128 + 128)
            dst[s * 256 : s * 256 + 128, cut] = jnp.where(lo2, e, roll64(d)).astype(BF)
            dst[s * 256 + 128 : s * 256 + 256, cut] = jnp.where(lo2, roll64(e), d).astype(BF)


def reduce4(R, C, part, out):
    k = C.sems(3)
    k0 = (1 - C.y) * 2 + (1 - C.c)
    k1 = (1 - C.y) * 2 + C.c
    k2 = C.y * 2 + (1 - C.c)
    R.p4[0] = part(k0).astype(BF)
    c0 = C.send(R.p4.at[0], R.l4.at[0], k, C.mate)
    v1 = part(k1)
    c0.wait_recv()
    R.p4[1] = (v1 + R.l4[0].astype(F32)).astype(BF)
    c1 = C.send(R.p4.at[1], R.l4.at[2], k + 1, C.yp)
    R.p4[2] = part(k2).astype(BF)
    c2 = C.send(R.p4.at[2], R.l4.at[1], k + 2, C.mate)
    out[...] = part(C.t)
    c2.wait_recv()
    c1.wait_recv()
    out[...] = out[...] + R.l4[1].astype(F32) + R.l4[2].astype(F32)


def gather4(R, C, buf):
    k = C.sems(3)
    mine = buf.at[C.t]
    cy = C.send(mine, mine, k, C.yp)
    cm = C.send(mine, mine, k + 1, C.mate)

    def wait():
        cy.wait_recv()
        fwd = C.send(buf.at[C.t_y], buf.at[C.t_y], k + 2, C.mate)
        cm.wait_recv()
        fwd.wait_recv()

    return wait


def gather8(R, C, buf):
    k = C.sems(7)
    mine = buf.at[C.x * 4 + C.t]
    cd = C.send(mine, mine, k, C.dg)
    cx = C.send(mine, mine, k + 1, C.xp)
    cy = C.send(mine, mine, k + 2, C.yp)
    cm = C.send(mine, mine, k + 3, C.mate)

    def wait():
        fw = []
        for i, (cp, slot) in enumerate(
            (
                (cy, C.x * 4 + C.t_y),
                (cx, (1 - C.x) * 4 + C.t),
                (cd, (1 - C.x) * 4 + C.t_y),
            )
        ):
            cp.wait_recv()
            fw.append(C.send(buf.at[slot], buf.at[slot], k + 4 + i, C.mate))
        cm.wait_recv()
        for cp in fw:
            cp.wait_recv()

    return wait


def stage_out(R, C):
    def part(k):
        return mm(R.otok[pl.ds(al(k * CH, CH), CH), :], R.wout[...])

    reduce4(R, C, part, R.x1)
    rows = R.tok.shape[0]
    own = pl.ds(al(C.t * CH, CH), CH)
    pos = C.t * CH + lax.broadcasted_iota(jnp.int32, (CH, rows), 0)
    col = lax.broadcasted_iota(jnp.int32, (CH, rows), 1)
    hot = jnp.where(
        R.routes[...] == lax.broadcasted_iota(jnp.int32, (8, rows), 0), 1.0, 0.0
    ).astype(BF)
    earlier = mm_bt(jnp.where(col < pos, 1.0, 0.0).astype(BF), hot)
    here = mm_bt(jnp.where(col == pos, 1.0, 0.0).astype(BF), hot)
    keep = jnp.where(earlier < CAP, here, 0.0)
    keep0, keep1 = keep[:, 0:1], keep[:, 1:2]
    x1 = R.x1[...] + R.tok[own, :].astype(F32) + R.par[2:3, :]
    R.x1[...] = x1
    n, r = norm_parts(x1)
    h2 = (n * R.par[3:4, :] + R.par[4:5, :]).astype(BF)
    slot = C.x * 4 + C.t
    R.H2[slot] = h2
    hf = h2.astype(F32)
    l0 = jnp.sum(hf * R.par[5:6, :], axis=1, keepdims=True)
    l1 = jnp.sum(hf * R.par[6:7, :], axis=1, keepdims=True)
    mx = jnp.maximum(l0, l1)
    e0, e1 = jnp.exp(l0 - mx), jnp.exp(l1 - mx)
    p0, p1 = e0 / (e0 + e1), e1 / (e0 + e1)
    gate = here[:, 0:1] * p0 + here[:, 1:2] * p1
    ln = lanes(CH)
    R.META[slot] = jnp.where(ln == 0, keep0, jnp.where(ln == 1, keep1, 0.0)).astype(BF)
    wait_h = gather8(R, C, R.H2)
    wait_m = gather8(R, C, R.META)
    gr = (gate * R.cot[own, :].astype(F32)).astype(BF)
    R.GG[slot] = (gr.astype(F32) * (keep0 + keep1)).astype(BF)
    wait_g = gather8(R, C, R.GG)
    cols = jnp.zeros((CH, 128), F32)
    for i, v in enumerate((p0, p1, here[:, 0:1], here[:, 1:2], gate, keep0, keep1)):
        cols = jnp.where(ln == i, v, cols)
    R.cols[...] = cols
    wait_h()
    wait_m()
    wait_g()


def gelu_both(h):
    half = 0.5 * (1.0 + lax.erf(h * 0.7071067811865476))
    return h * half, half + h * (jnp.exp(-0.5 * h * h) * 0.3989422804014327)


def stage_moe(R, C):
    def tile(i):
        two = pl.ds(al(2 * i, 2), 2)
        at = pl.ds(al(i * 256, 256), 256)
        h2 = R.H2[two].reshape(256, R.H2.shape[2])
        gg = R.GG[two].reshape(256, R.GG.shape[2])
        meta = R.META[two].reshape(256, 128).astype(F32)
        m0, m1 = meta[:, 0:1], meta[:, 1:2]
        half = R.wi.shape[2]
        bias0 = R.inb[0:1, pl.ds(al(C.x * half, half), half)].astype(F32)
        bias1 = R.inb[1:2, pl.ds(al(C.x * half, half), half)].astype(F32)
        for q in range(half // 256):
            cut = slice(q * 256, q * 256 + 256)
            h0 = mm(h2, R.wi[0, :, cut]) + bias0[:, cut]
            h1 = mm(h2, R.wi[1, :, cut]) + bias1[:, cut]
            act, slope = gelu_both(jnp.where(m0 > 0.0, h0, h1))
            R.A[0, at, cut] = (act * m0).astype(BF)
            R.A[1, at, cut] = (act * m1).astype(BF)
            d0 = mm_bt(gg, R.wb[0, cut, :])
            d1 = mm_bt(gg, R.wb[1, cut, :])
            dh = jnp.where(m0 > 0.0, d0, d1) * slope
            R.DH[0, at, cut] = (dh * m0).astype(BF)
            R.DH[1, at, cut] = (dh * m1).astype(BF)
        y = mm(R.A[0, at, :], R.wb[0]) + mm(R.A[1, at, :], R.wb[1])
        R.YP[two] = y.astype(BF).reshape(2, CH, y.shape[1])
        dx = mm_bt(R.DH[0, at, :], R.wi[0]) + mm_bt(R.DH[1, at, :], R.wi[1])
        R.DXP[two] = dx.astype(BF).reshape(2, CH, dx.shape[1])

    loop(4, tile)


def stage_moe_grads(R, C):
    rows = R.GG.shape[0] * CH

    def back(i):
        at = pl.ds(al(i * 128, 128), 128)
        gg = R.GG[...].reshape(rows, R.GG.shape[2])
        for e in range(2):
            R.gB[e, at, :] = mm_at(R.A[e, :, at], gg).astype(BF)

    loop(R.A.shape[2] // 128, back)

    def into(i):
        at = pl.ds(al(i * 128, 128), 128)
        h2t = R.H2[:, :, at].reshape(rows, 128)
        for e in range(2):
            R.gI[e, at, :] = mm_at(h2t, R.DH[e]).astype(BF)

    loop(R.gI.shape[1] // 128, into)


def reduce8(R, C, parts, land, stage, out):
    k = C.sems(7)
    order = ((1 - C.x, 1 - C.y), (1 - C.x, C.y), (C.x, 1 - C.y), (C.x, C.y))
    devs = (C.dg, C.xp, C.yp)
    cm = []
    for n, (xx, yy) in enumerate(order):
        cm.append(C.send(parts.at[xx * 4 + yy * 2 + 1 - C.c], land.at[n], k + n, C.mate))
    cr = []
    for n, (xx, yy) in enumerate(order):
        cm[n].wait_recv()
        v = parts[xx * 4 + yy * 2 + C.c].astype(F32) + land[n].astype(F32)
        if n < 3:
            stage[n] = v.astype(BF)
            cr.append(C.send(stage.at[n], land.at[4 + n], k + 4 + n, devs[n]))
        else:
            out[...] = v

    def wait():
        for n in range(3):
            cr[n].wait_recv()
        out[...] = (
            out[...] + land[4].astype(F32) + land[5].astype(F32) + land[6].astype(F32)
        )

    return wait


def norm_back(n, r, dn):
    return r * (
        dn - jnp.mean(dn, axis=-1, keepdims=True) - n * jnp.mean(dn * n, axis=-1, keepdims=True)
    )


def rowsum(v):
    return jnp.sum(v, axis=0, keepdims=True)


def stage_owner(R, C):
    own = pl.ds(al(C.t * CH, CH), CH)
    cols = R.cols[...]
    p0, p1, h0, h1, gate, k0, k1 = (cols[:, i : i + 1] for i in range(7))
    u = R.u[...] + k0 * R.par[7:8, :] + k1 * R.par[8:9, :]
    g = R.cot[own, :].astype(F32)
    x1 = R.x1[...]
    R.RES[C.t] = (x1 + gate * u).astype(BF)
    dg = jnp.sum(g * u, axis=1, keepdims=True) * gate
    dl0 = (dg * (h0 - p0)).astype(BF).astype(F32)
    dl1 = (dg * (h1 - p1)).astype(BF).astype(F32)
    h2 = R.H2[C.x * 4 + C.t].astype(F32)
    gg = R.GG[C.x * 4 + C.t].astype(F32)
    dh2 = R.dx[...] + dl0 * R.par[5:6, :] + dl1 * R.par[6:7, :]
    n, r = norm_parts(x1)
    dx1 = g + norm_back(n, r, dh2 * R.par[3:4, :])
    da = dx1.astype(BF)
    R.DA[C.t] = da
    R.x1[...] = dx1
    R.sm[0:1, :] = rowsum(dh2 * n)
    R.sm[1:2, :] = rowsum(dh2)
    R.sm[2:3, :] = rowsum(da.astype(F32))
    R.sm[3:4, :] = rowsum(h2 * dl0)
    R.sm[4:5, :] = rowsum(h2 * dl1)
    R.sm[5:6, :] = rowsum(gg * k0)
    R.sm[6:7, :] = rowsum(gg * k1)


def stage_out_back(R, C, n):
    seqs = R.prefix.shape[0]
    hp = n // seqs
    lo2 = lanes(128) < 64
    for s in range(seqs):
        da = R.DA[2 * s : 2 * s + 2].reshape(256, R.DA.shape[2])
        for pr in range(hp // 2):
            cut = slice(pr * 128, pr * 128 + 128)
            d = mm_bt(da, R.wout[cut, :])
            a, b = d[0:128], d[128:256]
            R.osend[s * hp + 2 * pr] = jnp.where(lo2, a, roll64(b)).astype(BF)
            R.osend[s * hp + 2 * pr + 1] = jnp.where(lo2, roll64(a), b).astype(BF)


def stage_out_grad(R, C):
    da = R.DA[...].reshape(R.otok.shape[0], R.DA.shape[2])
    for pr in range(R.otok.shape[1] // 128):
        cut = slice(pr * 128, pr * 128 + 128)
        R.gO[cut, :] = mm_at(R.otok[:, cut], da).astype(BF)


def stage_attend_back(R, C, n):
    lo2 = lanes(128) < 64
    ln2 = lanes(128)

    def hi_lo(v):
        hi = v.astype(BF).astype(F32)
        return hi, v - hi

    def unpack(b):
        f = R.dorecv[b].astype(F32)
        for u in range(2):
            at = pl.ds(al(b * 256 + u * 128, 128), 128)
            do = jnp.where(lo2, f if u == 0 else roll64(f), 0.0)
            of = R.of[at, :]
            hi, low = hi_lo(-jnp.sum(do * of, axis=1, keepdims=True))
            R.DO[at, :] = jnp.where(ln2 == 64, hi, jnp.where(ln2 == 65, low, do)).astype(BF)
            hi, low = hi_lo(-of[:, 64:65])
            q = R.Q[at, :].astype(F32)
            R.Q[at, :] = jnp.where(ln2 == 64, hi, jnp.where(ln2 == 65, low, q)).astype(BF)

    loop(n, unpack)
    T = 512
    total = R.Q.shape[0]
    nt = total // T
    half = nt // 2
    seqs = R.prefix.shape[0]
    prefix = R.prefix[C.dp // (n // seqs)]
    R.dq[...] = jnp.zeros_like(R.dq)
    k = C.sems(n)
    k2 = C.sems(n)

    def keys(jj):
        j = nt - 1 - jj
        kat = pl.ds(al(j * T, T), T)
        kk, vv = R.K[kat, :], R.V[kat, :]
        kpos = j * T + lax.broadcasted_iota(jnp.int32, (T, T), 0)

        def tile(i, carry):
            dk, dv = carry
            qat = pl.ds(al(i * T, T), T)
            q, do = R.Q[qat, :], R.DO[qat, :]
            qpos = i * T + lax.broadcasted_iota(jnp.int32, (1, T), 1)
            lim = jnp.maximum(qpos, prefix - 1)
            p = jnp.where(kpos <= lim, jnp.exp(mm_bt(kk, q)), 0.0)
            ds = (p * mm_bt(vv, do)).astype(BF)
            dv = dv + mm(p.astype(BF), do)
            dk = dk + mm(ds, q)
            R.dq[qat, :] = R.dq[qat, :] + mm_at(ds, kk)
            return dk, dv

        first = jnp.where(j >= half, j, 0)
        dk, dv = lax.fori_loop(
            first, nt, tile, (jnp.zeros((T, 128), F32), jnp.zeros((T, 128), F32))
        )
        lo = lanes(T) < 64
        kv = jnp.where(lo, dk, roll64(dv)).astype(BF)
        for u in range(2):
            b = j * 2 + u
            R.kvs[b] = kv[u * 256 : u * 256 + 256]

            @pl.when(b != C.dp)
            def _():
                C.rc(R.kvs.at[b], R.kvr.at[C.dp], k + b, (b, C.t), k + C.dp).start()

    loop(nt, keys)

    def queries(b):
        at = al(b * 256, 256)
        top = R.dq[pl.ds(at, 128), :] * 0.125
        bot = R.dq[pl.ds(al(at + 128, 128), 128), :] * 0.125
        R.osend[b] = jnp.where(lo2, top, roll64(bot)).astype(BF)

        @pl.when(b != C.dp)
        def _():
            C.rc(R.osend.at[b], R.dqrecv.at[C.dp], k2 + b, (b, C.t), k2 + C.dp).start()

    loop(n, queries)
    for src, dst, i in ((R.osend, R.dqrecv, 0), (R.kvs, R.kvr, 1)):
        mine = pltpu.make_async_copy(src.at[C.dp], dst.at[C.dp], C.lsem.at[i])
        mine.start()
        mine.wait()
    for src, dst, kk in ((R.kvs, R.kvr, k), (R.osend, R.dqrecv, k2)):
        for b in range(n):

            @pl.when(b != C.dp)
            def _():
                cp = C.rc(src.at[b], dst.at[b], kk + b, (b, C.t), kk + b)
                cp.wait_send()
                cp.wait_recv()

    hp = n // seqs
    lo = lanes(256) < 64
    for s in range(seqs):
        for pr in range(hp // 2):
            p = s * hp + 2 * pr
            cut = slice(pr * 128, pr * 128 + 128)
            e, d = R.kvr[p].astype(F32), R.kvr[p + 1].astype(F32)
            R.dproj[1, s * 256 : s * 256 + 256, cut] = jnp.where(lo, e, roll64(d)).astype(BF)
            R.dproj[2, s * 256 : s * 256 + 256, cut] = jnp.where(lo, roll64(e), d).astype(BF)
    unfold_heads(R.dqrecv, R.dproj.at[0], n, seqs)


def stage_qkv_back(R, C):
    def part(k):
        at = pl.ds(al(k * CH, CH), CH)
        return (
            mm_bt(R.dproj[0, at, :], R.wqkv[0])
            + mm_bt(R.dproj[1, at, :], R.wqkv[1])
            + mm_bt(R.dproj[2, at, :], R.wqkv[2])
        )

    reduce4(R, C, part, R.dx)
    own = pl.ds(al(C.t * CH, CH), CH)
    n, r = norm_parts(R.tok[own, :].astype(F32))
    dh1 = R.dx[...]
    R.GIN[C.t] = (R.x1[...] + norm_back(n, r, dh1 * R.par[0:1, :])).astype(BF)
    R.sm2[0:1, :] = rowsum(dh1 * n)
    R.sm2[1:2, :] = rowsum(dh1)


def stage_qkv_grad(R, C):
    def cols(i):
        at = pl.ds(al(i * 128, 128), 128)
        h = R.h1[:, at]
        for m in range(3):
            R.gQ[m, at, :] = mm_at(h, R.dproj[m]).astype(BF)

    loop(R.h1.shape[1] // 128, cols)


class Line:
    def __init__(self, C, nz, n, src, land, out, locals_at):
        self.C, self.nz, self.n = C, nz, n
        self.src, self.land, self.out = src, land, out
        self.red, self.bc, self.xs = C.sems(2 * n), C.sems(2 * n), C.sems(2 * n)
        self.loc = locals_at

    def place(self, d):
        C = self.C
        step = 1 if d == 0 else -1
        pos = C.z if d == 0 else self.nz - 1 - C.z
        up = (C.dp + 2 * step, C.t)
        down = (C.dp - 2 * step, C.t)
        return pos, up, down

    def copies(self, d, k):
        C = self.C
        pos, up, down = self.place(d)
        i = d * self.n + k
        mine = self.out(C.x, d, k)
        return pos, dict(
            red=lambda: C.rc(self.src(d, k), self.land(d, k), self.red + i, up),
            bc_src=lambda: C.rc(self.src(d, k), mine, self.bc + i, down),
            bc_out=lambda: C.rc(mine, mine, self.bc + i, down),
            xs_src=lambda: C.rc(self.src(d, k), mine, self.xs + i, C.xp),
            xs_out=lambda: C.rc(mine, mine, self.xs + i, C.xp),
            xs_in=lambda: C.rc(self.out(1 - C.x, d, k), self.out(1 - C.x, d, k), self.xs + i, C.xp),
            keep=lambda: pltpu.make_async_copy(self.src(d, k), mine, C.lsem.at[self.loc + i]),
        )

    def reduce(self, d, k):
        pos, c = self.copies(d, k)

        @pl.when(pos > 0)
        def _():
            c["red"]().wait_recv()
            s, l = self.src(d, k), self.land(d, k)
            rows = s.shape[0]

            def add(i):
                at = pl.ds(al(i * 16, 16), 16)
                s[at, :] = (s[at, :].astype(F32) + l[at, :].astype(F32)).astype(BF)

            loop(rows // 16, add)

        @pl.when(pos < self.nz - 1)
        def _():
            c["red"]().start()

        @pl.when(pos == self.nz - 1)
        def _():
            c["bc_src"]().start()
            c["xs_src"]().start()
            c["keep"]().start()

    def spread(self, d, k):
        pos, c = self.copies(d, k)

        @pl.when(pos < self.nz - 1)
        def _():
            c["bc_out"]().wait_recv()

            @pl.when(pos > 0)
            def _():
                c["bc_out"]().start()

            c["xs_out"]().start()

    def finish(self):
        def one(k):
            for d in range(2):
                pos, c = self.copies(d, k)
                c["xs_in"]().wait_recv()
                c["xs_out"]().wait_send()

                @pl.when(pos < self.nz - 1)
                def _():
                    c["red"]().wait_send()

                @pl.when(pos > 0)
                def _():
                    c["bc_out"]().wait_send()

                @pl.when(pos == self.nz - 1)
                def _():
                    c["keep"]().wait()

        loop(self.n, one)


def exchange_x(C, full, land, half):
    k = C.sems(1)
    lead = (slice(None),) * (len(full.shape) - 2)
    theirs = pl.ds(al((1 - C.x) * half, half), half)
    cp = C.send(full.at[lead + (theirs,)], land, k, C.xp)

    def wait():
        cp.wait_recv()
        groups = full.shape[0] if lead else 1
        for m in range(groups):

            def add(i):
                at = pl.ds(al(i * 16, 16), 16)
                own = pl.ds(al(C.x * half + i * 16, 16), 16)
                if lead:
                    v = full[m, own, :].astype(F32) + land[m, at, :].astype(F32)
                    full[m, own, :] = v.astype(BF)
                else:
                    v = full[own, :].astype(F32) + land[at, :].astype(F32)
                    full[own, :] = v.astype(BF)

            loop(half // 16, add)

    return wait


def stage_small(R, C, n):
    R.st[C.t, 0:8, :] = R.sm[...]
    R.st[C.t, 8:16, :] = R.sm2[...]
    k = C.sems(3)
    cps = [
        C.send(R.st.at[C.t], R.st.at[C.t], k + i, dev)
        for i, dev in enumerate((C.mate, C.yp, (C.dp, 3 - C.t)))
    ]
    for cp in cps:
        cp.wait_recv()
    tot = R.st[0] + R.st[1] + R.st[2] + R.st[3]
    sd = R.sd.at[C.dp]
    sd[0:8, :] = tot[0:8, :]
    sd[8:10, :] = tot[8:10, :]
    f = R.dproj.shape[2]

    def colsum(m):
        return rowsum(R.dproj[m].astype(F32))

    sd[10:11, 0:f] = colsum(0)
    sd[10:11, f : 2 * f] = colsum(2)
    half = R.DH.shape[2]
    for e in range(2):
        sd[11:12, e * half : (e + 1) * half] = rowsum(R.DH[e].astype(F32))
    k = C.sems(n)
    cps = [
        C.send(sd, R.sd.at[C.dp], k + o, (lax.rem(C.dp + o, n), C.t)) for o in range(1, n)
    ]
    for cp in cps:
        cp.wait_recv()
    tot = R.sd[0]
    for b in range(1, n):
        tot = tot + R.sd[b]
    R.osm[...] = tot
    for xx in range(2):
        v = R.sd[xx, 11:12, :]
        for b in range(2 + xx, n, 2):
            v = v + R.sd[b, 11:12, :]
        R.osm[11 + xx : 12 + xx, :] = v


class Refs:
    pass


ROWS_B, ROWS_I = 64, 128


def body(names, n, nz, *refs):
    R = Refs()
    for name, ref in zip(names, refs):
        setattr(R, name, ref)
    C = Ctx(R.ssem, R.rsem, R.lsem)
    sem, count = barrier_start(C, n)
    half = R.wi.shape[2]
    off = pl.ds(al(C.x * half, half), half)
    wcp = [
        pltpu.make_async_copy(R.w_in.at[:, :, off], R.wi, C.lsem.at[2]),
        pltpu.make_async_copy(R.w_back.at[:, off, :], R.wb, C.lsem.at[3]),
    ]
    for cp in wcp:
        cp.start()
    R.sm[...] = jnp.zeros_like(R.sm)
    R.sm2[...] = jnp.zeros_like(R.sm2)
    R.sd[...] = jnp.zeros_like(R.sd)
    stage_qkv(R, C)
    pl.semaphore_wait(sem, count)
    all_to_all(R, C, R.asend, R.arecv, n)()
    stage_attend(R, C, n)
    stage_out(R, C)
    for cp in wcp:
        cp.wait()
    stage_moe(R, C)
    wait_u = reduce8(R, C, R.YP, R.ly, R.sy, R.u)
    wait_x = reduce8(R, C, R.DXP, R.lx, R.sx, R.dx)
    stage_moe_grads(R, C)

    lb = Line(
        C, nz, half // ROWS_B,
        lambda d, k: R.gB.at[d, pl.ds(al(k * ROWS_B, ROWS_B), ROWS_B), :],
        lambda d, k: R.lB.at[d, pl.ds(al(k * ROWS_B, ROWS_B), ROWS_B), :],
        lambda h, d, k: R.oB.at[d, pl.ds(al(h * half + k * ROWS_B, ROWS_B), ROWS_B), :],
        4,
    )
    D = R.gI.shape[1]
    li = Line(
        C, nz, D // ROWS_I,
        lambda d, k: R.gI.at[d, pl.ds(al(k * ROWS_I, ROWS_I), ROWS_I), :],
        lambda d, k: R.lI.at[d, pl.ds(al(k * ROWS_I, ROWS_I), ROWS_I), :],
        lambda h, d, k: R.oI.at[
            d, pl.ds(al(k * ROWS_I, ROWS_I), ROWS_I), pl.ds(al(h * half, half), half)
        ],
        4 + 2 * lb.n,
    )

    wait_u()
    wait_x()
    stage_owner(R, C)
    wait_da = gather4(R, C, R.DA)
    wait_res = gather4(R, C, R.RES)
    wait_da()
    stage_out_back(R, C, n)
    wait_do = all_to_all(R, C, R.osend, R.dorecv, n)
    stage_out_grad(R, C)
    wait_do()
    C.drain()
    stage_attend_back(R, C, n)
    stage_qkv_back(R, C)
    wait_gin = gather4(R, C, R.GIN)
    stage_qkv_grad(R, C)
    F = R.gO.shape[0]
    hq, ho = D // 2, F // 2
    wq = exchange_x(C, R.gQ, R.xQ, hq)
    wo = exchange_x(C, R.gO, R.xO, ho)
    wq()
    wo()
    wait_gin()
    wait_res()
    qd, od = hq // 2, ho // 2
    lq = Line(
        C, nz, 3,
        lambda d, k: R.gQ.at[k, pl.ds(al(C.x * hq + d * qd, qd), qd), :],
        lambda d, k: R.lQ.at[d, k],
        lambda h, d, k: R.oQ.at[k, pl.ds(al(h * hq + d * qd, qd), qd), :],
        4 + 2 * lb.n + 2 * li.n,
    )
    lo = Line(
        C, nz, 1,
        lambda d, k: R.gO.at[pl.ds(al(C.x * ho + d * od, od), od), :],
        lambda d, k: R.lO.at[d],
        lambda h, d, k: R.oO.at[pl.ds(al(h * ho + d * od, od), od), :],
        4 + 2 * lb.n + 2 * li.n + 6,
    )
    work = [(L, k) for L in (lb, li, lq, lo) for k in range(L.n)]
    lag = 4
    for s in range(len(work) + lag):
        if s < len(work):
            L, k = work[s]
            L.reduce(0, k)
            L.reduce(1, k)
        if s >= lag:
            L, k = work[s - lag]
            L.spread(0, k)
            L.spread(1, k)
    stage_small(R, C, n)
    for L in (lb, li, lq, lo):
        L.finish()
    C.drain()


def fast_local(args, n, nt):
    (tokens, g1, b1, w_qkv, qvb, w_out, out_b, g2, b2, router, w_in, in_b, w_back, back_b,
     routes, prefix, cot) = args
    S, span, D = tokens.shape
    rows = S * span
    F = w_qkv.shape[2]
    H = w_in.shape[2]
    half = H // 2
    nz = n // 2
    total = n * span
    par = jnp.concatenate(
        [jnp.stack([g1, b1, out_b, g2, b2]), router.T, back_b, jnp.zeros((7, D), BF)], axis=0
    ).astype(F32)
    vm = pl.BlockSpec(memory_space=pltpu.VMEM)
    hbm = pl.BlockSpec(memory_space=pl.ANY)
    ins = [
        ("tok", tokens.reshape(rows, D), vm),
        ("par", par, vm),
        ("wqkv", w_qkv.transpose(1, 0, 2), vm),
        ("qvb", qvb, vm),
        ("wout", w_out, vm),
        ("routes", routes.reshape(1, rows), vm),
        ("prefix", prefix, pl.BlockSpec(memory_space=pltpu.SMEM)),
        ("cot", cot.reshape(rows, D), vm),
        ("inb", in_b, vm),
        ("w_in", w_in, hbm),
        ("w_back", w_back, hbm),
    ]
    sds = jax.ShapeDtypeStruct
    outs = [
        ("RES", sds((nt, CH, D), BF), vm),
        ("GIN", sds((nt, CH, D), BF), vm),
        ("oB", sds((2, H, D), BF), hbm),
        ("oI", sds((2, D, H), BF), hbm),
        ("oQ", sds((3, D, F), BF), hbm),
        ("oO", sds((F, D), BF), hbm),
        ("osm", sds((16, D), F32), vm),
    ]
    V = pltpu.VMEM
    nch = half // ROWS_B + D // ROWS_I + 4
    scr = [
        ("h1", V((rows, D), BF)),
        ("asend", V((n, 384, 128), BF)),
        ("arecv", V((n, 384, 128), BF)),
        ("Q", V((total, 128), BF)),
        ("K", V((total, 128), BF)),
        ("V", V((total, 128), BF)),
        ("DO", V((total, 128), BF)),
        ("of", V((total, 128), F32)),
        ("dq", V((total, 128), F32)),
        ("osend", V((n, 128, 128), BF)),
        ("orecv", V((n, 128, 128), BF)),
        ("dorecv", V((n, 128, 128), BF)),
        ("dqrecv", V((n, 128, 128), BF)),
        ("kvs", V((n, 256, 128), BF)),
        ("kvr", V((n, 256, 128), BF)),
        ("otok", V((rows, F), BF)),
        ("dproj", V((3, rows, F), BF)),
        ("p4", V((3, CH, D), BF)),
        ("l4", V((3, CH, D), BF)),
        ("x1", V((CH, D), F32)),
        ("u", V((CH, D), F32)),
        ("dx", V((CH, D), F32)),
        ("cols", V((CH, 128), F32)),
        ("H2", V((8, CH, D), BF)),
        ("GG", V((8, CH, D), BF)),
        ("META", V((8, CH, 128), BF)),
        ("wi", V((2, D, half), BF)),
        ("wb", V((2, half, D), BF)),
        ("A", V((2, 8 * CH, half), BF)),
        ("DH", V((2, 8 * CH, half), BF)),
        ("YP", V((8, CH, D), BF)),
        ("DXP", V((8, CH, D), BF)),
        ("ly", V((7, CH, D), BF)),
        ("lx", V((7, CH, D), BF)),
        ("sy", V((3, CH, D), BF)),
        ("sx", V((3, CH, D), BF)),
        ("DA", V((nt, CH, D), BF)),
        ("gB", V((2, half, D), BF)),
        ("gI", V((2, D, half), BF)),
        ("gQ", V((3, D, F), BF)),
        ("gO", V((F, D), BF)),
        ("lB", V((2, half, D), BF)),
        ("lI", V((2, D, half), BF)),
        ("xQ", V((3, D // 2, F), BF)),
        ("xO", V((F // 2, D), BF)),
        ("lQ", V((2, 3, D // 4, F), BF)),
        ("lO", V((2, F // 4, D), BF)),
        ("sm", V((8, D), F32)),
        ("sm2", V((8, D), F32)),
        ("st", V((4, 16, D), F32)),
        ("sd", V((n, 16, D), F32)),
        ("ssem", pltpu.SemaphoreType.DMA((120 + 6 * nch,))),
        ("rsem", pltpu.SemaphoreType.DMA((120 + 6 * nch,))),
        ("lsem", pltpu.SemaphoreType.DMA((8 + 2 * nch,))),
    ]
    names = [i[0] for i in ins] + [o[0] for o in outs] + [s[0] for s in scr]
    res, gin, oB, oI, oQ, oO, osm = pl.pallas_call(
        functools.partial(body, names, n, nz),
        out_shape=[o[1] for o in outs],
        in_specs=[i[2] for i in ins],
        out_specs=[o[2] for o in outs],
        scratch_shapes=[s[1] for s in scr],
        compiler_params=pltpu.CompilerParams(
            collective_id=0, has_side_effects=True, vmem_limit_bytes=67043328
        ),
        name="layer",
    )(*[i[1] for i in ins])
    inb = jnp.stack([osm[11].reshape(2, half), osm[12].reshape(2, half)], axis=1).reshape(2, H)
    return (
        res.reshape(S, span, D).astype(F32),
        gin.reshape(S, span, D).astype(F32),
        osm[8],
        osm[9],
        oQ.astype(F32).transpose(1, 0, 2),
        osm[10, : 2 * F].reshape(2, F),
        oO.astype(F32),
        osm[2],
        osm[0],
        osm[1],
        osm[3:5].T,
        oI.astype(F32),
        inb,
        oB.astype(F32),
        osm[5:7],
    )


SCALE = 0.125
EPSILON = 1e-05
MASKED = -1e30
HIGHEST = lax.Precision.HIGHEST


def layer_norm(values, norm_gain, norm_bias):
    centred = values - jnp.mean(values, axis=-1, keepdims=True)
    spread = jnp.mean(centred * centred, axis=-1, keepdims=True)
    return centred * lax.rsqrt(spread + EPSILON) * norm_gain + norm_bias


def heads_of(block, head_count):
    seq_count, row_count, feat_count = block.shape
    return block.reshape(seq_count, row_count, head_count, feat_count // head_count).transpose(
        0, 2, 1, 3
    )


def tokens_of(block):
    seq_count, head_count, row_count, head_width = block.shape
    return block.transpose(0, 2, 1, 3).reshape(seq_count, row_count, head_count * head_width)


def masked_scores(queries, key_heads, query_start, key_start, prefix):
    scores = (
        jnp.einsum("shqd,shkd->shqk", queries, key_heads, preferred_element_type=jnp.float32)
        * SCALE
    )
    query_pos = query_start + jnp.arange(queries.shape[2], dtype=jnp.int32)
    key_pos = key_start + jnp.arange(key_heads.shape[2], dtype=jnp.int32)
    visible_mask = (key_pos[None, None, :] <= query_pos[None, :, None]) | (
        key_pos[None, None, :] < prefix[:, None, None]
    )
    visible_mask = visible_mask[:, None]
    return (jnp.where(visible_mask, scores, MASKED), visible_mask)


def block_live(key_start, query_last, prefix):
    return jnp.any(key_start < prefix) | (key_start <= query_last)


def prob_grads(
    queries, key_heads, value_heads, douts, log_total, delta, query_start, key_start, prefix
):
    scores, visible_mask = masked_scores(queries, key_heads, query_start, key_start, prefix)
    probs = jnp.where(visible_mask, jnp.exp(scores - log_total[..., None]), 0.0)
    dprob = jnp.einsum("shqd,shkd->shqk", douts, value_heads, preferred_element_type=jnp.float32)
    dscore = (probs * (dprob - delta[..., None])).astype(jnp.bfloat16)
    return (probs, dscore)


def attend_fold(run_state, piece_rows, piece_start, queries, first_row, prefix):
    key_piece, value_piece = piece_rows
    head_count = queries.shape[1]
    row_count = key_piece.shape[1]
    block_width = math.gcd(row_count, 512)
    query_last = first_row + queries.shape[2] - 1

    def attend_update(block_index, state_now):
        key_start = block_index * block_width
        key_heads = heads_of(
            lax.dynamic_slice_in_dim(key_piece, block_index * block_width, block_width, 1),
            head_count,
        )
        value_heads = heads_of(
            lax.dynamic_slice_in_dim(value_piece, block_index * block_width, block_width, 1),
            head_count,
        )
        scores, visible_mask = masked_scores(queries, key_heads, first_row, key_start, prefix)
        run_max, run_sum, run_out = state_now
        new_max = jnp.maximum(run_max, jnp.max(scores, axis=-1))
        factor = jnp.exp(run_max - new_max)
        weights = jnp.where(visible_mask, jnp.exp(scores - new_max[..., None]), 0.0)
        run_sum = factor * run_sum + jnp.sum(weights, axis=-1)
        run_out = factor[..., None] * run_out + jnp.einsum(
            "shqk,shkd->shqd", weights, value_heads.astype(jnp.float32), precision=HIGHEST
        )
        return (new_max, run_sum, run_out)

    def attend_block_step(state_now, block_index):
        key_start = block_index * block_width
        is_live = block_live(key_start, query_last, prefix)
        return (
            lax.cond(
                is_live, functools.partial(attend_update, block_index), lambda unchanged: unchanged, state_now
            ),
            None,
        )

    run_state, unused = lax.scan(
        attend_block_step, run_state, jnp.arange(row_count // block_width, dtype=jnp.int32)
    )
    return run_state


def key_pass(queries, douts, log_total, delta, keys_all, values_all, first_row, prefix):
    head_count = queries.shape[1]
    total_rows = keys_all.shape[1]
    block_width = math.gcd(total_rows, 512)
    query_last = first_row + queries.shape[2] - 1

    def key_block_step(dquery, block_index):
        key_start = block_index * block_width

        def work(dquery_now):
            key_heads = heads_of(
                lax.dynamic_slice_in_dim(keys_all, key_start, block_width, 1), head_count
            )
            value_heads = heads_of(
                lax.dynamic_slice_in_dim(values_all, key_start, block_width, 1), head_count
            )
            probs, dscore = prob_grads(
                queries,
                key_heads,
                value_heads,
                douts,
                log_total,
                delta,
                first_row,
                key_start,
                prefix,
            )
            dquery_now = (
                dquery_now
                + jnp.einsum(
                    "shqk,shkd->shqd", dscore, key_heads, preferred_element_type=jnp.float32
                )
                * SCALE
            )
            return (dquery_now, ())

        def skipped(dquery_now):
            return (dquery_now, ())

        return lax.cond(block_live(key_start, query_last, prefix), work, skipped, dquery)

    dquery, key_parts = lax.scan(
        key_block_step,
        jnp.zeros(queries.shape, jnp.float32),
        jnp.arange(total_rows // block_width, dtype=jnp.int32),
    )
    return (dquery, ())


def query_fold(run_state, piece_rows, piece_start, key_heads, value_heads, first_row, prefix):
    query_piece, dout_piece, total_piece, delta_piece = piece_rows
    head_count = key_heads.shape[1]
    row_count = query_piece.shape[1]
    block_width = math.gcd(row_count, 512)

    def query_update(block_index, state_now):
        query_start = block_index * block_width
        offset = block_index * block_width
        queries = heads_of(
            lax.dynamic_slice_in_dim(query_piece, offset, block_width, 1), head_count
        )
        douts = heads_of(lax.dynamic_slice_in_dim(dout_piece, offset, block_width, 1), head_count)
        log_total = lax.dynamic_slice_in_dim(total_piece, offset, block_width, 1).transpose(0, 2, 1)
        delta = lax.dynamic_slice_in_dim(delta_piece, offset, block_width, 1).transpose(0, 2, 1)
        probs, dscore = prob_grads(
            queries, key_heads, value_heads, douts, log_total, delta, query_start, first_row, prefix
        )
        dkey_now, dvalue_now = state_now
        dkey_now = (
            dkey_now
            + jnp.einsum("shqk,shqd->shkd", dscore, queries, preferred_element_type=jnp.float32)
            * SCALE
        )
        dvalue_now = dvalue_now + jnp.einsum(
            "shqk,shqd->shkd", probs, douts.astype(jnp.float32), precision=HIGHEST
        )
        return (dkey_now, dvalue_now)

    def query_block_step(state_now, block_index):
        query_last = block_index * block_width + block_width - 1
        is_live = block_live(first_row, query_last, prefix)
        return (
            lax.cond(
                is_live, functools.partial(query_update, block_index), lambda unchanged: unchanged, state_now
            ),
            None,
        )

    run_state, unused = lax.scan(
        query_block_step, run_state, jnp.arange(row_count // block_width, dtype=jnp.int32)
    )
    return run_state


def local(
    tokens,
    ln1_gain,
    ln1_bias,
    w_qkv,
    qv_bias,
    w_out,
    out_bias,
    ln2_gain,
    ln2_bias,
    router,
    w_in,
    in_bias,
    w_back,
    back_bias,
    routes,
    prefix,
    cotangent,
):
    seq_count, span_len, model_width = tokens.shape
    tok_rows = seq_count * span_len
    local_feats = w_qkv.shape[2]
    head_count = local_feats // HEAD_DIM
    expert_count = w_in.shape[0]
    first_row = lax.axis_index("dp") * span_len
    local_shape = (seq_count, span_len, local_feats)
    source = tokens.reshape(tok_rows, model_width).astype(jnp.float32)
    normed_one, ln1_pull = jax.vjp(
        layer_norm, source, ln1_gain.astype(jnp.float32), ln1_bias.astype(jnp.float32)
    )
    hidden_one = normed_one.astype(jnp.bfloat16)
    projected = jnp.einsum("ti,icf->tcf", hidden_one, w_qkv, preferred_element_type=jnp.float32)
    bias_float = qv_bias.astype(jnp.float32)
    query_tok = (projected[:, 0] + bias_float[0]).astype(jnp.bfloat16).reshape(local_shape)
    key_tok = projected[:, 1].astype(jnp.bfloat16).reshape(local_shape)
    value_tok = (projected[:, 2] + bias_float[1]).astype(jnp.bfloat16).reshape(local_shape)
    queries = heads_of(query_tok, head_count)
    stat_shape = queries.shape[:3]
    start_state = (
        jnp.full(stat_shape, MASKED, jnp.float32),
        jnp.zeros(stat_shape, jnp.float32),
        jnp.zeros(queries.shape, jnp.float32),
    )
    fold_keys = functools.partial(attend_fold, queries=queries, first_row=first_row, prefix=prefix)
    run_max, run_sum, run_out = fold_keys(
        start_state,
        (
            lax.all_gather(key_tok, "dp", axis=1, tiled=True),
            lax.all_gather(value_tok, "dp", axis=1, tiled=True),
        ),
        jnp.int32(0),
    )
    mixed_heads = run_out / run_sum[..., None]
    log_total = run_max + jnp.log(run_sum)
    mixed_b = tokens_of(mixed_heads.astype(jnp.bfloat16)).reshape(tok_rows, local_feats)
    out_shift = out_bias.astype(jnp.float32)
    gain_two = ln2_gain.astype(jnp.float32)
    shift_two = ln2_bias.astype(jnp.float32)
    attn_part = jnp.dot(mixed_b, w_out, preferred_element_type=jnp.float32)
    attn_out = lax.psum(attn_part, "tensor") + out_shift
    residual = source + attn_out
    normed_two, ln2_pull = jax.vjp(layer_norm, residual, gain_two, shift_two)
    hidden_two = normed_two.astype(jnp.bfloat16)
    logits = jnp.dot(hidden_two, router, preferred_element_type=jnp.float32)
    chosen = routes.reshape(tok_rows)
    expert_ids = jnp.arange(expert_count, dtype=jnp.int32)
    expert_hot = (chosen[:, None] == expert_ids[None, :]).astype(jnp.int32)

    def gate_of(logit_vals):
        return jnp.sum(
            jnp.where(expert_hot == 1, jax.nn.softmax(logit_vals, axis=-1), 0.0), axis=-1
        )

    gate_value, gate_pull = jax.vjp(gate_of, logits)
    earlier = jnp.cumsum(expert_hot, axis=0, dtype=jnp.int32) - expert_hot
    slot_place = jnp.sum(earlier * expert_hot, axis=1, dtype=jnp.int32)
    slot_ids = jnp.arange(CAP, dtype=jnp.int32)
    select_mask = (expert_hot[:, :, None] == 1) & (
        slot_place[:, None, None] == slot_ids[None, None, :]
    )
    select = select_mask.astype(jnp.bfloat16)
    select_float = select_mask.astype(jnp.float32)
    dispatched = jnp.einsum(
        "tec,td->ecd", select, hidden_two, preferred_element_type=jnp.float32
    ).astype(jnp.bfloat16)
    pre_act = (
        jnp.einsum("ecd,edf->ecf", dispatched, w_in, preferred_element_type=jnp.float32)
        + in_bias.astype(jnp.float32)[:, None, :]
    )
    act_float, gelu_pull = jax.vjp(functools.partial(jax.nn.gelu, approximate=False), pre_act)
    active = act_float.astype(jnp.bfloat16)
    expert_part = jnp.einsum("ecf,efd->ecd", active, w_back, preferred_element_type=jnp.float32)
    expert_full = lax.psum(expert_part, "tensor") + back_bias.astype(jnp.float32)[:, None, :]
    combined = jnp.einsum("tec,ecd->td", select_float, expert_full, precision=HIGHEST)
    layer_rows = residual + gate_value[:, None] * combined
    grad_out = cotangent.reshape(tok_rows, model_width).astype(jnp.float32)
    dgate = jnp.sum(grad_out * combined, axis=-1)
    dlogit_b = gate_pull(dgate)[0].astype(jnp.bfloat16)
    gated_grad = (gate_value[:, None] * grad_out).astype(jnp.bfloat16)
    dexpert_b = jnp.einsum(
        "tec,td->ecd", select, gated_grad, preferred_element_type=jnp.float32
    ).astype(jnp.bfloat16)
    grad_back_bias = jnp.sum(dexpert_b, axis=1, dtype=jnp.float32)
    grad_w_back = jnp.einsum("ecf,ecd->efd", active, dexpert_b, preferred_element_type=jnp.float32)
    dactive = jnp.einsum("ecd,efd->ecf", dexpert_b, w_back, preferred_element_type=jnp.float32)
    dpre_b = gelu_pull(dactive)[0].astype(jnp.bfloat16)
    grad_in_bias = jnp.sum(dpre_b, axis=1, dtype=jnp.float32)
    grad_w_in = jnp.einsum("ecd,ecf->edf", dispatched, dpre_b, preferred_element_type=jnp.float32)
    slot_part = jnp.einsum("ecf,edf->ecd", dpre_b, w_in, preferred_element_type=jnp.float32)
    dslots = lax.psum(slot_part, "tensor")
    dnorm_two = jnp.einsum("tec,ecd->td", select_float, dslots, precision=HIGHEST) + jnp.einsum(
        "te,de->td", dlogit_b, router, preferred_element_type=jnp.float32
    )
    grad_router = jnp.einsum("td,te->de", hidden_two, dlogit_b, preferred_element_type=jnp.float32)
    dresid_norm, grad_ln2_gain, grad_ln2_bias = ln2_pull(dnorm_two)
    dresidual = grad_out + dresid_norm
    dattn_b = dresidual.astype(jnp.bfloat16)
    grad_out_bias = jnp.sum(dattn_b, axis=0, dtype=jnp.float32)
    grad_w_out = jnp.einsum("tf,td->fd", mixed_b, dattn_b, preferred_element_type=jnp.float32)
    dmixed_tok = (
        jnp.einsum("td,fd->tf", dattn_b, w_out, preferred_element_type=jnp.float32)
        .astype(jnp.bfloat16)
        .reshape(local_shape)
    )
    douts = heads_of(dmixed_tok, head_count)
    delta = jnp.sum(douts.astype(jnp.float32) * mixed_heads, axis=-1)
    keys_all, values_all = (
        lax.all_gather(key_tok, "dp", axis=1, tiled=True),
        lax.all_gather(value_tok, "dp", axis=1, tiled=True),
    )
    dquery, unused = key_pass(
        queries, douts, log_total, delta, keys_all, values_all, first_row, prefix
    )
    total_rows = log_total.transpose(0, 2, 1)
    delta_rows = delta.transpose(0, 2, 1)
    fold_rows = functools.partial(
        query_fold,
        key_heads=heads_of(key_tok, head_count),
        value_heads=heads_of(value_tok, head_count),
        first_row=first_row,
        prefix=prefix,
    )
    zero_heads = jnp.zeros(queries.shape, jnp.float32)
    dkey_heads, dvalue_heads = fold_rows(
        (zero_heads, zero_heads),
        (
            lax.all_gather(query_tok, "dp", axis=1, tiled=True),
            lax.all_gather(dmixed_tok, "dp", axis=1, tiled=True),
            lax.all_gather(total_rows.astype(jnp.bfloat16), "dp", axis=1, tiled=True).astype(
                jnp.float32
            ),
            lax.all_gather(delta_rows.astype(jnp.bfloat16), "dp", axis=1, tiled=True).astype(
                jnp.float32
            ),
        ),
        jnp.int32(0),
    )
    dkey = tokens_of(dkey_heads)
    dvalue = tokens_of(dvalue_heads)
    dquery_b = tokens_of(dquery).astype(jnp.bfloat16).reshape(tok_rows, local_feats)
    dkey_b = dkey.astype(jnp.bfloat16).reshape(tok_rows, local_feats)
    dvalue_b = dvalue.astype(jnp.bfloat16).reshape(tok_rows, local_feats)
    dproject = jnp.stack([dquery_b, dkey_b, dvalue_b], axis=1)
    grad_qv_bias = jnp.stack(
        [jnp.sum(dquery_b, axis=0, dtype=jnp.float32), jnp.sum(dvalue_b, axis=0, dtype=jnp.float32)]
    )
    grad_w_qkv = jnp.einsum("ti,tcf->icf", hidden_one, dproject, preferred_element_type=jnp.float32)
    norm_part = jnp.einsum("tcf,icf->ti", dproject, w_qkv, preferred_element_type=jnp.float32)
    dnorm_one = lax.psum(norm_part, "tensor")
    dsource_norm, grad_ln1_gain, grad_ln1_bias = ln1_pull(dnorm_one)
    input_grad = (dresidual + dsource_norm).reshape(seq_count, span_len, model_width)
    summed = lax.psum(
        (
            grad_ln1_gain,
            grad_ln1_bias,
            grad_w_qkv,
            grad_qv_bias,
            grad_w_out,
            grad_out_bias,
            grad_ln2_gain,
            grad_ln2_bias,
            grad_router,
            grad_w_in,
            grad_in_bias,
            grad_w_back,
            grad_back_bias,
        ),
        "dp",
    )
    layer_out = layer_rows.reshape(seq_count, span_len, model_width)
    return (layer_out, input_grad) + tuple(summed)


def solution(mesh):
    in_specs = (
        P(None, "dp", None),
        P(),
        P(),
        P(None, None, "tensor"),
        P(None, "tensor"),
        P("tensor", None),
        P(),
        P(),
        P(),
        P(),
        P(None, None, "tensor"),
        P(None, "tensor"),
        P(None, "tensor", None),
        P(),
        P(None, "dp", None),
        P(),
        P(None, "dp", None),
    )
    out_specs = (
        P(None, "dp", None),
        P(None, "dp", None),
        P(),
        P(),
        P(None, None, "tensor"),
        P(None, "tensor"),
        P("tensor", None),
        P(),
        P(),
        P(),
        P(),
        P(None, None, "tensor"),
        P(None, "tensor"),
        P(None, "tensor", None),
        P(),
    )
    n, nt = mesh.shape["dp"], mesh.shape["tensor"]

    def step(*args):
        tokens, w_qkv = args[0], args[3]
        heads = w_qkv.shape[2] // HEAD_DIM
        fits = (
            nt == 4
            and n % 2 == 0
            and n == tokens.shape[0] * heads
            and tokens.shape[0] * tokens.shape[1] == nt * CH
            and tokens.shape[1] == 256
        )
        return fast_local(args, n, nt) if fits else local(*args)

    return jax.shard_map(step, mesh=mesh, in_specs=in_specs, out_specs=out_specs, check_vma=False)
```

```python
import functools
import math

import jax
import jax.numpy as jnp
from jax import lax
from jax.experimental import pallas as pl
from jax.experimental.pallas import tpu as pltpu
from jax.sharding import PartitionSpec as P

F32 = jnp.float32
BF = jnp.bfloat16
MESH = pl.DeviceIdType.MESH
EPS = 1e-05
CAP = 320
HEAD_DIM = 64
NEG = -1e30
CH = 128


def mm(a, b):
    return lax.dot_general(a, b, (((1,), (0,)), ((), ())), preferred_element_type=F32)


def mm_bt(a, b):
    return lax.dot_general(a, b, (((1,), (1,)), ((), ())), preferred_element_type=F32)


def mm_at(a, b):
    return lax.dot_general(a, b, (((0,), (0,)), ((), ())), preferred_element_type=F32)


def loop(n, body):
    def step(i, carry):
        body(i)
        return carry

    lax.fori_loop(0, n, step, 0)


def al(v, m):
    return pl.multiple_of(v, m)


def lanes(rows):
    return lax.broadcasted_iota(jnp.int32, (rows, 128), 1)


def roll64(v):
    return pltpu.roll(v, 64, 1)


class Ctx:
    def __init__(self, ssem, rsem, lsem):
        self.ssem, self.rsem, self.lsem = ssem, rsem, lsem
        self.next = 0
        self.pending = []
        dp = lax.axis_index("dp")
        t = lax.axis_index("tensor")
        self.dp, self.t = dp, t
        self.z, self.x = dp // 2, lax.rem(dp, 2)
        self.y, self.c = t // 2, lax.rem(t, 2)
        x1 = 1 - self.x
        dpx = self.z * 2 + x1
        tm = self.y * 2 + 1 - self.c
        ty = (1 - self.y) * 2 + self.c
        self.mate = (dp, tm)
        self.yp = (dp, ty)
        self.xp = (dpx, t)
        self.dg = (dpx, ty)
        self.t_mate, self.t_y = tm, ty

    def sems(self, n):
        k = self.next
        self.next += n
        return k

    def rc(self, src, dst, k, dev, kr=None):
        return pltpu.make_async_remote_copy(
            src_ref=src,
            dst_ref=dst,
            send_sem=self.ssem.at[k],
            recv_sem=self.rsem.at[k if kr is None else kr],
            device_id=dev,
            device_id_type=MESH,
        )

    def send(self, src, dst, k, dev):
        cp = self.rc(src, dst, k, dev)
        cp.start()
        self.pending.append(cp)
        return cp

    def drain(self):
        for cp in self.pending:
            cp.wait_send()
        self.pending = []


def barrier_start(C, n_dp):
    sem = pltpu.get_barrier_semaphore()
    devs = [(lax.rem(C.dp + o, n_dp), C.t) for o in range(1, n_dp)]
    devs += [C.mate, C.yp, C.dg, (C.dp, 3 - C.t)]
    for d in devs:
        pl.semaphore_signal(sem, inc=1, device_id=d, device_id_type=MESH)
    return sem, len(devs)


def norm_parts(v):
    mean = jnp.mean(v, axis=-1, keepdims=True)
    cent = v - mean
    var = jnp.mean(cent * cent, axis=-1, keepdims=True)
    r = lax.rsqrt(var + EPS)
    return cent * r, r


def stage_qkv(R, C):
    rows = R.tok.shape[0]
    gain, bias = R.par[0:1, :], R.par[1:2, :]

    def ln(i):
        at = pl.ds(al(i * 32, 32), 32)
        n, _ = norm_parts(R.tok[at, :].astype(F32))
        R.h1[at, :] = (n * gain + bias).astype(BF)

    loop(rows // 32, ln)
    hp = R.wqkv.shape[2] // HEAD_DIM

    def seq(s):
        at = pl.ds(al(s * 256, 256), 256)
        h = R.h1[at, :]
        lo = lanes(256) < 64
        lo2 = lanes(128) < 64
        for pr in range(hp // 2):
            cut = slice(pr * 128, pr * 128 + 128)
            tq = (mm(h, R.wqkv[0, :, cut]) + R.qvb[0:1, cut].astype(F32)) * 0.125
            tk = mm(h, R.wqkv[1, :, cut])
            tv = mm(h, R.wqkv[2, :, cut]) + R.qvb[1:2, cut].astype(F32)
            p = s * hp + 2 * pr
            R.asend[p, 0:256, :] = jnp.where(lo, tq, roll64(tk)).astype(BF)
            R.asend[p + 1, 0:256, :] = jnp.where(lo, roll64(tq), tk).astype(BF)
            a, b = tv[0:128], tv[128:256]
            R.asend[p, 256:384, :] = jnp.where(lo2, a, roll64(b)).astype(BF)
            R.asend[p + 1, 256:384, :] = jnp.where(lo2, roll64(a), b).astype(BF)

    loop(rows // 256, seq)


def all_to_all(R, C, src, dst, n):
    k = C.sems(n)
    cps = [
        C.send(src.at[lax.rem(C.dp + o, n)], dst.at[C.dp], k + o, (lax.rem(C.dp + o, n), C.t))
        for o in range(1, n)
    ]
    mine = pltpu.make_async_copy(src.at[C.dp], dst.at[C.dp], C.lsem.at[0])
    mine.start()

    def wait():
        mine.wait()
        for cp in cps:
            cp.wait_recv()

    return wait


def stage_attend(R, C, n):
    lo = lanes(256) < 64
    lo2 = lanes(128) < 64
    one = jnp.where((lanes(256) == 64) | (lanes(256) == 65), 1.0, 0.0)
    one2 = one[0:128]

    def unpack(b):
        qk = R.arecv[b, 0:256, :].astype(F32)
        vf = R.arecv[b, 256:384, :].astype(F32)
        at = pl.ds(al(b * 256, 256), 256)
        R.Q[at, :] = jnp.where(lo, qk, 0.0).astype(BF)
        R.K[at, :] = jnp.where(lo, roll64(qk), one).astype(BF)
        R.V[pl.ds(al(b * 256, 128), 128), :] = jnp.where(lo2, vf, one2).astype(BF)
        R.V[pl.ds(al(b * 256 + 128, 128), 128), :] = jnp.where(lo2, roll64(vf), one2).astype(BF)

    loop(n, unpack)
    T = 512
    half = R.Q.shape[0] // 2 // T - 1
    seqs = R.prefix.shape[0]
    prefix = R.prefix[C.dp // (n // seqs)]
    k = C.sems(n)

    def rows_of(i):
        at = pl.ds(al(i * T, T), T)
        q = R.Q[at, :]
        qpos = i * T + lax.broadcasted_iota(jnp.int32, (T, 1), 0)
        lim = jnp.maximum(qpos, prefix - 1)

        def tile(j, carry):
            m, acc = carry
            kat = pl.ds(al(j * T, T), T)
            s = mm_bt(q, R.K[kat, :])
            kpos = j * T + lax.broadcasted_iota(jnp.int32, (T, T), 1)
            s = jnp.where(kpos <= lim, s, NEG)
            m2 = jnp.maximum(m, jnp.max(s, axis=1, keepdims=True))
            p = jnp.exp(s - m2).astype(BF)
            acc = acc * jnp.exp(m - m2) + mm(p, R.V[kat, :])
            return m2, acc

        m, acc = lax.fori_loop(
            0,
            jnp.maximum(i, half) + 1,
            tile,
            (jnp.full((T, 1), NEG, F32), jnp.zeros((T, 128), F32)),
        )
        total = acc[:, 64:65]
        o = acc / total
        lse = m + jnp.log(total)
        R.of[at, :] = jnp.where(lanes(T) < 64, o, lse)
        for u in range(2):
            b = i * 2 + u
            top, bot = o[u * 256 : u * 256 + 128], o[u * 256 + 128 : u * 256 + 256]
            R.osend[b] = jnp.where(lo2, top, roll64(bot)).astype(BF)

            @pl.when(b != C.dp)
            def _():
                C.rc(R.osend.at[b], R.orecv.at[C.dp], k + b, (b, C.t), k + C.dp).start()

    loop(R.Q.shape[0] // T, rows_of)
    mine = pltpu.make_async_copy(R.osend.at[C.dp], R.orecv.at[C.dp], C.lsem.at[0])
    mine.start()
    mine.wait()
    for b in range(n):

        @pl.when(b != C.dp)
        def _():
            cp = C.rc(R.osend.at[b], R.orecv.at[b], k + b, (b, C.t), k + b)
            cp.wait_send()
            cp.wait_recv()

    unfold_heads(R.orecv, R.otok, n, seqs)


def unfold_heads(src, dst, n, seqs):
    hp = n // seqs
    lo2 = lanes(128) < 64
    for s in range(seqs):
        for pr in range(hp // 2):
            e = src[s * hp + 2 * pr].astype(F32)
            d = src[s * hp + 2 * pr + 1].astype(F32)
            cut = slice(pr * 128, pr * 128 + 128)
            dst[s * 256 : s * 256 + 128, cut] = jnp.where(lo2, e, roll64(d)).astype(BF)
            dst[s * 256 + 128 : s * 256 + 256, cut] = jnp.where(lo2, roll64(e), d).astype(BF)


def reduce4(R, C, part, out):
    k = C.sems(3)
    k0 = (1 - C.y) * 2 + (1 - C.c)
    k1 = (1 - C.y) * 2 + C.c
    k2 = C.y * 2 + (1 - C.c)
    R.p4[0] = part(k0).astype(BF)
    c0 = C.send(R.p4.at[0], R.l4.at[0], k, C.mate)
    v1 = part(k1)
    c0.wait_recv()
    R.p4[1] = (v1 + R.l4[0].astype(F32)).astype(BF)
    c1 = C.send(R.p4.at[1], R.l4.at[2], k + 1, C.yp)
    R.p4[2] = part(k2).astype(BF)
    c2 = C.send(R.p4.at[2], R.l4.at[1], k + 2, C.mate)
    out[...] = part(C.t)
    c2.wait_recv()
    c1.wait_recv()
    out[...] = out[...] + R.l4[1].astype(F32) + R.l4[2].astype(F32)


def gather4(R, C, buf):
    k = C.sems(3)
    mine = buf.at[C.t]
    cy = C.send(mine, mine, k, C.yp)
    cm = C.send(mine, mine, k + 1, C.mate)

    def wait():
        cy.wait_recv()
        fwd = C.send(buf.at[C.t_y], buf.at[C.t_y], k + 2, C.mate)
        cm.wait_recv()
        fwd.wait_recv()

    return wait


def gather8(R, C, buf):
    k = C.sems(7)
    mine = buf.at[C.x * 4 + C.t]
    cd = C.send(mine, mine, k, C.dg)
    cx = C.send(mine, mine, k + 1, C.xp)
    cy = C.send(mine, mine, k + 2, C.yp)
    cm = C.send(mine, mine, k + 3, C.mate)

    def wait():
        fw = []
        for i, (cp, slot) in enumerate(
            (
                (cy, C.x * 4 + C.t_y),
                (cx, (1 - C.x) * 4 + C.t),
                (cd, (1 - C.x) * 4 + C.t_y),
            )
        ):
            cp.wait_recv()
            fw.append(C.send(buf.at[slot], buf.at[slot], k + 4 + i, C.mate))
        cm.wait_recv()
        for cp in fw:
            cp.wait_recv()

    return wait


def stage_out(R, C):
    def part(k):
        return mm(R.otok[pl.ds(al(k * CH, CH), CH), :], R.wout[...])

    reduce4(R, C, part, R.x1)
    rows = R.tok.shape[0]
    own = pl.ds(al(C.t * CH, CH), CH)
    pos = C.t * CH + lax.broadcasted_iota(jnp.int32, (CH, rows), 0)
    col = lax.broadcasted_iota(jnp.int32, (CH, rows), 1)
    hot = jnp.where(
        R.routes[...] == lax.broadcasted_iota(jnp.int32, (8, rows), 0), 1.0, 0.0
    ).astype(BF)
    earlier = mm_bt(jnp.where(col < pos, 1.0, 0.0).astype(BF), hot)
    here = mm_bt(jnp.where(col == pos, 1.0, 0.0).astype(BF), hot)
    keep = jnp.where(earlier < CAP, here, 0.0)
    keep0, keep1 = keep[:, 0:1], keep[:, 1:2]
    x1 = R.x1[...] + R.tok[own, :].astype(F32) + R.par[2:3, :]
    R.x1[...] = x1
    n, r = norm_parts(x1)
    h2 = (n * R.par[3:4, :] + R.par[4:5, :]).astype(BF)
    slot = C.x * 4 + C.t
    R.H2[slot] = h2
    hf = h2.astype(F32)
    l0 = jnp.sum(hf * R.par[5:6, :], axis=1, keepdims=True)
    l1 = jnp.sum(hf * R.par[6:7, :], axis=1, keepdims=True)
    mx = jnp.maximum(l0, l1)
    e0, e1 = jnp.exp(l0 - mx), jnp.exp(l1 - mx)
    p0, p1 = e0 / (e0 + e1), e1 / (e0 + e1)
    gate = here[:, 0:1] * p0 + here[:, 1:2] * p1
    ln = lanes(CH)
    R.META[slot] = jnp.where(ln == 0, keep0, jnp.where(ln == 1, keep1, 0.0)).astype(BF)
    wait_h = gather8(R, C, R.H2)
    wait_m = gather8(R, C, R.META)
    gr = (gate * R.cot[own, :].astype(F32)).astype(BF)
    R.GG[slot] = (gr.astype(F32) * (keep0 + keep1)).astype(BF)
    wait_g = gather8(R, C, R.GG)
    cols = jnp.zeros((CH, 128), F32)
    for i, v in enumerate((p0, p1, here[:, 0:1], here[:, 1:2], gate, keep0, keep1)):
        cols = jnp.where(ln == i, v, cols)
    R.cols[...] = cols
    wait_h()
    wait_m()
    wait_g()


def gelu_both(h):
    half = 0.5 * (1.0 + lax.erf(h * 0.7071067811865476))
    return h * half, half + h * (jnp.exp(-0.5 * h * h) * 0.3989422804014327)


def stage_moe(R, C):
    def tile(i):
        two = pl.ds(al(2 * i, 2), 2)
        at = pl.ds(al(i * 256, 256), 256)
        h2 = R.H2[two].reshape(256, R.H2.shape[2])
        gg = R.GG[two].reshape(256, R.GG.shape[2])
        meta = R.META[two].reshape(256, 128).astype(F32)
        m0, m1 = meta[:, 0:1], meta[:, 1:2]
        half = R.wi.shape[2]
        bias0 = R.inb[0:1, pl.ds(al(C.x * half, half), half)].astype(F32)
        bias1 = R.inb[1:2, pl.ds(al(C.x * half, half), half)].astype(F32)
        for q in range(half // 256):
            cut = slice(q * 256, q * 256 + 256)
            h0 = mm(h2, R.wi[0, :, cut]) + bias0[:, cut]
            h1 = mm(h2, R.wi[1, :, cut]) + bias1[:, cut]
            act, slope = gelu_both(jnp.where(m0 > 0.0, h0, h1))
            R.A[0, at, cut] = (act * m0).astype(BF)
            R.A[1, at, cut] = (act * m1).astype(BF)
            d0 = mm_bt(gg, R.wb[0, cut, :])
            d1 = mm_bt(gg, R.wb[1, cut, :])
            dh = jnp.where(m0 > 0.0, d0, d1) * slope
            R.DH[0, at, cut] = (dh * m0).astype(BF)
            R.DH[1, at, cut] = (dh * m1).astype(BF)
        y = mm(R.A[0, at, :], R.wb[0]) + mm(R.A[1, at, :], R.wb[1])
        R.YP[two] = y.astype(BF).reshape(2, CH, y.shape[1])
        dx = mm_bt(R.DH[0, at, :], R.wi[0]) + mm_bt(R.DH[1, at, :], R.wi[1])
        R.DXP[two] = dx.astype(BF).reshape(2, CH, dx.shape[1])

    loop(4, tile)


def put_wide(at, v):
    w = v.shape[1] // 2
    at[0:32, :] = v[:, 0:w].astype(BF)
    at[32:64, :] = v[:, w : 2 * w].astype(BF)


def stage_moe_grads(R, C, K, ring):
    rows = R.GG.shape[0] * CH

    def back(i):
        at = pl.ds(al(i * 128, 128), 128)
        gg = R.GG[...].reshape(rows, R.GG.shape[2])
        for e in range(2):
            v = mm_at(R.A[e, :, at], gg)
            for j in range(4):
                put_wide(R.G.at[e, 4 * i + j], v[32 * j : 32 * j + 32])

    loop(R.A.shape[2] // 128, back)
    ring.run(3)
    base = ring.take(R.H2.shape[2] // 128)

    def into(i):
        at = pl.ds(al(i * 128, 128), 128)
        h2t = R.H2[:, :, at].reshape(rows, 128)
        for e in range(2):
            v = mm_at(h2t, R.DH[e]).astype(BF)
            R.G[e, K.i0 + 2 * i] = v[0:64]
            R.G[e, K.i0 + 2 * i + 1] = v[64:128]
        ring.tick(base + i)

    loop(R.H2.shape[2] // 128, into)


def reduce8(R, C, parts, land, stage, out):
    k = C.sems(7)
    order = ((1 - C.x, 1 - C.y), (1 - C.x, C.y), (C.x, 1 - C.y), (C.x, C.y))
    devs = (C.dg, C.xp, C.yp)
    cm = []
    for n, (xx, yy) in enumerate(order):
        cm.append(C.send(parts.at[xx * 4 + yy * 2 + 1 - C.c], land.at[n], k + n, C.mate))
    cr = []
    for n, (xx, yy) in enumerate(order):
        cm[n].wait_recv()
        v = parts[xx * 4 + yy * 2 + C.c].astype(F32) + land[n].astype(F32)
        if n < 3:
            stage[n] = v.astype(BF)
            cr.append(C.send(stage.at[n], land.at[4 + n], k + 4 + n, devs[n]))
        else:
            out[...] = v

    def wait():
        for n in range(3):
            cr[n].wait_recv()
        out[...] = (
            out[...] + land[4].astype(F32) + land[5].astype(F32) + land[6].astype(F32)
        )

    return wait


def norm_back(n, r, dn):
    return r * (
        dn - jnp.mean(dn, axis=-1, keepdims=True) - n * jnp.mean(dn * n, axis=-1, keepdims=True)
    )


def rowsum(v):
    return jnp.sum(v, axis=0, keepdims=True)


def stage_owner(R, C):
    own = pl.ds(al(C.t * CH, CH), CH)
    cols = R.cols[...]
    p0, p1, h0, h1, gate, k0, k1 = (cols[:, i : i + 1] for i in range(7))
    u = R.u[...] + k0 * R.par[7:8, :] + k1 * R.par[8:9, :]
    g = R.cot[own, :].astype(F32)
    x1 = R.x1[...]
    R.RES[C.t] = (x1 + gate * u).astype(BF)
    dg = jnp.sum(g * u, axis=1, keepdims=True) * gate
    dl0 = (dg * (h0 - p0)).astype(BF).astype(F32)
    dl1 = (dg * (h1 - p1)).astype(BF).astype(F32)
    h2 = R.H2[C.x * 4 + C.t].astype(F32)
    gg = R.GG[C.x * 4 + C.t].astype(F32)
    dh2 = R.dx[...] + dl0 * R.par[5:6, :] + dl1 * R.par[6:7, :]
    n, r = norm_parts(x1)
    dx1 = g + norm_back(n, r, dh2 * R.par[3:4, :])
    da = dx1.astype(BF)
    R.DA[C.t] = da
    R.x1[...] = dx1
    R.sm[0:1, :] = rowsum(dh2 * n)
    R.sm[1:2, :] = rowsum(dh2)
    R.sm[2:3, :] = rowsum(da.astype(F32))
    R.sm[3:4, :] = rowsum(h2 * dl0)
    R.sm[4:5, :] = rowsum(h2 * dl1)
    R.sm[5:6, :] = rowsum(gg * k0)
    R.sm[6:7, :] = rowsum(gg * k1)


def stage_out_back(R, C, n):
    seqs = R.prefix.shape[0]
    hp = n // seqs
    lo2 = lanes(128) < 64
    for s in range(seqs):
        da = R.DA[2 * s : 2 * s + 2].reshape(256, R.DA.shape[2])
        for pr in range(hp // 2):
            cut = slice(pr * 128, pr * 128 + 128)
            d = mm_bt(da, R.wout[cut, :])
            a, b = d[0:128], d[128:256]
            R.osend[s * hp + 2 * pr] = jnp.where(lo2, a, roll64(b)).astype(BF)
            R.osend[s * hp + 2 * pr + 1] = jnp.where(lo2, roll64(a), b).astype(BF)


def tail_of(buf, d, c, n=1):
    return buf.at[d, 64 * c : 64 * (c + n), :]


def stage_out_grad(R, C):
    da = R.DA[...].reshape(R.otok.shape[0], R.DA.shape[2])
    ho = R.otok.shape[1] // 2
    k0 = R.G.shape[1] - 8
    for own, who in ((False, 1 - C.x), (True, C.x)):
        v = mm_at(R.otok[:, pl.ds(al(who * ho, ho), ho)], da)
        for d in range(2):
            for c in range(2):
                r = d * 64 + c * 32
                put_wide(R.G.at[d, k0 + c] if own else tail_of(R.A, d, c), v[r : r + 32])


def add_tail(R, c0, n):
    k0 = R.G.shape[1] - 8

    def one(c):
        for d in range(2):
            v = R.G[d, k0 + c0 + c].astype(F32) + R.wi[d, pl.ds(al((c0 + c) * 64, 64), 64), :].astype(F32)
            R.G[d, k0 + c0 + c] = v.astype(BF)

    loop(n, one)


def stage_attend_back(R, C, n, ring):
    lo2 = lanes(128) < 64
    ln2 = lanes(128)

    def hi_lo(v):
        hi = v.astype(BF).astype(F32)
        return hi, v - hi

    def unpack(b):
        f = R.dorecv[b].astype(F32)
        for u in range(2):
            at = pl.ds(al(b * 256 + u * 128, 128), 128)
            do = jnp.where(lo2, f if u == 0 else roll64(f), 0.0)
            of = R.of[at, :]
            hi, low = hi_lo(-jnp.sum(do * of, axis=1, keepdims=True))
            R.DO[at, :] = jnp.where(ln2 == 64, hi, jnp.where(ln2 == 65, low, do)).astype(BF)
            hi, low = hi_lo(-of[:, 64:65])
            q = R.Q[at, :].astype(F32)
            R.Q[at, :] = jnp.where(ln2 == 64, hi, jnp.where(ln2 == 65, low, q)).astype(BF)

    loop(n, unpack)
    T = 512
    total = R.Q.shape[0]
    nt = total // T
    half = nt // 2
    seqs = R.prefix.shape[0]
    prefix = R.prefix[C.dp // (n // seqs)]
    R.dq[...] = jnp.zeros_like(R.dq)
    k = C.sems(n)
    k2 = C.sems(n)
    base = ring.take(2 * nt)
    kvs, kvr, dqr = R.asend.at[:, 0:256], R.arecv.at[:, 0:256], R.arecv.at[:, 256:384]

    def keys(jj):
        ring.tick(base + 2 * jj)
        j = nt - 1 - jj
        kat = pl.ds(al(j * T, T), T)
        kk, vv = R.K[kat, :], R.V[kat, :]
        kpos = j * T + lax.broadcasted_iota(jnp.int32, (T, T), 0)

        def tile(i, carry):
            dk, dv = carry
            qat = pl.ds(al(i * T, T), T)
            q, do = R.Q[qat, :], R.DO[qat, :]
            qpos = i * T + lax.broadcasted_iota(jnp.int32, (1, T), 1)
            lim = jnp.maximum(qpos, prefix - 1)
            p = jnp.where(kpos <= lim, jnp.exp(mm_bt(kk, q)), 0.0)
            ds = (p * mm_bt(vv, do)).astype(BF)
            dv = dv + mm(p.astype(BF), do)
            dk = dk + mm(ds, q)
            R.dq[qat, :] = R.dq[qat, :] + mm_at(ds, kk)
            return dk, dv

        first = jnp.where(j >= half, j, 0)
        dk, dv = lax.fori_loop(
            first, nt, tile, (jnp.zeros((T, 128), F32), jnp.zeros((T, 128), F32))
        )
        lo = lanes(T) < 64
        kv = jnp.where(lo, dk, roll64(dv)).astype(BF)
        for u in range(2):
            b = j * 2 + u
            R.asend[b, 0:256, :] = kv[u * 256 : u * 256 + 256]

            @pl.when(b != C.dp)
            def _():
                C.rc(kvs.at[b], kvr.at[C.dp], k + b, (b, C.t), k + C.dp).start()

        ring.tick(base + 2 * jj + 1)

    loop(nt, keys)

    def queries(b):
        at = al(b * 256, 256)
        top = R.dq[pl.ds(at, 128), :] * 0.125
        bot = R.dq[pl.ds(al(at + 128, 128), 128), :] * 0.125
        R.osend[b] = jnp.where(lo2, top, roll64(bot)).astype(BF)

        @pl.when(b != C.dp)
        def _():
            C.rc(R.osend.at[b], dqr.at[C.dp], k2 + b, (b, C.t), k2 + C.dp).start()

    loop(n, queries)
    ring.run(2)
    for src, dst, i in ((R.osend, dqr, 0), (kvs, kvr, 1)):
        mine = pltpu.make_async_copy(src.at[C.dp], dst.at[C.dp], C.lsem.at[i])
        mine.start()
        mine.wait()
    for src, dst, kk in ((kvs, kvr, k), (R.osend, dqr, k2)):
        for b in range(n):

            @pl.when(b != C.dp)
            def _():
                cp = C.rc(src.at[b], dst.at[b], kk + b, (b, C.t), kk + b)
                cp.wait_send()
                cp.wait_recv()

    hp = n // seqs
    lo = lanes(256) < 64
    for s in range(seqs):
        for pr in range(hp // 2):
            p = s * hp + 2 * pr
            cut = slice(pr * 128, pr * 128 + 128)
            e, d = kvr[p].astype(F32), kvr[p + 1].astype(F32)
            R.dproj[1, s * 256 : s * 256 + 256, cut] = jnp.where(lo, e, roll64(d)).astype(BF)
            R.dproj[2, s * 256 : s * 256 + 256, cut] = jnp.where(lo, roll64(e), d).astype(BF)
    unfold_heads(dqr, R.dproj.at[0], n, seqs)


def stage_qkv_back(R, C):
    def part(k):
        at = pl.ds(al(k * CH, CH), CH)
        return (
            mm_bt(R.dproj[0, at, :], R.wqkv[0])
            + mm_bt(R.dproj[1, at, :], R.wqkv[1])
            + mm_bt(R.dproj[2, at, :], R.wqkv[2])
        )

    reduce4(R, C, part, R.dx)
    own = pl.ds(al(C.t * CH, CH), CH)
    n, r = norm_parts(R.tok[own, :].astype(F32))
    dh1 = R.dx[...]
    R.GIN[C.t] = (R.x1[...] + norm_back(n, r, dh1 * R.par[0:1, :])).astype(BF)
    R.sm2[0:1, :] = rowsum(dh1 * n)
    R.sm2[1:2, :] = rowsum(dh1)


def stage_qkv_grad(R, C):
    hq = R.h1.shape[1] // 2
    k = C.sems(2)
    cps = []
    k0 = R.G.shape[1] - 6
    for own, who in ((False, 1 - C.x), (True, C.x)):
        for d in range(2):
            for c in range(2):
                at = pl.ds(al(who * hq + (2 * d + c) * 128, 128), 128)
                h = R.h1[:, at]
                for m in range(3):
                    v = mm_at(h, R.dproj[m]).astype(BF)
                    w = v.shape[1]
                    i = 2 * m + c
                    dst = R.G.at[d, k0 + i] if own else tail_of(R.A, d, 2 + i)
                    dst[:, 0:w] = v[0:64]
                    dst[:, w : 2 * w] = v[64:128]
            if not own:
                cps.append(C.send(tail_of(R.A, d, 2, 6), tail_of(R.wi, d, 2, 6), k + d, C.xp))
    return cps


class Kinds:
    def __init__(self, nb, ni):
        self.i0 = nb
        self.o0 = nb + ni
        self.q0 = self.o0 + 2
        self.n = self.q0 + 6

    def emit(self, R, buf, h, d, k, sem):
        half = buf.shape[1]

        def put(src, dst):
            pltpu.make_async_copy(src, dst, sem).start()

        def wide(out, row):
            at = pl.ds(al(row, 32), 32)
            put(buf.at[0:32, :], out.at[at, 0:half])
            put(buf.at[32:64, :], out.at[at, half : 2 * half])

        @pl.when(k < self.i0)
        def _():
            wide(R.oB.at[d], h * (self.i0 * 32) + k * 32)

        @pl.when(jnp.logical_and(k >= self.i0, k < self.o0))
        def _():
            at = pl.ds(al((k - self.i0) * 64, 64), 64)
            put(buf, R.oI.at[d, at, pl.ds(al(h * half, half), half)])

        @pl.when(jnp.logical_and(k >= self.o0, k < self.q0))
        def _():
            wide(R.oO, h * 128 + d * 64 + (k - self.o0) * 32)

        @pl.when(k >= self.q0)
        def _():
            c = k - self.q0
            m = c // 2
            row = h * 512 + d * 256 + (c - 2 * m) * 128
            w = half // 2
            put(buf.at[:, 0:w], R.oQ.at[m, pl.ds(al(row, 64), 64), :])
            put(buf.at[:, w : 2 * w], R.oQ.at[m, pl.ds(al(row + 64, 64), 64), :])


class Ring:
    def __init__(self, R, C, K, w):
        self.R, self.C, self.K, self.w = R, C, K, w
        n = K.n
        self.a, self.b, self.x = C.sems(2 * n), C.sems(2 * n), C.sems(2 * n)
        self.cur = 0
        self.total = n + 5 * w + 1

    def take(self, n):
        base = self.cur
        self.cur += n
        return base

    def run(self, n):
        base = self.take(n)
        loop(n, lambda i: self.tick(base + i))

    def slot(self, buf, d, par, kind):
        sem = self.C.lsem.at[4 + kind * 4 + d * 2 + par]
        return pltpu.make_async_copy(buf.at[d, par], buf.at[d, par], sem)

    def xb(self, d, par):
        return self.R.A.at[d, pl.ds(al(512 + 64 * par, 64), 64), :]

    def tick(self, s):
        for d in range(2):
            self.half(s, d)

    def half(self, s, d):
        R, C, K, w = self.R, self.C, self.K, self.w
        n = K.n
        pos = C.z if d == 0 else 3 - C.z

        def dev(p):
            return ((p if d == 0 else 3 - p) * 2 + C.x, C.t)

        def act(k, cond):
            ok = jnp.logical_and(k >= 0, k < n)
            return ok if cond is None else jnp.logical_and(ok, cond)

        @pl.when(act(s, jnp.logical_or(pos == 0, pos == 3)))
        def _():
            i = d * n + s
            C.rc(R.G.at[d, s], R.L1.at[d, s], self.a + i, dev(1 + pos // 3)).start()

        k2 = s - w

        @pl.when(act(k2, pos == 2))
        def _():
            i = d * n + k2
            C.rc(R.G.at[d, k2], R.L1.at[d, k2], self.a + i, dev(1)).wait_recv()
            R.G[d, k2] = (R.G[d, k2].astype(F32) + R.L1[d, k2].astype(F32)).astype(BF)
            C.rc(R.G.at[d, k2], R.FN.at[d, k2], self.a + i, dev(1), self.b + i).start()

        k1 = s - 2 * w

        @pl.when(act(k1, pos == 1))
        def _():
            i = d * n + k1
            fn = R.FN.at[d, k1]
            C.rc(R.G.at[d, k1], R.L1.at[d, k1], self.a + i, dev(0)).wait_recv()
            C.rc(fn, fn, self.b + i, dev(2)).wait_recv()
            v = R.G[d, k1].astype(F32) + R.L1[d, k1].astype(F32) + R.FN[d, k1].astype(F32)
            R.FN[d, k1] = v.astype(BF)
            C.rc(fn, fn, self.b + i, dev(2)).start()
            C.rc(fn, fn, self.a + i, dev(0), self.b + i).start()

        lag = w * (2 + jnp.where(pos == 1, 0, 1) + jnp.where(pos == 3, 1, 0))
        kf = s - lag

        @pl.when(act(kf, None))
        def _():
            i = d * n + kf
            fn = R.FN.at[d, kf]

            @pl.when(pos != 1)
            def _():
                C.rc(fn, fn, self.b + i, dev(1)).wait_recv()

            @pl.when(pos == 2)
            def _():
                C.rc(fn, fn, self.b + i, dev(3)).start()

            C.rc(fn, R.XH.at[d, kf], self.x + i, C.xp).start()
            self.store(R.FN.at[d, kf], R.SF, 0, C.x, d, kf)

        kx = kf - w

        @pl.when(act(kx, None))
        def _():
            xh = R.XH.at[d, kx]
            C.rc(xh, xh, self.x + d * n + kx, C.xp).wait_recv()
            par = lax.rem(kx, 2)
            pltpu.make_async_copy(xh, self.xb(d, par), C.lsem.at[12 + d * 2 + par]).start()

        ky = kx - 1

        @pl.when(act(ky, None))
        def _():
            par = lax.rem(ky, 2)
            xb = self.xb(d, par)
            pltpu.make_async_copy(R.XH.at[d, ky], xb, C.lsem.at[12 + d * 2 + par]).wait()
            self.store(xb, R.SX, 1, 1 - C.x, d, ky)

    def store(self, src, buf, kind, h, d, k):
        par = lax.rem(k, 2)

        @pl.when(k >= 2)
        def _():
            self.slot(buf, d, par, kind).wait()

        buf[d, par] = src[...].astype(F32)
        self.K.emit(self.R, buf.at[d, par], h, d, k, self.C.lsem.at[4 + kind * 4 + d * 2 + par])

    def finish(self):
        R, C, n = self.R, self.C, self.K.n

        def one(k):
            for d in range(2):
                i = d * n + k
                pos = C.z if d == 0 else 3 - C.z
                fn = R.FN.at[d, k]
                C.rc(fn, fn, self.a + i, C.xp).wait_send()
                C.rc(fn, fn, self.x + i, C.xp).wait_send()

                @pl.when(jnp.logical_or(pos == 1, pos == 2))
                def _():
                    C.rc(fn, fn, self.b + i, C.xp).wait_send()

        loop(n, one)
        for d in range(2):
            for par in range(2):
                self.slot(R.SF, d, par, 0).wait()
                self.slot(R.SX, d, par, 1).wait()


def small_tensor(R, C):
    R.st[C.t, 0:8, :] = R.sm[...]
    R.st[C.t, 8:16, :] = R.sm2[...]
    k = C.sems(3)
    return [
        C.send(R.st.at[C.t], R.st.at[C.t], k + i, dev)
        for i, dev in enumerate((C.mate, C.yp, (C.dp, 3 - C.t)))
    ]


def small_dp(R, C, n, cps):
    for cp in cps:
        cp.wait_recv()
    tot = R.st[0] + R.st[1] + R.st[2] + R.st[3]
    sd = R.sd.at[C.dp]
    sd[0:8, :] = tot[0:8, :]
    sd[8:10, :] = tot[8:10, :]
    f = R.dproj.shape[2]

    def colsum(m):
        return rowsum(R.dproj[m].astype(F32))

    sd[10:11, 0:f] = colsum(0)
    sd[10:11, f : 2 * f] = colsum(2)
    half = R.DH.shape[2]
    for e in range(2):
        sd[11:12, e * half : (e + 1) * half] = rowsum(R.DH[e].astype(F32))
    k = C.sems(n)
    return [C.send(sd, R.sd.at[C.dp], k + o, (lax.rem(C.dp + o, n), C.t)) for o in range(1, n)]


def small_end(R, C, n, cps):
    for cp in cps:
        cp.wait_recv()
    tot = R.sd[0]
    for b in range(1, n):
        tot = tot + R.sd[b]
    R.osm[...] = tot
    for xx in range(2):
        v = R.sd[xx, 11:12, :]
        for b in range(2 + xx, n, 2):
            v = v + R.sd[b, 11:12, :]
        R.osm[11 + xx : 12 + xx, :] = v


class Refs:
    pass


LAG = 3


def body(names, n, *refs):
    R = Refs()
    for name, ref in zip(names, refs):
        setattr(R, name, ref)
    C = Ctx(R.ssem, R.rsem, R.lsem)
    sem, count = barrier_start(C, n)
    half = R.wi.shape[2]
    off = pl.ds(al(C.x * half, half), half)
    wcp = [
        pltpu.make_async_copy(R.w_in.at[:, :, off], R.wi, C.lsem.at[2]),
        pltpu.make_async_copy(R.w_back.at[:, off, :], R.wb, C.lsem.at[3]),
    ]
    for cp in wcp:
        cp.start()
    R.sm[...] = jnp.zeros_like(R.sm)
    R.sm2[...] = jnp.zeros_like(R.sm2)
    R.sd[...] = jnp.zeros_like(R.sd)
    stage_qkv(R, C)
    pl.semaphore_wait(sem, count)
    all_to_all(R, C, R.asend, R.arecv, n)()
    stage_attend(R, C, n)
    stage_out(R, C)
    for cp in wcp:
        cp.wait()
    stage_moe(R, C)
    K = Kinds(half // 32, R.H2.shape[2] // 64)
    ring = Ring(R, C, K, LAG)
    wait_u = reduce8(R, C, R.YP, R.ly, R.sy, R.u)
    wait_x = reduce8(R, C, R.DXP, R.lx, R.sx, R.dx)
    stage_moe_grads(R, C, K, ring)
    wait_u()
    ring.run(2)
    wait_x()
    stage_owner(R, C)
    wait_da = gather4(R, C, R.DA)
    wait_res = gather4(R, C, R.RES)
    ring.run(3)
    wait_da()
    stage_out_back(R, C, n)
    wait_do = all_to_all(R, C, R.osend, R.dorecv, n)
    stage_out_grad(R, C)
    xo = C.send(R.A.at[:, 0:128, :], R.wi.at[:, 0:128, :], C.sems(1), C.xp)
    ring.run(3)
    wait_do()
    C.drain()
    stage_attend_back(R, C, n, ring)
    stage_qkv_back(R, C)
    wait_gin = gather4(R, C, R.GIN)
    small = small_tensor(R, C)
    ring.run(2)
    xq = stage_qkv_grad(R, C)
    small = small_dp(R, C, n, small)
    xo.wait_recv()
    add_tail(R, 0, 2)
    ring.run(K.o0 - ring.cur)
    for cp in xq:
        cp.wait_recv()
    add_tail(R, 2, 6)
    wait_gin()
    wait_res()
    ring.run(ring.total - ring.cur)
    small_end(R, C, n, small)
    ring.finish()
    C.drain()


def fast_local(args, n, nt):
    (tokens, g1, b1, w_qkv, qvb, w_out, out_b, g2, b2, router, w_in, in_b, w_back, back_b,
     routes, prefix, cot) = args
    S, span, D = tokens.shape
    rows = S * span
    F = w_qkv.shape[2]
    H = w_in.shape[2]
    half = H // 2
    total = n * span
    par = jnp.concatenate(
        [jnp.stack([g1, b1, out_b, g2, b2]), router.T, back_b, jnp.zeros((7, D), BF)], axis=0
    ).astype(F32)
    vm = pl.BlockSpec(memory_space=pltpu.VMEM)
    hbm = pl.BlockSpec(memory_space=pl.ANY)
    ins = [
        ("tok", tokens.reshape(rows, D), vm),
        ("par", par, vm),
        ("wqkv", w_qkv.transpose(1, 0, 2), vm),
        ("qvb", qvb, vm),
        ("wout", w_out, vm),
        ("routes", routes.reshape(1, rows), vm),
        ("prefix", prefix, pl.BlockSpec(memory_space=pltpu.SMEM)),
        ("cot", cot.reshape(rows, D), vm),
        ("inb", in_b, vm),
        ("w_in", w_in, hbm),
        ("w_back", w_back, hbm),
    ]
    sds = jax.ShapeDtypeStruct
    nch = half // 32 + D // 64 + 8
    outs = [
        ("RES", sds((nt, CH, D), BF), vm),
        ("GIN", sds((nt, CH, D), BF), vm),
        ("oB", sds((2, H, D), F32), hbm),
        ("oI", sds((2, D, H), F32), hbm),
        ("oQ", sds((3, D, F), F32), hbm),
        ("oO", sds((F, D), F32), hbm),
        ("XH", sds((2, nch, 64, 512), BF), hbm),
        ("osm", sds((16, D), F32), vm),
    ]
    V = pltpu.VMEM
    scr = [
        ("h1", V((rows, D), BF)),
        ("asend", V((n, 384, 128), BF)),
        ("arecv", V((n, 384, 128), BF)),
        ("Q", V((total, 128), BF)),
        ("K", V((total, 128), BF)),
        ("V", V((total, 128), BF)),
        ("DO", V((total, 128), BF)),
        ("of", V((total, 128), F32)),
        ("dq", V((total, 128), F32)),
        ("osend", V((n, 128, 128), BF)),
        ("orecv", V((n, 128, 128), BF)),
        ("dorecv", V((n, 128, 128), BF)),
        ("otok", V((rows, F), BF)),
        ("dproj", V((3, rows, F), BF)),
        ("p4", V((3, CH, D), BF)),
        ("l4", V((3, CH, D), BF)),
        ("x1", V((CH, D), F32)),
        ("u", V((CH, D), F32)),
        ("dx", V((CH, D), F32)),
        ("cols", V((CH, 128), F32)),
        ("H2", V((8, CH, D), BF)),
        ("GG", V((8, CH, D), BF)),
        ("META", V((8, CH, 128), BF)),
        ("wi", V((2, D, half), BF)),
        ("wb", V((2, half, D), BF)),
        ("A", V((2, 8 * CH, half), BF)),
        ("DH", V((2, 8 * CH, half), BF)),
        ("YP", V((8, CH, D), BF)),
        ("DXP", V((8, CH, D), BF)),
        ("ly", V((7, CH, D), BF)),
        ("lx", V((7, CH, D), BF)),
        ("sy", V((3, CH, D), BF)),
        ("sx", V((3, CH, D), BF)),
        ("DA", V((nt, CH, D), BF)),
        ("G", V((2, nch, 64, 512), BF)),
        ("L1", V((2, nch, 64, 512), BF)),
        ("FN", V((2, nch, 64, 512), BF)),
        ("SF", V((2, 2, 64, 512), F32)),
        ("SX", V((2, 2, 64, 512), F32)),
        ("sm", V((8, D), F32)),
        ("sm2", V((8, D), F32)),
        ("st", V((4, 16, D), F32)),
        ("sd", V((n, 16, D), F32)),
        ("ssem", pltpu.SemaphoreType.DMA((128 + 6 * nch,))),
        ("rsem", pltpu.SemaphoreType.DMA((128 + 6 * nch,))),
        ("lsem", pltpu.SemaphoreType.DMA((16,))),
    ]
    names = [i[0] for i in ins] + [o[0] for o in outs] + [s[0] for s in scr]
    res, gin, oB, oI, oQ, oO, _, osm = pl.pallas_call(
        functools.partial(body, names, n),
        out_shape=[o[1] for o in outs],
        in_specs=[i[2] for i in ins],
        out_specs=[o[2] for o in outs],
        scratch_shapes=[s[1] for s in scr],
        compiler_params=pltpu.CompilerParams(
            collective_id=0, has_side_effects=True, vmem_limit_bytes=67043328
        ),
        name="layer",
    )(*[i[1] for i in ins])
    inb = jnp.stack([osm[11].reshape(2, half), osm[12].reshape(2, half)], axis=1).reshape(2, H)
    return (
        res.reshape(S, span, D).astype(F32),
        gin.reshape(S, span, D).astype(F32),
        osm[8],
        osm[9],
        oQ.transpose(1, 0, 2),
        osm[10, : 2 * F].reshape(2, F),
        oO,
        osm[2],
        osm[0],
        osm[1],
        osm[3:5].T,
        oI,
        inb,
        oB,
        osm[5:7],
    )


SCALE = 0.125
EPSILON = 1e-05
MASKED = -1e30
HIGHEST = lax.Precision.HIGHEST


def layer_norm(values, norm_gain, norm_bias):
    centred = values - jnp.mean(values, axis=-1, keepdims=True)
    spread = jnp.mean(centred * centred, axis=-1, keepdims=True)
    return centred * lax.rsqrt(spread + EPSILON) * norm_gain + norm_bias


def heads_of(block, head_count):
    seq_count, row_count, feat_count = block.shape
    return block.reshape(seq_count, row_count, head_count, feat_count // head_count).transpose(
        0, 2, 1, 3
    )


def tokens_of(block):
    seq_count, head_count, row_count, head_width = block.shape
    return block.transpose(0, 2, 1, 3).reshape(seq_count, row_count, head_count * head_width)


def masked_scores(queries, key_heads, query_start, key_start, prefix):
    scores = (
        jnp.einsum("shqd,shkd->shqk", queries, key_heads, preferred_element_type=jnp.float32)
        * SCALE
    )
    query_pos = query_start + jnp.arange(queries.shape[2], dtype=jnp.int32)
    key_pos = key_start + jnp.arange(key_heads.shape[2], dtype=jnp.int32)
    visible_mask = (key_pos[None, None, :] <= query_pos[None, :, None]) | (
        key_pos[None, None, :] < prefix[:, None, None]
    )
    visible_mask = visible_mask[:, None]
    return (jnp.where(visible_mask, scores, MASKED), visible_mask)


def block_live(key_start, query_last, prefix):
    return jnp.any(key_start < prefix) | (key_start <= query_last)


def prob_grads(
    queries, key_heads, value_heads, douts, log_total, delta, query_start, key_start, prefix
):
    scores, visible_mask = masked_scores(queries, key_heads, query_start, key_start, prefix)
    probs = jnp.where(visible_mask, jnp.exp(scores - log_total[..., None]), 0.0)
    dprob = jnp.einsum("shqd,shkd->shqk", douts, value_heads, preferred_element_type=jnp.float32)
    dscore = (probs * (dprob - delta[..., None])).astype(jnp.bfloat16)
    return (probs, dscore)


def attend_fold(run_state, piece_rows, piece_start, queries, first_row, prefix):
    key_piece, value_piece = piece_rows
    head_count = queries.shape[1]
    row_count = key_piece.shape[1]
    block_width = math.gcd(row_count, 512)
    query_last = first_row + queries.shape[2] - 1

    def attend_update(block_index, state_now):
        key_start = block_index * block_width
        key_heads = heads_of(
            lax.dynamic_slice_in_dim(key_piece, block_index * block_width, block_width, 1),
            head_count,
        )
        value_heads = heads_of(
            lax.dynamic_slice_in_dim(value_piece, block_index * block_width, block_width, 1),
            head_count,
        )
        scores, visible_mask = masked_scores(queries, key_heads, first_row, key_start, prefix)
        run_max, run_sum, run_out = state_now
        new_max = jnp.maximum(run_max, jnp.max(scores, axis=-1))
        factor = jnp.exp(run_max - new_max)
        weights = jnp.where(visible_mask, jnp.exp(scores - new_max[..., None]), 0.0)
        run_sum = factor * run_sum + jnp.sum(weights, axis=-1)
        run_out = factor[..., None] * run_out + jnp.einsum(
            "shqk,shkd->shqd", weights, value_heads.astype(jnp.float32), precision=HIGHEST
        )
        return (new_max, run_sum, run_out)

    def attend_block_step(state_now, block_index):
        key_start = block_index * block_width
        is_live = block_live(key_start, query_last, prefix)
        return (
            lax.cond(
                is_live, functools.partial(attend_update, block_index), lambda unchanged: unchanged, state_now
            ),
            None,
        )

    run_state, unused = lax.scan(
        attend_block_step, run_state, jnp.arange(row_count // block_width, dtype=jnp.int32)
    )
    return run_state


def key_pass(queries, douts, log_total, delta, keys_all, values_all, first_row, prefix):
    head_count = queries.shape[1]
    total_rows = keys_all.shape[1]
    block_width = math.gcd(total_rows, 512)
    query_last = first_row + queries.shape[2] - 1

    def key_block_step(dquery, block_index):
        key_start = block_index * block_width

        def work(dquery_now):
            key_heads = heads_of(
                lax.dynamic_slice_in_dim(keys_all, key_start, block_width, 1), head_count
            )
            value_heads = heads_of(
                lax.dynamic_slice_in_dim(values_all, key_start, block_width, 1), head_count
            )
            probs, dscore = prob_grads(
                queries,
                key_heads,
                value_heads,
                douts,
                log_total,
                delta,
                first_row,
                key_start,
                prefix,
            )
            dquery_now = (
                dquery_now
                + jnp.einsum(
                    "shqk,shkd->shqd", dscore, key_heads, preferred_element_type=jnp.float32
                )
                * SCALE
            )
            return (dquery_now, ())

        def skipped(dquery_now):
            return (dquery_now, ())

        return lax.cond(block_live(key_start, query_last, prefix), work, skipped, dquery)

    dquery, key_parts = lax.scan(
        key_block_step,
        jnp.zeros(queries.shape, jnp.float32),
        jnp.arange(total_rows // block_width, dtype=jnp.int32),
    )
    return (dquery, ())


def query_fold(run_state, piece_rows, piece_start, key_heads, value_heads, first_row, prefix):
    query_piece, dout_piece, total_piece, delta_piece = piece_rows
    head_count = key_heads.shape[1]
    row_count = query_piece.shape[1]
    block_width = math.gcd(row_count, 512)

    def query_update(block_index, state_now):
        query_start = block_index * block_width
        offset = block_index * block_width
        queries = heads_of(
            lax.dynamic_slice_in_dim(query_piece, offset, block_width, 1), head_count
        )
        douts = heads_of(lax.dynamic_slice_in_dim(dout_piece, offset, block_width, 1), head_count)
        log_total = lax.dynamic_slice_in_dim(total_piece, offset, block_width, 1).transpose(0, 2, 1)
        delta = lax.dynamic_slice_in_dim(delta_piece, offset, block_width, 1).transpose(0, 2, 1)
        probs, dscore = prob_grads(
            queries, key_heads, value_heads, douts, log_total, delta, query_start, first_row, prefix
        )
        dkey_now, dvalue_now = state_now
        dkey_now = (
            dkey_now
            + jnp.einsum("shqk,shqd->shkd", dscore, queries, preferred_element_type=jnp.float32)
            * SCALE
        )
        dvalue_now = dvalue_now + jnp.einsum(
            "shqk,shqd->shkd", probs, douts.astype(jnp.float32), precision=HIGHEST
        )
        return (dkey_now, dvalue_now)

    def query_block_step(state_now, block_index):
        query_last = block_index * block_width + block_width - 1
        is_live = block_live(first_row, query_last, prefix)
        return (
            lax.cond(
                is_live, functools.partial(query_update, block_index), lambda unchanged: unchanged, state_now
            ),
            None,
        )

    run_state, unused = lax.scan(
        query_block_step, run_state, jnp.arange(row_count // block_width, dtype=jnp.int32)
    )
    return run_state


def local(
    tokens,
    ln1_gain,
    ln1_bias,
    w_qkv,
    qv_bias,
    w_out,
    out_bias,
    ln2_gain,
    ln2_bias,
    router,
    w_in,
    in_bias,
    w_back,
    back_bias,
    routes,
    prefix,
    cotangent,
):
    seq_count, span_len, model_width = tokens.shape
    tok_rows = seq_count * span_len
    local_feats = w_qkv.shape[2]
    head_count = local_feats // HEAD_DIM
    expert_count = w_in.shape[0]
    first_row = lax.axis_index("dp") * span_len
    local_shape = (seq_count, span_len, local_feats)
    source = tokens.reshape(tok_rows, model_width).astype(jnp.float32)
    normed_one, ln1_pull = jax.vjp(
        layer_norm, source, ln1_gain.astype(jnp.float32), ln1_bias.astype(jnp.float32)
    )
    hidden_one = normed_one.astype(jnp.bfloat16)
    projected = jnp.einsum("ti,icf->tcf", hidden_one, w_qkv, preferred_element_type=jnp.float32)
    bias_float = qv_bias.astype(jnp.float32)
    query_tok = (projected[:, 0] + bias_float[0]).astype(jnp.bfloat16).reshape(local_shape)
    key_tok = projected[:, 1].astype(jnp.bfloat16).reshape(local_shape)
    value_tok = (projected[:, 2] + bias_float[1]).astype(jnp.bfloat16).reshape(local_shape)
    queries = heads_of(query_tok, head_count)
    stat_shape = queries.shape[:3]
    start_state = (
        jnp.full(stat_shape, MASKED, jnp.float32),
        jnp.zeros(stat_shape, jnp.float32),
        jnp.zeros(queries.shape, jnp.float32),
    )
    fold_keys = functools.partial(attend_fold, queries=queries, first_row=first_row, prefix=prefix)
    run_max, run_sum, run_out = fold_keys(
        start_state,
        (
            lax.all_gather(key_tok, "dp", axis=1, tiled=True),
            lax.all_gather(value_tok, "dp", axis=1, tiled=True),
        ),
        jnp.int32(0),
    )
    mixed_heads = run_out / run_sum[..., None]
    log_total = run_max + jnp.log(run_sum)
    mixed_b = tokens_of(mixed_heads.astype(jnp.bfloat16)).reshape(tok_rows, local_feats)
    out_shift = out_bias.astype(jnp.float32)
    gain_two = ln2_gain.astype(jnp.float32)
    shift_two = ln2_bias.astype(jnp.float32)
    attn_part = jnp.dot(mixed_b, w_out, preferred_element_type=jnp.float32)
    attn_out = lax.psum(attn_part, "tensor") + out_shift
    residual = source + attn_out
    normed_two, ln2_pull = jax.vjp(layer_norm, residual, gain_two, shift_two)
    hidden_two = normed_two.astype(jnp.bfloat16)
    logits = jnp.dot(hidden_two, router, preferred_element_type=jnp.float32)
    chosen = routes.reshape(tok_rows)
    expert_ids = jnp.arange(expert_count, dtype=jnp.int32)
    expert_hot = (chosen[:, None] == expert_ids[None, :]).astype(jnp.int32)

    def gate_of(logit_vals):
        return jnp.sum(
            jnp.where(expert_hot == 1, jax.nn.softmax(logit_vals, axis=-1), 0.0), axis=-1
        )

    gate_value, gate_pull = jax.vjp(gate_of, logits)
    earlier = jnp.cumsum(expert_hot, axis=0, dtype=jnp.int32) - expert_hot
    slot_place = jnp.sum(earlier * expert_hot, axis=1, dtype=jnp.int32)
    slot_ids = jnp.arange(CAP, dtype=jnp.int32)
    select_mask = (expert_hot[:, :, None] == 1) & (
        slot_place[:, None, None] == slot_ids[None, None, :]
    )
    select = select_mask.astype(jnp.bfloat16)
    select_float = select_mask.astype(jnp.float32)
    dispatched = jnp.einsum(
        "tec,td->ecd", select, hidden_two, preferred_element_type=jnp.float32
    ).astype(jnp.bfloat16)
    pre_act = (
        jnp.einsum("ecd,edf->ecf", dispatched, w_in, preferred_element_type=jnp.float32)
        + in_bias.astype(jnp.float32)[:, None, :]
    )
    act_float, gelu_pull = jax.vjp(functools.partial(jax.nn.gelu, approximate=False), pre_act)
    active = act_float.astype(jnp.bfloat16)
    expert_part = jnp.einsum("ecf,efd->ecd", active, w_back, preferred_element_type=jnp.float32)
    expert_full = lax.psum(expert_part, "tensor") + back_bias.astype(jnp.float32)[:, None, :]
    combined = jnp.einsum("tec,ecd->td", select_float, expert_full, precision=HIGHEST)
    layer_rows = residual + gate_value[:, None] * combined
    grad_out = cotangent.reshape(tok_rows, model_width).astype(jnp.float32)
    dgate = jnp.sum(grad_out * combined, axis=-1)
    dlogit_b = gate_pull(dgate)[0].astype(jnp.bfloat16)
    gated_grad = (gate_value[:, None] * grad_out).astype(jnp.bfloat16)
    dexpert_b = jnp.einsum(
        "tec,td->ecd", select, gated_grad, preferred_element_type=jnp.float32
    ).astype(jnp.bfloat16)
    grad_back_bias = jnp.sum(dexpert_b, axis=1, dtype=jnp.float32)
    grad_w_back = jnp.einsum("ecf,ecd->efd", active, dexpert_b, preferred_element_type=jnp.float32)
    dactive = jnp.einsum("ecd,efd->ecf", dexpert_b, w_back, preferred_element_type=jnp.float32)
    dpre_b = gelu_pull(dactive)[0].astype(jnp.bfloat16)
    grad_in_bias = jnp.sum(dpre_b, axis=1, dtype=jnp.float32)
    grad_w_in = jnp.einsum("ecd,ecf->edf", dispatched, dpre_b, preferred_element_type=jnp.float32)
    slot_part = jnp.einsum("ecf,edf->ecd", dpre_b, w_in, preferred_element_type=jnp.float32)
    dslots = lax.psum(slot_part, "tensor")
    dnorm_two = jnp.einsum("tec,ecd->td", select_float, dslots, precision=HIGHEST) + jnp.einsum(
        "te,de->td", dlogit_b, router, preferred_element_type=jnp.float32
    )
    grad_router = jnp.einsum("td,te->de", hidden_two, dlogit_b, preferred_element_type=jnp.float32)
    dresid_norm, grad_ln2_gain, grad_ln2_bias = ln2_pull(dnorm_two)
    dresidual = grad_out + dresid_norm
    dattn_b = dresidual.astype(jnp.bfloat16)
    grad_out_bias = jnp.sum(dattn_b, axis=0, dtype=jnp.float32)
    grad_w_out = jnp.einsum("tf,td->fd", mixed_b, dattn_b, preferred_element_type=jnp.float32)
    dmixed_tok = (
        jnp.einsum("td,fd->tf", dattn_b, w_out, preferred_element_type=jnp.float32)
        .astype(jnp.bfloat16)
        .reshape(local_shape)
    )
    douts = heads_of(dmixed_tok, head_count)
    delta = jnp.sum(douts.astype(jnp.float32) * mixed_heads, axis=-1)
    keys_all, values_all = (
        lax.all_gather(key_tok, "dp", axis=1, tiled=True),
        lax.all_gather(value_tok, "dp", axis=1, tiled=True),
    )
    dquery, unused = key_pass(
        queries, douts, log_total, delta, keys_all, values_all, first_row, prefix
    )
    total_rows = log_total.transpose(0, 2, 1)
    delta_rows = delta.transpose(0, 2, 1)
    fold_rows = functools.partial(
        query_fold,
        key_heads=heads_of(key_tok, head_count),
        value_heads=heads_of(value_tok, head_count),
        first_row=first_row,
        prefix=prefix,
    )
    zero_heads = jnp.zeros(queries.shape, jnp.float32)
    dkey_heads, dvalue_heads = fold_rows(
        (zero_heads, zero_heads),
        (
            lax.all_gather(query_tok, "dp", axis=1, tiled=True),
            lax.all_gather(dmixed_tok, "dp", axis=1, tiled=True),
            lax.all_gather(total_rows.astype(jnp.bfloat16), "dp", axis=1, tiled=True).astype(
                jnp.float32
            ),
            lax.all_gather(delta_rows.astype(jnp.bfloat16), "dp", axis=1, tiled=True).astype(
                jnp.float32
            ),
        ),
        jnp.int32(0),
    )
    dkey = tokens_of(dkey_heads)
    dvalue = tokens_of(dvalue_heads)
    dquery_b = tokens_of(dquery).astype(jnp.bfloat16).reshape(tok_rows, local_feats)
    dkey_b = dkey.astype(jnp.bfloat16).reshape(tok_rows, local_feats)
    dvalue_b = dvalue.astype(jnp.bfloat16).reshape(tok_rows, local_feats)
    dproject = jnp.stack([dquery_b, dkey_b, dvalue_b], axis=1)
    grad_qv_bias = jnp.stack(
        [jnp.sum(dquery_b, axis=0, dtype=jnp.float32), jnp.sum(dvalue_b, axis=0, dtype=jnp.float32)]
    )
    grad_w_qkv = jnp.einsum("ti,tcf->icf", hidden_one, dproject, preferred_element_type=jnp.float32)
    norm_part = jnp.einsum("tcf,icf->ti", dproject, w_qkv, preferred_element_type=jnp.float32)
    dnorm_one = lax.psum(norm_part, "tensor")
    dsource_norm, grad_ln1_gain, grad_ln1_bias = ln1_pull(dnorm_one)
    input_grad = (dresidual + dsource_norm).reshape(seq_count, span_len, model_width)
    summed = lax.psum(
        (
            grad_ln1_gain,
            grad_ln1_bias,
            grad_w_qkv,
            grad_qv_bias,
            grad_w_out,
            grad_out_bias,
            grad_ln2_gain,
            grad_ln2_bias,
            grad_router,
            grad_w_in,
            grad_in_bias,
            grad_w_back,
            grad_back_bias,
        ),
        "dp",
    )
    layer_out = layer_rows.reshape(seq_count, span_len, model_width)
    return (layer_out, input_grad) + tuple(summed)


def solution(mesh):
    in_specs = (
        P(None, "dp", None),
        P(),
        P(),
        P(None, None, "tensor"),
        P(None, "tensor"),
        P("tensor", None),
        P(),
        P(),
        P(),
        P(),
        P(None, None, "tensor"),
        P(None, "tensor"),
        P(None, "tensor", None),
        P(),
        P(None, "dp", None),
        P(),
        P(None, "dp", None),
    )
    out_specs = (
        P(None, "dp", None),
        P(None, "dp", None),
        P(),
        P(),
        P(None, None, "tensor"),
        P(None, "tensor"),
        P("tensor", None),
        P(),
        P(),
        P(),
        P(),
        P(None, None, "tensor"),
        P(None, "tensor"),
        P(None, "tensor", None),
        P(),
    )
    n, nt = mesh.shape["dp"], mesh.shape["tensor"]

    def step(*args):
        tokens, w_qkv = args[0], args[3]
        heads = w_qkv.shape[2] // HEAD_DIM
        fits = (
            nt == 4
            and n == 8
            and tokens.shape[2] == 1024
            and w_qkv.shape[2] == 256
            and args[10].shape == (2, 1024, 1024)
            and n == tokens.shape[0] * heads
            and tokens.shape[0] * tokens.shape[1] == nt * CH
            and tokens.shape[1] == 256
        )
        return fast_local(args, n, nt) if fits else local(*args)

    return jax.shard_map(step, mesh=mesh, in_specs=in_specs, out_specs=out_specs, check_vma=False)
```

```python
import functools
import math

import jax
import jax.numpy as jnp
from jax import lax
from jax.experimental import pallas as pl
from jax.experimental.pallas import tpu as pltpu
from jax.sharding import PartitionSpec as P

F32 = jnp.float32
BF = jnp.bfloat16
MESH = pl.DeviceIdType.MESH
EPS = 1e-05
CAP = 320
HEAD_DIM = 64
NEG = -1e30
CH = 128


def mm(a, b):
    return lax.dot_general(a, b, (((1,), (0,)), ((), ())), preferred_element_type=F32)


def mm_bt(a, b):
    return lax.dot_general(a, b, (((1,), (1,)), ((), ())), preferred_element_type=F32)


def mm_at(a, b):
    return lax.dot_general(a, b, (((0,), (0,)), ((), ())), preferred_element_type=F32)


def loop(n, body):
    def step(i, carry):
        body(i)
        return carry

    lax.fori_loop(0, n, step, 0)


def al(v, m):
    return pl.multiple_of(v, m)


def lanes(rows):
    return lax.broadcasted_iota(jnp.int32, (rows, 128), 1)


def roll64(v):
    return pltpu.roll(v, 64, 1)


class Ctx:
    def __init__(self, ssem, rsem, lsem):
        self.ssem, self.rsem, self.lsem = ssem, rsem, lsem
        self.next = 0
        self.pending = []
        dp = lax.axis_index("dp")
        t = lax.axis_index("tensor")
        self.dp, self.t = dp, t
        self.z, self.x = dp // 2, lax.rem(dp, 2)
        self.y, self.c = t // 2, lax.rem(t, 2)
        x1 = 1 - self.x
        dpx = self.z * 2 + x1
        tm = self.y * 2 + 1 - self.c
        ty = (1 - self.y) * 2 + self.c
        self.mate = (dp, tm)
        self.yp = (dp, ty)
        self.xp = (dpx, t)
        self.dg = (dpx, ty)
        self.t_mate, self.t_y = tm, ty

    def sems(self, n):
        k = self.next
        self.next += n
        return k

    def rc(self, src, dst, k, dev, kr=None):
        return pltpu.make_async_remote_copy(
            src_ref=src,
            dst_ref=dst,
            send_sem=self.ssem.at[k],
            recv_sem=self.rsem.at[k if kr is None else kr],
            device_id=dev,
            device_id_type=MESH,
        )

    def send(self, src, dst, k, dev):
        cp = self.rc(src, dst, k, dev)
        cp.start()
        self.pending.append(cp)
        return cp

    def drain(self):
        for cp in self.pending:
            cp.wait_send()
        self.pending = []


def barrier_start(C, n_dp):
    sem = pltpu.get_barrier_semaphore()
    devs = [(lax.rem(C.dp + o, n_dp), C.t) for o in range(1, n_dp)]
    devs += [C.mate, C.yp, C.dg, (C.dp, 3 - C.t)]
    for d in devs:
        pl.semaphore_signal(sem, inc=1, device_id=d, device_id_type=MESH)
    return sem, len(devs)


def norm_parts(v):
    mean = jnp.mean(v, axis=-1, keepdims=True)
    cent = v - mean
    var = jnp.mean(cent * cent, axis=-1, keepdims=True)
    r = lax.rsqrt(var + EPS)
    return cent * r, r


def stage_qkv(R, C, n):
    rows = R.tok.shape[0]
    gain, bias = R.par[0:1, :], R.par[1:2, :]
    hp = R.wqkv.shape[2] // HEAD_DIM
    k = C.sems(n)

    def seq(s):
        def ln(i):
            at = pl.ds(al(s * 256 + i * 32, 32), 32)
            n1, _ = norm_parts(R.tok[at, :].astype(F32))
            R.h1[at, :] = (n1 * gain + bias).astype(BF)

        loop(8, ln)
        at = pl.ds(al(s * 256, 256), 256)
        h = R.h1[at, :]
        lo = lanes(256) < 64
        lo2 = lanes(128) < 64
        for pr in range(hp // 2):
            cut = slice(pr * 128, pr * 128 + 128)
            tq = (mm(h, R.wqkv[0, :, cut]) + R.qvb[0:1, cut].astype(F32)) * 0.125
            tk = mm(h, R.wqkv[1, :, cut])
            tv = mm(h, R.wqkv[2, :, cut]) + R.qvb[1:2, cut].astype(F32)
            p = s * hp + 2 * pr
            R.asend[p, 0:256, :] = jnp.where(lo, tq, roll64(tk)).astype(BF)
            R.asend[p + 1, 0:256, :] = jnp.where(lo, roll64(tq), tk).astype(BF)
            a, b = tv[0:128], tv[128:256]
            R.asend[p, 256:384, :] = jnp.where(lo2, a, roll64(b)).astype(BF)
            R.asend[p + 1, 256:384, :] = jnp.where(lo2, roll64(a), b).astype(BF)
            for j in range(2):
                send_slice(C, R.asend, R.arecv, k, p + j)

    loop(rows // 256, seq)
    return lambda: wait_slices(C, R.asend, R.arecv, k, n, 0)


def send_slice(C, src, dst, k, p):
    @pl.when(p != C.dp)
    def _():
        C.rc(src.at[p], dst.at[C.dp], k + p, (p, C.t), k + C.dp).start()


def wait_slices(C, src, dst, k, n, sem):
    mine = pltpu.make_async_copy(src.at[C.dp], dst.at[C.dp], C.lsem.at[sem])
    mine.start()
    mine.wait()
    for b in range(n):

        @pl.when(b != C.dp)
        def _():
            cp = C.rc(src.at[b], dst.at[b], k + b, (b, C.t), k + b)
            cp.wait_send()
            cp.wait_recv()


def all_to_all(R, C, src, dst, n):
    k = C.sems(n)
    cps = [
        C.send(src.at[lax.rem(C.dp + o, n)], dst.at[C.dp], k + o, (lax.rem(C.dp + o, n), C.t))
        for o in range(1, n)
    ]
    mine = pltpu.make_async_copy(src.at[C.dp], dst.at[C.dp], C.lsem.at[0])
    mine.start()

    def wait():
        mine.wait()
        for cp in cps:
            cp.wait_recv()

    return wait


def stage_attend(R, C, n):
    lo = lanes(256) < 64
    lo2 = lanes(128) < 64
    one = jnp.where((lanes(256) == 64) | (lanes(256) == 65), 1.0, 0.0)
    one2 = one[0:128]

    def unpack(b):
        qk = R.arecv[b, 0:256, :].astype(F32)
        vf = R.arecv[b, 256:384, :].astype(F32)
        at = pl.ds(al(b * 256, 256), 256)
        R.Q[at, :] = jnp.where(lo, qk, 0.0).astype(BF)
        R.K[at, :] = jnp.where(lo, roll64(qk), one).astype(BF)
        R.V[pl.ds(al(b * 256, 128), 128), :] = jnp.where(lo2, vf, one2).astype(BF)
        R.V[pl.ds(al(b * 256 + 128, 128), 128), :] = jnp.where(lo2, roll64(vf), one2).astype(BF)

    loop(n, unpack)
    T = 512
    half = R.Q.shape[0] // 2 // T - 1
    seqs = R.prefix.shape[0]
    prefix = R.prefix[C.dp // (n // seqs)]
    k = C.sems(n)

    def rows_of(i):
        at = pl.ds(al(i * T, T), T)
        q = R.Q[at, :]
        qpos = i * T + lax.broadcasted_iota(jnp.int32, (T, 1), 0)
        lim = jnp.maximum(qpos, prefix - 1)

        def tile(j, carry):
            m, acc = carry
            kat = pl.ds(al(j * T, T), T)
            s = mm_bt(q, R.K[kat, :])
            kpos = j * T + lax.broadcasted_iota(jnp.int32, (T, T), 1)
            s = jnp.where(kpos <= lim, s, NEG)
            m2 = jnp.maximum(m, jnp.max(s, axis=1, keepdims=True))
            p = jnp.exp(s - m2).astype(BF)
            acc = acc * jnp.exp(m - m2) + mm(p, R.V[kat, :])
            return m2, acc

        m, acc = lax.fori_loop(
            0,
            jnp.maximum(i, half) + 1,
            tile,
            (jnp.full((T, 1), NEG, F32), jnp.zeros((T, 128), F32)),
        )
        total = acc[:, 64:65]
        o = acc / total
        lse = m + jnp.log(total)
        R.of[at, :] = jnp.where(lanes(T) < 64, o, lse)
        for u in range(2):
            b = i * 2 + u
            top, bot = o[u * 256 : u * 256 + 128], o[u * 256 + 128 : u * 256 + 256]
            R.osend[b] = jnp.where(lo2, top, roll64(bot)).astype(BF)

            @pl.when(b != C.dp)
            def _():
                C.rc(R.osend.at[b], R.orecv.at[C.dp], k + b, (b, C.t), k + C.dp).start()

    loop(R.Q.shape[0] // T, rows_of)
    mine = pltpu.make_async_copy(R.osend.at[C.dp], R.orecv.at[C.dp], C.lsem.at[0])
    mine.start()
    mine.wait()
    for b in range(n):

        @pl.when(b != C.dp)
        def _():
            cp = C.rc(R.osend.at[b], R.orecv.at[b], k + b, (b, C.t), k + b)
            cp.wait_send()
            cp.wait_recv()

    unfold_heads(R.orecv, R.otok, n, seqs)


def unfold_heads(src, dst, n, seqs):
    hp = n // seqs
    lo2 = lanes(128) < 64
    for s in range(seqs):
        for pr in range(hp // 2):
            e = src[s * hp + 2 * pr].astype(F32)
            d = src[s * hp + 2 * pr + 1].astype(F32)
            cut = slice(pr * 128, pr * 128 + 128)
            dst[s * 256 : s * 256 + 128, cut] = jnp.where(lo2, e, roll64(d)).astype(BF)
            dst[s * 256 + 128 : s * 256 + 256, cut] = jnp.where(lo2, roll64(e), d).astype(BF)


def swap_cot(R, C):
    k = C.sems(2)
    rows = R.cot.shape[0] // 2
    mine = pl.ds(al(C.c * rows, rows), rows)
    cp = C.send(R.cot.at[mine, :], R.cx.at[mine, :], k, C.xp)

    def wait():
        cp.wait_recv()
        C.send(R.cx.at[mine, :], R.cx.at[mine, :], k + 1, C.mate).wait_recv()

    return wait


def reduce4(R, C, part, out):
    k = C.sems(3)
    k0 = (1 - C.y) * 2 + (1 - C.c)
    k1 = (1 - C.y) * 2 + C.c
    k2 = C.y * 2 + (1 - C.c)
    R.p4[0] = part(k0).astype(BF)
    c0 = C.send(R.p4.at[0], R.l4.at[0], k, C.mate)
    v1 = part(k1)
    c0.wait_recv()
    R.p4[1] = (v1 + R.l4[0].astype(F32)).astype(BF)
    c1 = C.send(R.p4.at[1], R.l4.at[2], k + 1, C.yp)
    R.p4[2] = part(k2).astype(BF)
    c2 = C.send(R.p4.at[2], R.l4.at[1], k + 2, C.mate)
    out[...] = part(C.t)
    c2.wait_recv()
    c1.wait_recv()
    out[...] = out[...] + R.l4[1].astype(F32) + R.l4[2].astype(F32)


def gather4(R, C, buf):
    k = C.sems(3)
    mine = buf.at[C.t]
    cy = C.send(mine, mine, k, C.yp)
    cm = C.send(mine, mine, k + 1, C.mate)

    def wait():
        cy.wait_recv()
        fwd = C.send(buf.at[C.t_y], buf.at[C.t_y], k + 2, C.mate)
        cm.wait_recv()
        fwd.wait_recv()

    return wait


def gather8(R, C, buf):
    k = C.sems(7)
    mine = buf.at[C.x * 4 + C.t]
    cd = C.send(mine, mine, k, C.dg)
    cx = C.send(mine, mine, k + 1, C.xp)
    cy = C.send(mine, mine, k + 2, C.yp)
    cm = C.send(mine, mine, k + 3, C.mate)

    def wait():
        fw = []
        for i, (cp, slot) in enumerate(
            (
                (cy, C.x * 4 + C.t_y),
                (cx, (1 - C.x) * 4 + C.t),
                (cd, (1 - C.x) * 4 + C.t_y),
            )
        ):
            cp.wait_recv()
            fw.append(C.send(buf.at[slot], buf.at[slot], k + 4 + i, C.mate))
        cm.wait_recv()
        for cp in fw:
            cp.wait_recv()

    return wait


def stage_out(R, C):
    def part(k):
        return mm(R.otok[pl.ds(al(k * CH, CH), CH), :], R.wout[...])

    reduce4(R, C, part, R.x1)
    rows = R.tok.shape[0]
    own = pl.ds(al(C.t * CH, CH), CH)
    pos = C.t * CH + lax.broadcasted_iota(jnp.int32, (CH, rows), 0)
    col = lax.broadcasted_iota(jnp.int32, (CH, rows), 1)
    hot = jnp.where(
        R.routes[...] == lax.broadcasted_iota(jnp.int32, (8, rows), 0), 1.0, 0.0
    ).astype(BF)
    earlier = mm_bt(jnp.where(col < pos, 1.0, 0.0).astype(BF), hot)
    here = mm_bt(jnp.where(col == pos, 1.0, 0.0).astype(BF), hot)
    keep = jnp.where(earlier < CAP, here, 0.0)
    keep0, keep1 = keep[:, 0:1], keep[:, 1:2]
    x1 = R.x1[...] + R.tok[own, :].astype(F32) + R.par[2:3, :]
    R.x1[...] = x1
    n, r = norm_parts(x1)
    h2 = (n * R.par[3:4, :] + R.par[4:5, :]).astype(BF)
    slot = C.x * 4 + C.t
    R.H2[slot] = h2
    hf = h2.astype(F32)
    l0 = jnp.sum(hf * R.par[5:6, :], axis=1, keepdims=True)
    l1 = jnp.sum(hf * R.par[6:7, :], axis=1, keepdims=True)
    mx = jnp.maximum(l0, l1)
    e0, e1 = jnp.exp(l0 - mx), jnp.exp(l1 - mx)
    p0, p1 = e0 / (e0 + e1), e1 / (e0 + e1)
    gate = here[:, 0:1] * p0 + here[:, 1:2] * p1
    ln = lanes(CH)
    hi = gate.astype(BF).astype(F32)
    mid = (gate - hi).astype(BF).astype(F32)
    meta = jnp.zeros((CH, 128), F32)
    for i, v in enumerate((keep0, keep1, hi, mid, gate - hi - mid)):
        meta = jnp.where(ln == i, v, meta)
    R.META[slot] = meta.astype(BF)
    wait_h = gather8(R, C, R.H2)
    wait_m = gather8(R, C, R.META)
    cols = jnp.zeros((CH, 128), F32)
    for i, v in enumerate((p0, p1, here[:, 0:1], here[:, 1:2], gate, keep0, keep1)):
        cols = jnp.where(ln == i, v, cols)
    R.cols[...] = cols
    wait_h()
    wait_m()

    def gated(i):
        for xx, cot in ((C.x, R.cot), (1 - C.x, R.cx)):
            m = R.META[xx * 4 + i].astype(F32)
            gate = m[:, 2:3] + m[:, 3:4] + m[:, 4:5]
            g = cot[pl.ds(al(i * CH, CH), CH), :].astype(F32)
            gr = (gate * g).astype(BF).astype(F32)
            R.GG[xx * 4 + i] = (gr * (m[:, 0:1] + m[:, 1:2])).astype(BF)

    loop(4, gated)


def gelu_both(h):
    half = 0.5 * (1.0 + lax.erf(h * 0.7071067811865476))
    return h * half, half + h * (jnp.exp(-0.5 * h * h) * 0.3989422804014327)


def stage_moe(R, C):
    def tile(i):
        two = pl.ds(al(2 * i, 2), 2)
        at = pl.ds(al(i * 256, 256), 256)
        h2 = R.H2[two].reshape(256, R.H2.shape[2])
        gg = R.GG[two].reshape(256, R.GG.shape[2])
        meta = R.META[two].reshape(256, 128).astype(F32)
        m0, m1 = meta[:, 0:1], meta[:, 1:2]
        half = R.wi.shape[2]
        bias0 = R.inb[0:1, pl.ds(al(C.x * half, half), half)].astype(F32)
        bias1 = R.inb[1:2, pl.ds(al(C.x * half, half), half)].astype(F32)
        for q in range(half // 256):
            cut = slice(q * 256, q * 256 + 256)
            h0 = mm(h2, R.wi[0, :, cut]) + bias0[:, cut]
            h1 = mm(h2, R.wi[1, :, cut]) + bias1[:, cut]
            act, slope = gelu_both(jnp.where(m0 > 0.0, h0, h1))
            R.A[0, at, cut] = (act * m0).astype(BF)
            R.A[1, at, cut] = (act * m1).astype(BF)
            d0 = mm_bt(gg, R.wb[0, cut, :])
            d1 = mm_bt(gg, R.wb[1, cut, :])
            dh = jnp.where(m0 > 0.0, d0, d1) * slope
            R.DH[0, at, cut] = (dh * m0).astype(BF)
            R.DH[1, at, cut] = (dh * m1).astype(BF)
        y = mm(R.A[0, at, :], R.wb[0]) + mm(R.A[1, at, :], R.wb[1])
        R.YP[two] = y.astype(BF).reshape(2, CH, y.shape[1])
        dx = mm_bt(R.DH[0, at, :], R.wi[0]) + mm_bt(R.DH[1, at, :], R.wi[1])
        R.DXP[two] = dx.astype(BF).reshape(2, CH, dx.shape[1])

    loop(4, tile)


def put_wide(at, v):
    w = v.shape[1] // 2
    at[0:32, :] = v[:, 0:w].astype(BF)
    at[32:64, :] = v[:, w : 2 * w].astype(BF)


def stage_moe_grads(R, C, K, ring):
    rows = R.GG.shape[0] * CH

    def back(i):
        at = pl.ds(al(i * 128, 128), 128)
        gg = R.GG[...].reshape(rows, R.GG.shape[2])
        for e in range(2):
            v = mm_at(R.A[e, :, at], gg)
            for j in range(4):
                put_wide(R.G.at[e, 4 * i + j], v[32 * j : 32 * j + 32])

    loop(R.A.shape[2] // 128, back)
    ring.run(3)
    base = ring.take(R.H2.shape[2] // 256)

    def into(i):
        at = pl.ds(al(i * 128, 128), 128)
        h2t = R.H2[:, :, at].reshape(rows, 128)
        for e in range(2):
            v = mm_at(h2t, R.DH[e]).astype(BF)
            R.G[e, K.i0 + 2 * i] = v[0:64]
            R.G[e, K.i0 + 2 * i + 1] = v[64:128]

        @pl.when(lax.rem(i, 2) == 1)
        def _():
            ring.tick(base + i // 2)

    loop(R.H2.shape[2] // 128, into)


def reduce8(R, C, parts, land, stage, out):
    k = C.sems(7)
    order = ((1 - C.x, 1 - C.y), (1 - C.x, C.y), (C.x, 1 - C.y), (C.x, C.y))
    devs = (C.dg, C.xp, C.yp)
    cm = []
    for n, (xx, yy) in enumerate(order):
        cm.append(C.send(parts.at[xx * 4 + yy * 2 + 1 - C.c], land.at[n], k + n, C.mate))
    cr = []
    for n, (xx, yy) in enumerate(order):
        cm[n].wait_recv()
        v = parts[xx * 4 + yy * 2 + C.c].astype(F32) + land[n].astype(F32)
        if n < 3:
            stage[n] = v.astype(BF)
            cr.append(C.send(stage.at[n], land.at[4 + n], k + 4 + n, devs[n]))
        else:
            out[...] = v

    def wait():
        for n in range(3):
            cr[n].wait_recv()
        out[...] = (
            out[...] + land[4].astype(F32) + land[5].astype(F32) + land[6].astype(F32)
        )

    return wait


def norm_back(n, r, dn):
    return r * (
        dn - jnp.mean(dn, axis=-1, keepdims=True) - n * jnp.mean(dn * n, axis=-1, keepdims=True)
    )


def rowsum(v):
    return jnp.sum(v, axis=0, keepdims=True)


def stage_owner(R, C):
    own = pl.ds(al(C.t * CH, CH), CH)
    cols = R.cols[...]
    p0, p1, h0, h1, gate, k0, k1 = (cols[:, i : i + 1] for i in range(7))
    u = R.u[...] + k0 * R.par[7:8, :] + k1 * R.par[8:9, :]
    g = R.cot[own, :].astype(F32)
    x1 = R.x1[...]
    R.RES[C.t] = (x1 + gate * u).astype(BF)
    dg = jnp.sum(g * u, axis=1, keepdims=True) * gate
    dl0 = (dg * (h0 - p0)).astype(BF).astype(F32)
    dl1 = (dg * (h1 - p1)).astype(BF).astype(F32)
    h2 = R.H2[C.x * 4 + C.t].astype(F32)
    gg = R.GG[C.x * 4 + C.t].astype(F32)
    dh2 = R.dx[...] + dl0 * R.par[5:6, :] + dl1 * R.par[6:7, :]
    n, r = norm_parts(x1)
    dx1 = g + norm_back(n, r, dh2 * R.par[3:4, :])
    da = dx1.astype(BF)
    R.DA[C.t] = da
    R.x1[...] = dx1
    R.sm[0:1, :] = rowsum(dh2 * n)
    R.sm[1:2, :] = rowsum(dh2)
    R.sm[2:3, :] = rowsum(da.astype(F32))
    R.sm[3:4, :] = rowsum(h2 * dl0)
    R.sm[4:5, :] = rowsum(h2 * dl1)
    R.sm[5:6, :] = rowsum(gg * k0)
    R.sm[6:7, :] = rowsum(gg * k1)


def stage_out_back(R, C, n):
    seqs = R.prefix.shape[0]
    hp = n // seqs
    lo2 = lanes(128) < 64
    for s in range(seqs):
        da = R.DA[2 * s : 2 * s + 2].reshape(256, R.DA.shape[2])
        for pr in range(hp // 2):
            cut = slice(pr * 128, pr * 128 + 128)
            d = mm_bt(da, R.wout[cut, :])
            a, b = d[0:128], d[128:256]
            R.osend[s * hp + 2 * pr] = jnp.where(lo2, a, roll64(b)).astype(BF)
            R.osend[s * hp + 2 * pr + 1] = jnp.where(lo2, roll64(a), b).astype(BF)


def tail_of(buf, d, c, n=1):
    return buf.at[d, 64 * c : 64 * (c + n), :]


def stage_out_grad(R, C):
    da = R.DA[...].reshape(R.otok.shape[0], R.DA.shape[2])
    ho = R.otok.shape[1] // 2
    k0 = R.G.shape[1] - 8
    for own, who in ((False, 1 - C.x), (True, C.x)):
        v = mm_at(R.otok[:, pl.ds(al(who * ho, ho), ho)], da)
        for d in range(2):
            for c in range(2):
                r = d * 64 + c * 32
                put_wide(R.G.at[d, k0 + c] if own else tail_of(R.A, d, c), v[r : r + 32])


def add_tail(R, c0, n):
    k0 = R.G.shape[1] - 8

    def one(c):
        for d in range(2):
            v = R.G[d, k0 + c0 + c].astype(F32) + R.wi[d, pl.ds(al((c0 + c) * 64, 64), 64), :].astype(F32)
            R.G[d, k0 + c0 + c] = v.astype(BF)

    loop(n, one)


def stage_attend_back(R, C, n, ring, xo):
    lo2 = lanes(128) < 64
    ln2 = lanes(128)

    def hi_lo(v):
        hi = v.astype(BF).astype(F32)
        return hi, v - hi

    def unpack(b):
        f = R.dorecv[b].astype(F32)
        for u in range(2):
            at = pl.ds(al(b * 256 + u * 128, 128), 128)
            do = jnp.where(lo2, f if u == 0 else roll64(f), 0.0)
            of = R.of[at, :]
            hi, low = hi_lo(-jnp.sum(do * of, axis=1, keepdims=True))
            R.DO[at, :] = jnp.where(ln2 == 64, hi, jnp.where(ln2 == 65, low, do)).astype(BF)
            hi, low = hi_lo(-of[:, 64:65])
            q = R.Q[at, :].astype(F32)
            R.Q[at, :] = jnp.where(ln2 == 64, hi, jnp.where(ln2 == 65, low, q)).astype(BF)

    loop(n, unpack)
    T = 512
    total = R.Q.shape[0]
    nt = total // T
    half = nt // 2
    seqs = R.prefix.shape[0]
    prefix = R.prefix[C.dp // (n // seqs)]
    R.dq[...] = jnp.zeros_like(R.dq)
    k = C.sems(n)
    k2 = C.sems(n)
    base = ring.take(2 * nt)
    kvs, kvr, dqr = R.asend.at[:, 0:256], R.arecv.at[:, 0:256], R.arecv.at[:, 256:384]

    def keys(jj):
        ring.tick(base + 2 * jj)
        j = nt - 1 - jj
        kat = pl.ds(al(j * T, T), T)
        kk, vv = R.K[kat, :], R.V[kat, :]
        kpos = j * T + lax.broadcasted_iota(jnp.int32, (T, T), 0)

        def tile(i, carry):
            dk, dv = carry
            qat = pl.ds(al(i * T, T), T)
            q, do = R.Q[qat, :], R.DO[qat, :]
            qpos = i * T + lax.broadcasted_iota(jnp.int32, (1, T), 1)
            lim = jnp.maximum(qpos, prefix - 1)
            p = jnp.where(kpos <= lim, jnp.exp(mm_bt(kk, q)), 0.0)
            ds = (p * mm_bt(vv, do)).astype(BF)
            dv = dv + mm(p.astype(BF), do)
            dk = dk + mm(ds, q)
            R.dq[qat, :] = R.dq[qat, :] + mm_at(ds, kk)
            return dk, dv

        first = jnp.where(j >= half, j, 0)
        dk, dv = lax.fori_loop(
            first, nt, tile, (jnp.zeros((T, 128), F32), jnp.zeros((T, 128), F32))
        )
        lo = lanes(T) < 64
        kv = jnp.where(lo, dk, roll64(dv)).astype(BF)
        for u in range(2):
            b = j * 2 + u
            R.asend[b, 0:256, :] = kv[u * 256 : u * 256 + 256]

            @pl.when(b != C.dp)
            def _():
                C.rc(kvs.at[b], kvr.at[C.dp], k + b, (b, C.t), k + C.dp).start()

        ring.tick(base + 2 * jj + 1)

    loop(nt, keys)

    def queries(b):
        at = al(b * 256, 256)
        top = R.dq[pl.ds(at, 128), :] * 0.125
        bot = R.dq[pl.ds(al(at + 128, 128), 128), :] * 0.125
        R.osend[b] = jnp.where(lo2, top, roll64(bot)).astype(BF)

        @pl.when(b != C.dp)
        def _():
            C.rc(R.osend.at[b], dqr.at[C.dp], k2 + b, (b, C.t), k2 + C.dp).start()

    loop(n, queries)
    xo.wait_recv()
    add_tail(R, 0, 2)
    ring.run(T_KV)
    for src, dst, i in ((R.osend, dqr, 0), (kvs, kvr, 1)):
        mine = pltpu.make_async_copy(src.at[C.dp], dst.at[C.dp], C.lsem.at[i])
        mine.start()
        mine.wait()
    for src, dst, kk in ((kvs, kvr, k), (R.osend, dqr, k2)):
        for b in range(n):

            @pl.when(b != C.dp)
            def _():
                cp = C.rc(src.at[b], dst.at[b], kk + b, (b, C.t), kk + b)
                cp.wait_send()
                cp.wait_recv()

    hp = n // seqs
    lo = lanes(256) < 64
    for s in range(seqs):
        for pr in range(hp // 2):
            p = s * hp + 2 * pr
            cut = slice(pr * 128, pr * 128 + 128)
            e, d = kvr[p].astype(F32), kvr[p + 1].astype(F32)
            R.dproj[1, s * 256 : s * 256 + 256, cut] = jnp.where(lo, e, roll64(d)).astype(BF)
            R.dproj[2, s * 256 : s * 256 + 256, cut] = jnp.where(lo, roll64(e), d).astype(BF)
    unfold_heads(dqr, R.dproj.at[0], n, seqs)


def stage_qkv_back(R, C):
    def part(k):
        at = pl.ds(al(k * CH, CH), CH)
        return (
            mm_bt(R.dproj[0, at, :], R.wqkv[0])
            + mm_bt(R.dproj[1, at, :], R.wqkv[1])
            + mm_bt(R.dproj[2, at, :], R.wqkv[2])
        )

    reduce4(R, C, part, R.dx)
    own = pl.ds(al(C.t * CH, CH), CH)
    n, r = norm_parts(R.tok[own, :].astype(F32))
    dh1 = R.dx[...]
    R.GIN[C.t] = (R.x1[...] + norm_back(n, r, dh1 * R.par[0:1, :])).astype(BF)
    R.sm2[0:1, :] = rowsum(dh1 * n)
    R.sm2[1:2, :] = rowsum(dh1)


def stage_qkv_grad(R, C, ring):
    hq = R.h1.shape[1] // 2
    k = C.sems(2)
    cps = []
    k0 = R.G.shape[1] - 6
    for own, who in ((False, 1 - C.x), (True, C.x)):
        for d in range(2):
            for c in range(2):
                at = pl.ds(al(who * hq + (2 * d + c) * 128, 128), 128)
                h = R.h1[:, at]
                for m in range(3):
                    v = mm_at(h, R.dproj[m]).astype(BF)
                    w = v.shape[1]
                    i = 2 * m + c
                    dst = R.G.at[d, k0 + i] if own else tail_of(R.A, d, 2 + i)
                    dst[:, 0:w] = v[0:64]
                    dst[:, w : 2 * w] = v[64:128]
            ring.run(T_QG)
            if not own:
                cps.append(C.send(tail_of(R.A, d, 2, 6), tail_of(R.wi, d, 2, 6), k + d, C.xp))
    return cps


class Kinds:
    def __init__(self, nb, ni):
        self.i0 = nb
        self.o0 = nb + ni
        self.q0 = self.o0 + 2
        self.n = self.q0 + 6


class Sums:
    def __init__(self, R, C, n):
        self.R, self.C, self.n = R, C, n
        self.a, self.b = C.sems(2 * n), C.sems(2 * n)
        self.one = C.sems(6)

    def finish(self):
        R, C = self.R, self.C
        for d in range(2):
            pos = C.z if d == 0 else 3 - C.z
            fn = R.FN.at[d]
            C.rc(fn, fn, self.one + d, C.xp).wait_send()

            @pl.when(jnp.logical_or(pos == 1, pos == 2))
            def _():
                C.rc(fn, fn, self.one + 2 + d, C.xp).wait_send()

            cp = C.rc(fn, R.XH.at[d], self.one + 4 + d, C.xp)
            cp.wait_send()
            cp.wait_recv()
            pltpu.make_async_copy(fn, R.FH.at[d], C.lsem.at[4 + d]).wait()


class Ring:
    def __init__(self, sums, k0, k1, w):
        self.S, self.k0, self.k1, self.w = sums, k0, k1, w
        self.cur = 0
        self.total = k1 - k0 + 4 * w

    def take(self, n):
        base = self.cur
        self.cur += n
        return base

    def run(self, n):
        base = self.take(n)
        loop(n, lambda i: self.tick(base + i))

    def rest(self):
        self.run(self.total - self.cur)

    def tick(self, s):
        for d in range(2):
            self.half(s + self.k0, d)

    def half(self, s, d):
        S, w = self.S, self.w
        R, C, n, one = S.R, S.C, S.n, S.one
        pos = C.z if d == 0 else 3 - C.z

        def dev(p):
            return ((p if d == 0 else 3 - p) * 2 + C.x, C.t)

        def act(k, cond):
            ok = jnp.logical_and(k >= self.k0, k < self.k1)
            return ok if cond is None else jnp.logical_and(ok, cond)

        def toward(src, dst, kr, p):
            return C.rc(src, dst, one + d, dev(p), kr)

        def away(fn, i, p):
            return C.rc(fn, fn, one + 2 + d, dev(p), S.b + i)

        @pl.when(act(s, jnp.logical_or(pos == 0, pos == 3)))
        def _():
            toward(R.G.at[d, s], R.L1.at[d, s], S.a + d * n + s, 1 + pos // 3).start()

        k2 = s - w

        @pl.when(act(k2, pos == 2))
        def _():
            i = d * n + k2
            toward(R.G.at[d, k2], R.L1.at[d, k2], S.a + i, 1).wait_recv()
            R.G[d, k2] = (R.G[d, k2].astype(F32) + R.L1[d, k2].astype(F32)).astype(BF)
            toward(R.G.at[d, k2], R.FN.at[d, k2], S.b + i, 1).start()

        k1 = s - 2 * w

        @pl.when(act(k1, pos == 1))
        def _():
            i = d * n + k1
            fn = R.FN.at[d, k1]
            toward(R.G.at[d, k1], R.L1.at[d, k1], S.a + i, 0).wait_recv()
            away(fn, i, 2).wait_recv()
            v = R.G[d, k1].astype(F32) + R.L1[d, k1].astype(F32) + R.FN[d, k1].astype(F32)
            R.FN[d, k1] = v.astype(BF)
            away(fn, i, 2).start()
            toward(fn, fn, S.b + i, 0).start()

        lag = w * (2 + jnp.where(pos == 1, 0, 1) + jnp.where(pos == 3, 1, 0))
        kf = s - lag

        @pl.when(act(kf, None))
        def _():
            i = d * n + kf
            fn = R.FN.at[d, kf]

            @pl.when(pos != 1)
            def _():
                away(fn, i, 1).wait_recv()

            @pl.when(pos == 2)
            def _():
                away(fn, i, 3).start()

            C.rc(fn, R.XH.at[d, kf], one + 4 + d, C.xp).start()
            pltpu.make_async_copy(fn, R.FH.at[d, kf], C.lsem.at[4 + d]).start()


def small_tensor(R, C):
    R.st[C.t, 0:8, :] = R.sm[...]
    R.st[C.t, 8:16, :] = R.sm2[...]
    k = C.sems(3)
    return [
        C.send(R.st.at[C.t], R.st.at[C.t], k + i, dev)
        for i, dev in enumerate((C.mate, C.yp, (C.dp, 3 - C.t)))
    ]


def small_dp(R, C, n, cps):
    for cp in cps:
        cp.wait_recv()
    tot = R.st[0] + R.st[1] + R.st[2] + R.st[3]
    sd = R.sd.at[C.dp]
    sd[0:8, :] = tot[0:8, :]
    sd[8:10, :] = tot[8:10, :]
    f = R.dproj.shape[2]

    def colsum(m):
        return rowsum(R.dproj[m].astype(F32))

    sd[10:11, 0:f] = colsum(0)
    sd[10:11, f : 2 * f] = colsum(2)
    half = R.DH.shape[2]
    for e in range(2):
        sd[11:12, e * half : (e + 1) * half] = rowsum(R.DH[e].astype(F32))
    k = C.sems(n)
    return [C.send(sd, R.sd.at[C.dp], k + o, (lax.rem(C.dp + o, n), C.t)) for o in range(1, n)]


def small_end(R, C, n, cps):
    for cp in cps:
        cp.wait_recv()
    tot = R.sd[0]
    for b in range(1, n):
        tot = tot + R.sd[b]
    R.osm[...] = tot
    for xx in range(2):
        v = R.sd[xx, 11:12, :]
        for b in range(2 + xx, n, 2):
            v = v + R.sd[b, 11:12, :]
        R.osm[11 + xx : 12 + xx, :] = v


class Refs:
    pass


LAG = 3
LAG_Q = 2
T_U, T_OWN, T_DA, T_DO, T_KV, T_QB, T_QG = 3, 2, 3, 4, 3, 2, 1


def body(names, n, *refs):
    R = Refs()
    for name, ref in zip(names, refs):
        setattr(R, name, ref)
    C = Ctx(R.ssem, R.rsem, R.lsem)
    sem, count = barrier_start(C, n)
    half = R.wi.shape[2]
    off = pl.ds(al(C.x * half, half), half)
    wcp = [
        pltpu.make_async_copy(R.w_in.at[:, :, off], R.wi, C.lsem.at[2]),
        pltpu.make_async_copy(R.w_back.at[:, off, :], R.wb, C.lsem.at[3]),
    ]
    for cp in wcp:
        cp.start()
    R.sm[...] = jnp.zeros_like(R.sm)
    R.sm2[...] = jnp.zeros_like(R.sm2)
    R.sd[...] = jnp.zeros_like(R.sd)
    pl.semaphore_wait(sem, count)
    wait_qkv = stage_qkv(R, C, n)
    wait_qkv()
    wait_cot = swap_cot(R, C)
    stage_attend(R, C, n)
    wait_cot()
    stage_out(R, C)
    for cp in wcp:
        cp.wait()
    stage_moe(R, C)
    K = Kinds(half // 32, R.H2.shape[2] // 64)
    sums = Sums(R, C, K.n)
    ring = Ring(sums, 0, K.q0, LAG)
    last = Ring(sums, K.q0, K.n, LAG_Q)
    wait_u = reduce8(R, C, R.YP, R.ly, R.sy, R.u)
    wait_x = reduce8(R, C, R.DXP, R.lx, R.sx, R.dx)
    stage_moe_grads(R, C, K, ring)
    wait_u()
    ring.run(T_U)
    wait_x()
    stage_owner(R, C)
    wait_da = gather4(R, C, R.DA)
    wait_res = gather4(R, C, R.RES)
    ring.run(T_OWN + T_DA)
    wait_da()
    stage_out_back(R, C, n)
    wait_do = all_to_all(R, C, R.osend, R.dorecv, n)
    stage_out_grad(R, C)
    xo = C.send(R.A.at[:, 0:128, :], R.wi.at[:, 0:128, :], C.sems(1), C.xp)
    ring.run(T_DO)
    wait_do()
    C.drain()
    stage_attend_back(R, C, n, ring, xo)
    stage_qkv_back(R, C)
    wait_gin = gather4(R, C, R.GIN)
    small = small_tensor(R, C)
    ring.run(T_QB)
    xq = stage_qkv_grad(R, C, ring)
    small = small_dp(R, C, n, small)
    for cp in xq:
        cp.wait_recv()
    add_tail(R, 2, 6)
    for r in range(8):
        last.run(1)
        if ring.cur < ring.total:
            ring.run(1)
    wait_gin()
    wait_res()
    small_end(R, C, n, small)
    ring.rest()
    last.rest()
    sums.finish()
    C.drain()


def place_body(nb, ni, fh, xh, res, gin, osm, oB, oI, oQ, oO, oR, oG, *rest):
    vec, (cf, cx, cr, cg, vB, vI, vQ, vO, vR, vG, isem, osem) = rest[:9], rest[9:]
    x = lax.rem(lax.axis_index("dp"), 2)
    n = nb + ni + 8
    half = nb * 32
    cuts = ((0, nb), (nb, ni), (nb + ni, 8))
    srcs = ((fh, cf, x), (xh, cx, 1 - x))
    ins = {}
    for j, (src, buf, h) in enumerate(srcs):
        for d in range(2):
            for c, (k0, m) in enumerate(cuts):
                cp = pltpu.make_async_copy(
                    src.at[d, pl.ds(k0, m)], buf.at[d, pl.ds(k0, m)], isem.at[j * 6 + d * 3 + c]
                )
                cp.start()
                ins[j, d, c] = cp
    rows = [pltpu.make_async_copy(a, b, isem.at[12 + i]) for i, (a, b) in enumerate(((res, cr), (gin, cg)))]
    for cp in rows:
        cp.start()
    outs = []

    def put(src, dst):
        cp = pltpu.make_async_copy(src, dst, osem.at[len(outs)])
        cp.start()
        outs.append(cp)

    for j, (src, buf, h) in enumerate(srcs):
        for d in range(2):
            ins[j, d, 0].wait()

            def back(k):
                v = buf[d, k].astype(F32)
                at = pl.ds(al(k * 32, 32), 32)
                vB[j, d, at, 0:512] = v[0:32]
                vB[j, d, at, 512:1024] = v[32:64]

            loop(nb, back)
            put(vB.at[j, d], oB.at[d, pl.ds(al(h * half, half), half), :])
            ins[j, d, 1].wait()

            def into(k):
                vI[j, d, pl.ds(al(k * 64, 64), 64), :] = buf[d, nb + k].astype(F32)

            loop(ni, into)
            put(vI.at[j, d], oI.at[d, :, pl.ds(al(h * 512, 512), 512)])
    for j, (src, buf, h) in enumerate(srcs):
        for d in range(2):
            ins[j, d, 2].wait()
            for c in range(2):
                v = buf[d, nb + ni + c].astype(F32)
                at = pl.ds(al(h * 128 + d * 64 + c * 32, 32), 32)
                vO[at, 0:512] = v[0:32]
                vO[at, 512:1024] = v[32:64]
            for c in range(6):
                v = buf[d, nb + ni + 2 + c].astype(F32)
                row = h * 512 + d * 256 + (c % 2) * 128
                vQ[c // 2, pl.ds(al(row, 64), 64), :] = v[:, 0:256]
                vQ[c // 2, pl.ds(al(row + 64, 64), 64), :] = v[:, 256:512]
    put(vO, oO)
    put(vQ, oQ)
    for cp, src, buf, out in ((rows[0], cr, vR, oR), (rows[1], cg, vG, oG)):
        cp.wait()
        for t in range(src.shape[0]):
            buf[t] = src[t].astype(F32)
        put(buf, out)
    ln1g, ln1b, qv, outb, ln2g, ln2b, rout, inb, bb = vec
    for ref, r in ((ln1g, 8), (ln1b, 9), (outb, 2), (ln2g, 0), (ln2b, 1)):
        ref[...] = osm[r : r + 1, :]
    for i in range(2):
        qv[i : i + 1, :] = osm[10:11, i * 256 : i * 256 + 256]
        rout[i : i + 1, :] = osm[3 + i : 4 + i, :]
        bb[i : i + 1, :] = osm[5 + i : 6 + i, :]
        for e in range(2):
            inb[e : e + 1, i * 512 : i * 512 + 512] = osm[11 + i : 12 + i, e * 512 : e * 512 + 512]
    for cp in outs:
        cp.wait()


def place(fh, xh, res, gin, osm, nb, ni):
    sds = jax.ShapeDtypeStruct
    vm = pl.BlockSpec(memory_space=pltpu.VMEM)
    hbm = pl.BlockSpec(memory_space=pl.ANY)
    n, half = nb + ni + 8, nb * 32
    big = [(2, 2 * half, 1024), (2, ni * 64, 1024), (3, 1024, 256), (256, 1024), res.shape, gin.shape]
    row = (1, 1024)
    small = [row, row, (2, 256), row, row, row, (2, 1024), (2, 1024), (2, 1024)]
    V = pltpu.VMEM
    return pl.pallas_call(
        functools.partial(place_body, nb, ni),
        out_shape=[sds(v, F32) for v in big + small],
        in_specs=[hbm, hbm, hbm, hbm, vm],
        out_specs=[hbm] * len(big) + [vm] * len(small),
        scratch_shapes=[
            V((2, n, 64, 512), BF),
            V((2, n, 64, 512), BF),
            V(res.shape, BF),
            V(gin.shape, BF),
            V((2, 2, half, 1024), F32),
            V((2, 2, ni * 64, 512), F32),
            V((3, 1024, 256), F32),
            V((256, 1024), F32),
            V(res.shape, F32),
            V(gin.shape, F32),
            pltpu.SemaphoreType.DMA((14,)),
            pltpu.SemaphoreType.DMA((12,)),
        ],
        compiler_params=pltpu.CompilerParams(vmem_limit_bytes=60000000),
        name="place",
    )(fh, xh, res, gin, osm)


def fast_local(args, n, nt):
    (tokens, g1, b1, w_qkv, qvb, w_out, out_b, g2, b2, router, w_in, in_b, w_back, back_b,
     routes, prefix, cot) = args
    S, span, D = tokens.shape
    rows = S * span
    F = w_qkv.shape[2]
    H = w_in.shape[2]
    half = H // 2
    total = n * span
    par = jnp.concatenate(
        [jnp.stack([g1, b1, out_b, g2, b2]), router.T, back_b, jnp.zeros((7, D), BF)], axis=0
    ).astype(F32)
    vm = pl.BlockSpec(memory_space=pltpu.VMEM)
    hbm = pl.BlockSpec(memory_space=pl.ANY)
    ins = [
        ("tok", tokens.reshape(rows, D), vm),
        ("par", par, vm),
        ("wqkv", w_qkv.transpose(1, 0, 2), vm),
        ("qvb", qvb, vm),
        ("wout", w_out, vm),
        ("routes", routes.reshape(1, rows), vm),
        ("prefix", prefix, pl.BlockSpec(memory_space=pltpu.SMEM)),
        ("cot", cot.reshape(rows, D), vm),
        ("inb", in_b, vm),
        ("w_in", w_in, hbm),
        ("w_back", w_back, hbm),
    ]
    sds = jax.ShapeDtypeStruct
    nch = half // 32 + D // 64 + 8
    outs = [
        ("RES", sds((nt, CH, D), BF), vm),
        ("GIN", sds((nt, CH, D), BF), vm),
        ("FH", sds((2, nch, 64, 512), BF), hbm),
        ("XH", sds((2, nch, 64, 512), BF), hbm),
        ("osm", sds((16, D), F32), vm),
    ]
    V = pltpu.VMEM
    scr = [
        ("h1", V((rows, D), BF)),
        ("asend", V((n, 384, 128), BF)),
        ("arecv", V((n, 384, 128), BF)),
        ("Q", V((total, 128), BF)),
        ("K", V((total, 128), BF)),
        ("V", V((total, 128), BF)),
        ("DO", V((total, 128), BF)),
        ("of", V((total, 128), F32)),
        ("dq", V((total, 128), F32)),
        ("osend", V((n, 128, 128), BF)),
        ("orecv", V((n, 128, 128), BF)),
        ("dorecv", V((n, 128, 128), BF)),
        ("otok", V((rows, F), BF)),
        ("dproj", V((3, rows, F), BF)),
        ("p4", V((3, CH, D), BF)),
        ("l4", V((3, CH, D), BF)),
        ("x1", V((CH, D), F32)),
        ("u", V((CH, D), F32)),
        ("dx", V((CH, D), F32)),
        ("cols", V((CH, 128), F32)),
        ("H2", V((8, CH, D), BF)),
        ("GG", V((8, CH, D), BF)),
        ("META", V((8, CH, 128), BF)),
        ("cx", V((rows, D), BF)),
        ("wi", V((2, D, half), BF)),
        ("wb", V((2, half, D), BF)),
        ("A", V((2, 8 * CH, half), BF)),
        ("DH", V((2, 8 * CH, half), BF)),
        ("YP", V((8, CH, D), BF)),
        ("DXP", V((8, CH, D), BF)),
        ("ly", V((7, CH, D), BF)),
        ("lx", V((7, CH, D), BF)),
        ("sy", V((3, CH, D), BF)),
        ("sx", V((3, CH, D), BF)),
        ("DA", V((nt, CH, D), BF)),
        ("G", V((2, nch, 64, 512), BF)),
        ("L1", V((2, nch, 64, 512), BF)),
        ("FN", V((2, nch, 64, 512), BF)),
        ("sm", V((8, D), F32)),
        ("sm2", V((8, D), F32)),
        ("st", V((4, 16, D), F32)),
        ("sd", V((n, 16, D), F32)),
        ("ssem", pltpu.SemaphoreType.DMA((140 + 4 * nch,))),
        ("rsem", pltpu.SemaphoreType.DMA((140 + 4 * nch,))),
        ("lsem", pltpu.SemaphoreType.DMA((16,))),
    ]
    names = [i[0] for i in ins] + [o[0] for o in outs] + [s[0] for s in scr]
    res, gin, fh, xh, osm = pl.pallas_call(
        functools.partial(body, names, n),
        out_shape=[o[1] for o in outs],
        in_specs=[i[2] for i in ins],
        out_specs=[o[2] for o in outs],
        scratch_shapes=[s[1] for s in scr],
        compiler_params=pltpu.CompilerParams(
            collective_id=0, has_side_effects=True, vmem_limit_bytes=67043328
        ),
        name="layer",
    )(*[i[1] for i in ins])
    oB, oI, oQ, oO, oR, oG, ln1g, ln1b, qv, outb, ln2g, ln2b, rout, inb, bb = place(
        fh, xh, res, gin, osm, half // 32, D // 64
    )
    return (
        oR.reshape(S, span, D),
        oG.reshape(S, span, D),
        ln1g.reshape(D),
        ln1b.reshape(D),
        oQ.transpose(1, 0, 2),
        qv,
        oO,
        outb.reshape(D),
        ln2g.reshape(D),
        ln2b.reshape(D),
        rout.T,
        oI,
        inb,
        oB,
        bb,
    )


SCALE = 0.125
EPSILON = 1e-05
MASKED = -1e30
HIGHEST = lax.Precision.HIGHEST


def layer_norm(values, norm_gain, norm_bias):
    centred = values - jnp.mean(values, axis=-1, keepdims=True)
    spread = jnp.mean(centred * centred, axis=-1, keepdims=True)
    return centred * lax.rsqrt(spread + EPSILON) * norm_gain + norm_bias


def heads_of(block, head_count):
    seq_count, row_count, feat_count = block.shape
    return block.reshape(seq_count, row_count, head_count, feat_count // head_count).transpose(
        0, 2, 1, 3
    )


def tokens_of(block):
    seq_count, head_count, row_count, head_width = block.shape
    return block.transpose(0, 2, 1, 3).reshape(seq_count, row_count, head_count * head_width)


def masked_scores(queries, key_heads, query_start, key_start, prefix):
    scores = (
        jnp.einsum("shqd,shkd->shqk", queries, key_heads, preferred_element_type=jnp.float32)
        * SCALE
    )
    query_pos = query_start + jnp.arange(queries.shape[2], dtype=jnp.int32)
    key_pos = key_start + jnp.arange(key_heads.shape[2], dtype=jnp.int32)
    visible_mask = (key_pos[None, None, :] <= query_pos[None, :, None]) | (
        key_pos[None, None, :] < prefix[:, None, None]
    )
    visible_mask = visible_mask[:, None]
    return (jnp.where(visible_mask, scores, MASKED), visible_mask)


def block_live(key_start, query_last, prefix):
    return jnp.any(key_start < prefix) | (key_start <= query_last)


def prob_grads(
    queries, key_heads, value_heads, douts, log_total, delta, query_start, key_start, prefix
):
    scores, visible_mask = masked_scores(queries, key_heads, query_start, key_start, prefix)
    probs = jnp.where(visible_mask, jnp.exp(scores - log_total[..., None]), 0.0)
    dprob = jnp.einsum("shqd,shkd->shqk", douts, value_heads, preferred_element_type=jnp.float32)
    dscore = (probs * (dprob - delta[..., None])).astype(jnp.bfloat16)
    return (probs, dscore)


def attend_fold(run_state, piece_rows, piece_start, queries, first_row, prefix):
    key_piece, value_piece = piece_rows
    head_count = queries.shape[1]
    row_count = key_piece.shape[1]
    block_width = math.gcd(row_count, 512)
    query_last = first_row + queries.shape[2] - 1

    def attend_update(block_index, state_now):
        key_start = block_index * block_width
        key_heads = heads_of(
            lax.dynamic_slice_in_dim(key_piece, block_index * block_width, block_width, 1),
            head_count,
        )
        value_heads = heads_of(
            lax.dynamic_slice_in_dim(value_piece, block_index * block_width, block_width, 1),
            head_count,
        )
        scores, visible_mask = masked_scores(queries, key_heads, first_row, key_start, prefix)
        run_max, run_sum, run_out = state_now
        new_max = jnp.maximum(run_max, jnp.max(scores, axis=-1))
        factor = jnp.exp(run_max - new_max)
        weights = jnp.where(visible_mask, jnp.exp(scores - new_max[..., None]), 0.0)
        run_sum = factor * run_sum + jnp.sum(weights, axis=-1)
        run_out = factor[..., None] * run_out + jnp.einsum(
            "shqk,shkd->shqd", weights, value_heads.astype(jnp.float32), precision=HIGHEST
        )
        return (new_max, run_sum, run_out)

    def attend_block_step(state_now, block_index):
        key_start = block_index * block_width
        is_live = block_live(key_start, query_last, prefix)
        return (
            lax.cond(
                is_live, functools.partial(attend_update, block_index), lambda unchanged: unchanged, state_now
            ),
            None,
        )

    run_state, unused = lax.scan(
        attend_block_step, run_state, jnp.arange(row_count // block_width, dtype=jnp.int32)
    )
    return run_state


def key_pass(queries, douts, log_total, delta, keys_all, values_all, first_row, prefix):
    head_count = queries.shape[1]
    total_rows = keys_all.shape[1]
    block_width = math.gcd(total_rows, 512)
    query_last = first_row + queries.shape[2] - 1

    def key_block_step(dquery, block_index):
        key_start = block_index * block_width

        def work(dquery_now):
            key_heads = heads_of(
                lax.dynamic_slice_in_dim(keys_all, key_start, block_width, 1), head_count
            )
            value_heads = heads_of(
                lax.dynamic_slice_in_dim(values_all, key_start, block_width, 1), head_count
            )
            probs, dscore = prob_grads(
                queries,
                key_heads,
                value_heads,
                douts,
                log_total,
                delta,
                first_row,
                key_start,
                prefix,
            )
            dquery_now = (
                dquery_now
                + jnp.einsum(
                    "shqk,shkd->shqd", dscore, key_heads, preferred_element_type=jnp.float32
                )
                * SCALE
            )
            return (dquery_now, ())

        def skipped(dquery_now):
            return (dquery_now, ())

        return lax.cond(block_live(key_start, query_last, prefix), work, skipped, dquery)

    dquery, key_parts = lax.scan(
        key_block_step,
        jnp.zeros(queries.shape, jnp.float32),
        jnp.arange(total_rows // block_width, dtype=jnp.int32),
    )
    return (dquery, ())


def query_fold(run_state, piece_rows, piece_start, key_heads, value_heads, first_row, prefix):
    query_piece, dout_piece, total_piece, delta_piece = piece_rows
    head_count = key_heads.shape[1]
    row_count = query_piece.shape[1]
    block_width = math.gcd(row_count, 512)

    def query_update(block_index, state_now):
        query_start = block_index * block_width
        offset = block_index * block_width
        queries = heads_of(
            lax.dynamic_slice_in_dim(query_piece, offset, block_width, 1), head_count
        )
        douts = heads_of(lax.dynamic_slice_in_dim(dout_piece, offset, block_width, 1), head_count)
        log_total = lax.dynamic_slice_in_dim(total_piece, offset, block_width, 1).transpose(0, 2, 1)
        delta = lax.dynamic_slice_in_dim(delta_piece, offset, block_width, 1).transpose(0, 2, 1)
        probs, dscore = prob_grads(
            queries, key_heads, value_heads, douts, log_total, delta, query_start, first_row, prefix
        )
        dkey_now, dvalue_now = state_now
        dkey_now = (
            dkey_now
            + jnp.einsum("shqk,shqd->shkd", dscore, queries, preferred_element_type=jnp.float32)
            * SCALE
        )
        dvalue_now = dvalue_now + jnp.einsum(
            "shqk,shqd->shkd", probs, douts.astype(jnp.float32), precision=HIGHEST
        )
        return (dkey_now, dvalue_now)

    def query_block_step(state_now, block_index):
        query_last = block_index * block_width + block_width - 1
        is_live = block_live(first_row, query_last, prefix)
        return (
            lax.cond(
                is_live, functools.partial(query_update, block_index), lambda unchanged: unchanged, state_now
            ),
            None,
        )

    run_state, unused = lax.scan(
        query_block_step, run_state, jnp.arange(row_count // block_width, dtype=jnp.int32)
    )
    return run_state


def local(
    tokens,
    ln1_gain,
    ln1_bias,
    w_qkv,
    qv_bias,
    w_out,
    out_bias,
    ln2_gain,
    ln2_bias,
    router,
    w_in,
    in_bias,
    w_back,
    back_bias,
    routes,
    prefix,
    cotangent,
):
    seq_count, span_len, model_width = tokens.shape
    tok_rows = seq_count * span_len
    local_feats = w_qkv.shape[2]
    head_count = local_feats // HEAD_DIM
    expert_count = w_in.shape[0]
    first_row = lax.axis_index("dp") * span_len
    local_shape = (seq_count, span_len, local_feats)
    source = tokens.reshape(tok_rows, model_width).astype(jnp.float32)
    normed_one, ln1_pull = jax.vjp(
        layer_norm, source, ln1_gain.astype(jnp.float32), ln1_bias.astype(jnp.float32)
    )
    hidden_one = normed_one.astype(jnp.bfloat16)
    projected = jnp.einsum("ti,icf->tcf", hidden_one, w_qkv, preferred_element_type=jnp.float32)
    bias_float = qv_bias.astype(jnp.float32)
    query_tok = (projected[:, 0] + bias_float[0]).astype(jnp.bfloat16).reshape(local_shape)
    key_tok = projected[:, 1].astype(jnp.bfloat16).reshape(local_shape)
    value_tok = (projected[:, 2] + bias_float[1]).astype(jnp.bfloat16).reshape(local_shape)
    queries = heads_of(query_tok, head_count)
    stat_shape = queries.shape[:3]
    start_state = (
        jnp.full(stat_shape, MASKED, jnp.float32),
        jnp.zeros(stat_shape, jnp.float32),
        jnp.zeros(queries.shape, jnp.float32),
    )
    fold_keys = functools.partial(attend_fold, queries=queries, first_row=first_row, prefix=prefix)
    run_max, run_sum, run_out = fold_keys(
        start_state,
        (
            lax.all_gather(key_tok, "dp", axis=1, tiled=True),
            lax.all_gather(value_tok, "dp", axis=1, tiled=True),
        ),
        jnp.int32(0),
    )
    mixed_heads = run_out / run_sum[..., None]
    log_total = run_max + jnp.log(run_sum)
    mixed_b = tokens_of(mixed_heads.astype(jnp.bfloat16)).reshape(tok_rows, local_feats)
    out_shift = out_bias.astype(jnp.float32)
    gain_two = ln2_gain.astype(jnp.float32)
    shift_two = ln2_bias.astype(jnp.float32)
    attn_part = jnp.dot(mixed_b, w_out, preferred_element_type=jnp.float32)
    attn_out = lax.psum(attn_part, "tensor") + out_shift
    residual = source + attn_out
    normed_two, ln2_pull = jax.vjp(layer_norm, residual, gain_two, shift_two)
    hidden_two = normed_two.astype(jnp.bfloat16)
    logits = jnp.dot(hidden_two, router, preferred_element_type=jnp.float32)
    chosen = routes.reshape(tok_rows)
    expert_ids = jnp.arange(expert_count, dtype=jnp.int32)
    expert_hot = (chosen[:, None] == expert_ids[None, :]).astype(jnp.int32)

    def gate_of(logit_vals):
        return jnp.sum(
            jnp.where(expert_hot == 1, jax.nn.softmax(logit_vals, axis=-1), 0.0), axis=-1
        )

    gate_value, gate_pull = jax.vjp(gate_of, logits)
    earlier = jnp.cumsum(expert_hot, axis=0, dtype=jnp.int32) - expert_hot
    slot_place = jnp.sum(earlier * expert_hot, axis=1, dtype=jnp.int32)
    slot_ids = jnp.arange(CAP, dtype=jnp.int32)
    select_mask = (expert_hot[:, :, None] == 1) & (
        slot_place[:, None, None] == slot_ids[None, None, :]
    )
    select = select_mask.astype(jnp.bfloat16)
    select_float = select_mask.astype(jnp.float32)
    dispatched = jnp.einsum(
        "tec,td->ecd", select, hidden_two, preferred_element_type=jnp.float32
    ).astype(jnp.bfloat16)
    pre_act = (
        jnp.einsum("ecd,edf->ecf", dispatched, w_in, preferred_element_type=jnp.float32)
        + in_bias.astype(jnp.float32)[:, None, :]
    )
    act_float, gelu_pull = jax.vjp(functools.partial(jax.nn.gelu, approximate=False), pre_act)
    active = act_float.astype(jnp.bfloat16)
    expert_part = jnp.einsum("ecf,efd->ecd", active, w_back, preferred_element_type=jnp.float32)
    expert_full = lax.psum(expert_part, "tensor") + back_bias.astype(jnp.float32)[:, None, :]
    combined = jnp.einsum("tec,ecd->td", select_float, expert_full, precision=HIGHEST)
    layer_rows = residual + gate_value[:, None] * combined
    grad_out = cotangent.reshape(tok_rows, model_width).astype(jnp.float32)
    dgate = jnp.sum(grad_out * combined, axis=-1)
    dlogit_b = gate_pull(dgate)[0].astype(jnp.bfloat16)
    gated_grad = (gate_value[:, None] * grad_out).astype(jnp.bfloat16)
    dexpert_b = jnp.einsum(
        "tec,td->ecd", select, gated_grad, preferred_element_type=jnp.float32
    ).astype(jnp.bfloat16)
    grad_back_bias = jnp.sum(dexpert_b, axis=1, dtype=jnp.float32)
    grad_w_back = jnp.einsum("ecf,ecd->efd", active, dexpert_b, preferred_element_type=jnp.float32)
    dactive = jnp.einsum("ecd,efd->ecf", dexpert_b, w_back, preferred_element_type=jnp.float32)
    dpre_b = gelu_pull(dactive)[0].astype(jnp.bfloat16)
    grad_in_bias = jnp.sum(dpre_b, axis=1, dtype=jnp.float32)
    grad_w_in = jnp.einsum("ecd,ecf->edf", dispatched, dpre_b, preferred_element_type=jnp.float32)
    slot_part = jnp.einsum("ecf,edf->ecd", dpre_b, w_in, preferred_element_type=jnp.float32)
    dslots = lax.psum(slot_part, "tensor")
    dnorm_two = jnp.einsum("tec,ecd->td", select_float, dslots, precision=HIGHEST) + jnp.einsum(
        "te,de->td", dlogit_b, router, preferred_element_type=jnp.float32
    )
    grad_router = jnp.einsum("td,te->de", hidden_two, dlogit_b, preferred_element_type=jnp.float32)
    dresid_norm, grad_ln2_gain, grad_ln2_bias = ln2_pull(dnorm_two)
    dresidual = grad_out + dresid_norm
    dattn_b = dresidual.astype(jnp.bfloat16)
    grad_out_bias = jnp.sum(dattn_b, axis=0, dtype=jnp.float32)
    grad_w_out = jnp.einsum("tf,td->fd", mixed_b, dattn_b, preferred_element_type=jnp.float32)
    dmixed_tok = (
        jnp.einsum("td,fd->tf", dattn_b, w_out, preferred_element_type=jnp.float32)
        .astype(jnp.bfloat16)
        .reshape(local_shape)
    )
    douts = heads_of(dmixed_tok, head_count)
    delta = jnp.sum(douts.astype(jnp.float32) * mixed_heads, axis=-1)
    keys_all, values_all = (
        lax.all_gather(key_tok, "dp", axis=1, tiled=True),
        lax.all_gather(value_tok, "dp", axis=1, tiled=True),
    )
    dquery, unused = key_pass(
        queries, douts, log_total, delta, keys_all, values_all, first_row, prefix
    )
    total_rows = log_total.transpose(0, 2, 1)
    delta_rows = delta.transpose(0, 2, 1)
    fold_rows = functools.partial(
        query_fold,
        key_heads=heads_of(key_tok, head_count),
        value_heads=heads_of(value_tok, head_count),
        first_row=first_row,
        prefix=prefix,
    )
    zero_heads = jnp.zeros(queries.shape, jnp.float32)
    dkey_heads, dvalue_heads = fold_rows(
        (zero_heads, zero_heads),
        (
            lax.all_gather(query_tok, "dp", axis=1, tiled=True),
            lax.all_gather(dmixed_tok, "dp", axis=1, tiled=True),
            lax.all_gather(total_rows.astype(jnp.bfloat16), "dp", axis=1, tiled=True).astype(
                jnp.float32
            ),
            lax.all_gather(delta_rows.astype(jnp.bfloat16), "dp", axis=1, tiled=True).astype(
                jnp.float32
            ),
        ),
        jnp.int32(0),
    )
    dkey = tokens_of(dkey_heads)
    dvalue = tokens_of(dvalue_heads)
    dquery_b = tokens_of(dquery).astype(jnp.bfloat16).reshape(tok_rows, local_feats)
    dkey_b = dkey.astype(jnp.bfloat16).reshape(tok_rows, local_feats)
    dvalue_b = dvalue.astype(jnp.bfloat16).reshape(tok_rows, local_feats)
    dproject = jnp.stack([dquery_b, dkey_b, dvalue_b], axis=1)
    grad_qv_bias = jnp.stack(
        [jnp.sum(dquery_b, axis=0, dtype=jnp.float32), jnp.sum(dvalue_b, axis=0, dtype=jnp.float32)]
    )
    grad_w_qkv = jnp.einsum("ti,tcf->icf", hidden_one, dproject, preferred_element_type=jnp.float32)
    norm_part = jnp.einsum("tcf,icf->ti", dproject, w_qkv, preferred_element_type=jnp.float32)
    dnorm_one = lax.psum(norm_part, "tensor")
    dsource_norm, grad_ln1_gain, grad_ln1_bias = ln1_pull(dnorm_one)
    input_grad = (dresidual + dsource_norm).reshape(seq_count, span_len, model_width)
    summed = lax.psum(
        (
            grad_ln1_gain,
            grad_ln1_bias,
            grad_w_qkv,
            grad_qv_bias,
            grad_w_out,
            grad_out_bias,
            grad_ln2_gain,
            grad_ln2_bias,
            grad_router,
            grad_w_in,
            grad_in_bias,
            grad_w_back,
            grad_back_bias,
        ),
        "dp",
    )
    layer_out = layer_rows.reshape(seq_count, span_len, model_width)
    return (layer_out, input_grad) + tuple(summed)


def solution(mesh):
    in_specs = (
        P(None, "dp", None),
        P(),
        P(),
        P(None, None, "tensor"),
        P(None, "tensor"),
        P("tensor", None),
        P(),
        P(),
        P(),
        P(),
        P(None, None, "tensor"),
        P(None, "tensor"),
        P(None, "tensor", None),
        P(),
        P(None, "dp", None),
        P(),
        P(None, "dp", None),
    )
    out_specs = (
        P(None, "dp", None),
        P(None, "dp", None),
        P(),
        P(),
        P(None, None, "tensor"),
        P(None, "tensor"),
        P("tensor", None),
        P(),
        P(),
        P(),
        P(),
        P(None, None, "tensor"),
        P(None, "tensor"),
        P(None, "tensor", None),
        P(),
    )
    n, nt = mesh.shape["dp"], mesh.shape["tensor"]

    def step(*args):
        tokens, w_qkv = args[0], args[3]
        heads = w_qkv.shape[2] // HEAD_DIM
        fits = (
            nt == 4
            and n == 8
            and tokens.shape[2] == 1024
            and w_qkv.shape[2] == 256
            and args[10].shape == (2, 1024, 1024)
            and n == tokens.shape[0] * heads
            and tokens.shape[0] * tokens.shape[1] == nt * CH
            and tokens.shape[1] == 256
        )
        return fast_local(args, n, nt) if fits else local(*args)

    return jax.shard_map(step, mesh=mesh, in_specs=in_specs, out_specs=out_specs, check_vma=False)
```

```python
import functools
import math

import jax
import jax.numpy as jnp
from jax import lax
from jax.experimental import pallas as pl
from jax.experimental.pallas import tpu as pltpu
from jax.sharding import PartitionSpec as P

F32 = jnp.float32
BF = jnp.bfloat16
MESH = pl.DeviceIdType.MESH
EPS = 1e-05
CAP = 320
HEAD_DIM = 64
NEG = -1e30
CH = 128


def mm(a, b):
    return lax.dot_general(a, b, (((1,), (0,)), ((), ())), preferred_element_type=F32)


def mm_bt(a, b):
    return lax.dot_general(a, b, (((1,), (1,)), ((), ())), preferred_element_type=F32)


def mm_at(a, b):
    return lax.dot_general(a, b, (((0,), (0,)), ((), ())), preferred_element_type=F32)


def loop(n, body):
    def step(i, carry):
        body(i)
        return carry

    lax.fori_loop(0, n, step, 0)


def al(v, m):
    return pl.multiple_of(v, m)


def lanes(rows):
    return lax.broadcasted_iota(jnp.int32, (rows, 128), 1)


def roll64(v):
    return pltpu.roll(v, 64, 1)


class Ctx:
    def __init__(self, ssem, rsem, lsem):
        self.ssem, self.rsem, self.lsem = ssem, rsem, lsem
        self.next = 0
        self.pending = []
        dp = lax.axis_index("dp")
        t = lax.axis_index("tensor")
        self.dp, self.t = dp, t
        self.z, self.x = dp // 2, lax.rem(dp, 2)
        self.y, self.c = t // 2, lax.rem(t, 2)
        x1 = 1 - self.x
        dpx = self.z * 2 + x1
        tm = self.y * 2 + 1 - self.c
        ty = (1 - self.y) * 2 + self.c
        self.mate = (dp, tm)
        self.yp = (dp, ty)
        self.xp = (dpx, t)
        self.dg = (dpx, ty)
        self.t_mate, self.t_y = tm, ty

    def sems(self, n):
        k = self.next
        self.next += n
        return k

    def rc(self, src, dst, k, dev, kr=None):
        return pltpu.make_async_remote_copy(
            src_ref=src,
            dst_ref=dst,
            send_sem=self.ssem.at[k],
            recv_sem=self.rsem.at[k if kr is None else kr],
            device_id=dev,
            device_id_type=MESH,
        )

    def send(self, src, dst, k, dev):
        cp = self.rc(src, dst, k, dev)
        cp.start()
        self.pending.append(cp)
        return cp

    def drain(self):
        for cp in self.pending:
            cp.wait_send()
        self.pending = []


def barrier_start(C, n_dp):
    sem = pltpu.get_barrier_semaphore()
    devs = [(lax.rem(C.dp + o, n_dp), C.t) for o in range(1, n_dp)]
    devs += [C.mate, C.yp, C.dg, (C.dp, 3 - C.t)]
    for d in devs:
        pl.semaphore_signal(sem, inc=1, device_id=d, device_id_type=MESH)
    return sem, len(devs)


def norm_parts(v):
    mean = jnp.mean(v, axis=-1, keepdims=True)
    cent = v - mean
    var = jnp.mean(cent * cent, axis=-1, keepdims=True)
    r = lax.rsqrt(var + EPS)
    return cent * r, r


def stage_qkv(R, C, n):
    rows = R.tok.shape[0]
    gain, bias = R.par[0:1, :], R.par[1:2, :]
    hp = R.wqkv.shape[2] // HEAD_DIM
    k = C.sems(n)

    def seq(s):
        def ln(i):
            at = pl.ds(al(s * 256 + i * 32, 32), 32)
            n1, _ = norm_parts(R.tok[at, :].astype(F32))
            R.h1[at, :] = (n1 * gain + bias).astype(BF)

        loop(8, ln)
        at = pl.ds(al(s * 256, 256), 256)
        h = R.h1[at, :]
        lo = lanes(256) < 64
        lo2 = lanes(128) < 64
        for pr in range(hp // 2):
            cut = slice(pr * 128, pr * 128 + 128)
            tq = (mm(h, R.wqkv[0, :, cut]) + R.qvb[0:1, cut].astype(F32)) * 0.125
            tk = mm(h, R.wqkv[1, :, cut])
            tv = mm(h, R.wqkv[2, :, cut]) + R.qvb[1:2, cut].astype(F32)
            p = s * hp + 2 * pr
            R.asend[p, 0:256, :] = jnp.where(lo, tq, roll64(tk)).astype(BF)
            R.asend[p + 1, 0:256, :] = jnp.where(lo, roll64(tq), tk).astype(BF)
            a, b = tv[0:128], tv[128:256]
            R.asend[p, 256:384, :] = jnp.where(lo2, a, roll64(b)).astype(BF)
            R.asend[p + 1, 256:384, :] = jnp.where(lo2, roll64(a), b).astype(BF)
            for j in range(2):
                send_slice(C, R.asend, R.arecv, k, p + j)

    loop(rows // 256, seq)
    return lambda: wait_slices(C, R.asend, R.arecv, k, n, 0)


def send_slice(C, src, dst, k, p):
    @pl.when(p != C.dp)
    def _():
        C.rc(src.at[p], dst.at[C.dp], k + p, (p, C.t), k + C.dp).start()


def wait_slices(C, src, dst, k, n, sem):
    mine = pltpu.make_async_copy(src.at[C.dp], dst.at[C.dp], C.lsem.at[sem])
    mine.start()
    mine.wait()
    for b in range(n):

        @pl.when(b != C.dp)
        def _():
            cp = C.rc(src.at[b], dst.at[b], k + b, (b, C.t), k + b)
            cp.wait_send()
            cp.wait_recv()


def all_to_all(R, C, src, dst, n):
    k = C.sems(n)
    cps = [
        C.send(src.at[lax.rem(C.dp + o, n)], dst.at[C.dp], k + o, (lax.rem(C.dp + o, n), C.t))
        for o in range(1, n)
    ]
    mine = pltpu.make_async_copy(src.at[C.dp], dst.at[C.dp], C.lsem.at[0])
    mine.start()

    def wait():
        mine.wait()
        for cp in cps:
            cp.wait_recv()

    return wait


def stage_attend(R, C, n):
    lo = lanes(256) < 64
    lo2 = lanes(128) < 64
    one = jnp.where((lanes(256) == 64) | (lanes(256) == 65), 1.0, 0.0)
    one2 = one[0:128]

    def unpack(b):
        qk = R.arecv[b, 0:256, :].astype(F32)
        vf = R.arecv[b, 256:384, :].astype(F32)
        at = pl.ds(al(b * 256, 256), 256)
        R.Q[at, :] = jnp.where(lo, qk, 0.0).astype(BF)
        R.K[at, :] = jnp.where(lo, roll64(qk), one).astype(BF)
        R.V[pl.ds(al(b * 256, 128), 128), :] = jnp.where(lo2, vf, one2).astype(BF)
        R.V[pl.ds(al(b * 256 + 128, 128), 128), :] = jnp.where(lo2, roll64(vf), one2).astype(BF)

    loop(n, unpack)
    T = 512
    half = R.Q.shape[0] // 2 // T - 1
    seqs = R.prefix.shape[0]
    prefix = R.prefix[C.dp // (n // seqs)]
    k = C.sems(n)

    def rows_of(i):
        at = pl.ds(al(i * T, T), T)
        q = R.Q[at, :]
        qpos = i * T + lax.broadcasted_iota(jnp.int32, (T, 1), 0)
        lim = jnp.maximum(qpos, prefix - 1)

        def tile(j, carry):
            m, acc = carry
            kat = pl.ds(al(j * T, T), T)
            s = mm_bt(q, R.K[kat, :])
            kpos = j * T + lax.broadcasted_iota(jnp.int32, (T, T), 1)
            s = jnp.where(kpos <= lim, s, NEG)
            m2 = jnp.maximum(m, jnp.max(s, axis=1, keepdims=True))
            p = jnp.exp(s - m2).astype(BF)
            acc = acc * jnp.exp(m - m2) + mm(p, R.V[kat, :])
            return m2, acc

        m, acc = lax.fori_loop(
            0,
            jnp.maximum(i, half) + 1,
            tile,
            (jnp.full((T, 1), NEG, F32), jnp.zeros((T, 128), F32)),
        )
        total = acc[:, 64:65]
        o = acc / total
        lse = m + jnp.log(total)
        R.of[at, :] = jnp.where(lanes(T) < 64, o, lse)
        for u in range(2):
            b = i * 2 + u
            top, bot = o[u * 256 : u * 256 + 128], o[u * 256 + 128 : u * 256 + 256]
            R.osend[b] = jnp.where(lo2, top, roll64(bot)).astype(BF)

            @pl.when(b != C.dp)
            def _():
                C.rc(R.osend.at[b], R.orecv.at[C.dp], k + b, (b, C.t), k + C.dp).start()

    loop(R.Q.shape[0] // T, rows_of)
    mine = pltpu.make_async_copy(R.osend.at[C.dp], R.orecv.at[C.dp], C.lsem.at[0])
    mine.start()
    mine.wait()
    for b in range(n):

        @pl.when(b != C.dp)
        def _():
            cp = C.rc(R.osend.at[b], R.orecv.at[b], k + b, (b, C.t), k + b)
            cp.wait_send()
            cp.wait_recv()

    unfold_heads(R.orecv, R.otok, n, seqs)


def unfold_heads(src, dst, n, seqs):
    hp = n // seqs
    lo2 = lanes(128) < 64
    for s in range(seqs):
        for pr in range(hp // 2):
            e = src[s * hp + 2 * pr].astype(F32)
            d = src[s * hp + 2 * pr + 1].astype(F32)
            cut = slice(pr * 128, pr * 128 + 128)
            dst[s * 256 : s * 256 + 128, cut] = jnp.where(lo2, e, roll64(d)).astype(BF)
            dst[s * 256 + 128 : s * 256 + 256, cut] = jnp.where(lo2, roll64(e), d).astype(BF)


def swap_cot(R, C):
    k = C.sems(2)
    rows = R.cot.shape[0] // 2
    mine = pl.ds(al(C.c * rows, rows), rows)
    cp = C.send(R.cot.at[mine, :], R.cx.at[mine, :], k, C.xp)

    def wait():
        cp.wait_recv()
        C.send(R.cx.at[mine, :], R.cx.at[mine, :], k + 1, C.mate).wait_recv()

    return wait


def reduce4(R, C, part, out, fill=lambda: None):
    k = C.sems(3)
    k0 = (1 - C.y) * 2 + (1 - C.c)
    k1 = (1 - C.y) * 2 + C.c
    k2 = C.y * 2 + (1 - C.c)
    R.p4[0] = part(k0).astype(BF)
    c0 = C.send(R.p4.at[0], R.l4.at[0], k, C.mate)
    v1 = part(k1)
    fill()
    c0.wait_recv()
    R.p4[1] = (v1 + R.l4[0].astype(F32)).astype(BF)
    c1 = C.send(R.p4.at[1], R.l4.at[2], k + 1, C.yp)
    R.p4[2] = part(k2).astype(BF)
    c2 = C.send(R.p4.at[2], R.l4.at[1], k + 2, C.mate)
    out[...] = part(C.t)
    fill()
    c2.wait_recv()
    c1.wait_recv()
    out[...] = out[...] + R.l4[1].astype(F32) + R.l4[2].astype(F32)


def gather4(R, C, buf):
    k = C.sems(3)
    mine = buf.at[C.t]
    cy = C.send(mine, mine, k, C.yp)
    cm = C.send(mine, mine, k + 1, C.mate)

    def wait():
        cy.wait_recv()
        fwd = C.send(buf.at[C.t_y], buf.at[C.t_y], k + 2, C.mate)
        cm.wait_recv()
        fwd.wait_recv()

    return wait


def gather8(R, C, buf):
    k = C.sems(7)
    mine = buf.at[C.x * 4 + C.t]
    cd = C.send(mine, mine, k, C.dg)
    cx = C.send(mine, mine, k + 1, C.xp)
    cy = C.send(mine, mine, k + 2, C.yp)
    cm = C.send(mine, mine, k + 3, C.mate)

    def wait():
        fw = []
        for i, (cp, slot) in enumerate(
            (
                (cy, C.x * 4 + C.t_y),
                (cx, (1 - C.x) * 4 + C.t),
                (cd, (1 - C.x) * 4 + C.t_y),
            )
        ):
            cp.wait_recv()
            fw.append(C.send(buf.at[slot], buf.at[slot], k + 4 + i, C.mate))
        cm.wait_recv()
        for cp in fw:
            cp.wait_recv()

    return wait


def stage_out(R, C):
    def part(k):
        return mm(R.otok[pl.ds(al(k * CH, CH), CH), :], R.wout[...])

    reduce4(R, C, part, R.x1)
    rows = R.tok.shape[0]
    own = pl.ds(al(C.t * CH, CH), CH)
    pos = C.t * CH + lax.broadcasted_iota(jnp.int32, (CH, rows), 0)
    col = lax.broadcasted_iota(jnp.int32, (CH, rows), 1)
    hot = jnp.where(
        R.routes[...] == lax.broadcasted_iota(jnp.int32, (8, rows), 0), 1.0, 0.0
    ).astype(BF)
    earlier = mm_bt(jnp.where(col < pos, 1.0, 0.0).astype(BF), hot)
    here = mm_bt(jnp.where(col == pos, 1.0, 0.0).astype(BF), hot)
    keep = jnp.where(earlier < CAP, here, 0.0)
    keep0, keep1 = keep[:, 0:1], keep[:, 1:2]
    x1 = R.x1[...] + R.tok[own, :].astype(F32) + R.par[2:3, :]
    R.x1[...] = x1
    n, r = norm_parts(x1)
    h2 = (n * R.par[3:4, :] + R.par[4:5, :]).astype(BF)
    slot = C.x * 4 + C.t
    R.H2[slot] = h2
    hf = h2.astype(F32)
    l0 = jnp.sum(hf * R.par[5:6, :], axis=1, keepdims=True)
    l1 = jnp.sum(hf * R.par[6:7, :], axis=1, keepdims=True)
    mx = jnp.maximum(l0, l1)
    e0, e1 = jnp.exp(l0 - mx), jnp.exp(l1 - mx)
    p0, p1 = e0 / (e0 + e1), e1 / (e0 + e1)
    gate = here[:, 0:1] * p0 + here[:, 1:2] * p1
    ln = lanes(CH)
    hi = gate.astype(BF).astype(F32)
    mid = (gate - hi).astype(BF).astype(F32)
    meta = jnp.zeros((CH, 128), F32)
    for i, v in enumerate((keep0, keep1, hi, mid, gate - hi - mid)):
        meta = jnp.where(ln == i, v, meta)
    R.META[slot] = meta.astype(BF)
    wait_h = gather8(R, C, R.H2)
    wait_m = gather8(R, C, R.META)
    cols = jnp.zeros((CH, 128), F32)
    for i, v in enumerate((p0, p1, here[:, 0:1], here[:, 1:2], gate, keep0, keep1)):
        cols = jnp.where(ln == i, v, cols)
    R.cols[...] = cols
    wait_h()
    wait_m()

    def gated(i):
        for xx, cot in ((C.x, R.cot), (1 - C.x, R.cx)):
            m = R.META[xx * 4 + i].astype(F32)
            gate = m[:, 2:3] + m[:, 3:4] + m[:, 4:5]
            g = cot[pl.ds(al(i * CH, CH), CH), :].astype(F32)
            gr = (gate * g).astype(BF).astype(F32)
            R.GG[xx * 4 + i] = (gr * (m[:, 0:1] + m[:, 1:2])).astype(BF)

    loop(4, gated)


def gelu_both(h):
    half = 0.5 * (1.0 + lax.erf(h * 0.7071067811865476))
    return h * half, half + h * (jnp.exp(-0.5 * h * h) * 0.3989422804014327)


def stage_moe(R, C):
    def tile(i):
        two = pl.ds(al(2 * i, 2), 2)
        at = pl.ds(al(i * 256, 256), 256)
        h2 = R.H2[two].reshape(256, R.H2.shape[2])
        gg = R.GG[two].reshape(256, R.GG.shape[2])
        meta = R.META[two].reshape(256, 128).astype(F32)
        m0, m1 = meta[:, 0:1], meta[:, 1:2]
        half = R.wi.shape[2]
        bias0 = R.inb[0:1, pl.ds(al(C.x * half, half), half)].astype(F32)
        bias1 = R.inb[1:2, pl.ds(al(C.x * half, half), half)].astype(F32)
        for q in range(half // 256):
            cut = slice(q * 256, q * 256 + 256)
            h0 = mm(h2, R.wi[0, :, cut]) + bias0[:, cut]
            h1 = mm(h2, R.wi[1, :, cut]) + bias1[:, cut]
            act, slope = gelu_both(jnp.where(m0 > 0.0, h0, h1))
            R.A[0, at, cut] = (act * m0).astype(BF)
            R.A[1, at, cut] = (act * m1).astype(BF)
            d0 = mm_bt(gg, R.wb[0, cut, :])
            d1 = mm_bt(gg, R.wb[1, cut, :])
            dh = jnp.where(m0 > 0.0, d0, d1) * slope
            R.DH[0, at, cut] = (dh * m0).astype(BF)
            R.DH[1, at, cut] = (dh * m1).astype(BF)
        y = mm(R.A[0, at, :], R.wb[0]) + mm(R.A[1, at, :], R.wb[1])
        R.YP[two] = y.astype(BF).reshape(2, CH, y.shape[1])
        dx = mm_bt(R.DH[0, at, :], R.wi[0]) + mm_bt(R.DH[1, at, :], R.wi[1])
        R.DXP[two] = dx.astype(BF).reshape(2, CH, dx.shape[1])

    loop(4, tile)


def put_wide(at, v):
    w = v.shape[1] // 2
    at[0:32, :] = v[:, 0:w].astype(BF)
    at[32:64, :] = v[:, w : 2 * w].astype(BF)


def stage_moe_grads(R, C, K, ring):
    rows = R.GG.shape[0] * CH

    def back(i):
        at = pl.ds(al(i * 128, 128), 128)
        gg = R.GG[...].reshape(rows, R.GG.shape[2])
        for e in range(2):
            v = mm_at(R.A[e, :, at], gg)
            for j in range(4):
                put_wide(R.G.at[e, 4 * i + j], v[32 * j : 32 * j + 32])

    loop(R.A.shape[2] // 128, back)
    ring.run(3)
    base = ring.take(R.H2.shape[2] // 256)

    def into(i):
        at = pl.ds(al(i * 128, 128), 128)
        h2t = R.H2[:, :, at].reshape(rows, 128)
        for e in range(2):
            v = mm_at(h2t, R.DH[e]).astype(BF)
            R.G[e, K.i0 + 2 * i] = v[0:64]
            R.G[e, K.i0 + 2 * i + 1] = v[64:128]

        @pl.when(lax.rem(i, 2) == 1)
        def _():
            ring.tick(base + i // 2)

    loop(R.H2.shape[2] // 128, into)


def reduce8(R, C, parts, land, stage, out):
    k = C.sems(7)
    order = ((1 - C.x, 1 - C.y), (1 - C.x, C.y), (C.x, 1 - C.y), (C.x, C.y))
    devs = (C.dg, C.xp, C.yp)
    cm = []
    for n, (xx, yy) in enumerate(order):
        cm.append(C.send(parts.at[xx * 4 + yy * 2 + 1 - C.c], land.at[n], k + n, C.mate))
    cr = []
    for n, (xx, yy) in enumerate(order):
        cm[n].wait_recv()
        v = parts[xx * 4 + yy * 2 + C.c].astype(F32) + land[n].astype(F32)
        if n < 3:
            stage[n] = v.astype(BF)
            cr.append(C.send(stage.at[n], land.at[4 + n], k + 4 + n, devs[n]))
        else:
            out[...] = v

    def wait():
        for n in range(3):
            cr[n].wait_recv()
        out[...] = (
            out[...] + land[4].astype(F32) + land[5].astype(F32) + land[6].astype(F32)
        )

    return wait


def norm_back(n, r, dn):
    return r * (
        dn - jnp.mean(dn, axis=-1, keepdims=True) - n * jnp.mean(dn * n, axis=-1, keepdims=True)
    )


def rowsum(v):
    return jnp.sum(v, axis=0, keepdims=True)


def stage_owner(R, C):
    own = pl.ds(al(C.t * CH, CH), CH)
    cols = R.cols[...]
    p0, p1, h0, h1, gate, k0, k1 = (cols[:, i : i + 1] for i in range(7))
    u = R.u[...] + k0 * R.par[7:8, :] + k1 * R.par[8:9, :]
    g = R.cot[own, :].astype(F32)
    x1 = R.x1[...]
    R.RES[C.t] = (x1 + gate * u).astype(BF)
    dg = jnp.sum(g * u, axis=1, keepdims=True) * gate
    dl0 = (dg * (h0 - p0)).astype(BF).astype(F32)
    dl1 = (dg * (h1 - p1)).astype(BF).astype(F32)
    h2 = R.H2[C.x * 4 + C.t].astype(F32)
    gg = R.GG[C.x * 4 + C.t].astype(F32)
    dh2 = R.dx[...] + dl0 * R.par[5:6, :] + dl1 * R.par[6:7, :]
    n, r = norm_parts(x1)
    dx1 = g + norm_back(n, r, dh2 * R.par[3:4, :])
    da = dx1.astype(BF)
    R.DA[C.t] = da
    R.x1[...] = dx1
    R.sm[0:1, :] = rowsum(dh2 * n)
    R.sm[1:2, :] = rowsum(dh2)
    R.sm[2:3, :] = rowsum(da.astype(F32))
    R.sm[3:4, :] = rowsum(h2 * dl0)
    R.sm[4:5, :] = rowsum(h2 * dl1)
    R.sm[5:6, :] = rowsum(gg * k0)
    R.sm[6:7, :] = rowsum(gg * k1)


def stage_out_back(R, C, n):
    seqs = R.prefix.shape[0]
    hp = n // seqs
    lo2 = lanes(128) < 64
    for s in range(seqs):
        da = R.DA[2 * s : 2 * s + 2].reshape(256, R.DA.shape[2])
        for pr in range(hp // 2):
            cut = slice(pr * 128, pr * 128 + 128)
            d = mm_bt(da, R.wout[cut, :])
            a, b = d[0:128], d[128:256]
            R.osend[s * hp + 2 * pr] = jnp.where(lo2, a, roll64(b)).astype(BF)
            R.osend[s * hp + 2 * pr + 1] = jnp.where(lo2, roll64(a), b).astype(BF)


def tail_of(buf, d, c, n=1):
    return buf.at[d, 64 * c : 64 * (c + n), :]


def stage_out_grad(R, C):
    da = R.DA[...].reshape(R.otok.shape[0], R.DA.shape[2])
    ho = R.otok.shape[1] // 2
    k0 = R.G.shape[1] - 8
    for own, who in ((False, 1 - C.x), (True, C.x)):
        v = mm_at(R.otok[:, pl.ds(al(who * ho, ho), ho)], da)
        for d in range(2):
            for c in range(2):
                r = d * 64 + c * 32
                put_wide(R.G.at[d, k0 + c] if own else tail_of(R.A, d, c), v[r : r + 32])


def add_tail(R, c0, n):
    k0 = R.G.shape[1] - 8

    def one(c):
        for d in range(2):
            v = R.G[d, k0 + c0 + c].astype(F32) + R.wi[d, pl.ds(al((c0 + c) * 64, 64), 64), :].astype(F32)
            R.G[d, k0 + c0 + c] = v.astype(BF)

    loop(n, one)


def stage_attend_back(R, C, n, ring, xo):
    lo2 = lanes(128) < 64
    ln2 = lanes(128)

    def hi_lo(v):
        hi = v.astype(BF).astype(F32)
        return hi, v - hi

    def unpack(b):
        f = R.dorecv[b].astype(F32)
        for u in range(2):
            at = pl.ds(al(b * 256 + u * 128, 128), 128)
            do = jnp.where(lo2, f if u == 0 else roll64(f), 0.0)
            of = R.of[at, :]
            hi, low = hi_lo(-jnp.sum(do * of, axis=1, keepdims=True))
            R.DO[at, :] = jnp.where(ln2 == 64, hi, jnp.where(ln2 == 65, low, do)).astype(BF)
            hi, low = hi_lo(-of[:, 64:65])
            q = R.Q[at, :].astype(F32)
            R.Q[at, :] = jnp.where(ln2 == 64, hi, jnp.where(ln2 == 65, low, q)).astype(BF)

    loop(n, unpack)
    T = 512
    total = R.Q.shape[0]
    nt = total // T
    half = nt // 2
    seqs = R.prefix.shape[0]
    prefix = R.prefix[C.dp // (n // seqs)]
    R.dq[...] = jnp.zeros_like(R.dq)
    k = C.sems(n)
    k2 = C.sems(n)
    base = ring.take(T_AB * nt)
    kvs, kvr, dqr = R.asend.at[:, 0:256], R.arecv.at[:, 0:256], R.arecv.at[:, 256:384]

    def keys(jj):
        loop(T_AB // 2, lambda i: ring.tick(base + T_AB * jj + i))
        j = nt - 1 - jj
        kat = pl.ds(al(j * T, T), T)
        kk, vv = R.K[kat, :], R.V[kat, :]
        kpos = j * T + lax.broadcasted_iota(jnp.int32, (T, T), 0)

        def tile(i, carry):
            dk, dv = carry
            qat = pl.ds(al(i * T, T), T)
            q, do = R.Q[qat, :], R.DO[qat, :]
            qpos = i * T + lax.broadcasted_iota(jnp.int32, (1, T), 1)
            lim = jnp.maximum(qpos, prefix - 1)
            p = jnp.where(kpos <= lim, jnp.exp(mm_bt(kk, q)), 0.0)
            ds = (p * mm_bt(vv, do)).astype(BF)
            dv = dv + mm(p.astype(BF), do)
            dk = dk + mm(ds, q)
            R.dq[qat, :] = R.dq[qat, :] + mm_at(ds, kk)
            return dk, dv

        first = jnp.where(j >= half, j, 0)
        dk, dv = lax.fori_loop(
            first, nt, tile, (jnp.zeros((T, 128), F32), jnp.zeros((T, 128), F32))
        )
        lo = lanes(T) < 64
        kv = jnp.where(lo, dk, roll64(dv)).astype(BF)
        for u in range(2):
            b = j * 2 + u
            R.asend[b, 0:256, :] = kv[u * 256 : u * 256 + 256]

            @pl.when(b != C.dp)
            def _():
                C.rc(kvs.at[b], kvr.at[C.dp], k + b, (b, C.t), k + C.dp).start()

        loop(T_AB - T_AB // 2, lambda i: ring.tick(base + T_AB * jj + T_AB // 2 + i))

    loop(nt, keys)

    def queries(b):
        at = al(b * 256, 256)
        top = R.dq[pl.ds(at, 128), :] * 0.125
        bot = R.dq[pl.ds(al(at + 128, 128), 128), :] * 0.125
        R.osend[b] = jnp.where(lo2, top, roll64(bot)).astype(BF)

        @pl.when(b != C.dp)
        def _():
            C.rc(R.osend.at[b], dqr.at[C.dp], k2 + b, (b, C.t), k2 + C.dp).start()

    loop(n, queries)
    xo.wait_recv()
    add_tail(R, 0, 2)
    ring.run(T_KV)
    for src, dst, i in ((R.osend, dqr, 0), (kvs, kvr, 1)):
        mine = pltpu.make_async_copy(src.at[C.dp], dst.at[C.dp], C.lsem.at[i])
        mine.start()
        mine.wait()
    for src, dst, kk in ((kvs, kvr, k), (R.osend, dqr, k2)):
        for b in range(n):

            @pl.when(b != C.dp)
            def _():
                cp = C.rc(src.at[b], dst.at[b], kk + b, (b, C.t), kk + b)
                cp.wait_send()
                cp.wait_recv()

    hp = n // seqs
    lo = lanes(256) < 64
    for s in range(seqs):
        for pr in range(hp // 2):
            p = s * hp + 2 * pr
            cut = slice(pr * 128, pr * 128 + 128)
            e, d = kvr[p].astype(F32), kvr[p + 1].astype(F32)
            R.dproj[1, s * 256 : s * 256 + 256, cut] = jnp.where(lo, e, roll64(d)).astype(BF)
            R.dproj[2, s * 256 : s * 256 + 256, cut] = jnp.where(lo, roll64(e), d).astype(BF)
    unfold_heads(dqr, R.dproj.at[0], n, seqs)


def stage_qkv_back(R, C, fill):
    def part(k):
        at = pl.ds(al(k * CH, CH), CH)
        return (
            mm_bt(R.dproj[0, at, :], R.wqkv[0])
            + mm_bt(R.dproj[1, at, :], R.wqkv[1])
            + mm_bt(R.dproj[2, at, :], R.wqkv[2])
        )

    reduce4(R, C, part, R.dx, fill)
    own = pl.ds(al(C.t * CH, CH), CH)
    n, r = norm_parts(R.tok[own, :].astype(F32))
    dh1 = R.dx[...]
    R.GIN[C.t] = (R.x1[...] + norm_back(n, r, dh1 * R.par[0:1, :])).astype(BF)
    R.sm2[0:1, :] = rowsum(dh1 * n)
    R.sm2[1:2, :] = rowsum(dh1)


def stage_qkv_grad(R, C, ring):
    hq = R.h1.shape[1] // 2
    k = C.sems(2)
    cps = []
    k0 = R.G.shape[1] - 6
    for own, who in ((False, 1 - C.x), (True, C.x)):
        for d in range(2):
            for c in range(2):
                at = pl.ds(al(who * hq + (2 * d + c) * 128, 128), 128)
                h = R.h1[:, at]
                for m in range(3):
                    v = mm_at(h, R.dproj[m]).astype(BF)
                    w = v.shape[1]
                    i = 2 * m + c
                    dst = R.G.at[d, k0 + i] if own else tail_of(R.A, d, 2 + i)
                    dst[:, 0:w] = v[0:64]
                    dst[:, w : 2 * w] = v[64:128]
            ring.run(T_QG)
            if not own:
                cps.append(C.send(tail_of(R.A, d, 2, 6), tail_of(R.wi, d, 2, 6), k + d, C.xp))
    return cps


class Kinds:
    def __init__(self, nb, ni):
        self.i0 = nb
        self.o0 = nb + ni
        self.q0 = self.o0 + 2
        self.n = self.q0 + 6


class Sums:
    def __init__(self, R, C, n):
        self.R, self.C, self.n = R, C, n
        self.a, self.b = C.sems(2 * n), C.sems(2 * n)
        self.one = C.sems(6)

    def finish(self):
        R, C = self.R, self.C
        for d in range(2):
            pos = C.z if d == 0 else 3 - C.z
            fn = R.FN.at[d]
            C.rc(fn, fn, self.one + d, C.xp).wait_send()

            @pl.when(jnp.logical_or(pos == 1, pos == 2))
            def _():
                C.rc(fn, fn, self.one + 2 + d, C.xp).wait_send()

            cp = C.rc(fn, R.XH.at[d], self.one + 4 + d, C.xp)
            cp.wait_send()
            cp.wait_recv()
            pltpu.make_async_copy(fn, R.FH.at[d], C.lsem.at[4 + d]).wait()


class Ring:
    def __init__(self, sums, k0, k1, w):
        self.S, self.k0, self.k1, self.w = sums, k0, k1, w
        self.cur = 0
        self.total = k1 - k0 + 4 * w

    def take(self, n):
        base = self.cur
        self.cur += n
        return base

    def run(self, n):
        n = min(n, self.total - self.cur)
        if n <= 0:
            return
        base = self.take(n)
        loop(n, lambda i: self.tick(base + i))

    def rest(self):
        self.run(self.total - self.cur)

    def tick(self, s):
        for d in range(2):
            self.half(s + self.k0, d)

    def half(self, s, d):
        S, w = self.S, self.w
        R, C, n, one = S.R, S.C, S.n, S.one
        pos = C.z if d == 0 else 3 - C.z

        def dev(p):
            return ((p if d == 0 else 3 - p) * 2 + C.x, C.t)

        def act(k, cond):
            ok = jnp.logical_and(k >= self.k0, k < self.k1)
            return ok if cond is None else jnp.logical_and(ok, cond)

        def toward(src, dst, kr, p):
            return C.rc(src, dst, one + d, dev(p), kr)

        def away(fn, i, p):
            return C.rc(fn, fn, one + 2 + d, dev(p), S.b + i)

        @pl.when(act(s, jnp.logical_or(pos == 0, pos == 3)))
        def _():
            toward(R.G.at[d, s], R.L1.at[d, s], S.a + d * n + s, 1 + pos // 3).start()

        k2 = s - w

        @pl.when(act(k2, pos == 2))
        def _():
            i = d * n + k2
            toward(R.G.at[d, k2], R.L1.at[d, k2], S.a + i, 1).wait_recv()
            R.G[d, k2] = (R.G[d, k2].astype(F32) + R.L1[d, k2].astype(F32)).astype(BF)
            toward(R.G.at[d, k2], R.FN.at[d, k2], S.b + i, 1).start()

        k1 = s - 2 * w

        @pl.when(act(k1, pos == 1))
        def _():
            i = d * n + k1
            fn = R.FN.at[d, k1]
            toward(R.G.at[d, k1], R.L1.at[d, k1], S.a + i, 0).wait_recv()
            away(fn, i, 2).wait_recv()
            v = R.G[d, k1].astype(F32) + R.L1[d, k1].astype(F32) + R.FN[d, k1].astype(F32)
            R.FN[d, k1] = v.astype(BF)
            away(fn, i, 2).start()
            toward(fn, fn, S.b + i, 0).start()

        lag = w * (2 + jnp.where(pos == 1, 0, 1) + jnp.where(pos == 3, 1, 0))
        kf = s - lag

        @pl.when(act(kf, None))
        def _():
            i = d * n + kf
            fn = R.FN.at[d, kf]

            @pl.when(pos != 1)
            def _():
                away(fn, i, 1).wait_recv()

            @pl.when(pos == 2)
            def _():
                away(fn, i, 3).start()

            C.rc(fn, R.XH.at[d, kf], one + 4 + d, C.xp).start()
            pltpu.make_async_copy(fn, R.FH.at[d, kf], C.lsem.at[4 + d]).start()


def small_tensor(R, C):
    R.st[C.t, 0:8, :] = R.sm[...]
    R.st[C.t, 8:16, :] = R.sm2[...]
    k = C.sems(3)
    return [
        C.send(R.st.at[C.t], R.st.at[C.t], k + i, dev)
        for i, dev in enumerate((C.mate, C.yp, (C.dp, 3 - C.t)))
    ]


def small_dp(R, C, n, cps):
    for cp in cps:
        cp.wait_recv()
    tot = R.st[0] + R.st[1] + R.st[2] + R.st[3]
    sd = R.sd.at[C.dp]
    sd[0:8, :] = tot[0:8, :]
    sd[8:10, :] = tot[8:10, :]
    f = R.dproj.shape[2]

    def colsum(m):
        return rowsum(R.dproj[m].astype(F32))

    sd[10:11, 0:f] = colsum(0)
    sd[10:11, f : 2 * f] = colsum(2)
    half = R.DH.shape[2]
    for e in range(2):
        sd[11:12, e * half : (e + 1) * half] = rowsum(R.DH[e].astype(F32))
    k = C.sems(n)
    return [C.send(sd, R.sd.at[C.dp], k + o, (lax.rem(C.dp + o, n), C.t)) for o in range(1, n)]


def small_end(R, C, n, cps):
    for cp in cps:
        cp.wait_recv()
    tot = R.sd[0]
    for b in range(1, n):
        tot = tot + R.sd[b]
    R.osm[...] = tot
    for xx in range(2):
        v = R.sd[xx, 11:12, :]
        for b in range(2 + xx, n, 2):
            v = v + R.sd[b, 11:12, :]
        R.osm[11 + xx : 12 + xx, :] = v


class Refs:
    pass


LAG = 3
LAG_Q = 2
T_U, T_DA, T_DO, T_AB, T_KV, T_QB, T_QG = 3, 5, 4, 2, 3, 2, 1


def body(names, n, *refs):
    R = Refs()
    for name, ref in zip(names, refs):
        setattr(R, name, ref)
    C = Ctx(R.ssem, R.rsem, R.lsem)
    sem, count = barrier_start(C, n)
    half = R.wi.shape[2]
    off = pl.ds(al(C.x * half, half), half)
    wcp = [
        pltpu.make_async_copy(R.w_in.at[:, :, off], R.wi, C.lsem.at[2]),
        pltpu.make_async_copy(R.w_back.at[:, off, :], R.wb, C.lsem.at[3]),
    ]
    for cp in wcp:
        cp.start()
    for i, ref in enumerate((R.g1, R.b1, R.outb, R.g2, R.b2)):
        R.par[i : i + 1, :] = ref[...].astype(F32).reshape(1, ref.shape[0])
    R.par[5:7, :] = R.router[...].astype(F32)
    R.par[7:9, :] = R.backb[...].astype(F32)
    R.sm[...] = jnp.zeros_like(R.sm)
    R.sm2[...] = jnp.zeros_like(R.sm2)
    R.sd[...] = jnp.zeros_like(R.sd)
    pl.semaphore_wait(sem, count)
    wait_qkv = stage_qkv(R, C, n)
    wait_qkv()
    wait_cot = swap_cot(R, C)
    stage_attend(R, C, n)
    wait_cot()
    stage_out(R, C)
    for cp in wcp:
        cp.wait()
    stage_moe(R, C)
    K = Kinds(half // 32, R.H2.shape[2] // 64)
    sums = Sums(R, C, K.n)
    ring = Ring(sums, 0, K.q0, LAG)
    last = Ring(sums, K.q0, K.n, LAG_Q)
    wait_u = reduce8(R, C, R.YP, R.ly, R.sy, R.u)
    wait_x = reduce8(R, C, R.DXP, R.lx, R.sx, R.dx)
    stage_moe_grads(R, C, K, ring)
    wait_u()
    ring.run(T_U)
    wait_x()
    stage_owner(R, C)
    wait_da = gather4(R, C, R.DA)
    wait_res = gather4(R, C, R.RES)
    ring.run(T_DA)
    wait_da()
    stage_out_back(R, C, n)
    wait_do = all_to_all(R, C, R.osend, R.dorecv, n)
    stage_out_grad(R, C)
    xo = C.send(R.A.at[:, 0:128, :], R.wi.at[:, 0:128, :], C.sems(1), C.xp)
    ring.run(T_DO)
    wait_do()
    C.drain()
    stage_attend_back(R, C, n, ring, xo)
    xq = stage_qkv_grad(R, C, ring)
    stage_qkv_back(R, C, lambda: ring.run(T_QB))
    wait_gin = gather4(R, C, R.GIN)
    small = small_tensor(R, C)
    for cp in xq:
        cp.wait_recv()
    add_tail(R, 2, 6)
    for r in range(8):
        last.run(1)
        ring.run(1)
        if r == 2:
            small = small_dp(R, C, n, small)
    wait_gin()
    wait_res()
    small_end(R, C, n, small)
    ring.rest()
    last.rest()
    sums.finish()
    C.drain()


def place_body(nb, ni, fh, xh, res, gin, osm, oB, oI, oQ, oO, oR, oG, *rest):
    vec, (cf, cx, cr, cg, vB, vI, vQ, vO, vR, vG, isem, osem) = rest[:9], rest[9:]
    x = lax.rem(lax.axis_index("dp"), 2)
    n = nb + ni + 8
    half = nb * 32
    cuts = ((0, nb), (nb, ni), (nb + ni, 8))
    srcs = ((fh, cf, x), (xh, cx, 1 - x))
    ins = {}
    for j, (src, buf, h) in enumerate(srcs):
        for d in range(2):
            for c, (k0, m) in enumerate(cuts):
                cp = pltpu.make_async_copy(
                    src.at[d, pl.ds(k0, m)], buf.at[d, pl.ds(k0, m)], isem.at[j * 6 + d * 3 + c]
                )
                cp.start()
                ins[j, d, c] = cp
    rows = [pltpu.make_async_copy(a, b, isem.at[12 + i]) for i, (a, b) in enumerate(((res, cr), (gin, cg)))]
    for cp in rows:
        cp.start()
    outs = []

    def put(src, dst):
        cp = pltpu.make_async_copy(src, dst, osem.at[len(outs)])
        cp.start()
        outs.append(cp)

    for j, (src, buf, h) in enumerate(srcs):
        for d in range(2):
            ins[j, d, 0].wait()

            def back(k):
                v = buf[d, k].astype(F32)
                at = pl.ds(al(k * 32, 32), 32)
                vB[j, d, at, 0:512] = v[0:32]
                vB[j, d, at, 512:1024] = v[32:64]

            loop(nb, back)
            put(vB.at[j, d], oB.at[d, pl.ds(al(h * half, half), half), :])
            ins[j, d, 1].wait()

            def into(k):
                vI[j, d, pl.ds(al(k * 64, 64), 64), :] = buf[d, nb + k].astype(F32)

            loop(ni, into)
            put(vI.at[j, d], oI.at[d, :, pl.ds(al(h * 512, 512), 512)])
    for j, (src, buf, h) in enumerate(srcs):
        for d in range(2):
            ins[j, d, 2].wait()
            for c in range(2):
                v = buf[d, nb + ni + c].astype(F32)
                at = pl.ds(al(h * 128 + d * 64 + c * 32, 32), 32)
                vO[at, 0:512] = v[0:32]
                vO[at, 512:1024] = v[32:64]
            for c in range(6):
                v = buf[d, nb + ni + 2 + c].astype(F32)
                row = h * 512 + d * 256 + (c % 2) * 128
                vQ[c // 2, pl.ds(al(row, 64), 64), :] = v[:, 0:256]
                vQ[c // 2, pl.ds(al(row + 64, 64), 64), :] = v[:, 256:512]
    put(vO, oO)
    put(vQ, oQ)
    for cp, src, buf, out in ((rows[0], cr, vR, oR), (rows[1], cg, vG, oG)):
        cp.wait()
        for t in range(src.shape[0]):
            buf[t] = src[t].astype(F32)
        put(buf, out)
    ln1g, ln1b, qv, outb, ln2g, ln2b, rout, inb, bb = vec
    for ref, r in ((ln1g, 8), (ln1b, 9), (outb, 2), (ln2g, 0), (ln2b, 1)):
        ref[...] = osm[r : r + 1, :]
    for i in range(2):
        qv[i : i + 1, :] = osm[10:11, i * 256 : i * 256 + 256]
        rout[i : i + 1, :] = osm[3 + i : 4 + i, :]
        bb[i : i + 1, :] = osm[5 + i : 6 + i, :]
        for e in range(2):
            inb[e : e + 1, i * 512 : i * 512 + 512] = osm[11 + i : 12 + i, e * 512 : e * 512 + 512]
    for cp in outs:
        cp.wait()


def place(fh, xh, res, gin, osm, nb, ni):
    sds = jax.ShapeDtypeStruct
    vm = pl.BlockSpec(memory_space=pltpu.VMEM)
    hbm = pl.BlockSpec(memory_space=pl.ANY)
    n, half = nb + ni + 8, nb * 32
    big = [(2, 2 * half, 1024), (2, ni * 64, 1024), (3, 1024, 256), (256, 1024), res.shape, gin.shape]
    row = (1, 1024)
    small = [row, row, (2, 256), row, row, row, (2, 1024), (2, 1024), (2, 1024)]
    V = pltpu.VMEM
    return pl.pallas_call(
        functools.partial(place_body, nb, ni),
        out_shape=[sds(v, F32) for v in big + small],
        in_specs=[hbm, hbm, hbm, hbm, vm],
        out_specs=[hbm] * len(big) + [vm] * len(small),
        scratch_shapes=[
            V((2, n, 64, 512), BF),
            V((2, n, 64, 512), BF),
            V(res.shape, BF),
            V(gin.shape, BF),
            V((2, 2, half, 1024), F32),
            V((2, 2, ni * 64, 512), F32),
            V((3, 1024, 256), F32),
            V((256, 1024), F32),
            V(res.shape, F32),
            V(gin.shape, F32),
            pltpu.SemaphoreType.DMA((14,)),
            pltpu.SemaphoreType.DMA((12,)),
        ],
        compiler_params=pltpu.CompilerParams(vmem_limit_bytes=60000000),
        name="place",
    )(fh, xh, res, gin, osm)


def fast_local(args, n, nt):
    (tokens, g1, b1, w_qkv, qvb, w_out, out_b, g2, b2, router, w_in, in_b, w_back, back_b,
     routes, prefix, cot) = args
    S, span, D = tokens.shape
    rows = S * span
    F = w_qkv.shape[2]
    H = w_in.shape[2]
    half = H // 2
    total = n * span
    vm = pl.BlockSpec(memory_space=pltpu.VMEM)
    hbm = pl.BlockSpec(memory_space=pl.ANY)
    ins = [
        ("tok", tokens.reshape(rows, D), vm),
        ("g1", g1, vm),
        ("b1", b1, vm),
        ("outb", out_b, vm),
        ("g2", g2, vm),
        ("b2", b2, vm),
        ("router", router.T, vm),
        ("backb", back_b, vm),
        ("wqkv", w_qkv.transpose(1, 0, 2), vm),
        ("qvb", qvb, vm),
        ("wout", w_out, vm),
        ("routes", routes.reshape(1, rows), vm),
        ("prefix", prefix, pl.BlockSpec(memory_space=pltpu.SMEM)),
        ("cot", cot.reshape(rows, D), vm),
        ("inb", in_b, vm),
        ("w_in", w_in, hbm),
        ("w_back", w_back, hbm),
    ]
    sds = jax.ShapeDtypeStruct
    nch = half // 32 + D // 64 + 8
    outs = [
        ("RES", sds((nt, CH, D), BF), vm),
        ("GIN", sds((nt, CH, D), BF), vm),
        ("FH", sds((2, nch, 64, 512), BF), hbm),
        ("XH", sds((2, nch, 64, 512), BF), hbm),
        ("osm", sds((16, D), F32), vm),
    ]
    V = pltpu.VMEM
    scr = [
        ("h1", V((rows, D), BF)),
        ("asend", V((n, 384, 128), BF)),
        ("arecv", V((n, 384, 128), BF)),
        ("Q", V((total, 128), BF)),
        ("K", V((total, 128), BF)),
        ("V", V((total, 128), BF)),
        ("DO", V((total, 128), BF)),
        ("of", V((total, 128), F32)),
        ("dq", V((total, 128), F32)),
        ("osend", V((n, 128, 128), BF)),
        ("orecv", V((n, 128, 128), BF)),
        ("dorecv", V((n, 128, 128), BF)),
        ("otok", V((rows, F), BF)),
        ("dproj", V((3, rows, F), BF)),
        ("p4", V((3, CH, D), BF)),
        ("l4", V((3, CH, D), BF)),
        ("x1", V((CH, D), F32)),
        ("u", V((CH, D), F32)),
        ("dx", V((CH, D), F32)),
        ("cols", V((CH, 128), F32)),
        ("H2", V((8, CH, D), BF)),
        ("GG", V((8, CH, D), BF)),
        ("META", V((8, CH, 128), BF)),
        ("cx", V((rows, D), BF)),
        ("par", V((16, D), F32)),
        ("wi", V((2, D, half), BF)),
        ("wb", V((2, half, D), BF)),
        ("A", V((2, 8 * CH, half), BF)),
        ("DH", V((2, 8 * CH, half), BF)),
        ("YP", V((8, CH, D), BF)),
        ("DXP", V((8, CH, D), BF)),
        ("ly", V((7, CH, D), BF)),
        ("lx", V((7, CH, D), BF)),
        ("sy", V((3, CH, D), BF)),
        ("sx", V((3, CH, D), BF)),
        ("DA", V((nt, CH, D), BF)),
        ("G", V((2, nch, 64, 512), BF)),
        ("L1", V((2, nch, 64, 512), BF)),
        ("FN", V((2, nch, 64, 512), BF)),
        ("sm", V((8, D), F32)),
        ("sm2", V((8, D), F32)),
        ("st", V((4, 16, D), F32)),
        ("sd", V((n, 16, D), F32)),
        ("ssem", pltpu.SemaphoreType.DMA((140 + 4 * nch,))),
        ("rsem", pltpu.SemaphoreType.DMA((140 + 4 * nch,))),
        ("lsem", pltpu.SemaphoreType.DMA((16,))),
    ]
    names = [i[0] for i in ins] + [o[0] for o in outs] + [s[0] for s in scr]
    res, gin, fh, xh, osm = pl.pallas_call(
        functools.partial(body, names, n),
        out_shape=[o[1] for o in outs],
        in_specs=[i[2] for i in ins],
        out_specs=[o[2] for o in outs],
        scratch_shapes=[s[1] for s in scr],
        compiler_params=pltpu.CompilerParams(
            collective_id=0, has_side_effects=True, vmem_limit_bytes=67043328
        ),
        name="layer",
    )(*[i[1] for i in ins])
    oB, oI, oQ, oO, oR, oG, ln1g, ln1b, qv, outb, ln2g, ln2b, rout, inb, bb = place(
        fh, xh, res, gin, osm, half // 32, D // 64
    )
    return (
        oR.reshape(S, span, D),
        oG.reshape(S, span, D),
        ln1g.reshape(D),
        ln1b.reshape(D),
        oQ.transpose(1, 0, 2),
        qv,
        oO,
        outb.reshape(D),
        ln2g.reshape(D),
        ln2b.reshape(D),
        rout.T,
        oI,
        inb,
        oB,
        bb,
    )


SCALE = 0.125
EPSILON = 1e-05
MASKED = -1e30
HIGHEST = lax.Precision.HIGHEST


def layer_norm(values, norm_gain, norm_bias):
    centred = values - jnp.mean(values, axis=-1, keepdims=True)
    spread = jnp.mean(centred * centred, axis=-1, keepdims=True)
    return centred * lax.rsqrt(spread + EPSILON) * norm_gain + norm_bias


def heads_of(block, head_count):
    seq_count, row_count, feat_count = block.shape
    return block.reshape(seq_count, row_count, head_count, feat_count // head_count).transpose(
        0, 2, 1, 3
    )


def tokens_of(block):
    seq_count, head_count, row_count, head_width = block.shape
    return block.transpose(0, 2, 1, 3).reshape(seq_count, row_count, head_count * head_width)


def masked_scores(queries, key_heads, query_start, key_start, prefix):
    scores = (
        jnp.einsum("shqd,shkd->shqk", queries, key_heads, preferred_element_type=jnp.float32)
        * SCALE
    )
    query_pos = query_start + jnp.arange(queries.shape[2], dtype=jnp.int32)
    key_pos = key_start + jnp.arange(key_heads.shape[2], dtype=jnp.int32)
    visible_mask = (key_pos[None, None, :] <= query_pos[None, :, None]) | (
        key_pos[None, None, :] < prefix[:, None, None]
    )
    visible_mask = visible_mask[:, None]
    return (jnp.where(visible_mask, scores, MASKED), visible_mask)


def block_live(key_start, query_last, prefix):
    return jnp.any(key_start < prefix) | (key_start <= query_last)


def prob_grads(
    queries, key_heads, value_heads, douts, log_total, delta, query_start, key_start, prefix
):
    scores, visible_mask = masked_scores(queries, key_heads, query_start, key_start, prefix)
    probs = jnp.where(visible_mask, jnp.exp(scores - log_total[..., None]), 0.0)
    dprob = jnp.einsum("shqd,shkd->shqk", douts, value_heads, preferred_element_type=jnp.float32)
    dscore = (probs * (dprob - delta[..., None])).astype(jnp.bfloat16)
    return (probs, dscore)


def attend_fold(run_state, piece_rows, piece_start, queries, first_row, prefix):
    key_piece, value_piece = piece_rows
    head_count = queries.shape[1]
    row_count = key_piece.shape[1]
    block_width = math.gcd(row_count, 512)
    query_last = first_row + queries.shape[2] - 1

    def attend_update(block_index, state_now):
        key_start = block_index * block_width
        key_heads = heads_of(
            lax.dynamic_slice_in_dim(key_piece, block_index * block_width, block_width, 1),
            head_count,
        )
        value_heads = heads_of(
            lax.dynamic_slice_in_dim(value_piece, block_index * block_width, block_width, 1),
            head_count,
        )
        scores, visible_mask = masked_scores(queries, key_heads, first_row, key_start, prefix)
        run_max, run_sum, run_out = state_now
        new_max = jnp.maximum(run_max, jnp.max(scores, axis=-1))
        factor = jnp.exp(run_max - new_max)
        weights = jnp.where(visible_mask, jnp.exp(scores - new_max[..., None]), 0.0)
        run_sum = factor * run_sum + jnp.sum(weights, axis=-1)
        run_out = factor[..., None] * run_out + jnp.einsum(
            "shqk,shkd->shqd", weights, value_heads.astype(jnp.float32), precision=HIGHEST
        )
        return (new_max, run_sum, run_out)

    def attend_block_step(state_now, block_index):
        key_start = block_index * block_width
        is_live = block_live(key_start, query_last, prefix)
        return (
            lax.cond(
                is_live, functools.partial(attend_update, block_index), lambda unchanged: unchanged, state_now
            ),
            None,
        )

    run_state, unused = lax.scan(
        attend_block_step, run_state, jnp.arange(row_count // block_width, dtype=jnp.int32)
    )
    return run_state


def key_pass(queries, douts, log_total, delta, keys_all, values_all, first_row, prefix):
    head_count = queries.shape[1]
    total_rows = keys_all.shape[1]
    block_width = math.gcd(total_rows, 512)
    query_last = first_row + queries.shape[2] - 1

    def key_block_step(dquery, block_index):
        key_start = block_index * block_width

        def work(dquery_now):
            key_heads = heads_of(
                lax.dynamic_slice_in_dim(keys_all, key_start, block_width, 1), head_count
            )
            value_heads = heads_of(
                lax.dynamic_slice_in_dim(values_all, key_start, block_width, 1), head_count
            )
            probs, dscore = prob_grads(
                queries,
                key_heads,
                value_heads,
                douts,
                log_total,
                delta,
                first_row,
                key_start,
                prefix,
            )
            dquery_now = (
                dquery_now
                + jnp.einsum(
                    "shqk,shkd->shqd", dscore, key_heads, preferred_element_type=jnp.float32
                )
                * SCALE
            )
            return (dquery_now, ())

        def skipped(dquery_now):
            return (dquery_now, ())

        return lax.cond(block_live(key_start, query_last, prefix), work, skipped, dquery)

    dquery, key_parts = lax.scan(
        key_block_step,
        jnp.zeros(queries.shape, jnp.float32),
        jnp.arange(total_rows // block_width, dtype=jnp.int32),
    )
    return (dquery, ())


def query_fold(run_state, piece_rows, piece_start, key_heads, value_heads, first_row, prefix):
    query_piece, dout_piece, total_piece, delta_piece = piece_rows
    head_count = key_heads.shape[1]
    row_count = query_piece.shape[1]
    block_width = math.gcd(row_count, 512)

    def query_update(block_index, state_now):
        query_start = block_index * block_width
        offset = block_index * block_width
        queries = heads_of(
            lax.dynamic_slice_in_dim(query_piece, offset, block_width, 1), head_count
        )
        douts = heads_of(lax.dynamic_slice_in_dim(dout_piece, offset, block_width, 1), head_count)
        log_total = lax.dynamic_slice_in_dim(total_piece, offset, block_width, 1).transpose(0, 2, 1)
        delta = lax.dynamic_slice_in_dim(delta_piece, offset, block_width, 1).transpose(0, 2, 1)
        probs, dscore = prob_grads(
            queries, key_heads, value_heads, douts, log_total, delta, query_start, first_row, prefix
        )
        dkey_now, dvalue_now = state_now
        dkey_now = (
            dkey_now
            + jnp.einsum("shqk,shqd->shkd", dscore, queries, preferred_element_type=jnp.float32)
            * SCALE
        )
        dvalue_now = dvalue_now + jnp.einsum(
            "shqk,shqd->shkd", probs, douts.astype(jnp.float32), precision=HIGHEST
        )
        return (dkey_now, dvalue_now)

    def query_block_step(state_now, block_index):
        query_last = block_index * block_width + block_width - 1
        is_live = block_live(first_row, query_last, prefix)
        return (
            lax.cond(
                is_live, functools.partial(query_update, block_index), lambda unchanged: unchanged, state_now
            ),
            None,
        )

    run_state, unused = lax.scan(
        query_block_step, run_state, jnp.arange(row_count // block_width, dtype=jnp.int32)
    )
    return run_state


def local(
    tokens,
    ln1_gain,
    ln1_bias,
    w_qkv,
    qv_bias,
    w_out,
    out_bias,
    ln2_gain,
    ln2_bias,
    router,
    w_in,
    in_bias,
    w_back,
    back_bias,
    routes,
    prefix,
    cotangent,
):
    seq_count, span_len, model_width = tokens.shape
    tok_rows = seq_count * span_len
    local_feats = w_qkv.shape[2]
    head_count = local_feats // HEAD_DIM
    expert_count = w_in.shape[0]
    first_row = lax.axis_index("dp") * span_len
    local_shape = (seq_count, span_len, local_feats)
    source = tokens.reshape(tok_rows, model_width).astype(jnp.float32)
    normed_one, ln1_pull = jax.vjp(
        layer_norm, source, ln1_gain.astype(jnp.float32), ln1_bias.astype(jnp.float32)
    )
    hidden_one = normed_one.astype(jnp.bfloat16)
    projected = jnp.einsum("ti,icf->tcf", hidden_one, w_qkv, preferred_element_type=jnp.float32)
    bias_float = qv_bias.astype(jnp.float32)
    query_tok = (projected[:, 0] + bias_float[0]).astype(jnp.bfloat16).reshape(local_shape)
    key_tok = projected[:, 1].astype(jnp.bfloat16).reshape(local_shape)
    value_tok = (projected[:, 2] + bias_float[1]).astype(jnp.bfloat16).reshape(local_shape)
    queries = heads_of(query_tok, head_count)
    stat_shape = queries.shape[:3]
    start_state = (
        jnp.full(stat_shape, MASKED, jnp.float32),
        jnp.zeros(stat_shape, jnp.float32),
        jnp.zeros(queries.shape, jnp.float32),
    )
    fold_keys = functools.partial(attend_fold, queries=queries, first_row=first_row, prefix=prefix)
    run_max, run_sum, run_out = fold_keys(
        start_state,
        (
            lax.all_gather(key_tok, "dp", axis=1, tiled=True),
            lax.all_gather(value_tok, "dp", axis=1, tiled=True),
        ),
        jnp.int32(0),
    )
    mixed_heads = run_out / run_sum[..., None]
    log_total = run_max + jnp.log(run_sum)
    mixed_b = tokens_of(mixed_heads.astype(jnp.bfloat16)).reshape(tok_rows, local_feats)
    out_shift = out_bias.astype(jnp.float32)
    gain_two = ln2_gain.astype(jnp.float32)
    shift_two = ln2_bias.astype(jnp.float32)
    attn_part = jnp.dot(mixed_b, w_out, preferred_element_type=jnp.float32)
    attn_out = lax.psum(attn_part, "tensor") + out_shift
    residual = source + attn_out
    normed_two, ln2_pull = jax.vjp(layer_norm, residual, gain_two, shift_two)
    hidden_two = normed_two.astype(jnp.bfloat16)
    logits = jnp.dot(hidden_two, router, preferred_element_type=jnp.float32)
    chosen = routes.reshape(tok_rows)
    expert_ids = jnp.arange(expert_count, dtype=jnp.int32)
    expert_hot = (chosen[:, None] == expert_ids[None, :]).astype(jnp.int32)

    def gate_of(logit_vals):
        return jnp.sum(
            jnp.where(expert_hot == 1, jax.nn.softmax(logit_vals, axis=-1), 0.0), axis=-1
        )

    gate_value, gate_pull = jax.vjp(gate_of, logits)
    earlier = jnp.cumsum(expert_hot, axis=0, dtype=jnp.int32) - expert_hot
    slot_place = jnp.sum(earlier * expert_hot, axis=1, dtype=jnp.int32)
    slot_ids = jnp.arange(CAP, dtype=jnp.int32)
    select_mask = (expert_hot[:, :, None] == 1) & (
        slot_place[:, None, None] == slot_ids[None, None, :]
    )
    select = select_mask.astype(jnp.bfloat16)
    select_float = select_mask.astype(jnp.float32)
    dispatched = jnp.einsum(
        "tec,td->ecd", select, hidden_two, preferred_element_type=jnp.float32
    ).astype(jnp.bfloat16)
    pre_act = (
        jnp.einsum("ecd,edf->ecf", dispatched, w_in, preferred_element_type=jnp.float32)
        + in_bias.astype(jnp.float32)[:, None, :]
    )
    act_float, gelu_pull = jax.vjp(functools.partial(jax.nn.gelu, approximate=False), pre_act)
    active = act_float.astype(jnp.bfloat16)
    expert_part = jnp.einsum("ecf,efd->ecd", active, w_back, preferred_element_type=jnp.float32)
    expert_full = lax.psum(expert_part, "tensor") + back_bias.astype(jnp.float32)[:, None, :]
    combined = jnp.einsum("tec,ecd->td", select_float, expert_full, precision=HIGHEST)
    layer_rows = residual + gate_value[:, None] * combined
    grad_out = cotangent.reshape(tok_rows, model_width).astype(jnp.float32)
    dgate = jnp.sum(grad_out * combined, axis=-1)
    dlogit_b = gate_pull(dgate)[0].astype(jnp.bfloat16)
    gated_grad = (gate_value[:, None] * grad_out).astype(jnp.bfloat16)
    dexpert_b = jnp.einsum(
        "tec,td->ecd", select, gated_grad, preferred_element_type=jnp.float32
    ).astype(jnp.bfloat16)
    grad_back_bias = jnp.sum(dexpert_b, axis=1, dtype=jnp.float32)
    grad_w_back = jnp.einsum("ecf,ecd->efd", active, dexpert_b, preferred_element_type=jnp.float32)
    dactive = jnp.einsum("ecd,efd->ecf", dexpert_b, w_back, preferred_element_type=jnp.float32)
    dpre_b = gelu_pull(dactive)[0].astype(jnp.bfloat16)
    grad_in_bias = jnp.sum(dpre_b, axis=1, dtype=jnp.float32)
    grad_w_in = jnp.einsum("ecd,ecf->edf", dispatched, dpre_b, preferred_element_type=jnp.float32)
    slot_part = jnp.einsum("ecf,edf->ecd", dpre_b, w_in, preferred_element_type=jnp.float32)
    dslots = lax.psum(slot_part, "tensor")
    dnorm_two = jnp.einsum("tec,ecd->td", select_float, dslots, precision=HIGHEST) + jnp.einsum(
        "te,de->td", dlogit_b, router, preferred_element_type=jnp.float32
    )
    grad_router = jnp.einsum("td,te->de", hidden_two, dlogit_b, preferred_element_type=jnp.float32)
    dresid_norm, grad_ln2_gain, grad_ln2_bias = ln2_pull(dnorm_two)
    dresidual = grad_out + dresid_norm
    dattn_b = dresidual.astype(jnp.bfloat16)
    grad_out_bias = jnp.sum(dattn_b, axis=0, dtype=jnp.float32)
    grad_w_out = jnp.einsum("tf,td->fd", mixed_b, dattn_b, preferred_element_type=jnp.float32)
    dmixed_tok = (
        jnp.einsum("td,fd->tf", dattn_b, w_out, preferred_element_type=jnp.float32)
        .astype(jnp.bfloat16)
        .reshape(local_shape)
    )
    douts = heads_of(dmixed_tok, head_count)
    delta = jnp.sum(douts.astype(jnp.float32) * mixed_heads, axis=-1)
    keys_all, values_all = (
        lax.all_gather(key_tok, "dp", axis=1, tiled=True),
        lax.all_gather(value_tok, "dp", axis=1, tiled=True),
    )
    dquery, unused = key_pass(
        queries, douts, log_total, delta, keys_all, values_all, first_row, prefix
    )
    total_rows = log_total.transpose(0, 2, 1)
    delta_rows = delta.transpose(0, 2, 1)
    fold_rows = functools.partial(
        query_fold,
        key_heads=heads_of(key_tok, head_count),
        value_heads=heads_of(value_tok, head_count),
        first_row=first_row,
        prefix=prefix,
    )
    zero_heads = jnp.zeros(queries.shape, jnp.float32)
    dkey_heads, dvalue_heads = fold_rows(
        (zero_heads, zero_heads),
        (
            lax.all_gather(query_tok, "dp", axis=1, tiled=True),
            lax.all_gather(dmixed_tok, "dp", axis=1, tiled=True),
            lax.all_gather(total_rows.astype(jnp.bfloat16), "dp", axis=1, tiled=True).astype(
                jnp.float32
            ),
            lax.all_gather(delta_rows.astype(jnp.bfloat16), "dp", axis=1, tiled=True).astype(
                jnp.float32
            ),
        ),
        jnp.int32(0),
    )
    dkey = tokens_of(dkey_heads)
    dvalue = tokens_of(dvalue_heads)
    dquery_b = tokens_of(dquery).astype(jnp.bfloat16).reshape(tok_rows, local_feats)
    dkey_b = dkey.astype(jnp.bfloat16).reshape(tok_rows, local_feats)
    dvalue_b = dvalue.astype(jnp.bfloat16).reshape(tok_rows, local_feats)
    dproject = jnp.stack([dquery_b, dkey_b, dvalue_b], axis=1)
    grad_qv_bias = jnp.stack(
        [jnp.sum(dquery_b, axis=0, dtype=jnp.float32), jnp.sum(dvalue_b, axis=0, dtype=jnp.float32)]
    )
    grad_w_qkv = jnp.einsum("ti,tcf->icf", hidden_one, dproject, preferred_element_type=jnp.float32)
    norm_part = jnp.einsum("tcf,icf->ti", dproject, w_qkv, preferred_element_type=jnp.float32)
    dnorm_one = lax.psum(norm_part, "tensor")
    dsource_norm, grad_ln1_gain, grad_ln1_bias = ln1_pull(dnorm_one)
    input_grad = (dresidual + dsource_norm).reshape(seq_count, span_len, model_width)
    summed = lax.psum(
        (
            grad_ln1_gain,
            grad_ln1_bias,
            grad_w_qkv,
            grad_qv_bias,
            grad_w_out,
            grad_out_bias,
            grad_ln2_gain,
            grad_ln2_bias,
            grad_router,
            grad_w_in,
            grad_in_bias,
            grad_w_back,
            grad_back_bias,
        ),
        "dp",
    )
    layer_out = layer_rows.reshape(seq_count, span_len, model_width)
    return (layer_out, input_grad) + tuple(summed)


def solution(mesh):
    in_specs = (
        P(None, "dp", None),
        P(),
        P(),
        P(None, None, "tensor"),
        P(None, "tensor"),
        P("tensor", None),
        P(),
        P(),
        P(),
        P(),
        P(None, None, "tensor"),
        P(None, "tensor"),
        P(None, "tensor", None),
        P(),
        P(None, "dp", None),
        P(),
        P(None, "dp", None),
    )
    out_specs = (
        P(None, "dp", None),
        P(None, "dp", None),
        P(),
        P(),
        P(None, None, "tensor"),
        P(None, "tensor"),
        P("tensor", None),
        P(),
        P(),
        P(),
        P(),
        P(None, None, "tensor"),
        P(None, "tensor"),
        P(None, "tensor", None),
        P(),
    )
    n, nt = mesh.shape["dp"], mesh.shape["tensor"]

    def step(*args):
        tokens, w_qkv = args[0], args[3]
        heads = w_qkv.shape[2] // HEAD_DIM
        fits = (
            nt == 4
            and n == 8
            and tokens.shape[2] == 1024
            and w_qkv.shape[2] == 256
            and args[10].shape == (2, 1024, 1024)
            and n == tokens.shape[0] * heads
            and tokens.shape[0] * tokens.shape[1] == nt * CH
            and tokens.shape[1] == 256
        )
        return fast_local(args, n, nt) if fits else local(*args)

    return jax.shard_map(step, mesh=mesh, in_specs=in_specs, out_specs=out_specs, check_vma=False)
```

```python
import functools
import math

import jax
import jax.numpy as jnp
from jax import lax
from jax.experimental import pallas as pl
from jax.experimental.pallas import tpu as pltpu
from jax.sharding import PartitionSpec as P

F32 = jnp.float32
BF = jnp.bfloat16
MESH = pl.DeviceIdType.MESH
EPS = 1e-05
CAP = 320
HEAD_DIM = 64
NEG = -1e30
CH = 128


def mm(a, b):
    return lax.dot_general(a, b, (((1,), (0,)), ((), ())), preferred_element_type=F32)


def mm_bt(a, b):
    return lax.dot_general(a, b, (((1,), (1,)), ((), ())), preferred_element_type=F32)


def mm_at(a, b):
    return lax.dot_general(a, b, (((0,), (0,)), ((), ())), preferred_element_type=F32)


def loop(n, body):
    def step(i, carry):
        body(i)
        return carry

    lax.fori_loop(0, n, step, 0)


def al(v, m):
    return pl.multiple_of(v, m)


def lanes(rows):
    return lax.broadcasted_iota(jnp.int32, (rows, 128), 1)


def roll64(v):
    return pltpu.roll(v, 64, 1)


class Ctx:
    def __init__(self, ssem, rsem, lsem):
        self.ssem, self.rsem, self.lsem = ssem, rsem, lsem
        self.next = 0
        self.pending = []
        dp = lax.axis_index("dp")
        t = lax.axis_index("tensor")
        self.dp, self.t = dp, t
        self.z, self.x = dp // 2, lax.rem(dp, 2)
        self.y, self.c = t // 2, lax.rem(t, 2)
        x1 = 1 - self.x
        dpx = self.z * 2 + x1
        tm = self.y * 2 + 1 - self.c
        ty = (1 - self.y) * 2 + self.c
        self.mate = (dp, tm)
        self.yp = (dp, ty)
        self.xp = (dpx, t)
        self.dg = (dpx, ty)
        self.t_mate, self.t_y = tm, ty

    def sems(self, n):
        k = self.next
        self.next += n
        return k

    def rc(self, src, dst, k, dev, kr=None):
        return pltpu.make_async_remote_copy(
            src_ref=src,
            dst_ref=dst,
            send_sem=self.ssem.at[k],
            recv_sem=self.rsem.at[k if kr is None else kr],
            device_id=dev,
            device_id_type=MESH,
        )

    def send(self, src, dst, k, dev):
        cp = self.rc(src, dst, k, dev)
        cp.start()
        self.pending.append(cp)
        return cp

    def drain(self):
        for cp in self.pending:
            cp.wait_send()
        self.pending = []


def barrier_start(C, n_dp):
    sem = pltpu.get_barrier_semaphore()
    devs = [(lax.rem(C.dp + o, n_dp), C.t) for o in range(1, n_dp)]
    devs += [C.mate, C.yp, C.dg, (C.dp, 3 - C.t)]
    for d in devs:
        pl.semaphore_signal(sem, inc=1, device_id=d, device_id_type=MESH)
    return sem, len(devs)


def norm_parts(v):
    mean = jnp.mean(v, axis=-1, keepdims=True)
    cent = v - mean
    var = jnp.mean(cent * cent, axis=-1, keepdims=True)
    r = lax.rsqrt(var + EPS)
    return cent * r, r


def stage_qkv(R, C, n):
    rows = R.tok.shape[0]
    gain, bias = R.par[0:1, :], R.par[1:2, :]
    hp = R.wqkv.shape[2] // HEAD_DIM
    k = C.sems(n)

    def seq(s):
        def ln(i):
            at = pl.ds(al(s * 256 + i * 32, 32), 32)
            n1, _ = norm_parts(R.tok[at, :].astype(F32))
            R.h1[at, :] = (n1 * gain + bias).astype(BF)

        loop(8, ln)
        at = pl.ds(al(s * 256, 256), 256)
        h = R.h1[at, :]
        lo = lanes(256) < 64
        lo2 = lanes(128) < 64
        for pr in range(hp // 2):
            cut = slice(pr * 128, pr * 128 + 128)
            tq = (mm(h, R.wqkv[0, :, cut]) + R.qvb[0:1, cut].astype(F32)) * 0.125
            tk = mm(h, R.wqkv[1, :, cut])
            tv = mm(h, R.wqkv[2, :, cut]) + R.qvb[1:2, cut].astype(F32)
            p = s * hp + 2 * pr
            R.asend[p, 0:256, :] = jnp.where(lo, tq, roll64(tk)).astype(BF)
            R.asend[p + 1, 0:256, :] = jnp.where(lo, roll64(tq), tk).astype(BF)
            a, b = tv[0:128], tv[128:256]
            R.asend[p, 256:384, :] = jnp.where(lo2, a, roll64(b)).astype(BF)
            R.asend[p + 1, 256:384, :] = jnp.where(lo2, roll64(a), b).astype(BF)
            for j in range(2):
                send_slice(C, R.asend, R.arecv, k, p + j)

    loop(rows // 256, seq)
    return lambda: wait_slices(C, R.asend, R.arecv, k, n, 0)


def send_slice(C, src, dst, k, p):
    @pl.when(p != C.dp)
    def _():
        C.rc(src.at[p], dst.at[C.dp], k + p, (p, C.t), k + C.dp).start()


def wait_slices(C, src, dst, k, n, sem):
    mine = pltpu.make_async_copy(src.at[C.dp], dst.at[C.dp], C.lsem.at[sem])
    mine.start()
    mine.wait()
    for b in range(n):

        @pl.when(b != C.dp)
        def _():
            cp = C.rc(src.at[b], dst.at[b], k + b, (b, C.t), k + b)
            cp.wait_send()
            cp.wait_recv()


def all_to_all(R, C, src, dst, n):
    k = C.sems(n)
    cps = [
        C.send(src.at[lax.rem(C.dp + o, n)], dst.at[C.dp], k + o, (lax.rem(C.dp + o, n), C.t))
        for o in range(1, n)
    ]
    mine = pltpu.make_async_copy(src.at[C.dp], dst.at[C.dp], C.lsem.at[0])
    mine.start()

    def wait():
        mine.wait()
        for cp in cps:
            cp.wait_recv()

    return wait


def stage_attend(R, C, n):
    lo = lanes(256) < 64
    lo2 = lanes(128) < 64
    one = jnp.where((lanes(256) == 64) | (lanes(256) == 65), 1.0, 0.0)
    one2 = one[0:128]

    def unpack(b):
        qk = R.arecv[b, 0:256, :].astype(F32)
        vf = R.arecv[b, 256:384, :].astype(F32)
        at = pl.ds(al(b * 256, 256), 256)
        R.Q[at, :] = jnp.where(lo, qk, 0.0).astype(BF)
        R.K[at, :] = jnp.where(lo, roll64(qk), one).astype(BF)
        R.V[pl.ds(al(b * 256, 128), 128), :] = jnp.where(lo2, vf, one2).astype(BF)
        R.V[pl.ds(al(b * 256 + 128, 128), 128), :] = jnp.where(lo2, roll64(vf), one2).astype(BF)

    loop(n, unpack)
    T = 512
    half = R.Q.shape[0] // 2 // T - 1
    seqs = R.prefix.shape[0]
    prefix = R.prefix[C.dp // (n // seqs)]
    k = C.sems(n)

    def rows_of(i):
        at = pl.ds(al(i * T, T), T)
        q = R.Q[at, :]
        qpos = i * T + lax.broadcasted_iota(jnp.int32, (T, 1), 0)
        lim = jnp.maximum(qpos, prefix - 1)

        def tile(j, carry):
            m, acc = carry
            kat = pl.ds(al(j * T, T), T)
            s = mm_bt(q, R.K[kat, :])
            kpos = j * T + lax.broadcasted_iota(jnp.int32, (T, T), 1)
            s = jnp.where(kpos <= lim, s, NEG)
            m2 = jnp.maximum(m, jnp.max(s, axis=1, keepdims=True))
            p = jnp.exp(s - m2).astype(BF)
            acc = acc * jnp.exp(m - m2) + mm(p, R.V[kat, :])
            return m2, acc

        m, acc = lax.fori_loop(
            0,
            jnp.maximum(i, half) + 1,
            tile,
            (jnp.full((T, 1), NEG, F32), jnp.zeros((T, 128), F32)),
        )
        total = acc[:, 64:65]
        o = acc / total
        lse = m + jnp.log(total)
        R.of[at, :] = jnp.where(lanes(T) < 64, o, lse)
        for u in range(2):
            b = i * 2 + u
            top, bot = o[u * 256 : u * 256 + 128], o[u * 256 + 128 : u * 256 + 256]
            R.osend[b] = jnp.where(lo2, top, roll64(bot)).astype(BF)

            @pl.when(b != C.dp)
            def _():
                C.rc(R.osend.at[b], R.orecv.at[C.dp], k + b, (b, C.t), k + C.dp).start()

    loop(R.Q.shape[0] // T, rows_of)
    mine = pltpu.make_async_copy(R.osend.at[C.dp], R.orecv.at[C.dp], C.lsem.at[0])
    mine.start()
    mine.wait()
    for b in range(n):

        @pl.when(b != C.dp)
        def _():
            cp = C.rc(R.osend.at[b], R.orecv.at[b], k + b, (b, C.t), k + b)
            cp.wait_send()
            cp.wait_recv()

    unfold_heads(R.orecv, R.otok, n, seqs)


def unfold_heads(src, dst, n, seqs):
    hp = n // seqs
    lo2 = lanes(128) < 64
    for s in range(seqs):
        for pr in range(hp // 2):
            e = src[s * hp + 2 * pr].astype(F32)
            d = src[s * hp + 2 * pr + 1].astype(F32)
            cut = slice(pr * 128, pr * 128 + 128)
            dst[s * 256 : s * 256 + 128, cut] = jnp.where(lo2, e, roll64(d)).astype(BF)
            dst[s * 256 + 128 : s * 256 + 256, cut] = jnp.where(lo2, roll64(e), d).astype(BF)


def swap_cot(R, C):
    k = C.sems(2)
    rows = R.cot.shape[0] // 2
    mine = pl.ds(al(C.c * rows, rows), rows)
    cp = C.send(R.cot.at[mine, :], R.cx.at[mine, :], k, C.xp)

    def wait():
        cp.wait_recv()
        C.send(R.cx.at[mine, :], R.cx.at[mine, :], k + 1, C.mate).wait_recv()

    return wait


def reduce4(R, C, part, out, fill=lambda: None):
    k = C.sems(3)
    k0 = (1 - C.y) * 2 + (1 - C.c)
    k1 = (1 - C.y) * 2 + C.c
    k2 = C.y * 2 + (1 - C.c)
    R.p4[0] = part(k0).astype(BF)
    c0 = C.send(R.p4.at[0], R.l4.at[0], k, C.mate)
    v1 = part(k1)
    fill()
    c0.wait_recv()
    R.p4[1] = (v1 + R.l4[0].astype(F32)).astype(BF)
    c1 = C.send(R.p4.at[1], R.l4.at[2], k + 1, C.yp)
    R.p4[2] = part(k2).astype(BF)
    c2 = C.send(R.p4.at[2], R.l4.at[1], k + 2, C.mate)
    out[...] = part(C.t)
    fill()
    c2.wait_recv()
    c1.wait_recv()
    out[...] = out[...] + R.l4[1].astype(F32) + R.l4[2].astype(F32)


def gather4(R, C, buf):
    k = C.sems(3)
    mine = buf.at[C.t]
    cy = C.send(mine, mine, k, C.yp)
    cm = C.send(mine, mine, k + 1, C.mate)

    def wait():
        cy.wait_recv()
        fwd = C.send(buf.at[C.t_y], buf.at[C.t_y], k + 2, C.mate)
        cm.wait_recv()
        fwd.wait_recv()

    return wait


def gather8(R, C, buf):
    k = C.sems(7)
    mine = buf.at[C.x * 4 + C.t]
    cd = C.send(mine, mine, k, C.dg)
    cx = C.send(mine, mine, k + 1, C.xp)
    cy = C.send(mine, mine, k + 2, C.yp)
    cm = C.send(mine, mine, k + 3, C.mate)

    def wait():
        fw = []
        for i, (cp, slot) in enumerate(
            (
                (cy, C.x * 4 + C.t_y),
                (cx, (1 - C.x) * 4 + C.t),
                (cd, (1 - C.x) * 4 + C.t_y),
            )
        ):
            cp.wait_recv()
            fw.append(C.send(buf.at[slot], buf.at[slot], k + 4 + i, C.mate))
        cm.wait_recv()
        for cp in fw:
            cp.wait_recv()

    return wait


def stage_out(R, C):
    def part(k):
        return mm(R.otok[pl.ds(al(k * CH, CH), CH), :], R.wout[...])

    reduce4(R, C, part, R.x1)
    rows = R.tok.shape[0]
    own = pl.ds(al(C.t * CH, CH), CH)
    pos = C.t * CH + lax.broadcasted_iota(jnp.int32, (CH, rows), 0)
    col = lax.broadcasted_iota(jnp.int32, (CH, rows), 1)
    hot = jnp.where(
        R.routes[...] == lax.broadcasted_iota(jnp.int32, (8, rows), 0), 1.0, 0.0
    ).astype(BF)
    earlier = mm_bt(jnp.where(col < pos, 1.0, 0.0).astype(BF), hot)
    here = mm_bt(jnp.where(col == pos, 1.0, 0.0).astype(BF), hot)
    keep = jnp.where(earlier < CAP, here, 0.0)
    keep0, keep1 = keep[:, 0:1], keep[:, 1:2]
    x1 = R.x1[...] + R.tok[own, :].astype(F32) + R.par[2:3, :]
    R.x1[...] = x1
    n, r = norm_parts(x1)
    h2 = (n * R.par[3:4, :] + R.par[4:5, :]).astype(BF)
    slot = C.x * 4 + C.t
    R.H2[slot] = h2
    hf = h2.astype(F32)
    l0 = jnp.sum(hf * R.par[5:6, :], axis=1, keepdims=True)
    l1 = jnp.sum(hf * R.par[6:7, :], axis=1, keepdims=True)
    mx = jnp.maximum(l0, l1)
    e0, e1 = jnp.exp(l0 - mx), jnp.exp(l1 - mx)
    p0, p1 = e0 / (e0 + e1), e1 / (e0 + e1)
    gate = here[:, 0:1] * p0 + here[:, 1:2] * p1
    ln = lanes(CH)
    hi = gate.astype(BF).astype(F32)
    mid = (gate - hi).astype(BF).astype(F32)
    meta = jnp.zeros((CH, 128), F32)
    for i, v in enumerate((keep0, keep1, hi, mid, gate - hi - mid)):
        meta = jnp.where(ln == i, v, meta)
    R.META[slot] = meta.astype(BF)
    wait_h = gather8(R, C, R.H2)
    wait_m = gather8(R, C, R.META)
    cols = jnp.zeros((CH, 128), F32)
    for i, v in enumerate((p0, p1, here[:, 0:1], here[:, 1:2], gate, keep0, keep1)):
        cols = jnp.where(ln == i, v, cols)
    R.cols[...] = cols
    wait_h()
    wait_m()

    def gated(i):
        for xx, cot in ((C.x, R.cot), (1 - C.x, R.cx)):
            m = R.META[xx * 4 + i].astype(F32)
            gate = m[:, 2:3] + m[:, 3:4] + m[:, 4:5]
            g = cot[pl.ds(al(i * CH, CH), CH), :].astype(F32)
            gr = (gate * g).astype(BF).astype(F32)
            R.GG[xx * 4 + i] = (gr * (m[:, 0:1] + m[:, 1:2])).astype(BF)

    loop(4, gated)


def gelu_both(h):
    half = 0.5 * (1.0 + lax.erf(h * 0.7071067811865476))
    return h * half, half + h * (jnp.exp(-0.5 * h * h) * 0.3989422804014327)


class Reduce8:
    def __init__(self, C, parts, land, stage, out):
        self.C, self.parts, self.land, self.stage, self.out = C, parts, land, stage, out
        self.k = C.sems(7)

    def place(self, n):
        C = self.C
        a, b = n // 2, lax.rem(n, 2)
        xx = (1 - C.x) * (1 - a) + C.x * a
        yy = (1 - C.y) * (1 - b) + C.y * b
        return xx, yy

    def swap(self, n):
        C = self.C
        xx, yy = self.place(n)
        src = self.parts.at[xx * 4 + yy * 2 + 1 - C.c]
        return C.rc(src, self.land.at[n], self.k + n, C.mate)

    def added(self, n):
        C = self.C
        xx, yy = self.place(n)
        self.swap(n).wait_recv()
        return self.parts[xx * 4 + yy * 2 + C.c].astype(F32) + self.land[n].astype(F32)

    def cross(self, n):
        C = self.C
        xx, yy = self.place(n)
        dev = (C.z * 2 + xx, yy * 2 + C.c)
        return C.rc(self.stage.at[n], self.land.at[4 + n], self.k + 4 + n, dev)

    def forward(self, n):
        self.stage[n] = self.added(n).astype(BF)
        self.cross(n).start()

    def keep(self):
        self.out[...] = self.added(3)
        self.C.pending += [self.swap(n) for n in range(4)] + [self.cross(n) for n in range(3)]

    def wait(self):
        for n in range(3):
            self.cross(n).wait_recv()
        v = self.out[...]
        for n in range(3):
            v = v + self.land[4 + n].astype(F32)
        self.out[...] = v


def stage_moe(R, C, sums):
    def tile(n):
        xx, yy = sums[0].place(n)
        i = xx * 2 + yy
        two = pl.ds(al(2 * i, 2), 2)
        at = pl.ds(al(i * 256, 256), 256)
        h2 = R.H2[two].reshape(256, R.H2.shape[2])
        gg = R.GG[two].reshape(256, R.GG.shape[2])
        meta = R.META[two].reshape(256, 128).astype(F32)
        m0, m1 = meta[:, 0:1], meta[:, 1:2]
        half = R.wi.shape[2]
        bias0 = R.inb[0:1, pl.ds(al(C.x * half, half), half)].astype(F32)
        bias1 = R.inb[1:2, pl.ds(al(C.x * half, half), half)].astype(F32)
        for q in range(half // 256):
            cut = slice(q * 256, q * 256 + 256)
            h0 = mm(h2, R.wi[0, :, cut]) + bias0[:, cut]
            h1 = mm(h2, R.wi[1, :, cut]) + bias1[:, cut]
            act, slope = gelu_both(jnp.where(m0 > 0.0, h0, h1))
            R.A[0, at, cut] = (act * m0).astype(BF)
            R.A[1, at, cut] = (act * m1).astype(BF)
            d0 = mm_bt(gg, R.wb[0, cut, :])
            d1 = mm_bt(gg, R.wb[1, cut, :])
            dh = jnp.where(m0 > 0.0, d0, d1) * slope
            R.DH[0, at, cut] = (dh * m0).astype(BF)
            R.DH[1, at, cut] = (dh * m1).astype(BF)
        y = mm(R.A[0, at, :], R.wb[0]) + mm(R.A[1, at, :], R.wb[1])
        R.YP[two] = y.astype(BF).reshape(2, CH, y.shape[1])
        dx = mm_bt(R.DH[0, at, :], R.wi[0]) + mm_bt(R.DH[1, at, :], R.wi[1])
        R.DXP[two] = dx.astype(BF).reshape(2, CH, dx.shape[1])
        for r in sums:
            r.swap(n).start()

        @pl.when(n > 0)
        def _():
            for r in sums:
                r.forward(n - 1)

    loop(4, tile)
    for r in sums:
        r.keep()


def put_wide(at, v):
    w = v.shape[1] // 2
    at[0:32, :] = v[:, 0:w].astype(BF)
    at[32:64, :] = v[:, w : 2 * w].astype(BF)


def stage_moe_grads(R, C, K, ring):
    rows = R.GG.shape[0] * CH

    def back(i):
        at = pl.ds(al(i * 128, 128), 128)
        gg = R.GG[...].reshape(rows, R.GG.shape[2])
        for e in range(2):
            v = mm_at(R.A[e, :, at], gg)
            for j in range(4):
                put_wide(R.G.at[e, 4 * i + j], v[32 * j : 32 * j + 32])

    loop(R.A.shape[2] // 128, back)
    ring.run(3)
    base = ring.take(R.H2.shape[2] // 256)

    def into(i):
        at = pl.ds(al(i * 128, 128), 128)
        h2t = R.H2[:, :, at].reshape(rows, 128)
        for e in range(2):
            v = mm_at(h2t, R.DH[e]).astype(BF)
            R.G[e, K.i0 + 2 * i] = v[0:64]
            R.G[e, K.i0 + 2 * i + 1] = v[64:128]

        @pl.when(lax.rem(i, 2) == 1)
        def _():
            ring.tick(base + i // 2)

    loop(R.H2.shape[2] // 128, into)


def norm_back(n, r, dn):
    return r * (
        dn - jnp.mean(dn, axis=-1, keepdims=True) - n * jnp.mean(dn * n, axis=-1, keepdims=True)
    )


def rowsum(v):
    return jnp.sum(v, axis=0, keepdims=True)


def stage_owner(R, C):
    own = pl.ds(al(C.t * CH, CH), CH)
    cols = R.cols[...]
    p0, p1, h0, h1, gate, k0, k1 = (cols[:, i : i + 1] for i in range(7))
    u = R.u[...] + k0 * R.par[7:8, :] + k1 * R.par[8:9, :]
    g = R.cot[own, :].astype(F32)
    x1 = R.x1[...]
    R.RES[C.t] = (x1 + gate * u).astype(BF)
    dg = jnp.sum(g * u, axis=1, keepdims=True) * gate
    dl0 = (dg * (h0 - p0)).astype(BF).astype(F32)
    dl1 = (dg * (h1 - p1)).astype(BF).astype(F32)
    h2 = R.H2[C.x * 4 + C.t].astype(F32)
    gg = R.GG[C.x * 4 + C.t].astype(F32)
    dh2 = R.dx[...] + dl0 * R.par[5:6, :] + dl1 * R.par[6:7, :]
    n, r = norm_parts(x1)
    dx1 = g + norm_back(n, r, dh2 * R.par[3:4, :])
    da = dx1.astype(BF)
    R.DA[C.t] = da
    R.x1[...] = dx1
    R.sm[0:1, :] = rowsum(dh2 * n)
    R.sm[1:2, :] = rowsum(dh2)
    R.sm[2:3, :] = rowsum(da.astype(F32))
    R.sm[3:4, :] = rowsum(h2 * dl0)
    R.sm[4:5, :] = rowsum(h2 * dl1)
    R.sm[5:6, :] = rowsum(gg * k0)
    R.sm[6:7, :] = rowsum(gg * k1)


def stage_out_back(R, C, n):
    seqs = R.prefix.shape[0]
    hp = n // seqs
    lo2 = lanes(128) < 64
    for s in range(seqs):
        da = R.DA[2 * s : 2 * s + 2].reshape(256, R.DA.shape[2])
        for pr in range(hp // 2):
            cut = slice(pr * 128, pr * 128 + 128)
            d = mm_bt(da, R.wout[cut, :])
            a, b = d[0:128], d[128:256]
            R.osend[s * hp + 2 * pr] = jnp.where(lo2, a, roll64(b)).astype(BF)
            R.osend[s * hp + 2 * pr + 1] = jnp.where(lo2, roll64(a), b).astype(BF)


def tail_of(buf, d, c, n=1):
    return buf.at[d, 64 * c : 64 * (c + n), :]


def stage_out_grad(R, C):
    da = R.DA[...].reshape(R.otok.shape[0], R.DA.shape[2])
    ho = R.otok.shape[1] // 2
    k0 = R.G.shape[1] - 8
    for own, who in ((False, 1 - C.x), (True, C.x)):
        v = mm_at(R.otok[:, pl.ds(al(who * ho, ho), ho)], da)
        for d in range(2):
            for c in range(2):
                r = d * 64 + c * 32
                put_wide(R.G.at[d, k0 + c] if own else tail_of(R.A, d, c), v[r : r + 32])


def add_tail(R, c0, n):
    k0 = R.G.shape[1] - 8

    def one(c):
        for d in range(2):
            v = R.G[d, k0 + c0 + c].astype(F32) + R.wi[d, pl.ds(al((c0 + c) * 64, 64), 64), :].astype(F32)
            R.G[d, k0 + c0 + c] = v.astype(BF)

    loop(n, one)


def stage_attend_back(R, C, n, ring, xo):
    lo2 = lanes(128) < 64
    ln2 = lanes(128)

    def hi_lo(v):
        hi = v.astype(BF).astype(F32)
        return hi, v - hi

    def unpack(b):
        f = R.dorecv[b].astype(F32)
        for u in range(2):
            at = pl.ds(al(b * 256 + u * 128, 128), 128)
            do = jnp.where(lo2, f if u == 0 else roll64(f), 0.0)
            of = R.of[at, :]
            hi, low = hi_lo(-jnp.sum(do * of, axis=1, keepdims=True))
            R.DO[at, :] = jnp.where(ln2 == 64, hi, jnp.where(ln2 == 65, low, do)).astype(BF)
            hi, low = hi_lo(-of[:, 64:65])
            q = R.Q[at, :].astype(F32)
            R.Q[at, :] = jnp.where(ln2 == 64, hi, jnp.where(ln2 == 65, low, q)).astype(BF)

    loop(n, unpack)
    T = 512
    total = R.Q.shape[0]
    nt = total // T
    half = nt // 2
    seqs = R.prefix.shape[0]
    prefix = R.prefix[C.dp // (n // seqs)]
    R.dq[...] = jnp.zeros_like(R.dq)
    k = C.sems(n)
    k2 = C.sems(n)
    base = ring.take(T_AB * nt)
    kvs, kvr, dqr = R.asend.at[:, 0:256], R.arecv.at[:, 0:256], R.arecv.at[:, 256:384]

    def keys(jj):
        loop(T_AB // 2, lambda i: ring.tick(base + T_AB * jj + i))
        j = nt - 1 - jj
        kat = pl.ds(al(j * T, T), T)
        kk, vv = R.K[kat, :], R.V[kat, :]
        kpos = j * T + lax.broadcasted_iota(jnp.int32, (T, T), 0)

        def tile(i, carry):
            dk, dv = carry
            qat = pl.ds(al(i * T, T), T)
            q, do = R.Q[qat, :], R.DO[qat, :]
            qpos = i * T + lax.broadcasted_iota(jnp.int32, (1, T), 1)
            lim = jnp.maximum(qpos, prefix - 1)
            p = jnp.where(kpos <= lim, jnp.exp(mm_bt(kk, q)), 0.0)
            ds = (p * mm_bt(vv, do)).astype(BF)
            dv = dv + mm(p.astype(BF), do)
            dk = dk + mm(ds, q)
            R.dq[qat, :] = R.dq[qat, :] + mm_at(ds, kk)
            return dk, dv

        first = jnp.where(j >= half, j, 0)
        dk, dv = lax.fori_loop(
            first, nt, tile, (jnp.zeros((T, 128), F32), jnp.zeros((T, 128), F32))
        )
        lo = lanes(T) < 64
        kv = jnp.where(lo, dk, roll64(dv)).astype(BF)
        for u in range(2):
            b = j * 2 + u
            R.asend[b, 0:256, :] = kv[u * 256 : u * 256 + 256]

            @pl.when(b != C.dp)
            def _():
                C.rc(kvs.at[b], kvr.at[C.dp], k + b, (b, C.t), k + C.dp).start()

        loop(T_AB - T_AB // 2, lambda i: ring.tick(base + T_AB * jj + T_AB // 2 + i))

    loop(nt, keys)

    def queries(b):
        at = al(b * 256, 256)
        top = R.dq[pl.ds(at, 128), :] * 0.125
        bot = R.dq[pl.ds(al(at + 128, 128), 128), :] * 0.125
        R.osend[b] = jnp.where(lo2, top, roll64(bot)).astype(BF)

        @pl.when(b != C.dp)
        def _():
            C.rc(R.osend.at[b], dqr.at[C.dp], k2 + b, (b, C.t), k2 + C.dp).start()

    loop(n, queries)
    xo.wait_recv()
    add_tail(R, 0, 2)
    ring.run(T_KV)
    for src, dst, i in ((R.osend, dqr, 0), (kvs, kvr, 1)):
        mine = pltpu.make_async_copy(src.at[C.dp], dst.at[C.dp], C.lsem.at[i])
        mine.start()
        mine.wait()
    for src, dst, kk in ((kvs, kvr, k), (R.osend, dqr, k2)):
        for b in range(n):

            @pl.when(b != C.dp)
            def _():
                cp = C.rc(src.at[b], dst.at[b], kk + b, (b, C.t), kk + b)
                cp.wait_send()
                cp.wait_recv()

    hp = n // seqs
    lo = lanes(256) < 64
    for s in range(seqs):
        for pr in range(hp // 2):
            p = s * hp + 2 * pr
            cut = slice(pr * 128, pr * 128 + 128)
            e, d = kvr[p].astype(F32), kvr[p + 1].astype(F32)
            R.dproj[1, s * 256 : s * 256 + 256, cut] = jnp.where(lo, e, roll64(d)).astype(BF)
            R.dproj[2, s * 256 : s * 256 + 256, cut] = jnp.where(lo, roll64(e), d).astype(BF)
    unfold_heads(dqr, R.dproj.at[0], n, seqs)


def stage_qkv_back(R, C, fill):
    def part(k):
        at = pl.ds(al(k * CH, CH), CH)
        return (
            mm_bt(R.dproj[0, at, :], R.wqkv[0])
            + mm_bt(R.dproj[1, at, :], R.wqkv[1])
            + mm_bt(R.dproj[2, at, :], R.wqkv[2])
        )

    reduce4(R, C, part, R.dx, fill)
    own = pl.ds(al(C.t * CH, CH), CH)
    n, r = norm_parts(R.tok[own, :].astype(F32))
    dh1 = R.dx[...]
    R.GIN[C.t] = (R.x1[...] + norm_back(n, r, dh1 * R.par[0:1, :])).astype(BF)
    R.sm2[0:1, :] = rowsum(dh1 * n)
    R.sm2[1:2, :] = rowsum(dh1)


def stage_qkv_grad(R, C, ring):
    hq = R.h1.shape[1] // 2
    k = C.sems(2)
    cps = []
    k0 = R.G.shape[1] - 6
    for own, who in ((False, 1 - C.x), (True, C.x)):
        for d in range(2):
            for c in range(2):
                at = pl.ds(al(who * hq + (2 * d + c) * 128, 128), 128)
                h = R.h1[:, at]
                for m in range(3):
                    v = mm_at(h, R.dproj[m]).astype(BF)
                    w = v.shape[1]
                    i = 2 * m + c
                    dst = R.G.at[d, k0 + i] if own else tail_of(R.A, d, 2 + i)
                    dst[:, 0:w] = v[0:64]
                    dst[:, w : 2 * w] = v[64:128]
            ring.run(T_QG)
            if not own:
                cps.append(C.send(tail_of(R.A, d, 2, 6), tail_of(R.wi, d, 2, 6), k + d, C.xp))
    return cps


class Kinds:
    def __init__(self, nb, ni):
        self.i0 = nb
        self.o0 = nb + ni
        self.q0 = self.o0 + 2
        self.n = self.q0 + 6


class Sums:
    def __init__(self, R, C, n):
        self.R, self.C, self.n = R, C, n
        self.a, self.b = C.sems(2 * n), C.sems(2 * n)
        self.one = C.sems(6)

    def finish(self):
        R, C = self.R, self.C
        for d in range(2):
            pos = C.z if d == 0 else 3 - C.z
            fn = R.FN.at[d]
            C.rc(fn, fn, self.one + d, C.xp).wait_send()

            @pl.when(jnp.logical_or(pos == 1, pos == 2))
            def _():
                C.rc(fn, fn, self.one + 2 + d, C.xp).wait_send()

            cp = C.rc(fn, R.XH.at[d], self.one + 4 + d, C.xp)
            cp.wait_send()
            cp.wait_recv()
            pltpu.make_async_copy(fn, R.FH.at[d], C.lsem.at[4 + d]).wait()


class Ring:
    def __init__(self, sums, k0, k1, w):
        self.S, self.k0, self.k1, self.w = sums, k0, k1, w
        self.cur = 0
        self.total = k1 - k0 + 4 * w

    def take(self, n):
        base = self.cur
        self.cur += n
        return base

    def run(self, n):
        n = min(n, self.total - self.cur)
        if n <= 0:
            return
        base = self.take(n)
        loop(n, lambda i: self.tick(base + i))

    def rest(self):
        self.run(self.total - self.cur)

    def tick(self, s):
        for d in range(2):
            self.half(s + self.k0, d)

    def half(self, s, d):
        S, w = self.S, self.w
        R, C, n, one = S.R, S.C, S.n, S.one
        pos = C.z if d == 0 else 3 - C.z

        def dev(p):
            return ((p if d == 0 else 3 - p) * 2 + C.x, C.t)

        def act(k, cond):
            ok = jnp.logical_and(k >= self.k0, k < self.k1)
            return ok if cond is None else jnp.logical_and(ok, cond)

        def toward(src, dst, kr, p):
            return C.rc(src, dst, one + d, dev(p), kr)

        def away(fn, i, p):
            return C.rc(fn, fn, one + 2 + d, dev(p), S.b + i)

        @pl.when(act(s, jnp.logical_or(pos == 0, pos == 3)))
        def _():
            toward(R.G.at[d, s], R.L1.at[d, s], S.a + d * n + s, 1 + pos // 3).start()

        k2 = s - w

        @pl.when(act(k2, pos == 2))
        def _():
            i = d * n + k2
            toward(R.G.at[d, k2], R.L1.at[d, k2], S.a + i, 1).wait_recv()
            R.G[d, k2] = (R.G[d, k2].astype(F32) + R.L1[d, k2].astype(F32)).astype(BF)
            toward(R.G.at[d, k2], R.FN.at[d, k2], S.b + i, 1).start()

        k1 = s - 2 * w

        @pl.when(act(k1, pos == 1))
        def _():
            i = d * n + k1
            fn = R.FN.at[d, k1]
            toward(R.G.at[d, k1], R.L1.at[d, k1], S.a + i, 0).wait_recv()
            away(fn, i, 2).wait_recv()
            v = R.G[d, k1].astype(F32) + R.L1[d, k1].astype(F32) + R.FN[d, k1].astype(F32)
            R.FN[d, k1] = v.astype(BF)
            away(fn, i, 2).start()
            toward(fn, fn, S.b + i, 0).start()

        lag = w * (2 + jnp.where(pos == 1, 0, 1) + jnp.where(pos == 3, 1, 0))
        kf = s - lag

        @pl.when(act(kf, None))
        def _():
            i = d * n + kf
            fn = R.FN.at[d, kf]

            @pl.when(pos != 1)
            def _():
                away(fn, i, 1).wait_recv()

            @pl.when(pos == 2)
            def _():
                away(fn, i, 3).start()

            C.rc(fn, R.XH.at[d, kf], one + 4 + d, C.xp).start()
            pltpu.make_async_copy(fn, R.FH.at[d, kf], C.lsem.at[4 + d]).start()


def small_tensor(R, C):
    R.st[C.t, 0:8, :] = R.sm[...]
    R.st[C.t, 8:16, :] = R.sm2[...]
    k = C.sems(3)
    return [
        C.send(R.st.at[C.t], R.st.at[C.t], k + i, dev)
        for i, dev in enumerate((C.mate, C.yp, (C.dp, 3 - C.t)))
    ]


def small_dp(R, C, n, cps):
    for cp in cps:
        cp.wait_recv()
    tot = R.st[0] + R.st[1] + R.st[2] + R.st[3]
    sd = R.sd.at[C.dp]
    sd[0:8, :] = tot[0:8, :]
    sd[8:10, :] = tot[8:10, :]
    f = R.dproj.shape[2]

    def colsum(m):
        return rowsum(R.dproj[m].astype(F32))

    sd[10:11, 0:f] = colsum(0)
    sd[10:11, f : 2 * f] = colsum(2)
    half = R.DH.shape[2]
    for e in range(2):
        sd[11:12, e * half : (e + 1) * half] = rowsum(R.DH[e].astype(F32))
    k = C.sems(n)
    return [C.send(sd, R.sd.at[C.dp], k + o, (lax.rem(C.dp + o, n), C.t)) for o in range(1, n)]


def small_end(R, C, n, cps):
    for cp in cps:
        cp.wait_recv()
    tot = R.sd[0]
    for b in range(1, n):
        tot = tot + R.sd[b]
    R.osm[...] = tot
    for xx in range(2):
        v = R.sd[xx, 11:12, :]
        for b in range(2 + xx, n, 2):
            v = v + R.sd[b, 11:12, :]
        R.osm[11 + xx : 12 + xx, :] = v


class Refs:
    pass


LAG = 3
LAG_Q = 2
T_U, T_DA, T_DO, T_AB, T_KV, T_QB, T_QG = 3, 5, 4, 2, 4, 3, 1


def body(names, n, *refs):
    R = Refs()
    for name, ref in zip(names, refs):
        setattr(R, name, ref)
    C = Ctx(R.ssem, R.rsem, R.lsem)
    sem, count = barrier_start(C, n)
    half = R.wi.shape[2]
    off = pl.ds(al(C.x * half, half), half)
    wcp = [
        pltpu.make_async_copy(R.w_in.at[:, :, off], R.wi, C.lsem.at[2]),
        pltpu.make_async_copy(R.w_back.at[:, off, :], R.wb, C.lsem.at[3]),
    ]
    for cp in wcp:
        cp.start()
    for i, ref in enumerate((R.g1, R.b1, R.outb, R.g2, R.b2)):
        R.par[i : i + 1, :] = ref[...].astype(F32).reshape(1, ref.shape[0])
    R.par[5:7, :] = R.router[...].astype(F32)
    R.par[7:9, :] = R.backb[...].astype(F32)
    R.sm[...] = jnp.zeros_like(R.sm)
    R.sm2[...] = jnp.zeros_like(R.sm2)
    R.sd[...] = jnp.zeros_like(R.sd)
    pl.semaphore_wait(sem, count)
    wait_qkv = stage_qkv(R, C, n)
    wait_qkv()
    wait_cot = swap_cot(R, C)
    stage_attend(R, C, n)
    wait_cot()
    stage_out(R, C)
    for cp in wcp:
        cp.wait()
    over_u = Reduce8(C, R.YP, R.ly, R.sy, R.u)
    over_x = Reduce8(C, R.DXP, R.lx, R.sx, R.dx)
    stage_moe(R, C, (over_u, over_x))
    K = Kinds(half // 32, R.H2.shape[2] // 64)
    sums = Sums(R, C, K.n)
    ring = Ring(sums, 0, K.q0, LAG)
    last = Ring(sums, K.q0, K.n, LAG_Q)
    stage_moe_grads(R, C, K, ring)
    over_u.wait()
    ring.run(T_U)
    over_x.wait()
    stage_owner(R, C)
    wait_da = gather4(R, C, R.DA)
    wait_res = gather4(R, C, R.RES)
    ring.run(T_DA)
    wait_da()
    stage_out_back(R, C, n)
    wait_do = all_to_all(R, C, R.osend, R.dorecv, n)
    stage_out_grad(R, C)
    ring.run(T_DO)
    wait_do()
    C.drain()
    xo = C.send(R.A.at[:, 0:128, :], R.wi.at[:, 0:128, :], C.sems(1), C.xp)
    stage_attend_back(R, C, n, ring, xo)
    xq = stage_qkv_grad(R, C, ring)
    stage_qkv_back(R, C, lambda: ring.run(T_QB))
    wait_gin = gather4(R, C, R.GIN)
    small = small_tensor(R, C)
    for cp in xq:
        cp.wait_recv()
    add_tail(R, 2, 6)
    for r in range(8):
        last.run(1)
        ring.run(1)
        if r == 2:
            small = small_dp(R, C, n, small)
    wait_gin()
    wait_res()
    small_end(R, C, n, small)
    ring.rest()
    last.rest()
    sums.finish()
    C.drain()


def place_body(nb, ni, fh, xh, res, gin, osm, oB, oI, oQ, oO, oR, oG, *rest):
    vec, (cf, cx, cr, cg, vB, vI, vQ, vO, vR, vG, isem, osem) = rest[:9], rest[9:]
    x = lax.rem(lax.axis_index("dp"), 2)
    n = nb + ni + 8
    half = nb * 32
    cuts = ((0, nb), (nb, ni), (nb + ni, 8))
    srcs = ((fh, cf, x), (xh, cx, 1 - x))
    ins = {}
    for j, (src, buf, h) in enumerate(srcs):
        for d in range(2):
            for c, (k0, m) in enumerate(cuts):
                cp = pltpu.make_async_copy(
                    src.at[d, pl.ds(k0, m)], buf.at[d, pl.ds(k0, m)], isem.at[j * 6 + d * 3 + c]
                )
                cp.start()
                ins[j, d, c] = cp
    rows = [pltpu.make_async_copy(a, b, isem.at[12 + i]) for i, (a, b) in enumerate(((res, cr), (gin, cg)))]
    for cp in rows:
        cp.start()
    outs = []

    def put(src, dst):
        cp = pltpu.make_async_copy(src, dst, osem.at[len(outs)])
        cp.start()
        outs.append(cp)

    for j, (src, buf, h) in enumerate(srcs):
        for d in range(2):
            ins[j, d, 0].wait()

            def back(k):
                v = buf[d, k].astype(F32)
                at = pl.ds(al(k * 32, 32), 32)
                vB[j, d, at, 0:512] = v[0:32]
                vB[j, d, at, 512:1024] = v[32:64]

            loop(nb, back)
            put(vB.at[j, d], oB.at[d, pl.ds(al(h * half, half), half), :])
            ins[j, d, 1].wait()

            def into(k):
                vI[j, d, pl.ds(al(k * 64, 64), 64), :] = buf[d, nb + k].astype(F32)

            loop(ni, into)
            put(vI.at[j, d], oI.at[d, :, pl.ds(al(h * 512, 512), 512)])
    for j, (src, buf, h) in enumerate(srcs):
        for d in range(2):
            ins[j, d, 2].wait()
            for c in range(2):
                v = buf[d, nb + ni + c].astype(F32)
                at = pl.ds(al(h * 128 + d * 64 + c * 32, 32), 32)
                vO[at, 0:512] = v[0:32]
                vO[at, 512:1024] = v[32:64]
            for c in range(6):
                v = buf[d, nb + ni + 2 + c].astype(F32)
                row = h * 512 + d * 256 + (c % 2) * 128
                vQ[c // 2, pl.ds(al(row, 64), 64), :] = v[:, 0:256]
                vQ[c // 2, pl.ds(al(row + 64, 64), 64), :] = v[:, 256:512]
    put(vO, oO)
    put(vQ, oQ)
    for cp, src, buf, out in ((rows[0], cr, vR, oR), (rows[1], cg, vG, oG)):
        cp.wait()
        for t in range(src.shape[0]):
            buf[t] = src[t].astype(F32)
        put(buf, out)
    ln1g, ln1b, qv, outb, ln2g, ln2b, rout, inb, bb = vec
    for ref, r in ((ln1g, 8), (ln1b, 9), (outb, 2), (ln2g, 0), (ln2b, 1)):
        ref[...] = osm[r : r + 1, :]
    for i in range(2):
        qv[i : i + 1, :] = osm[10:11, i * 256 : i * 256 + 256]
        rout[i : i + 1, :] = osm[3 + i : 4 + i, :]
        bb[i : i + 1, :] = osm[5 + i : 6 + i, :]
        for e in range(2):
            inb[e : e + 1, i * 512 : i * 512 + 512] = osm[11 + i : 12 + i, e * 512 : e * 512 + 512]
    for cp in outs:
        cp.wait()


def place(fh, xh, res, gin, osm, nb, ni):
    sds = jax.ShapeDtypeStruct
    vm = pl.BlockSpec(memory_space=pltpu.VMEM)
    hbm = pl.BlockSpec(memory_space=pl.ANY)
    n, half = nb + ni + 8, nb * 32
    big = [(2, 2 * half, 1024), (2, ni * 64, 1024), (3, 1024, 256), (256, 1024), res.shape, gin.shape]
    row = (1, 1024)
    small = [row, row, (2, 256), row, row, row, (2, 1024), (2, 1024), (2, 1024)]
    V = pltpu.VMEM
    return pl.pallas_call(
        functools.partial(place_body, nb, ni),
        out_shape=[sds(v, F32) for v in big + small],
        in_specs=[hbm, hbm, hbm, hbm, vm],
        out_specs=[hbm] * len(big) + [vm] * len(small),
        scratch_shapes=[
            V((2, n, 64, 512), BF),
            V((2, n, 64, 512), BF),
            V(res.shape, BF),
            V(gin.shape, BF),
            V((2, 2, half, 1024), F32),
            V((2, 2, ni * 64, 512), F32),
            V((3, 1024, 256), F32),
            V((256, 1024), F32),
            V(res.shape, F32),
            V(gin.shape, F32),
            pltpu.SemaphoreType.DMA((14,)),
            pltpu.SemaphoreType.DMA((12,)),
        ],
        compiler_params=pltpu.CompilerParams(vmem_limit_bytes=60000000),
        name="place",
    )(fh, xh, res, gin, osm)


def fast_local(args, n, nt):
    (tokens, g1, b1, w_qkv, qvb, w_out, out_b, g2, b2, router, w_in, in_b, w_back, back_b,
     routes, prefix, cot) = args
    S, span, D = tokens.shape
    rows = S * span
    F = w_qkv.shape[2]
    H = w_in.shape[2]
    half = H // 2
    total = n * span
    vm = pl.BlockSpec(memory_space=pltpu.VMEM)
    hbm = pl.BlockSpec(memory_space=pl.ANY)
    ins = [
        ("tok", tokens.reshape(rows, D), vm),
        ("g1", g1, vm),
        ("b1", b1, vm),
        ("outb", out_b, vm),
        ("g2", g2, vm),
        ("b2", b2, vm),
        ("router", router.T, vm),
        ("backb", back_b, vm),
        ("wqkv", w_qkv.transpose(1, 0, 2), vm),
        ("qvb", qvb, vm),
        ("wout", w_out, vm),
        ("routes", routes.reshape(1, rows), vm),
        ("prefix", prefix, pl.BlockSpec(memory_space=pltpu.SMEM)),
        ("cot", cot.reshape(rows, D), vm),
        ("inb", in_b, vm),
        ("w_in", w_in, hbm),
        ("w_back", w_back, hbm),
    ]
    sds = jax.ShapeDtypeStruct
    nch = half // 32 + D // 64 + 8
    outs = [
        ("RES", sds((nt, CH, D), BF), vm),
        ("GIN", sds((nt, CH, D), BF), vm),
        ("FH", sds((2, nch, 64, 512), BF), hbm),
        ("XH", sds((2, nch, 64, 512), BF), hbm),
        ("osm", sds((16, D), F32), vm),
    ]
    V = pltpu.VMEM
    scr = [
        ("h1", V((rows, D), BF)),
        ("asend", V((n, 384, 128), BF)),
        ("arecv", V((n, 384, 128), BF)),
        ("Q", V((total, 128), BF)),
        ("K", V((total, 128), BF)),
        ("V", V((total, 128), BF)),
        ("DO", V((total, 128), BF)),
        ("of", V((total, 128), F32)),
        ("dq", V((total, 128), F32)),
        ("osend", V((n, 128, 128), BF)),
        ("orecv", V((n, 128, 128), BF)),
        ("dorecv", V((n, 128, 128), BF)),
        ("otok", V((rows, F), BF)),
        ("dproj", V((3, rows, F), BF)),
        ("p4", V((3, CH, D), BF)),
        ("l4", V((3, CH, D), BF)),
        ("x1", V((CH, D), F32)),
        ("u", V((CH, D), F32)),
        ("dx", V((CH, D), F32)),
        ("cols", V((CH, 128), F32)),
        ("H2", V((8, CH, D), BF)),
        ("GG", V((8, CH, D), BF)),
        ("META", V((8, CH, 128), BF)),
        ("cx", V((rows, D), BF)),
        ("par", V((16, D), F32)),
        ("wi", V((2, D, half), BF)),
        ("wb", V((2, half, D), BF)),
        ("A", V((2, 8 * CH, half), BF)),
        ("DH", V((2, 8 * CH, half), BF)),
        ("YP", V((8, CH, D), BF)),
        ("DXP", V((8, CH, D), BF)),
        ("ly", V((7, CH, D), BF)),
        ("lx", V((7, CH, D), BF)),
        ("sy", V((3, CH, D), BF)),
        ("sx", V((3, CH, D), BF)),
        ("DA", V((nt, CH, D), BF)),
        ("G", V((2, nch, 64, 512), BF)),
        ("L1", V((2, nch, 64, 512), BF)),
        ("FN", V((2, nch, 64, 512), BF)),
        ("sm", V((8, D), F32)),
        ("sm2", V((8, D), F32)),
        ("st", V((4, 16, D), F32)),
        ("sd", V((n, 16, D), F32)),
        ("ssem", pltpu.SemaphoreType.DMA((140 + 4 * nch,))),
        ("rsem", pltpu.SemaphoreType.DMA((140 + 4 * nch,))),
        ("lsem", pltpu.SemaphoreType.DMA((16,))),
    ]
    names = [i[0] for i in ins] + [o[0] for o in outs] + [s[0] for s in scr]
    res, gin, fh, xh, osm = pl.pallas_call(
        functools.partial(body, names, n),
        out_shape=[o[1] for o in outs],
        in_specs=[i[2] for i in ins],
        out_specs=[o[2] for o in outs],
        scratch_shapes=[s[1] for s in scr],
        compiler_params=pltpu.CompilerParams(
            collective_id=0, has_side_effects=True, vmem_limit_bytes=67043328
        ),
        name="layer",
    )(*[i[1] for i in ins])
    oB, oI, oQ, oO, oR, oG, ln1g, ln1b, qv, outb, ln2g, ln2b, rout, inb, bb = place(
        fh, xh, res, gin, osm, half // 32, D // 64
    )
    return (
        oR.reshape(S, span, D),
        oG.reshape(S, span, D),
        ln1g.reshape(D),
        ln1b.reshape(D),
        oQ.transpose(1, 0, 2),
        qv,
        oO,
        outb.reshape(D),
        ln2g.reshape(D),
        ln2b.reshape(D),
        rout.T,
        oI,
        inb,
        oB,
        bb,
    )


SCALE = 0.125
EPSILON = 1e-05
MASKED = -1e30
HIGHEST = lax.Precision.HIGHEST


def layer_norm(values, norm_gain, norm_bias):
    centred = values - jnp.mean(values, axis=-1, keepdims=True)
    spread = jnp.mean(centred * centred, axis=-1, keepdims=True)
    return centred * lax.rsqrt(spread + EPSILON) * norm_gain + norm_bias


def heads_of(block, head_count):
    seq_count, row_count, feat_count = block.shape
    return block.reshape(seq_count, row_count, head_count, feat_count // head_count).transpose(
        0, 2, 1, 3
    )


def tokens_of(block):
    seq_count, head_count, row_count, head_width = block.shape
    return block.transpose(0, 2, 1, 3).reshape(seq_count, row_count, head_count * head_width)


def masked_scores(queries, key_heads, query_start, key_start, prefix):
    scores = (
        jnp.einsum("shqd,shkd->shqk", queries, key_heads, preferred_element_type=jnp.float32)
        * SCALE
    )
    query_pos = query_start + jnp.arange(queries.shape[2], dtype=jnp.int32)
    key_pos = key_start + jnp.arange(key_heads.shape[2], dtype=jnp.int32)
    visible_mask = (key_pos[None, None, :] <= query_pos[None, :, None]) | (
        key_pos[None, None, :] < prefix[:, None, None]
    )
    visible_mask = visible_mask[:, None]
    return (jnp.where(visible_mask, scores, MASKED), visible_mask)


def block_live(key_start, query_last, prefix):
    return jnp.any(key_start < prefix) | (key_start <= query_last)


def prob_grads(
    queries, key_heads, value_heads, douts, log_total, delta, query_start, key_start, prefix
):
    scores, visible_mask = masked_scores(queries, key_heads, query_start, key_start, prefix)
    probs = jnp.where(visible_mask, jnp.exp(scores - log_total[..., None]), 0.0)
    dprob = jnp.einsum("shqd,shkd->shqk", douts, value_heads, preferred_element_type=jnp.float32)
    dscore = (probs * (dprob - delta[..., None])).astype(jnp.bfloat16)
    return (probs, dscore)


def attend_fold(run_state, piece_rows, piece_start, queries, first_row, prefix):
    key_piece, value_piece = piece_rows
    head_count = queries.shape[1]
    row_count = key_piece.shape[1]
    block_width = math.gcd(row_count, 512)
    query_last = first_row + queries.shape[2] - 1

    def attend_update(block_index, state_now):
        key_start = block_index * block_width
        key_heads = heads_of(
            lax.dynamic_slice_in_dim(key_piece, block_index * block_width, block_width, 1),
            head_count,
        )
        value_heads = heads_of(
            lax.dynamic_slice_in_dim(value_piece, block_index * block_width, block_width, 1),
            head_count,
        )
        scores, visible_mask = masked_scores(queries, key_heads, first_row, key_start, prefix)
        run_max, run_sum, run_out = state_now
        new_max = jnp.maximum(run_max, jnp.max(scores, axis=-1))
        factor = jnp.exp(run_max - new_max)
        weights = jnp.where(visible_mask, jnp.exp(scores - new_max[..., None]), 0.0)
        run_sum = factor * run_sum + jnp.sum(weights, axis=-1)
        run_out = factor[..., None] * run_out + jnp.einsum(
            "shqk,shkd->shqd", weights, value_heads.astype(jnp.float32), precision=HIGHEST
        )
        return (new_max, run_sum, run_out)

    def attend_block_step(state_now, block_index):
        key_start = block_index * block_width
        is_live = block_live(key_start, query_last, prefix)
        return (
            lax.cond(
                is_live, functools.partial(attend_update, block_index), lambda unchanged: unchanged, state_now
            ),
            None,
        )

    run_state, unused = lax.scan(
        attend_block_step, run_state, jnp.arange(row_count // block_width, dtype=jnp.int32)
    )
    return run_state


def key_pass(queries, douts, log_total, delta, keys_all, values_all, first_row, prefix):
    head_count = queries.shape[1]
    total_rows = keys_all.shape[1]
    block_width = math.gcd(total_rows, 512)
    query_last = first_row + queries.shape[2] - 1

    def key_block_step(dquery, block_index):
        key_start = block_index * block_width

        def work(dquery_now):
            key_heads = heads_of(
                lax.dynamic_slice_in_dim(keys_all, key_start, block_width, 1), head_count
            )
            value_heads = heads_of(
                lax.dynamic_slice_in_dim(values_all, key_start, block_width, 1), head_count
            )
            probs, dscore = prob_grads(
                queries,
                key_heads,
                value_heads,
                douts,
                log_total,
                delta,
                first_row,
                key_start,
                prefix,
            )
            dquery_now = (
                dquery_now
                + jnp.einsum(
                    "shqk,shkd->shqd", dscore, key_heads, preferred_element_type=jnp.float32
                )
                * SCALE
            )
            return (dquery_now, ())

        def skipped(dquery_now):
            return (dquery_now, ())

        return lax.cond(block_live(key_start, query_last, prefix), work, skipped, dquery)

    dquery, key_parts = lax.scan(
        key_block_step,
        jnp.zeros(queries.shape, jnp.float32),
        jnp.arange(total_rows // block_width, dtype=jnp.int32),
    )
    return (dquery, ())


def query_fold(run_state, piece_rows, piece_start, key_heads, value_heads, first_row, prefix):
    query_piece, dout_piece, total_piece, delta_piece = piece_rows
    head_count = key_heads.shape[1]
    row_count = query_piece.shape[1]
    block_width = math.gcd(row_count, 512)

    def query_update(block_index, state_now):
        query_start = block_index * block_width
        offset = block_index * block_width
        queries = heads_of(
            lax.dynamic_slice_in_dim(query_piece, offset, block_width, 1), head_count
        )
        douts = heads_of(lax.dynamic_slice_in_dim(dout_piece, offset, block_width, 1), head_count)
        log_total = lax.dynamic_slice_in_dim(total_piece, offset, block_width, 1).transpose(0, 2, 1)
        delta = lax.dynamic_slice_in_dim(delta_piece, offset, block_width, 1).transpose(0, 2, 1)
        probs, dscore = prob_grads(
            queries, key_heads, value_heads, douts, log_total, delta, query_start, first_row, prefix
        )
        dkey_now, dvalue_now = state_now
        dkey_now = (
            dkey_now
            + jnp.einsum("shqk,shqd->shkd", dscore, queries, preferred_element_type=jnp.float32)
            * SCALE
        )
        dvalue_now = dvalue_now + jnp.einsum(
            "shqk,shqd->shkd", probs, douts.astype(jnp.float32), precision=HIGHEST
        )
        return (dkey_now, dvalue_now)

    def query_block_step(state_now, block_index):
        query_last = block_index * block_width + block_width - 1
        is_live = block_live(first_row, query_last, prefix)
        return (
            lax.cond(
                is_live, functools.partial(query_update, block_index), lambda unchanged: unchanged, state_now
            ),
            None,
        )

    run_state, unused = lax.scan(
        query_block_step, run_state, jnp.arange(row_count // block_width, dtype=jnp.int32)
    )
    return run_state


def local(
    tokens,
    ln1_gain,
    ln1_bias,
    w_qkv,
    qv_bias,
    w_out,
    out_bias,
    ln2_gain,
    ln2_bias,
    router,
    w_in,
    in_bias,
    w_back,
    back_bias,
    routes,
    prefix,
    cotangent,
):
    seq_count, span_len, model_width = tokens.shape
    tok_rows = seq_count * span_len
    local_feats = w_qkv.shape[2]
    head_count = local_feats // HEAD_DIM
    expert_count = w_in.shape[0]
    first_row = lax.axis_index("dp") * span_len
    local_shape = (seq_count, span_len, local_feats)
    source = tokens.reshape(tok_rows, model_width).astype(jnp.float32)
    normed_one, ln1_pull = jax.vjp(
        layer_norm, source, ln1_gain.astype(jnp.float32), ln1_bias.astype(jnp.float32)
    )
    hidden_one = normed_one.astype(jnp.bfloat16)
    projected = jnp.einsum("ti,icf->tcf", hidden_one, w_qkv, preferred_element_type=jnp.float32)
    bias_float = qv_bias.astype(jnp.float32)
    query_tok = (projected[:, 0] + bias_float[0]).astype(jnp.bfloat16).reshape(local_shape)
    key_tok = projected[:, 1].astype(jnp.bfloat16).reshape(local_shape)
    value_tok = (projected[:, 2] + bias_float[1]).astype(jnp.bfloat16).reshape(local_shape)
    queries = heads_of(query_tok, head_count)
    stat_shape = queries.shape[:3]
    start_state = (
        jnp.full(stat_shape, MASKED, jnp.float32),
        jnp.zeros(stat_shape, jnp.float32),
        jnp.zeros(queries.shape, jnp.float32),
    )
    fold_keys = functools.partial(attend_fold, queries=queries, first_row=first_row, prefix=prefix)
    run_max, run_sum, run_out = fold_keys(
        start_state,
        (
            lax.all_gather(key_tok, "dp", axis=1, tiled=True),
            lax.all_gather(value_tok, "dp", axis=1, tiled=True),
        ),
        jnp.int32(0),
    )
    mixed_heads = run_out / run_sum[..., None]
    log_total = run_max + jnp.log(run_sum)
    mixed_b = tokens_of(mixed_heads.astype(jnp.bfloat16)).reshape(tok_rows, local_feats)
    out_shift = out_bias.astype(jnp.float32)
    gain_two = ln2_gain.astype(jnp.float32)
    shift_two = ln2_bias.astype(jnp.float32)
    attn_part = jnp.dot(mixed_b, w_out, preferred_element_type=jnp.float32)
    attn_out = lax.psum(attn_part, "tensor") + out_shift
    residual = source + attn_out
    normed_two, ln2_pull = jax.vjp(layer_norm, residual, gain_two, shift_two)
    hidden_two = normed_two.astype(jnp.bfloat16)
    logits = jnp.dot(hidden_two, router, preferred_element_type=jnp.float32)
    chosen = routes.reshape(tok_rows)
    expert_ids = jnp.arange(expert_count, dtype=jnp.int32)
    expert_hot = (chosen[:, None] == expert_ids[None, :]).astype(jnp.int32)

    def gate_of(logit_vals):
        return jnp.sum(
            jnp.where(expert_hot == 1, jax.nn.softmax(logit_vals, axis=-1), 0.0), axis=-1
        )

    gate_value, gate_pull = jax.vjp(gate_of, logits)
    earlier = jnp.cumsum(expert_hot, axis=0, dtype=jnp.int32) - expert_hot
    slot_place = jnp.sum(earlier * expert_hot, axis=1, dtype=jnp.int32)
    slot_ids = jnp.arange(CAP, dtype=jnp.int32)
    select_mask = (expert_hot[:, :, None] == 1) & (
        slot_place[:, None, None] == slot_ids[None, None, :]
    )
    select = select_mask.astype(jnp.bfloat16)
    select_float = select_mask.astype(jnp.float32)
    dispatched = jnp.einsum(
        "tec,td->ecd", select, hidden_two, preferred_element_type=jnp.float32
    ).astype(jnp.bfloat16)
    pre_act = (
        jnp.einsum("ecd,edf->ecf", dispatched, w_in, preferred_element_type=jnp.float32)
        + in_bias.astype(jnp.float32)[:, None, :]
    )
    act_float, gelu_pull = jax.vjp(functools.partial(jax.nn.gelu, approximate=False), pre_act)
    active = act_float.astype(jnp.bfloat16)
    expert_part = jnp.einsum("ecf,efd->ecd", active, w_back, preferred_element_type=jnp.float32)
    expert_full = lax.psum(expert_part, "tensor") + back_bias.astype(jnp.float32)[:, None, :]
    combined = jnp.einsum("tec,ecd->td", select_float, expert_full, precision=HIGHEST)
    layer_rows = residual + gate_value[:, None] * combined
    grad_out = cotangent.reshape(tok_rows, model_width).astype(jnp.float32)
    dgate = jnp.sum(grad_out * combined, axis=-1)
    dlogit_b = gate_pull(dgate)[0].astype(jnp.bfloat16)
    gated_grad = (gate_value[:, None] * grad_out).astype(jnp.bfloat16)
    dexpert_b = jnp.einsum(
        "tec,td->ecd", select, gated_grad, preferred_element_type=jnp.float32
    ).astype(jnp.bfloat16)
    grad_back_bias = jnp.sum(dexpert_b, axis=1, dtype=jnp.float32)
    grad_w_back = jnp.einsum("ecf,ecd->efd", active, dexpert_b, preferred_element_type=jnp.float32)
    dactive = jnp.einsum("ecd,efd->ecf", dexpert_b, w_back, preferred_element_type=jnp.float32)
    dpre_b = gelu_pull(dactive)[0].astype(jnp.bfloat16)
    grad_in_bias = jnp.sum(dpre_b, axis=1, dtype=jnp.float32)
    grad_w_in = jnp.einsum("ecd,ecf->edf", dispatched, dpre_b, preferred_element_type=jnp.float32)
    slot_part = jnp.einsum("ecf,edf->ecd", dpre_b, w_in, preferred_element_type=jnp.float32)
    dslots = lax.psum(slot_part, "tensor")
    dnorm_two = jnp.einsum("tec,ecd->td", select_float, dslots, precision=HIGHEST) + jnp.einsum(
        "te,de->td", dlogit_b, router, preferred_element_type=jnp.float32
    )
    grad_router = jnp.einsum("td,te->de", hidden_two, dlogit_b, preferred_element_type=jnp.float32)
    dresid_norm, grad_ln2_gain, grad_ln2_bias = ln2_pull(dnorm_two)
    dresidual = grad_out + dresid_norm
    dattn_b = dresidual.astype(jnp.bfloat16)
    grad_out_bias = jnp.sum(dattn_b, axis=0, dtype=jnp.float32)
    grad_w_out = jnp.einsum("tf,td->fd", mixed_b, dattn_b, preferred_element_type=jnp.float32)
    dmixed_tok = (
        jnp.einsum("td,fd->tf", dattn_b, w_out, preferred_element_type=jnp.float32)
        .astype(jnp.bfloat16)
        .reshape(local_shape)
    )
    douts = heads_of(dmixed_tok, head_count)
    delta = jnp.sum(douts.astype(jnp.float32) * mixed_heads, axis=-1)
    keys_all, values_all = (
        lax.all_gather(key_tok, "dp", axis=1, tiled=True),
        lax.all_gather(value_tok, "dp", axis=1, tiled=True),
    )
    dquery, unused = key_pass(
        queries, douts, log_total, delta, keys_all, values_all, first_row, prefix
    )
    total_rows = log_total.transpose(0, 2, 1)
    delta_rows = delta.transpose(0, 2, 1)
    fold_rows = functools.partial(
        query_fold,
        key_heads=heads_of(key_tok, head_count),
        value_heads=heads_of(value_tok, head_count),
        first_row=first_row,
        prefix=prefix,
    )
    zero_heads = jnp.zeros(queries.shape, jnp.float32)
    dkey_heads, dvalue_heads = fold_rows(
        (zero_heads, zero_heads),
        (
            lax.all_gather(query_tok, "dp", axis=1, tiled=True),
            lax.all_gather(dmixed_tok, "dp", axis=1, tiled=True),
            lax.all_gather(total_rows.astype(jnp.bfloat16), "dp", axis=1, tiled=True).astype(
                jnp.float32
            ),
            lax.all_gather(delta_rows.astype(jnp.bfloat16), "dp", axis=1, tiled=True).astype(
                jnp.float32
            ),
        ),
        jnp.int32(0),
    )
    dkey = tokens_of(dkey_heads)
    dvalue = tokens_of(dvalue_heads)
    dquery_b = tokens_of(dquery).astype(jnp.bfloat16).reshape(tok_rows, local_feats)
    dkey_b = dkey.astype(jnp.bfloat16).reshape(tok_rows, local_feats)
    dvalue_b = dvalue.astype(jnp.bfloat16).reshape(tok_rows, local_feats)
    dproject = jnp.stack([dquery_b, dkey_b, dvalue_b], axis=1)
    grad_qv_bias = jnp.stack(
        [jnp.sum(dquery_b, axis=0, dtype=jnp.float32), jnp.sum(dvalue_b, axis=0, dtype=jnp.float32)]
    )
    grad_w_qkv = jnp.einsum("ti,tcf->icf", hidden_one, dproject, preferred_element_type=jnp.float32)
    norm_part = jnp.einsum("tcf,icf->ti", dproject, w_qkv, preferred_element_type=jnp.float32)
    dnorm_one = lax.psum(norm_part, "tensor")
    dsource_norm, grad_ln1_gain, grad_ln1_bias = ln1_pull(dnorm_one)
    input_grad = (dresidual + dsource_norm).reshape(seq_count, span_len, model_width)
    summed = lax.psum(
        (
            grad_ln1_gain,
            grad_ln1_bias,
            grad_w_qkv,
            grad_qv_bias,
            grad_w_out,
            grad_out_bias,
            grad_ln2_gain,
            grad_ln2_bias,
            grad_router,
            grad_w_in,
            grad_in_bias,
            grad_w_back,
            grad_back_bias,
        ),
        "dp",
    )
    layer_out = layer_rows.reshape(seq_count, span_len, model_width)
    return (layer_out, input_grad) + tuple(summed)


def solution(mesh):
    in_specs = (
        P(None, "dp", None),
        P(),
        P(),
        P(None, None, "tensor"),
        P(None, "tensor"),
        P("tensor", None),
        P(),
        P(),
        P(),
        P(),
        P(None, None, "tensor"),
        P(None, "tensor"),
        P(None, "tensor", None),
        P(),
        P(None, "dp", None),
        P(),
        P(None, "dp", None),
    )
    out_specs = (
        P(None, "dp", None),
        P(None, "dp", None),
        P(),
        P(),
        P(None, None, "tensor"),
        P(None, "tensor"),
        P("tensor", None),
        P(),
        P(),
        P(),
        P(),
        P(None, None, "tensor"),
        P(None, "tensor"),
        P(None, "tensor", None),
        P(),
    )
    n, nt = mesh.shape["dp"], mesh.shape["tensor"]

    def step(*args):
        tokens, w_qkv = args[0], args[3]
        heads = w_qkv.shape[2] // HEAD_DIM
        fits = (
            nt == 4
            and n == 8
            and tokens.shape[2] == 1024
            and w_qkv.shape[2] == 256
            and args[10].shape == (2, 1024, 1024)
            and n == tokens.shape[0] * heads
            and tokens.shape[0] * tokens.shape[1] == nt * CH
            and tokens.shape[1] == 256
        )
        return fast_local(args, n, nt) if fits else local(*args)

    return jax.shard_map(step, mesh=mesh, in_specs=in_specs, out_specs=out_specs, check_vma=False)
```

```python
import functools
import math

import jax
import jax.numpy as jnp
from jax import lax
from jax.experimental import pallas as pl
from jax.experimental.pallas import tpu as pltpu
from jax.sharding import PartitionSpec as P

F32 = jnp.float32
BF = jnp.bfloat16
MESH = pl.DeviceIdType.MESH
EPS = 1e-05
CAP = 320
HEAD_DIM = 64
NEG = -1e30
CH = 128


def mm(a, b):
    return lax.dot_general(a, b, (((1,), (0,)), ((), ())), preferred_element_type=F32)


def mm_bt(a, b):
    return lax.dot_general(a, b, (((1,), (1,)), ((), ())), preferred_element_type=F32)


def mm_at(a, b):
    return lax.dot_general(a, b, (((0,), (0,)), ((), ())), preferred_element_type=F32)


def loop(n, body):
    def step(i, carry):
        body(i)
        return carry

    lax.fori_loop(0, n, step, 0)


def al(v, m):
    return pl.multiple_of(v, m)


def lanes(rows):
    return lax.broadcasted_iota(jnp.int32, (rows, 128), 1)


def roll64(v):
    return pltpu.roll(v, 64, 1)


class Ctx:
    def __init__(self, ssem, rsem, lsem):
        self.ssem, self.rsem, self.lsem = ssem, rsem, lsem
        self.next = 0
        self.pending = []
        dp = lax.axis_index("dp")
        t = lax.axis_index("tensor")
        self.dp, self.t = dp, t
        self.z, self.x = dp // 2, lax.rem(dp, 2)
        self.y, self.c = t // 2, lax.rem(t, 2)
        x1 = 1 - self.x
        dpx = self.z * 2 + x1
        tm = self.y * 2 + 1 - self.c
        ty = (1 - self.y) * 2 + self.c
        self.mate = (dp, tm)
        self.yp = (dp, ty)
        self.xp = (dpx, t)
        self.dg = (dpx, ty)
        self.t_mate, self.t_y = tm, ty

    def sems(self, n):
        k = self.next
        self.next += n
        return k

    def rc(self, src, dst, k, dev, kr=None):
        return pltpu.make_async_remote_copy(
            src_ref=src,
            dst_ref=dst,
            send_sem=self.ssem.at[k],
            recv_sem=self.rsem.at[k if kr is None else kr],
            device_id=dev,
            device_id_type=MESH,
        )

    def send(self, src, dst, k, dev):
        cp = self.rc(src, dst, k, dev)
        cp.start()
        self.pending.append(cp)
        return cp

    def drain(self):
        for cp in self.pending:
            cp.wait_send()
        self.pending = []


def barrier_start(C, n_dp):
    sem = pltpu.get_barrier_semaphore()
    devs = [(lax.rem(C.dp + o, n_dp), C.t) for o in range(1, n_dp)]
    devs += [C.mate, C.yp, C.dg, (C.dp, 3 - C.t)]
    for d in devs:
        pl.semaphore_signal(sem, inc=1, device_id=d, device_id_type=MESH)
    return sem, len(devs)


def norm_parts(v):
    mean = jnp.mean(v, axis=-1, keepdims=True)
    cent = v - mean
    var = jnp.mean(cent * cent, axis=-1, keepdims=True)
    r = lax.rsqrt(var + EPS)
    return cent * r, r


def stage_qkv(R, C, n):
    rows = R.tok.shape[0]
    gain, bias = R.par[0:1, :], R.par[1:2, :]
    hp = R.wqkv.shape[2] // HEAD_DIM
    k = C.sems(n)

    def seq(s):
        def ln(i):
            at = pl.ds(al(s * 256 + i * 32, 32), 32)
            n1, _ = norm_parts(R.tok[at, :].astype(F32))
            R.h1[at, :] = (n1 * gain + bias).astype(BF)

        loop(8, ln)
        at = pl.ds(al(s * 256, 256), 256)
        h = R.h1[at, :]
        lo = lanes(256) < 64
        lo2 = lanes(128) < 64
        for pr in range(hp // 2):
            cut = slice(pr * 128, pr * 128 + 128)
            tq = (mm(h, R.wqkv[0, :, cut]) + R.qvb[0:1, cut].astype(F32)) * 0.125
            tk = mm(h, R.wqkv[1, :, cut])
            tv = mm(h, R.wqkv[2, :, cut]) + R.qvb[1:2, cut].astype(F32)
            p = s * hp + 2 * pr
            R.asend[p, 0:256, :] = jnp.where(lo, tq, roll64(tk)).astype(BF)
            R.asend[p + 1, 0:256, :] = jnp.where(lo, roll64(tq), tk).astype(BF)
            a, b = tv[0:128], tv[128:256]
            R.asend[p, 256:384, :] = jnp.where(lo2, a, roll64(b)).astype(BF)
            R.asend[p + 1, 256:384, :] = jnp.where(lo2, roll64(a), b).astype(BF)
            for j in range(2):
                send_slice(C, R.asend, R.arecv, k, p + j)

    loop(rows // 256, seq)
    return lambda: wait_slices(C, R.asend, R.arecv, k, n, 0)


def send_slice(C, src, dst, k, p):
    @pl.when(p != C.dp)
    def _():
        C.rc(src.at[p], dst.at[C.dp], k + p, (p, C.t), k + C.dp).start()


def wait_slices(C, src, dst, k, n, sem):
    mine = pltpu.make_async_copy(src.at[C.dp], dst.at[C.dp], C.lsem.at[sem])
    mine.start()
    mine.wait()
    for b in range(n):

        @pl.when(b != C.dp)
        def _():
            cp = C.rc(src.at[b], dst.at[b], k + b, (b, C.t), k + b)
            cp.wait_send()
            cp.wait_recv()


def all_to_all(R, C, src, dst, n):
    k = C.sems(n)
    cps = [
        C.send(src.at[lax.rem(C.dp + o, n)], dst.at[C.dp], k + o, (lax.rem(C.dp + o, n), C.t))
        for o in range(1, n)
    ]
    mine = pltpu.make_async_copy(src.at[C.dp], dst.at[C.dp], C.lsem.at[0])
    mine.start()

    def wait():
        mine.wait()
        for cp in cps:
            cp.wait_recv()

    return wait


def stage_attend(R, C, n):
    lo = lanes(256) < 64
    lo2 = lanes(128) < 64
    one = jnp.where((lanes(256) == 64) | (lanes(256) == 65), 1.0, 0.0)
    one2 = one[0:128]

    def unpack(b):
        qk = R.arecv[b, 0:256, :].astype(F32)
        vf = R.arecv[b, 256:384, :].astype(F32)
        at = pl.ds(al(b * 256, 256), 256)
        R.Q[at, :] = jnp.where(lo, qk, 0.0).astype(BF)
        R.K[at, :] = jnp.where(lo, roll64(qk), one).astype(BF)
        R.V[pl.ds(al(b * 256, 128), 128), :] = jnp.where(lo2, vf, one2).astype(BF)
        R.V[pl.ds(al(b * 256 + 128, 128), 128), :] = jnp.where(lo2, roll64(vf), one2).astype(BF)

    loop(n, unpack)
    T = 512
    half = R.Q.shape[0] // 2 // T - 1
    seqs = R.prefix.shape[0]
    prefix = R.prefix[C.dp // (n // seqs)]
    k = C.sems(n)

    def rows_of(i):
        at = pl.ds(al(i * T, T), T)
        q = R.Q[at, :]
        qpos = i * T + lax.broadcasted_iota(jnp.int32, (T, 1), 0)
        lim = jnp.maximum(qpos, prefix - 1)

        def tile(j, carry):
            m, acc = carry
            kat = pl.ds(al(j * T, T), T)
            s = mm_bt(q, R.K[kat, :])
            kpos = j * T + lax.broadcasted_iota(jnp.int32, (T, T), 1)
            s = jnp.where(kpos <= lim, s, NEG)
            m2 = jnp.maximum(m, jnp.max(s, axis=1, keepdims=True))
            p = jnp.exp(s - m2).astype(BF)
            acc = acc * jnp.exp(m - m2) + mm(p, R.V[kat, :])
            return m2, acc

        m, acc = lax.fori_loop(
            0,
            jnp.maximum(i, half) + 1,
            tile,
            (jnp.full((T, 1), NEG, F32), jnp.zeros((T, 128), F32)),
        )
        total = acc[:, 64:65]
        o = acc / total
        lse = m + jnp.log(total)
        R.of[at, :] = jnp.where(lanes(T) < 64, o, lse)
        for u in range(2):
            b = i * 2 + u
            top, bot = o[u * 256 : u * 256 + 128], o[u * 256 + 128 : u * 256 + 256]
            R.osend[b] = jnp.where(lo2, top, roll64(bot)).astype(BF)

            @pl.when(b != C.dp)
            def _():
                C.rc(R.osend.at[b], R.orecv.at[C.dp], k + b, (b, C.t), k + C.dp).start()

    loop(R.Q.shape[0] // T, rows_of)
    mine = pltpu.make_async_copy(R.osend.at[C.dp], R.orecv.at[C.dp], C.lsem.at[0])
    mine.start()
    mine.wait()
    for b in range(n):

        @pl.when(b != C.dp)
        def _():
            cp = C.rc(R.osend.at[b], R.orecv.at[b], k + b, (b, C.t), k + b)
            cp.wait_send()
            cp.wait_recv()

    unfold_heads(R.orecv, R.otok, n, seqs)


def unfold_heads(src, dst, n, seqs):
    hp = n // seqs
    lo2 = lanes(128) < 64
    for s in range(seqs):
        for pr in range(hp // 2):
            e = src[s * hp + 2 * pr].astype(F32)
            d = src[s * hp + 2 * pr + 1].astype(F32)
            cut = slice(pr * 128, pr * 128 + 128)
            dst[s * 256 : s * 256 + 128, cut] = jnp.where(lo2, e, roll64(d)).astype(BF)
            dst[s * 256 + 128 : s * 256 + 256, cut] = jnp.where(lo2, roll64(e), d).astype(BF)


def swap_cot(R, C):
    k = C.sems(2)
    rows = R.cot.shape[0] // 2
    mine = pl.ds(al(C.c * rows, rows), rows)
    cp = C.send(R.cot.at[mine, :], R.cx.at[mine, :], k, C.xp)

    def wait():
        cp.wait_recv()
        C.send(R.cx.at[mine, :], R.cx.at[mine, :], k + 1, C.mate).wait_recv()

    return wait


def reduce4(R, C, part, out, fill=lambda: None):
    k = C.sems(3)
    k0 = (1 - C.y) * 2 + (1 - C.c)
    k1 = (1 - C.y) * 2 + C.c
    k2 = C.y * 2 + (1 - C.c)
    R.p4[0] = part(k0).astype(BF)
    c0 = C.send(R.p4.at[0], R.l4.at[0], k, C.mate)
    v1 = part(k1)
    fill()
    c0.wait_recv()
    R.p4[1] = (v1 + R.l4[0].astype(F32)).astype(BF)
    c1 = C.send(R.p4.at[1], R.l4.at[2], k + 1, C.yp)
    R.p4[2] = part(k2).astype(BF)
    c2 = C.send(R.p4.at[2], R.l4.at[1], k + 2, C.mate)
    out[...] = part(C.t)
    fill()
    c2.wait_recv()
    c1.wait_recv()
    out[...] = out[...] + R.l4[1].astype(F32) + R.l4[2].astype(F32)


def gather4(R, C, buf):
    k = C.sems(3)
    mine = buf.at[C.t]
    cy = C.send(mine, mine, k, C.yp)
    cm = C.send(mine, mine, k + 1, C.mate)

    def wait():
        cy.wait_recv()
        fwd = C.send(buf.at[C.t_y], buf.at[C.t_y], k + 2, C.mate)
        cm.wait_recv()
        fwd.wait_recv()

    return wait


def gather8(R, C, buf):
    k = C.sems(7)
    mine = buf.at[C.x * 4 + C.t]
    cd = C.send(mine, mine, k, C.dg)
    cx = C.send(mine, mine, k + 1, C.xp)
    cy = C.send(mine, mine, k + 2, C.yp)
    cm = C.send(mine, mine, k + 3, C.mate)

    def wait():
        fw = []
        for i, (cp, slot) in enumerate(
            (
                (cy, C.x * 4 + C.t_y),
                (cx, (1 - C.x) * 4 + C.t),
                (cd, (1 - C.x) * 4 + C.t_y),
            )
        ):
            cp.wait_recv()
            fw.append(C.send(buf.at[slot], buf.at[slot], k + 4 + i, C.mate))
        cm.wait_recv()
        for cp in fw:
            cp.wait_recv()

    return wait


def stage_out(R, C):
    def part(k):
        return mm(R.otok[pl.ds(al(k * CH, CH), CH), :], R.wout[...])

    reduce4(R, C, part, R.x1)
    rows = R.tok.shape[0]
    own = pl.ds(al(C.t * CH, CH), CH)
    pos = C.t * CH + lax.broadcasted_iota(jnp.int32, (CH, rows), 0)
    col = lax.broadcasted_iota(jnp.int32, (CH, rows), 1)
    hot = jnp.where(
        R.routes[...] == lax.broadcasted_iota(jnp.int32, (8, rows), 0), 1.0, 0.0
    ).astype(BF)
    earlier = mm_bt(jnp.where(col < pos, 1.0, 0.0).astype(BF), hot)
    here = mm_bt(jnp.where(col == pos, 1.0, 0.0).astype(BF), hot)
    keep = jnp.where(earlier < CAP, here, 0.0)
    keep0, keep1 = keep[:, 0:1], keep[:, 1:2]
    x1 = R.x1[...] + R.tok[own, :].astype(F32) + R.par[2:3, :]
    R.x1[...] = x1
    n, r = norm_parts(x1)
    h2 = (n * R.par[3:4, :] + R.par[4:5, :]).astype(BF)
    slot = C.x * 4 + C.t
    R.H2[slot] = h2
    hf = h2.astype(F32)
    l0 = jnp.sum(hf * R.par[5:6, :], axis=1, keepdims=True)
    l1 = jnp.sum(hf * R.par[6:7, :], axis=1, keepdims=True)
    mx = jnp.maximum(l0, l1)
    e0, e1 = jnp.exp(l0 - mx), jnp.exp(l1 - mx)
    p0, p1 = e0 / (e0 + e1), e1 / (e0 + e1)
    gate = here[:, 0:1] * p0 + here[:, 1:2] * p1
    ln = lanes(CH)
    hi = gate.astype(BF).astype(F32)
    mid = (gate - hi).astype(BF).astype(F32)
    meta = jnp.zeros((CH, 128), F32)
    for i, v in enumerate((keep0, keep1, hi, mid, gate - hi - mid)):
        meta = jnp.where(ln == i, v, meta)
    R.META[slot] = meta.astype(BF)
    wait_h = gather8(R, C, R.H2)
    wait_m = gather8(R, C, R.META)
    cols = jnp.zeros((CH, 128), F32)
    for i, v in enumerate((p0, p1, here[:, 0:1], here[:, 1:2], gate, keep0, keep1)):
        cols = jnp.where(ln == i, v, cols)
    R.cols[...] = cols
    wait_h()
    wait_m()

    def gated(i):
        for xx, cot in ((C.x, R.cot), (1 - C.x, R.cx)):
            m = R.META[xx * 4 + i].astype(F32)
            gate = m[:, 2:3] + m[:, 3:4] + m[:, 4:5]
            g = cot[pl.ds(al(i * CH, CH), CH), :].astype(F32)
            gr = (gate * g).astype(BF).astype(F32)
            R.GG[xx * 4 + i] = (gr * (m[:, 0:1] + m[:, 1:2])).astype(BF)

    loop(4, gated)


def gelu_both(h):
    half = 0.5 * (1.0 + lax.erf(h * 0.7071067811865476))
    return h * half, half + h * (jnp.exp(-0.5 * h * h) * 0.3989422804014327)


class Reduce8:
    def __init__(self, C, parts, land, stage, out):
        self.C, self.parts, self.land, self.stage, self.out = C, parts, land, stage, out
        self.k = C.sems(7)

    def place(self, n):
        C = self.C
        a, b = n // 2, lax.rem(n, 2)
        xx = (1 - C.x) * (1 - a) + C.x * a
        yy = (1 - C.y) * (1 - b) + C.y * b
        return xx, yy

    def swap(self, n):
        C = self.C
        xx, yy = self.place(n)
        src = self.parts.at[xx * 4 + yy * 2 + 1 - C.c]
        return C.rc(src, self.land.at[n], self.k + n, C.mate)

    def added(self, n):
        C = self.C
        xx, yy = self.place(n)
        self.swap(n).wait_recv()
        return self.parts[xx * 4 + yy * 2 + C.c].astype(F32) + self.land[n].astype(F32)

    def cross(self, n):
        C = self.C
        xx, yy = self.place(n)
        dev = (C.z * 2 + xx, yy * 2 + C.c)
        return C.rc(self.stage.at[n], self.land.at[4 + n], self.k + 4 + n, dev)

    def forward(self, n):
        self.stage[n] = self.added(n).astype(BF)
        self.cross(n).start()

    def keep(self):
        self.out[...] = self.added(3)
        self.C.pending += [self.swap(n) for n in range(4)] + [self.cross(n) for n in range(3)]

    def wait(self):
        for n in range(3):
            self.cross(n).wait_recv()
        v = self.out[...]
        for n in range(3):
            v = v + self.land[4 + n].astype(F32)
        self.out[...] = v


def stage_moe(R, C, sums):
    def tile(n):
        xx, yy = sums[0].place(n)
        i = xx * 2 + yy
        two = pl.ds(al(2 * i, 2), 2)
        at = pl.ds(al(i * 256, 256), 256)
        h2 = R.H2[two].reshape(256, R.H2.shape[2])
        gg = R.GG[two].reshape(256, R.GG.shape[2])
        meta = R.META[two].reshape(256, 128).astype(F32)
        m0, m1 = meta[:, 0:1], meta[:, 1:2]
        half = R.wi.shape[2]
        bias0 = R.inb[0:1, pl.ds(al(C.x * half, half), half)].astype(F32)
        bias1 = R.inb[1:2, pl.ds(al(C.x * half, half), half)].astype(F32)
        for q in range(half // 256):
            cut = slice(q * 256, q * 256 + 256)
            h0 = mm(h2, R.wi[0, :, cut]) + bias0[:, cut]
            h1 = mm(h2, R.wi[1, :, cut]) + bias1[:, cut]
            act, slope = gelu_both(jnp.where(m0 > 0.0, h0, h1))
            R.A[0, at, cut] = (act * m0).astype(BF)
            R.A[1, at, cut] = (act * m1).astype(BF)
            d0 = mm_bt(gg, R.wb[0, cut, :])
            d1 = mm_bt(gg, R.wb[1, cut, :])
            dh = jnp.where(m0 > 0.0, d0, d1) * slope
            R.DH[0, at, cut] = (dh * m0).astype(BF)
            R.DH[1, at, cut] = (dh * m1).astype(BF)
        y = mm(R.A[0, at, :], R.wb[0]) + mm(R.A[1, at, :], R.wb[1])
        R.YP[two] = y.astype(BF).reshape(2, CH, y.shape[1])
        dx = mm_bt(R.DH[0, at, :], R.wi[0]) + mm_bt(R.DH[1, at, :], R.wi[1])
        R.DXP[two] = dx.astype(BF).reshape(2, CH, dx.shape[1])
        for r in sums:
            r.swap(n).start()

        @pl.when(n > 0)
        def _():
            for r in sums:
                r.forward(n - 1)

    loop(4, tile)
    for r in sums:
        r.keep()


def put_wide(at, v):
    w = v.shape[1] // 2
    at[0:32, :] = v[:, 0:w].astype(BF)
    at[32:64, :] = v[:, w : 2 * w].astype(BF)


def stage_moe_grads(R, C, K, ring):
    rows = R.GG.shape[0] * CH

    def back(i):
        at = pl.ds(al(i * 128, 128), 128)
        gg = R.GG[...].reshape(rows, R.GG.shape[2])
        for e in range(2):
            v = mm_at(R.A[e, :, at], gg)
            for j in range(4):
                put_wide(R.G.at[e, 4 * i + j], v[32 * j : 32 * j + 32])

    loop(R.A.shape[2] // 128, back)
    ring.run(3)
    base = ring.take(R.H2.shape[2] // 256)

    def into(i):
        at = pl.ds(al(i * 128, 128), 128)
        h2t = R.H2[:, :, at].reshape(rows, 128)
        for e in range(2):
            v = mm_at(h2t, R.DH[e]).astype(BF)
            R.G[e, K.i0 + 2 * i] = v[0:64]
            R.G[e, K.i0 + 2 * i + 1] = v[64:128]

        @pl.when(lax.rem(i, 2) == 1)
        def _():
            ring.tick(base + i // 2)

    loop(R.H2.shape[2] // 128, into)


def norm_back(n, r, dn):
    return r * (
        dn - jnp.mean(dn, axis=-1, keepdims=True) - n * jnp.mean(dn * n, axis=-1, keepdims=True)
    )


def rowsum(v):
    return jnp.sum(v, axis=0, keepdims=True)


def stage_owner(R, C):
    own = pl.ds(al(C.t * CH, CH), CH)
    cols = R.cols[...]
    p0, p1, h0, h1, gate, k0, k1 = (cols[:, i : i + 1] for i in range(7))
    u = R.u[...] + k0 * R.par[7:8, :] + k1 * R.par[8:9, :]
    g = R.cot[own, :].astype(F32)
    x1 = R.x1[...]
    R.RES[C.t] = (x1 + gate * u).astype(BF)
    dg = jnp.sum(g * u, axis=1, keepdims=True) * gate
    dl0 = (dg * (h0 - p0)).astype(BF).astype(F32)
    dl1 = (dg * (h1 - p1)).astype(BF).astype(F32)
    h2 = R.H2[C.x * 4 + C.t].astype(F32)
    gg = R.GG[C.x * 4 + C.t].astype(F32)
    dh2 = R.dx[...] + dl0 * R.par[5:6, :] + dl1 * R.par[6:7, :]
    n, r = norm_parts(x1)
    dx1 = g + norm_back(n, r, dh2 * R.par[3:4, :])
    da = dx1.astype(BF)
    R.DA[C.t] = da
    R.x1[...] = dx1
    R.sm[0:1, :] = rowsum(dh2 * n)
    R.sm[1:2, :] = rowsum(dh2)
    R.sm[2:3, :] = rowsum(da.astype(F32))
    R.sm[3:4, :] = rowsum(h2 * dl0)
    R.sm[4:5, :] = rowsum(h2 * dl1)
    R.sm[5:6, :] = rowsum(gg * k0)
    R.sm[6:7, :] = rowsum(gg * k1)


def stage_out_back(R, C, n):
    seqs = R.prefix.shape[0]
    hp = n // seqs
    lo2 = lanes(128) < 64
    for s in range(seqs):
        da = R.DA[2 * s : 2 * s + 2].reshape(256, R.DA.shape[2])
        for pr in range(hp // 2):
            cut = slice(pr * 128, pr * 128 + 128)
            d = mm_bt(da, R.wout[cut, :])
            a, b = d[0:128], d[128:256]
            R.osend[s * hp + 2 * pr] = jnp.where(lo2, a, roll64(b)).astype(BF)
            R.osend[s * hp + 2 * pr + 1] = jnp.where(lo2, roll64(a), b).astype(BF)


def tail_of(buf, d, c, n=1):
    return buf.at[d, 64 * c : 64 * (c + n), :]


def stage_out_grad(R, C):
    da = R.DA[...].reshape(R.otok.shape[0], R.DA.shape[2])
    ho = R.otok.shape[1] // 2
    k0 = R.G.shape[1] - 8
    for own, who in ((False, 1 - C.x), (True, C.x)):
        v = mm_at(R.otok[:, pl.ds(al(who * ho, ho), ho)], da)
        for d in range(2):
            for c in range(2):
                r = d * 64 + c * 32
                put_wide(R.G.at[d, k0 + c] if own else tail_of(R.A, d, c), v[r : r + 32])


def add_tail(R, c0, n):
    k0 = R.G.shape[1] - 8

    def one(c):
        for d in range(2):
            v = R.G[d, k0 + c0 + c].astype(F32) + R.wi[d, pl.ds(al((c0 + c) * 64, 64), 64), :].astype(F32)
            R.G[d, k0 + c0 + c] = v.astype(BF)

    loop(n, one)


def stage_attend_back(R, C, n, ring, xo):
    lo2 = lanes(128) < 64
    ln2 = lanes(128)

    def hi_lo(v):
        hi = v.astype(BF).astype(F32)
        return hi, v - hi

    def unpack(b):
        f = R.dorecv[b].astype(F32)
        for u in range(2):
            at = pl.ds(al(b * 256 + u * 128, 128), 128)
            do = jnp.where(lo2, f if u == 0 else roll64(f), 0.0)
            of = R.of[at, :]
            hi, low = hi_lo(-jnp.sum(do * of, axis=1, keepdims=True))
            R.DO[at, :] = jnp.where(ln2 == 64, hi, jnp.where(ln2 == 65, low, do)).astype(BF)
            hi, low = hi_lo(-of[:, 64:65])
            q = R.Q[at, :].astype(F32)
            R.Q[at, :] = jnp.where(ln2 == 64, hi, jnp.where(ln2 == 65, low, q)).astype(BF)

    loop(n, unpack)
    T = 512
    total = R.Q.shape[0]
    nt = total // T
    half = nt // 2
    seqs = R.prefix.shape[0]
    prefix = R.prefix[C.dp // (n // seqs)]
    R.dq[...] = jnp.zeros_like(R.dq)
    k = C.sems(n)
    k2 = C.sems(n)
    base = ring.take(T_AB * nt)
    kvs, kvr, dqr = R.asend.at[:, 0:256], R.arecv.at[:, 0:256], R.arecv.at[:, 256:384]

    def keys(jj):
        loop(T_AB // 2, lambda i: ring.tick(base + T_AB * jj + i))
        j = nt - 1 - jj
        kat = pl.ds(al(j * T, T), T)
        kk, vv = R.K[kat, :], R.V[kat, :]
        kpos = j * T + lax.broadcasted_iota(jnp.int32, (T, T), 0)

        def tile(i, carry):
            dk, dv = carry
            qat = pl.ds(al(i * T, T), T)
            q, do = R.Q[qat, :], R.DO[qat, :]
            qpos = i * T + lax.broadcasted_iota(jnp.int32, (1, T), 1)
            lim = jnp.maximum(qpos, prefix - 1)
            p = jnp.where(kpos <= lim, jnp.exp(mm_bt(kk, q)), 0.0)
            ds = (p * mm_bt(vv, do)).astype(BF)
            dv = dv + mm(p.astype(BF), do)
            dk = dk + mm(ds, q)
            R.dq[qat, :] = R.dq[qat, :] + mm_at(ds, kk)
            return dk, dv

        first = jnp.where(j >= half, j, 0)
        dk, dv = lax.fori_loop(
            first, nt, tile, (jnp.zeros((T, 128), F32), jnp.zeros((T, 128), F32))
        )
        lo = lanes(T) < 64
        kv = jnp.where(lo, dk, roll64(dv)).astype(BF)
        for u in range(2):
            b = j * 2 + u
            R.asend[b, 0:256, :] = kv[u * 256 : u * 256 + 256]

            @pl.when(b != C.dp)
            def _():
                C.rc(kvs.at[b], kvr.at[C.dp], k + b, (b, C.t), k + C.dp).start()

        loop(T_AB - T_AB // 2, lambda i: ring.tick(base + T_AB * jj + T_AB // 2 + i))

    loop(nt, keys)

    def queries(b):
        at = al(b * 256, 256)
        top = R.dq[pl.ds(at, 128), :] * 0.125
        bot = R.dq[pl.ds(al(at + 128, 128), 128), :] * 0.125
        R.osend[b] = jnp.where(lo2, top, roll64(bot)).astype(BF)

        @pl.when(b != C.dp)
        def _():
            C.rc(R.osend.at[b], dqr.at[C.dp], k2 + b, (b, C.t), k2 + C.dp).start()

    loop(n, queries)
    xo.wait_recv()
    add_tail(R, 0, 2)
    ring.run(T_KV)
    for src, dst, i in ((R.osend, dqr, 0), (kvs, kvr, 1)):
        mine = pltpu.make_async_copy(src.at[C.dp], dst.at[C.dp], C.lsem.at[i])
        mine.start()
        mine.wait()
    for src, dst, kk in ((kvs, kvr, k), (R.osend, dqr, k2)):
        for b in range(n):

            @pl.when(b != C.dp)
            def _():
                cp = C.rc(src.at[b], dst.at[b], kk + b, (b, C.t), kk + b)
                cp.wait_send()
                cp.wait_recv()

    hp = n // seqs
    lo = lanes(256) < 64
    for s in range(seqs):
        for pr in range(hp // 2):
            p = s * hp + 2 * pr
            cut = slice(pr * 128, pr * 128 + 128)
            e, d = kvr[p].astype(F32), kvr[p + 1].astype(F32)
            R.dproj[1, s * 256 : s * 256 + 256, cut] = jnp.where(lo, e, roll64(d)).astype(BF)
            R.dproj[2, s * 256 : s * 256 + 256, cut] = jnp.where(lo, roll64(e), d).astype(BF)
    unfold_heads(dqr, R.dproj.at[0], n, seqs)


def stage_qkv_back(R, C, fill):
    def part(k):
        at = pl.ds(al(k * CH, CH), CH)
        return (
            mm_bt(R.dproj[0, at, :], R.wqkv[0])
            + mm_bt(R.dproj[1, at, :], R.wqkv[1])
            + mm_bt(R.dproj[2, at, :], R.wqkv[2])
        )

    reduce4(R, C, part, R.dx, fill)
    own = pl.ds(al(C.t * CH, CH), CH)
    n, r = norm_parts(R.tok[own, :].astype(F32))
    dh1 = R.dx[...]
    R.GIN[C.t] = (R.x1[...] + norm_back(n, r, dh1 * R.par[0:1, :])).astype(BF)
    R.sm2[0:1, :] = rowsum(dh1 * n)
    R.sm2[1:2, :] = rowsum(dh1)


def stage_qkv_grad(R, C, ring):
    hq = R.h1.shape[1] // 2
    k = C.sems(2)
    cps = []
    k0 = R.G.shape[1] - 6
    for own, who in ((False, 1 - C.x), (True, C.x)):
        for d in range(2):
            for c in range(2):
                at = pl.ds(al(who * hq + (2 * d + c) * 128, 128), 128)
                h = R.h1[:, at]
                for m in range(3):
                    v = mm_at(h, R.dproj[m]).astype(BF)
                    w = v.shape[1]
                    i = 2 * m + c
                    dst = R.G.at[d, k0 + i] if own else tail_of(R.A, d, 2 + i)
                    dst[:, 0:w] = v[0:64]
                    dst[:, w : 2 * w] = v[64:128]
            ring.run(T_QG)
            if not own:
                cps.append(C.send(tail_of(R.A, d, 2, 6), tail_of(R.wi, d, 2, 6), k + d, C.xp))
    return cps


class Kinds:
    def __init__(self, nb, ni):
        self.i0 = nb
        self.o0 = nb + ni
        self.q0 = self.o0 + 2
        self.n = self.q0 + 6


class Sums:
    def __init__(self, R, C, n, via):
        self.R, self.C, self.n, self.via = R, C, n, via
        self.a, self.b = C.sems(2 * n), C.sems(2 * n)
        self.one, self.v = C.sems(10), C.sems(2 * via)

    def finish(self):
        R, C = self.R, self.C
        for d in range(2):
            pos = C.z if d == 0 else 3 - C.z
            fn = R.FN.at[d]
            C.rc(fn, fn, self.one + d, C.xp).wait_send()

            @pl.when(jnp.logical_or(pos == 1, pos == 2))
            def _():
                C.rc(fn, fn, self.one + 2 + d, C.xp).wait_send()

            tail, head = pl.ds(self.via, self.n - self.via), pl.ds(0, self.via)
            cp = C.rc(R.FN.at[d, tail], R.XH.at[d, tail], self.one + 4 + d, C.xp)
            cp.wait_send()
            cp.wait_recv()
            odd = lax.rem(pos, 2) == 1

            @pl.when(odd)
            def _():
                for i in (6, 8):
                    C.rc(R.FN.at[d, head], R.XH.at[d, head], self.one + i + d, C.xp).wait_send()

            @pl.when(jnp.logical_not(odd))
            def _():
                def got(k):
                    xh = R.XH.at[d, k]
                    i = self.v + d * self.via + k
                    C.rc(xh, xh, self.one + 8 + d, C.xp, i).wait_recv()

                loop(self.via, got)

            pltpu.make_async_copy(fn, R.FH.at[d], C.lsem.at[4 + d]).wait()


class Ring:
    def __init__(self, sums, k0, k1, w):
        self.S, self.k0, self.k1, self.w = sums, k0, k1, w
        self.cur = 0
        self.total = k1 - k0 + 4 * w

    def take(self, n):
        base = self.cur
        self.cur += n
        return base

    def run(self, n):
        n = min(n, self.total - self.cur)
        if n <= 0:
            return
        base = self.take(n)
        loop(n, lambda i: self.tick(base + i))

    def rest(self):
        self.run(self.total - self.cur)

    def tick(self, s):
        for d in range(2):
            self.half(s + self.k0, d)

    def half(self, s, d):
        S, w = self.S, self.w
        R, C, n, one = S.R, S.C, S.n, S.one
        pos = C.z if d == 0 else 3 - C.z

        def dev(p):
            return ((p if d == 0 else 3 - p) * 2 + C.x, C.t)

        def act(k, cond):
            ok = jnp.logical_and(k >= self.k0, k < self.k1)
            return ok if cond is None else jnp.logical_and(ok, cond)

        def toward(src, dst, kr, p):
            return C.rc(src, dst, one + d, dev(p), kr)

        def away(fn, i, p):
            return C.rc(fn, fn, one + 2 + d, dev(p), S.b + i)

        @pl.when(act(s, jnp.logical_or(pos == 0, pos == 3)))
        def _():
            toward(R.G.at[d, s], R.L1.at[d, s], S.a + d * n + s, 1 + pos // 3).start()

        k2 = s - w

        @pl.when(act(k2, pos == 2))
        def _():
            i = d * n + k2
            toward(R.G.at[d, k2], R.L1.at[d, k2], S.a + i, 1).wait_recv()
            R.G[d, k2] = (R.G[d, k2].astype(F32) + R.L1[d, k2].astype(F32)).astype(BF)
            toward(R.G.at[d, k2], R.FN.at[d, k2], S.b + i, 1).start()

        k1 = s - 2 * w

        @pl.when(act(k1, pos == 1))
        def _():
            i = d * n + k1
            fn = R.FN.at[d, k1]
            toward(R.G.at[d, k1], R.L1.at[d, k1], S.a + i, 0).wait_recv()
            away(fn, i, 2).wait_recv()
            v = R.G[d, k1].astype(F32) + R.L1[d, k1].astype(F32) + R.FN[d, k1].astype(F32)
            R.FN[d, k1] = v.astype(BF)
            away(fn, i, 2).start()
            toward(fn, fn, S.b + i, 0).start()

        lag = w * (2 + jnp.where(pos == 1, 0, 1) + jnp.where(pos == 3, 1, 0))
        kf = s - lag
        odd = lax.rem(pos, 2) == 1

        @pl.when(act(kf, None))
        def _():
            i = d * n + kf
            fn = R.FN.at[d, kf]

            @pl.when(pos != 1)
            def _():
                away(fn, i, 1).wait_recv()

            @pl.when(pos == 2)
            def _():
                away(fn, i, 3).start()

            @pl.when(kf >= S.via)
            def _():
                C.rc(fn, R.XH.at[d, kf], one + 4 + d, C.xp).start()

            @pl.when(jnp.logical_and(kf < S.via, odd))
            def _():
                i = S.v + d * S.via + kf
                C.rc(fn, R.XH.at[d, kf], one + 6 + d, C.xp, i).start()

            pltpu.make_async_copy(fn, R.FH.at[d, kf], C.lsem.at[4 + d]).start()

        if self.k0 < S.via:
            kv = kf - w

            @pl.when(act(kv, jnp.logical_and(odd, kv < S.via)))
            def _():
                xh = R.XH.at[d, kv]
                cp = C.rc(xh, xh, one + 8 + d, dev(pos - 1), S.v + d * S.via + kv)
                cp.wait_recv()
                cp.start()


def small_tensor(R, C):
    R.st[C.t, 0:8, :] = R.sm[...]
    R.st[C.t, 8:16, :] = R.sm2[...]
    k = C.sems(3)
    return [
        C.send(R.st.at[C.t], R.st.at[C.t], k + i, dev)
        for i, dev in enumerate((C.mate, C.yp, (C.dp, 3 - C.t)))
    ]


def small_dp(R, C, n, cps):
    for cp in cps:
        cp.wait_recv()
    tot = R.st[0] + R.st[1] + R.st[2] + R.st[3]
    sd = R.sd.at[C.dp]
    sd[0:8, :] = tot[0:8, :]
    sd[8:10, :] = tot[8:10, :]
    f = R.dproj.shape[2]

    def colsum(m):
        return rowsum(R.dproj[m].astype(F32))

    sd[10:11, 0:f] = colsum(0)
    sd[10:11, f : 2 * f] = colsum(2)
    half = R.DH.shape[2]
    for e in range(2):
        sd[11:12, e * half : (e + 1) * half] = rowsum(R.DH[e].astype(F32))
    k = C.sems(n)
    return [C.send(sd, R.sd.at[C.dp], k + o, (lax.rem(C.dp + o, n), C.t)) for o in range(1, n)]


def small_end(R, C, n, cps):
    for cp in cps:
        cp.wait_recv()
    tot = R.sd[0]
    for b in range(1, n):
        tot = tot + R.sd[b]
    R.osm[...] = tot
    for xx in range(2):
        v = R.sd[xx, 11:12, :]
        for b in range(2 + xx, n, 2):
            v = v + R.sd[b, 11:12, :]
        R.osm[11 + xx : 12 + xx, :] = v


class Refs:
    pass


LAG = 3
LAG_Q = 2
T_U, T_DA, T_DO, T_AB, T_KV, T_QB, T_QG = 3, 5, 4, 2, 4, 3, 1


def body(names, n, *refs):
    R = Refs()
    for name, ref in zip(names, refs):
        setattr(R, name, ref)
    C = Ctx(R.ssem, R.rsem, R.lsem)
    sem, count = barrier_start(C, n)
    half = R.wi.shape[2]
    off = pl.ds(al(C.x * half, half), half)
    wcp = [
        pltpu.make_async_copy(R.w_in.at[:, :, off], R.wi, C.lsem.at[2]),
        pltpu.make_async_copy(R.w_back.at[:, off, :], R.wb, C.lsem.at[3]),
    ]
    for cp in wcp:
        cp.start()
    for i, ref in enumerate((R.g1, R.b1, R.outb, R.g2, R.b2)):
        R.par[i : i + 1, :] = ref[...].astype(F32).reshape(1, ref.shape[0])
    R.par[5:7, :] = R.router[...].astype(F32)
    R.par[7:9, :] = R.backb[...].astype(F32)
    R.sm[...] = jnp.zeros_like(R.sm)
    R.sm2[...] = jnp.zeros_like(R.sm2)
    R.sd[...] = jnp.zeros_like(R.sd)
    pl.semaphore_wait(sem, count)
    wait_qkv = stage_qkv(R, C, n)
    wait_qkv()
    wait_cot = swap_cot(R, C)
    stage_attend(R, C, n)
    wait_cot()
    stage_out(R, C)
    for cp in wcp:
        cp.wait()
    over_u = Reduce8(C, R.YP, R.ly, R.sy, R.u)
    over_x = Reduce8(C, R.DXP, R.lx, R.sx, R.dx)
    stage_moe(R, C, (over_u, over_x))
    K = Kinds(half // 32, R.H2.shape[2] // 64)
    sums = Sums(R, C, K.n, K.i0)
    ring = Ring(sums, 0, K.q0, LAG)
    last = Ring(sums, K.q0, K.n, LAG_Q)
    stage_moe_grads(R, C, K, ring)
    over_u.wait()
    ring.run(T_U)
    over_x.wait()
    stage_owner(R, C)
    wait_da = gather4(R, C, R.DA)
    wait_res = gather4(R, C, R.RES)
    ring.run(T_DA)
    wait_da()
    stage_out_back(R, C, n)
    wait_do = all_to_all(R, C, R.osend, R.dorecv, n)
    stage_out_grad(R, C)
    ring.run(T_DO)
    wait_do()
    C.drain()
    xo = C.send(R.A.at[:, 0:128, :], R.wi.at[:, 0:128, :], C.sems(1), C.xp)
    stage_attend_back(R, C, n, ring, xo)
    xq = stage_qkv_grad(R, C, ring)
    stage_qkv_back(R, C, lambda: ring.run(T_QB))
    wait_gin = gather4(R, C, R.GIN)
    small = small_tensor(R, C)
    for cp in xq:
        cp.wait_recv()
    add_tail(R, 2, 6)
    for r in range(8):
        last.run(1)
        ring.run(1)
        if r == 2:
            small = small_dp(R, C, n, small)
    wait_gin()
    wait_res()
    small_end(R, C, n, small)
    ring.rest()
    last.rest()
    sums.finish()
    C.drain()


def place_body(nb, ni, fh, xh, res, gin, osm, oB, oI, oQ, oO, oR, oG, *rest):
    vec, (cf, cx, cr, cg, vB, vI, vQ, vO, vR, vG, isem, osem) = rest[:9], rest[9:]
    x = lax.rem(lax.axis_index("dp"), 2)
    n = nb + ni + 8
    half = nb * 32
    cuts = ((0, nb), (nb, ni), (nb + ni, 8))
    srcs = ((fh, cf, x), (xh, cx, 1 - x))
    ins = {}
    for j, (src, buf, h) in enumerate(srcs):
        for d in range(2):
            for c, (k0, m) in enumerate(cuts):
                cp = pltpu.make_async_copy(
                    src.at[d, pl.ds(k0, m)], buf.at[d, pl.ds(k0, m)], isem.at[j * 6 + d * 3 + c]
                )
                cp.start()
                ins[j, d, c] = cp
    rows = [pltpu.make_async_copy(a, b, isem.at[12 + i]) for i, (a, b) in enumerate(((res, cr), (gin, cg)))]
    for cp in rows:
        cp.start()
    outs = []

    def put(src, dst):
        cp = pltpu.make_async_copy(src, dst, osem.at[len(outs)])
        cp.start()
        outs.append(cp)

    for j, (src, buf, h) in enumerate(srcs):
        for d in range(2):
            ins[j, d, 0].wait()

            def back(k):
                v = buf[d, k].astype(F32)
                at = pl.ds(al(k * 32, 32), 32)
                vB[j, d, at, 0:512] = v[0:32]
                vB[j, d, at, 512:1024] = v[32:64]

            loop(nb, back)
            put(vB.at[j, d], oB.at[d, pl.ds(al(h * half, half), half), :])
            ins[j, d, 1].wait()

            def into(k):
                vI[j, d, pl.ds(al(k * 64, 64), 64), :] = buf[d, nb + k].astype(F32)

            loop(ni, into)
            put(vI.at[j, d], oI.at[d, :, pl.ds(al(h * 512, 512), 512)])
    for j, (src, buf, h) in enumerate(srcs):
        for d in range(2):
            ins[j, d, 2].wait()
            for c in range(2):
                v = buf[d, nb + ni + c].astype(F32)
                at = pl.ds(al(h * 128 + d * 64 + c * 32, 32), 32)
                vO[at, 0:512] = v[0:32]
                vO[at, 512:1024] = v[32:64]
            for c in range(6):
                v = buf[d, nb + ni + 2 + c].astype(F32)
                row = h * 512 + d * 256 + (c % 2) * 128
                vQ[c // 2, pl.ds(al(row, 64), 64), :] = v[:, 0:256]
                vQ[c // 2, pl.ds(al(row + 64, 64), 64), :] = v[:, 256:512]
    put(vO, oO)
    put(vQ, oQ)
    for cp, src, buf, out in ((rows[0], cr, vR, oR), (rows[1], cg, vG, oG)):
        cp.wait()
        for t in range(src.shape[0]):
            buf[t] = src[t].astype(F32)
        put(buf, out)
    ln1g, ln1b, qv, outb, ln2g, ln2b, rout, inb, bb = vec
    for ref, r in ((ln1g, 8), (ln1b, 9), (outb, 2), (ln2g, 0), (ln2b, 1)):
        ref[...] = osm[r : r + 1, :]
    for i in range(2):
        qv[i : i + 1, :] = osm[10:11, i * 256 : i * 256 + 256]
        rout[i : i + 1, :] = osm[3 + i : 4 + i, :]
        bb[i : i + 1, :] = osm[5 + i : 6 + i, :]
        for e in range(2):
            inb[e : e + 1, i * 512 : i * 512 + 512] = osm[11 + i : 12 + i, e * 512 : e * 512 + 512]
    for cp in outs:
        cp.wait()


def place(fh, xh, res, gin, osm, nb, ni):
    sds = jax.ShapeDtypeStruct
    vm = pl.BlockSpec(memory_space=pltpu.VMEM)
    hbm = pl.BlockSpec(memory_space=pl.ANY)
    n, half = nb + ni + 8, nb * 32
    big = [(2, 2 * half, 1024), (2, ni * 64, 1024), (3, 1024, 256), (256, 1024), res.shape, gin.shape]
    row = (1, 1024)
    small = [row, row, (2, 256), row, row, row, (2, 1024), (2, 1024), (2, 1024)]
    V = pltpu.VMEM
    return pl.pallas_call(
        functools.partial(place_body, nb, ni),
        out_shape=[sds(v, F32) for v in big + small],
        in_specs=[hbm, hbm, hbm, hbm, vm],
        out_specs=[hbm] * len(big) + [vm] * len(small),
        scratch_shapes=[
            V((2, n, 64, 512), BF),
            V((2, n, 64, 512), BF),
            V(res.shape, BF),
            V(gin.shape, BF),
            V((2, 2, half, 1024), F32),
            V((2, 2, ni * 64, 512), F32),
            V((3, 1024, 256), F32),
            V((256, 1024), F32),
            V(res.shape, F32),
            V(gin.shape, F32),
            pltpu.SemaphoreType.DMA((14,)),
            pltpu.SemaphoreType.DMA((12,)),
        ],
        compiler_params=pltpu.CompilerParams(vmem_limit_bytes=60000000),
        name="place",
    )(fh, xh, res, gin, osm)


def fast_local(args, n, nt):
    (tokens, g1, b1, w_qkv, qvb, w_out, out_b, g2, b2, router, w_in, in_b, w_back, back_b,
     routes, prefix, cot) = args
    S, span, D = tokens.shape
    rows = S * span
    F = w_qkv.shape[2]
    H = w_in.shape[2]
    half = H // 2
    total = n * span
    vm = pl.BlockSpec(memory_space=pltpu.VMEM)
    hbm = pl.BlockSpec(memory_space=pl.ANY)
    ins = [
        ("tok", tokens.reshape(rows, D), vm),
        ("g1", g1, vm),
        ("b1", b1, vm),
        ("outb", out_b, vm),
        ("g2", g2, vm),
        ("b2", b2, vm),
        ("router", router.T, vm),
        ("backb", back_b, vm),
        ("wqkv", w_qkv.transpose(1, 0, 2), vm),
        ("qvb", qvb, vm),
        ("wout", w_out, vm),
        ("routes", routes.reshape(1, rows), vm),
        ("prefix", prefix, pl.BlockSpec(memory_space=pltpu.SMEM)),
        ("cot", cot.reshape(rows, D), vm),
        ("inb", in_b, vm),
        ("w_in", w_in, hbm),
        ("w_back", w_back, hbm),
    ]
    sds = jax.ShapeDtypeStruct
    nch = half // 32 + D // 64 + 8
    outs = [
        ("RES", sds((nt, CH, D), BF), vm),
        ("GIN", sds((nt, CH, D), BF), vm),
        ("FH", sds((2, nch, 64, 512), BF), hbm),
        ("XH", sds((2, nch, 64, 512), BF), hbm),
        ("osm", sds((16, D), F32), vm),
    ]
    V = pltpu.VMEM
    scr = [
        ("h1", V((rows, D), BF)),
        ("asend", V((n, 384, 128), BF)),
        ("arecv", V((n, 384, 128), BF)),
        ("Q", V((total, 128), BF)),
        ("K", V((total, 128), BF)),
        ("V", V((total, 128), BF)),
        ("DO", V((total, 128), BF)),
        ("of", V((total, 128), F32)),
        ("dq", V((total, 128), F32)),
        ("osend", V((n, 128, 128), BF)),
        ("orecv", V((n, 128, 128), BF)),
        ("dorecv", V((n, 128, 128), BF)),
        ("otok", V((rows, F), BF)),
        ("dproj", V((3, rows, F), BF)),
        ("p4", V((3, CH, D), BF)),
        ("l4", V((3, CH, D), BF)),
        ("x1", V((CH, D), F32)),
        ("u", V((CH, D), F32)),
        ("dx", V((CH, D), F32)),
        ("cols", V((CH, 128), F32)),
        ("H2", V((8, CH, D), BF)),
        ("GG", V((8, CH, D), BF)),
        ("META", V((8, CH, 128), BF)),
        ("cx", V((rows, D), BF)),
        ("par", V((16, D), F32)),
        ("wi", V((2, D, half), BF)),
        ("wb", V((2, half, D), BF)),
        ("A", V((2, 8 * CH, half), BF)),
        ("DH", V((2, 8 * CH, half), BF)),
        ("YP", V((8, CH, D), BF)),
        ("DXP", V((8, CH, D), BF)),
        ("ly", V((7, CH, D), BF)),
        ("lx", V((7, CH, D), BF)),
        ("sy", V((3, CH, D), BF)),
        ("sx", V((3, CH, D), BF)),
        ("DA", V((nt, CH, D), BF)),
        ("G", V((2, nch, 64, 512), BF)),
        ("L1", V((2, nch, 64, 512), BF)),
        ("FN", V((2, nch, 64, 512), BF)),
        ("sm", V((8, D), F32)),
        ("sm2", V((8, D), F32)),
        ("st", V((4, 16, D), F32)),
        ("sd", V((n, 16, D), F32)),
        ("ssem", pltpu.SemaphoreType.DMA((180 + 4 * nch,))),
        ("rsem", pltpu.SemaphoreType.DMA((180 + 4 * nch,))),
        ("lsem", pltpu.SemaphoreType.DMA((16,))),
    ]
    names = [i[0] for i in ins] + [o[0] for o in outs] + [s[0] for s in scr]
    res, gin, fh, xh, osm = pl.pallas_call(
        functools.partial(body, names, n),
        out_shape=[o[1] for o in outs],
        in_specs=[i[2] for i in ins],
        out_specs=[o[2] for o in outs],
        scratch_shapes=[s[1] for s in scr],
        compiler_params=pltpu.CompilerParams(
            collective_id=0, has_side_effects=True, vmem_limit_bytes=67043328
        ),
        name="layer",
    )(*[i[1] for i in ins])
    oB, oI, oQ, oO, oR, oG, ln1g, ln1b, qv, outb, ln2g, ln2b, rout, inb, bb = place(
        fh, xh, res, gin, osm, half // 32, D // 64
    )
    return (
        oR.reshape(S, span, D),
        oG.reshape(S, span, D),
        ln1g.reshape(D),
        ln1b.reshape(D),
        oQ.transpose(1, 0, 2),
        qv,
        oO,
        outb.reshape(D),
        ln2g.reshape(D),
        ln2b.reshape(D),
        rout.T,
        oI,
        inb,
        oB,
        bb,
    )


SCALE = 0.125
EPSILON = 1e-05
MASKED = -1e30
HIGHEST = lax.Precision.HIGHEST


def layer_norm(values, norm_gain, norm_bias):
    centred = values - jnp.mean(values, axis=-1, keepdims=True)
    spread = jnp.mean(centred * centred, axis=-1, keepdims=True)
    return centred * lax.rsqrt(spread + EPSILON) * norm_gain + norm_bias


def heads_of(block, head_count):
    seq_count, row_count, feat_count = block.shape
    return block.reshape(seq_count, row_count, head_count, feat_count // head_count).transpose(
        0, 2, 1, 3
    )


def tokens_of(block):
    seq_count, head_count, row_count, head_width = block.shape
    return block.transpose(0, 2, 1, 3).reshape(seq_count, row_count, head_count * head_width)


def masked_scores(queries, key_heads, query_start, key_start, prefix):
    scores = (
        jnp.einsum("shqd,shkd->shqk", queries, key_heads, preferred_element_type=jnp.float32)
        * SCALE
    )
    query_pos = query_start + jnp.arange(queries.shape[2], dtype=jnp.int32)
    key_pos = key_start + jnp.arange(key_heads.shape[2], dtype=jnp.int32)
    visible_mask = (key_pos[None, None, :] <= query_pos[None, :, None]) | (
        key_pos[None, None, :] < prefix[:, None, None]
    )
    visible_mask = visible_mask[:, None]
    return (jnp.where(visible_mask, scores, MASKED), visible_mask)


def block_live(key_start, query_last, prefix):
    return jnp.any(key_start < prefix) | (key_start <= query_last)


def prob_grads(
    queries, key_heads, value_heads, douts, log_total, delta, query_start, key_start, prefix
):
    scores, visible_mask = masked_scores(queries, key_heads, query_start, key_start, prefix)
    probs = jnp.where(visible_mask, jnp.exp(scores - log_total[..., None]), 0.0)
    dprob = jnp.einsum("shqd,shkd->shqk", douts, value_heads, preferred_element_type=jnp.float32)
    dscore = (probs * (dprob - delta[..., None])).astype(jnp.bfloat16)
    return (probs, dscore)


def attend_fold(run_state, piece_rows, piece_start, queries, first_row, prefix):
    key_piece, value_piece = piece_rows
    head_count = queries.shape[1]
    row_count = key_piece.shape[1]
    block_width = math.gcd(row_count, 512)
    query_last = first_row + queries.shape[2] - 1

    def attend_update(block_index, state_now):
        key_start = block_index * block_width
        key_heads = heads_of(
            lax.dynamic_slice_in_dim(key_piece, block_index * block_width, block_width, 1),
            head_count,
        )
        value_heads = heads_of(
            lax.dynamic_slice_in_dim(value_piece, block_index * block_width, block_width, 1),
            head_count,
        )
        scores, visible_mask = masked_scores(queries, key_heads, first_row, key_start, prefix)
        run_max, run_sum, run_out = state_now
        new_max = jnp.maximum(run_max, jnp.max(scores, axis=-1))
        factor = jnp.exp(run_max - new_max)
        weights = jnp.where(visible_mask, jnp.exp(scores - new_max[..., None]), 0.0)
        run_sum = factor * run_sum + jnp.sum(weights, axis=-1)
        run_out = factor[..., None] * run_out + jnp.einsum(
            "shqk,shkd->shqd", weights, value_heads.astype(jnp.float32), precision=HIGHEST
        )
        return (new_max, run_sum, run_out)

    def attend_block_step(state_now, block_index):
        key_start = block_index * block_width
        is_live = block_live(key_start, query_last, prefix)
        return (
            lax.cond(
                is_live, functools.partial(attend_update, block_index), lambda unchanged: unchanged, state_now
            ),
            None,
        )

    run_state, unused = lax.scan(
        attend_block_step, run_state, jnp.arange(row_count // block_width, dtype=jnp.int32)
    )
    return run_state


def key_pass(queries, douts, log_total, delta, keys_all, values_all, first_row, prefix):
    head_count = queries.shape[1]
    total_rows = keys_all.shape[1]
    block_width = math.gcd(total_rows, 512)
    query_last = first_row + queries.shape[2] - 1

    def key_block_step(dquery, block_index):
        key_start = block_index * block_width

        def work(dquery_now):
            key_heads = heads_of(
                lax.dynamic_slice_in_dim(keys_all, key_start, block_width, 1), head_count
            )
            value_heads = heads_of(
                lax.dynamic_slice_in_dim(values_all, key_start, block_width, 1), head_count
            )
            probs, dscore = prob_grads(
                queries,
                key_heads,
                value_heads,
                douts,
                log_total,
                delta,
                first_row,
                key_start,
                prefix,
            )
            dquery_now = (
                dquery_now
                + jnp.einsum(
                    "shqk,shkd->shqd", dscore, key_heads, preferred_element_type=jnp.float32
                )
                * SCALE
            )
            return (dquery_now, ())

        def skipped(dquery_now):
            return (dquery_now, ())

        return lax.cond(block_live(key_start, query_last, prefix), work, skipped, dquery)

    dquery, key_parts = lax.scan(
        key_block_step,
        jnp.zeros(queries.shape, jnp.float32),
        jnp.arange(total_rows // block_width, dtype=jnp.int32),
    )
    return (dquery, ())


def query_fold(run_state, piece_rows, piece_start, key_heads, value_heads, first_row, prefix):
    query_piece, dout_piece, total_piece, delta_piece = piece_rows
    head_count = key_heads.shape[1]
    row_count = query_piece.shape[1]
    block_width = math.gcd(row_count, 512)

    def query_update(block_index, state_now):
        query_start = block_index * block_width
        offset = block_index * block_width
        queries = heads_of(
            lax.dynamic_slice_in_dim(query_piece, offset, block_width, 1), head_count
        )
        douts = heads_of(lax.dynamic_slice_in_dim(dout_piece, offset, block_width, 1), head_count)
        log_total = lax.dynamic_slice_in_dim(total_piece, offset, block_width, 1).transpose(0, 2, 1)
        delta = lax.dynamic_slice_in_dim(delta_piece, offset, block_width, 1).transpose(0, 2, 1)
        probs, dscore = prob_grads(
            queries, key_heads, value_heads, douts, log_total, delta, query_start, first_row, prefix
        )
        dkey_now, dvalue_now = state_now
        dkey_now = (
            dkey_now
            + jnp.einsum("shqk,shqd->shkd", dscore, queries, preferred_element_type=jnp.float32)
            * SCALE
        )
        dvalue_now = dvalue_now + jnp.einsum(
            "shqk,shqd->shkd", probs, douts.astype(jnp.float32), precision=HIGHEST
        )
        return (dkey_now, dvalue_now)

    def query_block_step(state_now, block_index):
        query_last = block_index * block_width + block_width - 1
        is_live = block_live(first_row, query_last, prefix)
        return (
            lax.cond(
                is_live, functools.partial(query_update, block_index), lambda unchanged: unchanged, state_now
            ),
            None,
        )

    run_state, unused = lax.scan(
        query_block_step, run_state, jnp.arange(row_count // block_width, dtype=jnp.int32)
    )
    return run_state


def local(
    tokens,
    ln1_gain,
    ln1_bias,
    w_qkv,
    qv_bias,
    w_out,
    out_bias,
    ln2_gain,
    ln2_bias,
    router,
    w_in,
    in_bias,
    w_back,
    back_bias,
    routes,
    prefix,
    cotangent,
):
    seq_count, span_len, model_width = tokens.shape
    tok_rows = seq_count * span_len
    local_feats = w_qkv.shape[2]
    head_count = local_feats // HEAD_DIM
    expert_count = w_in.shape[0]
    first_row = lax.axis_index("dp") * span_len
    local_shape = (seq_count, span_len, local_feats)
    source = tokens.reshape(tok_rows, model_width).astype(jnp.float32)
    normed_one, ln1_pull = jax.vjp(
        layer_norm, source, ln1_gain.astype(jnp.float32), ln1_bias.astype(jnp.float32)
    )
    hidden_one = normed_one.astype(jnp.bfloat16)
    projected = jnp.einsum("ti,icf->tcf", hidden_one, w_qkv, preferred_element_type=jnp.float32)
    bias_float = qv_bias.astype(jnp.float32)
    query_tok = (projected[:, 0] + bias_float[0]).astype(jnp.bfloat16).reshape(local_shape)
    key_tok = projected[:, 1].astype(jnp.bfloat16).reshape(local_shape)
    value_tok = (projected[:, 2] + bias_float[1]).astype(jnp.bfloat16).reshape(local_shape)
    queries = heads_of(query_tok, head_count)
    stat_shape = queries.shape[:3]
    start_state = (
        jnp.full(stat_shape, MASKED, jnp.float32),
        jnp.zeros(stat_shape, jnp.float32),
        jnp.zeros(queries.shape, jnp.float32),
    )
    fold_keys = functools.partial(attend_fold, queries=queries, first_row=first_row, prefix=prefix)
    run_max, run_sum, run_out = fold_keys(
        start_state,
        (
            lax.all_gather(key_tok, "dp", axis=1, tiled=True),
            lax.all_gather(value_tok, "dp", axis=1, tiled=True),
        ),
        jnp.int32(0),
    )
    mixed_heads = run_out / run_sum[..., None]
    log_total = run_max + jnp.log(run_sum)
    mixed_b = tokens_of(mixed_heads.astype(jnp.bfloat16)).reshape(tok_rows, local_feats)
    out_shift = out_bias.astype(jnp.float32)
    gain_two = ln2_gain.astype(jnp.float32)
    shift_two = ln2_bias.astype(jnp.float32)
    attn_part = jnp.dot(mixed_b, w_out, preferred_element_type=jnp.float32)
    attn_out = lax.psum(attn_part, "tensor") + out_shift
    residual = source + attn_out
    normed_two, ln2_pull = jax.vjp(layer_norm, residual, gain_two, shift_two)
    hidden_two = normed_two.astype(jnp.bfloat16)
    logits = jnp.dot(hidden_two, router, preferred_element_type=jnp.float32)
    chosen = routes.reshape(tok_rows)
    expert_ids = jnp.arange(expert_count, dtype=jnp.int32)
    expert_hot = (chosen[:, None] == expert_ids[None, :]).astype(jnp.int32)

    def gate_of(logit_vals):
        return jnp.sum(
            jnp.where(expert_hot == 1, jax.nn.softmax(logit_vals, axis=-1), 0.0), axis=-1
        )

    gate_value, gate_pull = jax.vjp(gate_of, logits)
    earlier = jnp.cumsum(expert_hot, axis=0, dtype=jnp.int32) - expert_hot
    slot_place = jnp.sum(earlier * expert_hot, axis=1, dtype=jnp.int32)
    slot_ids = jnp.arange(CAP, dtype=jnp.int32)
    select_mask = (expert_hot[:, :, None] == 1) & (
        slot_place[:, None, None] == slot_ids[None, None, :]
    )
    select = select_mask.astype(jnp.bfloat16)
    select_float = select_mask.astype(jnp.float32)
    dispatched = jnp.einsum(
        "tec,td->ecd", select, hidden_two, preferred_element_type=jnp.float32
    ).astype(jnp.bfloat16)
    pre_act = (
        jnp.einsum("ecd,edf->ecf", dispatched, w_in, preferred_element_type=jnp.float32)
        + in_bias.astype(jnp.float32)[:, None, :]
    )
    act_float, gelu_pull = jax.vjp(functools.partial(jax.nn.gelu, approximate=False), pre_act)
    active = act_float.astype(jnp.bfloat16)
    expert_part = jnp.einsum("ecf,efd->ecd", active, w_back, preferred_element_type=jnp.float32)
    expert_full = lax.psum(expert_part, "tensor") + back_bias.astype(jnp.float32)[:, None, :]
    combined = jnp.einsum("tec,ecd->td", select_float, expert_full, precision=HIGHEST)
    layer_rows = residual + gate_value[:, None] * combined
    grad_out = cotangent.reshape(tok_rows, model_width).astype(jnp.float32)
    dgate = jnp.sum(grad_out * combined, axis=-1)
    dlogit_b = gate_pull(dgate)[0].astype(jnp.bfloat16)
    gated_grad = (gate_value[:, None] * grad_out).astype(jnp.bfloat16)
    dexpert_b = jnp.einsum(
        "tec,td->ecd", select, gated_grad, preferred_element_type=jnp.float32
    ).astype(jnp.bfloat16)
    grad_back_bias = jnp.sum(dexpert_b, axis=1, dtype=jnp.float32)
    grad_w_back = jnp.einsum("ecf,ecd->efd", active, dexpert_b, preferred_element_type=jnp.float32)
    dactive = jnp.einsum("ecd,efd->ecf", dexpert_b, w_back, preferred_element_type=jnp.float32)
    dpre_b = gelu_pull(dactive)[0].astype(jnp.bfloat16)
    grad_in_bias = jnp.sum(dpre_b, axis=1, dtype=jnp.float32)
    grad_w_in = jnp.einsum("ecd,ecf->edf", dispatched, dpre_b, preferred_element_type=jnp.float32)
    slot_part = jnp.einsum("ecf,edf->ecd", dpre_b, w_in, preferred_element_type=jnp.float32)
    dslots = lax.psum(slot_part, "tensor")
    dnorm_two = jnp.einsum("tec,ecd->td", select_float, dslots, precision=HIGHEST) + jnp.einsum(
        "te,de->td", dlogit_b, router, preferred_element_type=jnp.float32
    )
    grad_router = jnp.einsum("td,te->de", hidden_two, dlogit_b, preferred_element_type=jnp.float32)
    dresid_norm, grad_ln2_gain, grad_ln2_bias = ln2_pull(dnorm_two)
    dresidual = grad_out + dresid_norm
    dattn_b = dresidual.astype(jnp.bfloat16)
    grad_out_bias = jnp.sum(dattn_b, axis=0, dtype=jnp.float32)
    grad_w_out = jnp.einsum("tf,td->fd", mixed_b, dattn_b, preferred_element_type=jnp.float32)
    dmixed_tok = (
        jnp.einsum("td,fd->tf", dattn_b, w_out, preferred_element_type=jnp.float32)
        .astype(jnp.bfloat16)
        .reshape(local_shape)
    )
    douts = heads_of(dmixed_tok, head_count)
    delta = jnp.sum(douts.astype(jnp.float32) * mixed_heads, axis=-1)
    keys_all, values_all = (
        lax.all_gather(key_tok, "dp", axis=1, tiled=True),
        lax.all_gather(value_tok, "dp", axis=1, tiled=True),
    )
    dquery, unused = key_pass(
        queries, douts, log_total, delta, keys_all, values_all, first_row, prefix
    )
    total_rows = log_total.transpose(0, 2, 1)
    delta_rows = delta.transpose(0, 2, 1)
    fold_rows = functools.partial(
        query_fold,
        key_heads=heads_of(key_tok, head_count),
        value_heads=heads_of(value_tok, head_count),
        first_row=first_row,
        prefix=prefix,
    )
    zero_heads = jnp.zeros(queries.shape, jnp.float32)
    dkey_heads, dvalue_heads = fold_rows(
        (zero_heads, zero_heads),
        (
            lax.all_gather(query_tok, "dp", axis=1, tiled=True),
            lax.all_gather(dmixed_tok, "dp", axis=1, tiled=True),
            lax.all_gather(total_rows.astype(jnp.bfloat16), "dp", axis=1, tiled=True).astype(
                jnp.float32
            ),
            lax.all_gather(delta_rows.astype(jnp.bfloat16), "dp", axis=1, tiled=True).astype(
                jnp.float32
            ),
        ),
        jnp.int32(0),
    )
    dkey = tokens_of(dkey_heads)
    dvalue = tokens_of(dvalue_heads)
    dquery_b = tokens_of(dquery).astype(jnp.bfloat16).reshape(tok_rows, local_feats)
    dkey_b = dkey.astype(jnp.bfloat16).reshape(tok_rows, local_feats)
    dvalue_b = dvalue.astype(jnp.bfloat16).reshape(tok_rows, local_feats)
    dproject = jnp.stack([dquery_b, dkey_b, dvalue_b], axis=1)
    grad_qv_bias = jnp.stack(
        [jnp.sum(dquery_b, axis=0, dtype=jnp.float32), jnp.sum(dvalue_b, axis=0, dtype=jnp.float32)]
    )
    grad_w_qkv = jnp.einsum("ti,tcf->icf", hidden_one, dproject, preferred_element_type=jnp.float32)
    norm_part = jnp.einsum("tcf,icf->ti", dproject, w_qkv, preferred_element_type=jnp.float32)
    dnorm_one = lax.psum(norm_part, "tensor")
    dsource_norm, grad_ln1_gain, grad_ln1_bias = ln1_pull(dnorm_one)
    input_grad = (dresidual + dsource_norm).reshape(seq_count, span_len, model_width)
    summed = lax.psum(
        (
            grad_ln1_gain,
            grad_ln1_bias,
            grad_w_qkv,
            grad_qv_bias,
            grad_w_out,
            grad_out_bias,
            grad_ln2_gain,
            grad_ln2_bias,
            grad_router,
            grad_w_in,
            grad_in_bias,
            grad_w_back,
            grad_back_bias,
        ),
        "dp",
    )
    layer_out = layer_rows.reshape(seq_count, span_len, model_width)
    return (layer_out, input_grad) + tuple(summed)


def solution(mesh):
    in_specs = (
        P(None, "dp", None),
        P(),
        P(),
        P(None, None, "tensor"),
        P(None, "tensor"),
        P("tensor", None),
        P(),
        P(),
        P(),
        P(),
        P(None, None, "tensor"),
        P(None, "tensor"),
        P(None, "tensor", None),
        P(),
        P(None, "dp", None),
        P(),
        P(None, "dp", None),
    )
    out_specs = (
        P(None, "dp", None),
        P(None, "dp", None),
        P(),
        P(),
        P(None, None, "tensor"),
        P(None, "tensor"),
        P("tensor", None),
        P(),
        P(),
        P(),
        P(),
        P(None, None, "tensor"),
        P(None, "tensor"),
        P(None, "tensor", None),
        P(),
    )
    n, nt = mesh.shape["dp"], mesh.shape["tensor"]

    def step(*args):
        tokens, w_qkv = args[0], args[3]
        heads = w_qkv.shape[2] // HEAD_DIM
        fits = (
            nt == 4
            and n == 8
            and tokens.shape[2] == 1024
            and w_qkv.shape[2] == 256
            and args[10].shape == (2, 1024, 1024)
            and n == tokens.shape[0] * heads
            and tokens.shape[0] * tokens.shape[1] == nt * CH
            and tokens.shape[1] == 256
        )
        return fast_local(args, n, nt) if fits else local(*args)

    return jax.shard_map(step, mesh=mesh, in_specs=in_specs, out_specs=out_specs, check_vma=False)
```

```python
import functools
import math

import jax
import jax.numpy as jnp
from jax import lax
from jax.experimental import pallas as pl
from jax.experimental.pallas import tpu as pltpu
from jax.sharding import PartitionSpec as P

F32 = jnp.float32
BF = jnp.bfloat16
MESH = pl.DeviceIdType.MESH
EPS = 1e-05
CAP = 320
HEAD_DIM = 64
NEG = -1e30
CH = 128


def mm(a, b):
    return lax.dot_general(a, b, (((1,), (0,)), ((), ())), preferred_element_type=F32)


def mm_bt(a, b):
    return lax.dot_general(a, b, (((1,), (1,)), ((), ())), preferred_element_type=F32)


def mm_at(a, b):
    return lax.dot_general(a, b, (((0,), (0,)), ((), ())), preferred_element_type=F32)


def loop(n, body):
    def step(i, carry):
        body(i)
        return carry

    lax.fori_loop(0, n, step, 0)


def al(v, m):
    return pl.multiple_of(v, m)


def lanes(rows):
    return lax.broadcasted_iota(jnp.int32, (rows, 128), 1)


def roll64(v):
    return pltpu.roll(v, 64, 1)


class Ctx:
    def __init__(self, ssem, rsem, lsem):
        self.ssem, self.rsem, self.lsem = ssem, rsem, lsem
        self.next = 0
        self.pending = []
        dp = lax.axis_index("dp")
        t = lax.axis_index("tensor")
        self.dp, self.t = dp, t
        self.z, self.x = dp // 2, lax.rem(dp, 2)
        self.y, self.c = t // 2, lax.rem(t, 2)
        x1 = 1 - self.x
        dpx = self.z * 2 + x1
        tm = self.y * 2 + 1 - self.c
        ty = (1 - self.y) * 2 + self.c
        self.mate = (dp, tm)
        self.yp = (dp, ty)
        self.xp = (dpx, t)
        self.dg = (dpx, ty)
        self.t_mate, self.t_y = tm, ty

    def sems(self, n):
        k = self.next
        self.next += n
        return k

    def rc(self, src, dst, k, dev, kr=None):
        return pltpu.make_async_remote_copy(
            src_ref=src,
            dst_ref=dst,
            send_sem=self.ssem.at[k],
            recv_sem=self.rsem.at[k if kr is None else kr],
            device_id=dev,
            device_id_type=MESH,
        )

    def send(self, src, dst, k, dev):
        cp = self.rc(src, dst, k, dev)
        cp.start()
        self.pending.append(cp)
        return cp

    def drain(self):
        for cp in self.pending:
            cp.wait_send()
        self.pending = []


def barrier_start(C, n_dp):
    sem = pltpu.get_barrier_semaphore()
    devs = [(lax.rem(C.dp + o, n_dp), C.t) for o in range(1, n_dp)]
    devs += [C.mate, C.yp, C.dg, (C.dp, 3 - C.t)]
    for d in devs:
        pl.semaphore_signal(sem, inc=1, device_id=d, device_id_type=MESH)
    return sem, len(devs)


def norm_parts(v):
    mean = jnp.mean(v, axis=-1, keepdims=True)
    cent = v - mean
    var = jnp.mean(cent * cent, axis=-1, keepdims=True)
    r = lax.rsqrt(var + EPS)
    return cent * r, r


def stage_qkv(R, C, n):
    rows = R.tok.shape[0]
    gain, bias = R.par[0:1, :], R.par[1:2, :]
    hp = R.wqkv.shape[2] // HEAD_DIM
    k = C.sems(n)

    def seq(s):
        def ln(i):
            at = pl.ds(al(s * 256 + i * 32, 32), 32)
            n1, _ = norm_parts(R.tok[at, :].astype(F32))
            R.h1[at, :] = (n1 * gain + bias).astype(BF)

        loop(8, ln)
        at = pl.ds(al(s * 256, 256), 256)
        h = R.h1[at, :]
        lo = lanes(256) < 64
        lo2 = lanes(128) < 64
        for pr in range(hp // 2):
            cut = slice(pr * 128, pr * 128 + 128)
            tq = (mm(h, R.wqkv[0, :, cut]) + R.qvb[0:1, cut].astype(F32)) * 0.125
            tk = mm(h, R.wqkv[1, :, cut])
            tv = mm(h, R.wqkv[2, :, cut]) + R.qvb[1:2, cut].astype(F32)
            p = s * hp + 2 * pr
            R.asend[p, 0:256, :] = jnp.where(lo, tq, roll64(tk)).astype(BF)
            R.asend[p + 1, 0:256, :] = jnp.where(lo, roll64(tq), tk).astype(BF)
            a, b = tv[0:128], tv[128:256]
            R.asend[p, 256:384, :] = jnp.where(lo2, a, roll64(b)).astype(BF)
            R.asend[p + 1, 256:384, :] = jnp.where(lo2, roll64(a), b).astype(BF)
            for j in range(2):
                send_slice(C, R.asend, R.arecv, k, p + j)

    loop(rows // 256, seq)
    return lambda: wait_slices(C, R.asend, R.arecv, k, n, 0)


def send_slice(C, src, dst, k, p):
    @pl.when(p != C.dp)
    def _():
        C.rc(src.at[p], dst.at[C.dp], k + p, (p, C.t), k + C.dp).start()


def wait_slices(C, src, dst, k, n, sem):
    mine = pltpu.make_async_copy(src.at[C.dp], dst.at[C.dp], C.lsem.at[sem])
    mine.start()
    mine.wait()
    for b in range(n):

        @pl.when(b != C.dp)
        def _():
            cp = C.rc(src.at[b], dst.at[b], k + b, (b, C.t), k + b)
            cp.wait_send()
            cp.wait_recv()


def all_to_all(R, C, src, dst, n):
    k = C.sems(n)
    cps = [
        C.send(src.at[lax.rem(C.dp + o, n)], dst.at[C.dp], k + o, (lax.rem(C.dp + o, n), C.t))
        for o in range(1, n)
    ]
    mine = pltpu.make_async_copy(src.at[C.dp], dst.at[C.dp], C.lsem.at[0])
    mine.start()

    def wait():
        mine.wait()
        for cp in cps:
            cp.wait_recv()

    return wait


def stage_attend(R, C, n):
    lo = lanes(256) < 64
    lo2 = lanes(128) < 64
    one = jnp.where((lanes(256) == 64) | (lanes(256) == 65), 1.0, 0.0)
    one2 = one[0:128]

    def unpack(b):
        qk = R.arecv[b, 0:256, :].astype(F32)
        vf = R.arecv[b, 256:384, :].astype(F32)
        at = pl.ds(al(b * 256, 256), 256)
        R.Q[at, :] = jnp.where(lo, qk, 0.0).astype(BF)
        R.K[at, :] = jnp.where(lo, roll64(qk), one).astype(BF)
        R.V[pl.ds(al(b * 256, 128), 128), :] = jnp.where(lo2, vf, one2).astype(BF)
        R.V[pl.ds(al(b * 256 + 128, 128), 128), :] = jnp.where(lo2, roll64(vf), one2).astype(BF)

    loop(n, unpack)
    T = 512
    half = R.Q.shape[0] // 2 // T - 1
    seqs = R.prefix.shape[0]
    prefix = R.prefix[C.dp // (n // seqs)]
    k = C.sems(n)

    def rows_of(i):
        at = pl.ds(al(i * T, T), T)
        q = R.Q[at, :]
        qpos = i * T + lax.broadcasted_iota(jnp.int32, (T, 1), 0)
        lim = jnp.maximum(qpos, prefix - 1)

        def tile(j, carry):
            m, acc = carry
            kat = pl.ds(al(j * T, T), T)
            s = mm_bt(q, R.K[kat, :])
            kpos = j * T + lax.broadcasted_iota(jnp.int32, (T, T), 1)
            s = jnp.where(kpos <= lim, s, NEG)
            m2 = jnp.maximum(m, jnp.max(s, axis=1, keepdims=True))
            p = jnp.exp(s - m2).astype(BF)
            acc = acc * jnp.exp(m - m2) + mm(p, R.V[kat, :])
            return m2, acc

        m, acc = lax.fori_loop(
            0,
            jnp.maximum(i, half) + 1,
            tile,
            (jnp.full((T, 1), NEG, F32), jnp.zeros((T, 128), F32)),
        )
        total = acc[:, 64:65]
        o = acc / total
        lse = m + jnp.log(total)
        R.of[at, :] = jnp.where(lanes(T) < 64, o, lse)
        for u in range(2):
            b = i * 2 + u
            top, bot = o[u * 256 : u * 256 + 128], o[u * 256 + 128 : u * 256 + 256]
            R.osend[b] = jnp.where(lo2, top, roll64(bot)).astype(BF)

            @pl.when(b != C.dp)
            def _():
                C.rc(R.osend.at[b], R.orecv.at[C.dp], k + b, (b, C.t), k + C.dp).start()

    loop(R.Q.shape[0] // T, rows_of)
    mine = pltpu.make_async_copy(R.osend.at[C.dp], R.orecv.at[C.dp], C.lsem.at[0])
    mine.start()
    mine.wait()
    for b in range(n):

        @pl.when(b != C.dp)
        def _():
            cp = C.rc(R.osend.at[b], R.orecv.at[b], k + b, (b, C.t), k + b)
            cp.wait_send()
            cp.wait_recv()

    unfold_heads(R.orecv, R.otok, n, seqs)


def unfold_heads(src, dst, n, seqs):
    hp = n // seqs
    lo2 = lanes(128) < 64
    for s in range(seqs):
        for pr in range(hp // 2):
            e = src[s * hp + 2 * pr].astype(F32)
            d = src[s * hp + 2 * pr + 1].astype(F32)
            cut = slice(pr * 128, pr * 128 + 128)
            dst[s * 256 : s * 256 + 128, cut] = jnp.where(lo2, e, roll64(d)).astype(BF)
            dst[s * 256 + 128 : s * 256 + 256, cut] = jnp.where(lo2, roll64(e), d).astype(BF)


def swap_cot(R, C):
    k = C.sems(2)
    rows = R.cot.shape[0] // 2
    mine = pl.ds(al(C.c * rows, rows), rows)
    cp = C.send(R.cot.at[mine, :], R.cx.at[mine, :], k, C.xp)

    def wait():
        cp.wait_recv()
        C.send(R.cx.at[mine, :], R.cx.at[mine, :], k + 1, C.mate).wait_recv()

    return wait


def reduce4(R, C, part, out, fill=lambda: None):
    k = C.sems(3)
    k0 = (1 - C.y) * 2 + (1 - C.c)
    k1 = (1 - C.y) * 2 + C.c
    k2 = C.y * 2 + (1 - C.c)
    R.p4[0] = part(k0).astype(BF)
    c0 = C.send(R.p4.at[0], R.l4.at[0], k, C.mate)
    v1 = part(k1)
    fill()
    c0.wait_recv()
    R.p4[1] = (v1 + R.l4[0].astype(F32)).astype(BF)
    c1 = C.send(R.p4.at[1], R.l4.at[2], k + 1, C.yp)
    R.p4[2] = part(k2).astype(BF)
    c2 = C.send(R.p4.at[2], R.l4.at[1], k + 2, C.mate)
    out[...] = part(C.t)
    fill()
    c2.wait_recv()
    c1.wait_recv()
    out[...] = out[...] + R.l4[1].astype(F32) + R.l4[2].astype(F32)


def gather4(R, C, buf):
    k = C.sems(3)
    mine = buf.at[C.t]
    cy = C.send(mine, mine, k, C.yp)
    cm = C.send(mine, mine, k + 1, C.mate)

    def wait():
        cy.wait_recv()
        fwd = C.send(buf.at[C.t_y], buf.at[C.t_y], k + 2, C.mate)
        cm.wait_recv()
        fwd.wait_recv()

    return wait


def gather8(R, C, buf):
    k = C.sems(7)
    mine = buf.at[C.x * 4 + C.t]
    cd = C.send(mine, mine, k, C.dg)
    cx = C.send(mine, mine, k + 1, C.xp)
    cy = C.send(mine, mine, k + 2, C.yp)
    cm = C.send(mine, mine, k + 3, C.mate)

    def wait():
        fw = []
        for i, (cp, slot) in enumerate(
            (
                (cy, C.x * 4 + C.t_y),
                (cx, (1 - C.x) * 4 + C.t),
                (cd, (1 - C.x) * 4 + C.t_y),
            )
        ):
            cp.wait_recv()
            fw.append(C.send(buf.at[slot], buf.at[slot], k + 4 + i, C.mate))
        cm.wait_recv()
        for cp in fw:
            cp.wait_recv()

    return wait


def stage_out(R, C):
    def part(k):
        return mm(R.otok[pl.ds(al(k * CH, CH), CH), :], R.wout[...])

    reduce4(R, C, part, R.x1)
    rows = R.tok.shape[0]
    own = pl.ds(al(C.t * CH, CH), CH)
    pos = C.t * CH + lax.broadcasted_iota(jnp.int32, (CH, rows), 0)
    col = lax.broadcasted_iota(jnp.int32, (CH, rows), 1)
    hot = jnp.where(
        R.routes[...] == lax.broadcasted_iota(jnp.int32, (8, rows), 0), 1.0, 0.0
    ).astype(BF)
    earlier = mm_bt(jnp.where(col < pos, 1.0, 0.0).astype(BF), hot)
    here = mm_bt(jnp.where(col == pos, 1.0, 0.0).astype(BF), hot)
    keep = jnp.where(earlier < CAP, here, 0.0)
    keep0, keep1 = keep[:, 0:1], keep[:, 1:2]
    x1 = R.x1[...] + R.tok[own, :].astype(F32) + R.par[2:3, :]
    R.x1[...] = x1
    n, r = norm_parts(x1)
    h2 = (n * R.par[3:4, :] + R.par[4:5, :]).astype(BF)
    slot = C.x * 4 + C.t
    R.H2[slot] = h2
    hf = h2.astype(F32)
    l0 = jnp.sum(hf * R.par[5:6, :], axis=1, keepdims=True)
    l1 = jnp.sum(hf * R.par[6:7, :], axis=1, keepdims=True)
    mx = jnp.maximum(l0, l1)
    e0, e1 = jnp.exp(l0 - mx), jnp.exp(l1 - mx)
    p0, p1 = e0 / (e0 + e1), e1 / (e0 + e1)
    gate = here[:, 0:1] * p0 + here[:, 1:2] * p1
    ln = lanes(CH)
    hi = gate.astype(BF).astype(F32)
    mid = (gate - hi).astype(BF).astype(F32)
    meta = jnp.zeros((CH, 128), F32)
    for i, v in enumerate((keep0, keep1, hi, mid, gate - hi - mid)):
        meta = jnp.where(ln == i, v, meta)
    R.META[slot] = meta.astype(BF)
    wait_h = gather8(R, C, R.H2)
    wait_m = gather8(R, C, R.META)
    cols = jnp.zeros((CH, 128), F32)
    for i, v in enumerate((p0, p1, here[:, 0:1], here[:, 1:2], gate, keep0, keep1)):
        cols = jnp.where(ln == i, v, cols)
    R.cols[...] = cols
    wait_h()
    wait_m()

    def gated(i):
        for xx, cot in ((C.x, R.cot), (1 - C.x, R.cx)):
            m = R.META[xx * 4 + i].astype(F32)
            gate = m[:, 2:3] + m[:, 3:4] + m[:, 4:5]
            g = cot[pl.ds(al(i * CH, CH), CH), :].astype(F32)
            gr = (gate * g).astype(BF).astype(F32)
            R.GG[xx * 4 + i] = (gr * (m[:, 0:1] + m[:, 1:2])).astype(BF)

    loop(4, gated)


def gelu_both(h):
    half = 0.5 * (1.0 + lax.erf(h * 0.7071067811865476))
    return h * half, half + h * (jnp.exp(-0.5 * h * h) * 0.3989422804014327)


class Reduce8:
    def __init__(self, C, parts, land, stage, out):
        self.C, self.parts, self.land, self.stage, self.out = C, parts, land, stage, out
        self.k = C.sems(7)

    def place(self, n):
        C = self.C
        a, b = n // 2, lax.rem(n, 2)
        xx = (1 - C.x) * (1 - a) + C.x * a
        yy = (1 - C.y) * (1 - b) + C.y * b
        return xx, yy

    def swap(self, n):
        C = self.C
        xx, yy = self.place(n)
        src = self.parts.at[xx * 4 + yy * 2 + 1 - C.c]
        return C.rc(src, self.land.at[n], self.k + n, C.mate)

    def added(self, n):
        C = self.C
        xx, yy = self.place(n)
        self.swap(n).wait_recv()
        return self.parts[xx * 4 + yy * 2 + C.c].astype(F32) + self.land[n].astype(F32)

    def cross(self, n):
        C = self.C
        xx, yy = self.place(n)
        dev = (C.z * 2 + xx, yy * 2 + C.c)
        return C.rc(self.stage.at[n], self.land.at[4 + n], self.k + 4 + n, dev)

    def forward(self, n):
        self.stage[n] = self.added(n).astype(BF)
        self.cross(n).start()

    def keep(self):
        self.out[...] = self.added(3)
        self.C.pending += [self.swap(n) for n in range(4)] + [self.cross(n) for n in range(3)]

    def wait(self):
        for n in range(3):
            self.cross(n).wait_recv()
        v = self.out[...]
        for n in range(3):
            v = v + self.land[4 + n].astype(F32)
        self.out[...] = v


def stage_moe(R, C, sums):
    def tile(n):
        xx, yy = sums[0].place(n)
        i = xx * 2 + yy
        two = pl.ds(al(2 * i, 2), 2)
        at = pl.ds(al(i * 256, 256), 256)
        h2 = R.H2[two].reshape(256, R.H2.shape[2])
        gg = R.GG[two].reshape(256, R.GG.shape[2])
        meta = R.META[two].reshape(256, 128).astype(F32)
        m0, m1 = meta[:, 0:1], meta[:, 1:2]
        half = R.wi.shape[2]
        bias0 = R.inb[0:1, pl.ds(al(C.x * half, half), half)].astype(F32)
        bias1 = R.inb[1:2, pl.ds(al(C.x * half, half), half)].astype(F32)
        for q in range(half // 256):
            cut = slice(q * 256, q * 256 + 256)
            h0 = mm(h2, R.wi[0, :, cut]) + bias0[:, cut]
            h1 = mm(h2, R.wi[1, :, cut]) + bias1[:, cut]
            act, slope = gelu_both(jnp.where(m0 > 0.0, h0, h1))
            R.A[0, at, cut] = (act * m0).astype(BF)
            R.A[1, at, cut] = (act * m1).astype(BF)
            d0 = mm_bt(gg, R.wb[0, cut, :])
            d1 = mm_bt(gg, R.wb[1, cut, :])
            dh = jnp.where(m0 > 0.0, d0, d1) * slope
            R.DH[0, at, cut] = (dh * m0).astype(BF)
            R.DH[1, at, cut] = (dh * m1).astype(BF)
        y = mm(R.A[0, at, :], R.wb[0]) + mm(R.A[1, at, :], R.wb[1])
        R.YP[two] = y.astype(BF).reshape(2, CH, y.shape[1])
        dx = mm_bt(R.DH[0, at, :], R.wi[0]) + mm_bt(R.DH[1, at, :], R.wi[1])
        R.DXP[two] = dx.astype(BF).reshape(2, CH, dx.shape[1])
        for r in sums:
            r.swap(n).start()

        @pl.when(n > 0)
        def _():
            for r in sums:
                r.forward(n - 1)

    loop(4, tile)
    for r in sums:
        r.keep()


def put_wide(at, v):
    w = v.shape[1] // 2
    at[0:32, :] = v[:, 0:w].astype(BF)
    at[32:64, :] = v[:, w : 2 * w].astype(BF)


def stage_moe_grads(R, C, K, ring):
    rows = R.GG.shape[0] * CH

    def back(i):
        at = pl.ds(al(i * 128, 128), 128)
        gg = R.GG[...].reshape(rows, R.GG.shape[2])
        for e in range(2):
            v = mm_at(R.A[e, :, at], gg)
            for j in range(4):
                put_wide(R.G.at[e, 4 * i + j], v[32 * j : 32 * j + 32])

    loop(R.A.shape[2] // 128, back)
    ring.run(3)
    base = ring.take(R.H2.shape[2] // 256)

    def into(i):
        at = pl.ds(al(i * 128, 128), 128)
        h2t = R.H2[:, :, at].reshape(rows, 128)
        for e in range(2):
            v = mm_at(h2t, R.DH[e]).astype(BF)
            R.G[e, K.i0 + 2 * i] = v[0:64]
            R.G[e, K.i0 + 2 * i + 1] = v[64:128]

        @pl.when(lax.rem(i, 2) == 1)
        def _():
            ring.tick(base + i // 2)

    loop(R.H2.shape[2] // 128, into)


def norm_back(n, r, dn):
    return r * (
        dn - jnp.mean(dn, axis=-1, keepdims=True) - n * jnp.mean(dn * n, axis=-1, keepdims=True)
    )


def rowsum(v):
    return jnp.sum(v, axis=0, keepdims=True)


def stage_owner(R, C):
    own = pl.ds(al(C.t * CH, CH), CH)
    cols = R.cols[...]
    p0, p1, h0, h1, gate, k0, k1 = (cols[:, i : i + 1] for i in range(7))
    u = R.u[...] + k0 * R.par[7:8, :] + k1 * R.par[8:9, :]
    g = R.cot[own, :].astype(F32)
    x1 = R.x1[...]
    R.RES[C.t] = (x1 + gate * u).astype(BF)
    dg = jnp.sum(g * u, axis=1, keepdims=True) * gate
    dl0 = (dg * (h0 - p0)).astype(BF).astype(F32)
    dl1 = (dg * (h1 - p1)).astype(BF).astype(F32)
    h2 = R.H2[C.x * 4 + C.t].astype(F32)
    gg = R.GG[C.x * 4 + C.t].astype(F32)
    dh2 = R.dx[...] + dl0 * R.par[5:6, :] + dl1 * R.par[6:7, :]
    n, r = norm_parts(x1)
    dx1 = g + norm_back(n, r, dh2 * R.par[3:4, :])
    da = dx1.astype(BF)
    R.DA[C.t] = da
    R.x1[...] = dx1
    R.sm[0:1, :] = rowsum(dh2 * n)
    R.sm[1:2, :] = rowsum(dh2)
    R.sm[2:3, :] = rowsum(da.astype(F32))
    R.sm[3:4, :] = rowsum(h2 * dl0)
    R.sm[4:5, :] = rowsum(h2 * dl1)
    R.sm[5:6, :] = rowsum(gg * k0)
    R.sm[6:7, :] = rowsum(gg * k1)


def stage_out_back(R, C, n):
    seqs = R.prefix.shape[0]
    hp = n // seqs
    lo2 = lanes(128) < 64
    for s in range(seqs):
        da = R.DA[2 * s : 2 * s + 2].reshape(256, R.DA.shape[2])
        for pr in range(hp // 2):
            cut = slice(pr * 128, pr * 128 + 128)
            d = mm_bt(da, R.wout[cut, :])
            a, b = d[0:128], d[128:256]
            R.osend[s * hp + 2 * pr] = jnp.where(lo2, a, roll64(b)).astype(BF)
            R.osend[s * hp + 2 * pr + 1] = jnp.where(lo2, roll64(a), b).astype(BF)


def tail_of(buf, d, c, n=1):
    return buf.at[d, 64 * c : 64 * (c + n), :]


def stage_out_grad(R, C):
    da = R.DA[...].reshape(R.otok.shape[0], R.DA.shape[2])
    ho = R.otok.shape[1] // 2
    k0 = R.G.shape[1] - 8
    for own, who in ((False, 1 - C.x), (True, C.x)):
        v = mm_at(R.otok[:, pl.ds(al(who * ho, ho), ho)], da)
        for d in range(2):
            for c in range(2):
                r = d * 64 + c * 32
                put_wide(R.G.at[d, k0 + c] if own else tail_of(R.A, d, c), v[r : r + 32])


def add_tail(R, c0, n):
    k0 = R.G.shape[1] - 8

    def one(c):
        for d in range(2):
            v = R.G[d, k0 + c0 + c].astype(F32) + R.wi[d, pl.ds(al((c0 + c) * 64, 64), 64), :].astype(F32)
            R.G[d, k0 + c0 + c] = v.astype(BF)

    loop(n, one)


def stage_attend_back(R, C, n, ring, xo):
    lo2 = lanes(128) < 64
    ln2 = lanes(128)

    def hi_lo(v):
        hi = v.astype(BF).astype(F32)
        return hi, v - hi

    def unpack(b):
        f = R.dorecv[b].astype(F32)
        for u in range(2):
            at = pl.ds(al(b * 256 + u * 128, 128), 128)
            do = jnp.where(lo2, f if u == 0 else roll64(f), 0.0)
            of = R.of[at, :]
            hi, low = hi_lo(-jnp.sum(do * of, axis=1, keepdims=True))
            R.DO[at, :] = jnp.where(ln2 == 64, hi, jnp.where(ln2 == 65, low, do)).astype(BF)
            hi, low = hi_lo(-of[:, 64:65])
            q = R.Q[at, :].astype(F32)
            R.Q[at, :] = jnp.where(ln2 == 64, hi, jnp.where(ln2 == 65, low, q)).astype(BF)

    loop(n, unpack)
    T = 512
    total = R.Q.shape[0]
    nt = total // T
    half = nt // 2
    seqs = R.prefix.shape[0]
    prefix = R.prefix[C.dp // (n // seqs)]
    R.dq[...] = jnp.zeros_like(R.dq)
    k = C.sems(n)
    k2 = C.sems(n)
    base = ring.take(T_AB * nt)
    kvs, kvr, dqr = R.asend.at[:, 0:256], R.arecv.at[:, 0:256], R.arecv.at[:, 256:384]

    def keys(jj):
        loop(T_AB // 2, lambda i: ring.tick(base + T_AB * jj + i))
        j = nt - 1 - jj
        kat = pl.ds(al(j * T, T), T)
        kk, vv = R.K[kat, :], R.V[kat, :]
        kpos = j * T + lax.broadcasted_iota(jnp.int32, (T, T), 0)

        def tile(i, carry):
            dk, dv = carry
            qat = pl.ds(al(i * T, T), T)
            q, do = R.Q[qat, :], R.DO[qat, :]
            qpos = i * T + lax.broadcasted_iota(jnp.int32, (1, T), 1)
            lim = jnp.maximum(qpos, prefix - 1)
            p = jnp.where(kpos <= lim, jnp.exp(mm_bt(kk, q)), 0.0)
            ds = (p * mm_bt(vv, do)).astype(BF)
            dv = dv + mm(p.astype(BF), do)
            dk = dk + mm(ds, q)
            R.dq[qat, :] = R.dq[qat, :] + mm_at(ds, kk)
            return dk, dv

        first = jnp.where(j >= half, j, 0)
        dk, dv = lax.fori_loop(
            first, nt, tile, (jnp.zeros((T, 128), F32), jnp.zeros((T, 128), F32))
        )
        lo = lanes(T) < 64
        kv = jnp.where(lo, dk, roll64(dv)).astype(BF)
        for u in range(2):
            b = j * 2 + u
            R.asend[b, 0:256, :] = kv[u * 256 : u * 256 + 256]

            @pl.when(b != C.dp)
            def _():
                C.rc(kvs.at[b], kvr.at[C.dp], k + b, (b, C.t), k + C.dp).start()

        loop(T_AB - T_AB // 2, lambda i: ring.tick(base + T_AB * jj + T_AB // 2 + i))

    loop(nt, keys)

    def queries(b):
        at = al(b * 256, 256)
        top = R.dq[pl.ds(at, 128), :] * 0.125
        bot = R.dq[pl.ds(al(at + 128, 128), 128), :] * 0.125
        R.osend[b] = jnp.where(lo2, top, roll64(bot)).astype(BF)

        @pl.when(b != C.dp)
        def _():
            C.rc(R.osend.at[b], dqr.at[C.dp], k2 + b, (b, C.t), k2 + C.dp).start()

    loop(n, queries)
    xo.wait_recv()
    add_tail(R, 0, 2)
    ring.run(T_KV)
    for src, dst, i in ((R.osend, dqr, 0), (kvs, kvr, 1)):
        mine = pltpu.make_async_copy(src.at[C.dp], dst.at[C.dp], C.lsem.at[i])
        mine.start()
        mine.wait()
    for src, dst, kk in ((kvs, kvr, k), (R.osend, dqr, k2)):
        for b in range(n):

            @pl.when(b != C.dp)
            def _():
                cp = C.rc(src.at[b], dst.at[b], kk + b, (b, C.t), kk + b)
                cp.wait_send()
                cp.wait_recv()

    hp = n // seqs
    lo = lanes(256) < 64
    for s in range(seqs):
        for pr in range(hp // 2):
            p = s * hp + 2 * pr
            cut = slice(pr * 128, pr * 128 + 128)
            e, d = kvr[p].astype(F32), kvr[p + 1].astype(F32)
            R.dproj[1, s * 256 : s * 256 + 256, cut] = jnp.where(lo, e, roll64(d)).astype(BF)
            R.dproj[2, s * 256 : s * 256 + 256, cut] = jnp.where(lo, roll64(e), d).astype(BF)
    unfold_heads(dqr, R.dproj.at[0], n, seqs)


def stage_qkv_back(R, C, fill):
    def part(k):
        at = pl.ds(al(k * CH, CH), CH)
        return (
            mm_bt(R.dproj[0, at, :], R.wqkv[0])
            + mm_bt(R.dproj[1, at, :], R.wqkv[1])
            + mm_bt(R.dproj[2, at, :], R.wqkv[2])
        )

    reduce4(R, C, part, R.dx, fill)
    own = pl.ds(al(C.t * CH, CH), CH)
    n, r = norm_parts(R.tok[own, :].astype(F32))
    dh1 = R.dx[...]
    R.GIN[C.t] = (R.x1[...] + norm_back(n, r, dh1 * R.par[0:1, :])).astype(BF)
    R.sm2[0:1, :] = rowsum(dh1 * n)
    R.sm2[1:2, :] = rowsum(dh1)


def stage_qkv_grad(R, C, ring):
    hq = R.h1.shape[1] // 2
    k = C.sems(2)
    cps = []
    k0 = R.G.shape[1] - 6
    for own, who in ((False, 1 - C.x), (True, C.x)):
        for d in range(2):
            for c in range(2):
                at = pl.ds(al(who * hq + (2 * d + c) * 128, 128), 128)
                h = R.h1[:, at]
                for m in range(3):
                    v = mm_at(h, R.dproj[m]).astype(BF)
                    w = v.shape[1]
                    i = 2 * m + c
                    dst = R.G.at[d, k0 + i] if own else tail_of(R.A, d, 2 + i)
                    dst[:, 0:w] = v[0:64]
                    dst[:, w : 2 * w] = v[64:128]
            ring.run(T_QG)
            if not own:
                cps.append(C.send(tail_of(R.A, d, 2, 6), tail_of(R.wi, d, 2, 6), k + d, C.xp))
    return cps


class Kinds:
    def __init__(self, nb, ni):
        self.i0 = nb
        self.o0 = nb + ni
        self.q0 = self.o0 + 2
        self.n = self.q0 + 6


class Sums:
    def __init__(self, R, C, n):
        self.R, self.C, self.n = R, C, n
        self.a, self.b = C.sems(2 * n), C.sems(2 * n)
        self.one = C.sems(10)

    def finish(self, cut):
        R, C = self.R, self.C
        for d in range(2):
            pos = C.z if d == 0 else 3 - C.z
            fn = R.FN.at[d]

            def sent(k0, m, i):
                part = R.FN.at[d, pl.ds(k0, m)]
                C.rc(part, part, self.one + i + d, C.xp).wait_send()

            rest = self.n - cut
            sent(cut, rest, 0)

            @pl.when(jnp.logical_or(pos == 1, pos == 2))
            def _():
                sent(cut, rest, 2)

            @pl.when(pos < 3)
            def _():
                sent(0, cut, 6)

            @pl.when(pos > 0)
            def _():
                sent(0, cut, 8)

            cp = C.rc(fn, R.XH.at[d], self.one + 4 + d, C.xp)
            cp.wait_send()
            cp.wait_recv()
            pltpu.make_async_copy(fn, R.FH.at[d], C.lsem.at[4 + d]).wait()


class Ring:
    def __init__(self, sums, k0, k1, w):
        self.S, self.k0, self.k1, self.w = sums, k0, k1, w
        self.cur = 0
        self.total = k1 - k0 + 4 * w

    def take(self, n):
        base = self.cur
        self.cur += n
        return base

    def run(self, n):
        n = min(n, self.total - self.cur)
        if n <= 0:
            return
        base = self.take(n)
        loop(n, lambda i: self.tick(base + i))

    def rest(self):
        self.run(self.total - self.cur)

    def tick(self, s):
        for d in range(2):
            self.half(s + self.k0, d)

    def half(self, s, d):
        S, w = self.S, self.w
        R, C, n, one = S.R, S.C, S.n, S.one
        pos = C.z if d == 0 else 3 - C.z

        def dev(p):
            return ((p if d == 0 else 3 - p) * 2 + C.x, C.t)

        def act(k, cond):
            ok = jnp.logical_and(k >= self.k0, k < self.k1)
            return ok if cond is None else jnp.logical_and(ok, cond)

        def toward(src, dst, kr, p):
            return C.rc(src, dst, one + d, dev(p), kr)

        def away(fn, i, p):
            return C.rc(fn, fn, one + 2 + d, dev(p), S.b + i)

        @pl.when(act(s, jnp.logical_or(pos == 0, pos == 3)))
        def _():
            toward(R.G.at[d, s], R.L1.at[d, s], S.a + d * n + s, 1 + pos // 3).start()

        k2 = s - w

        @pl.when(act(k2, pos == 2))
        def _():
            i = d * n + k2
            toward(R.G.at[d, k2], R.L1.at[d, k2], S.a + i, 1).wait_recv()
            R.G[d, k2] = (R.G[d, k2].astype(F32) + R.L1[d, k2].astype(F32)).astype(BF)
            toward(R.G.at[d, k2], R.FN.at[d, k2], S.b + i, 1).start()

        k1 = s - 2 * w

        @pl.when(act(k1, pos == 1))
        def _():
            i = d * n + k1
            fn = R.FN.at[d, k1]
            toward(R.G.at[d, k1], R.L1.at[d, k1], S.a + i, 0).wait_recv()
            away(fn, i, 2).wait_recv()
            v = R.G[d, k1].astype(F32) + R.L1[d, k1].astype(F32) + R.FN[d, k1].astype(F32)
            R.FN[d, k1] = v.astype(BF)
            away(fn, i, 2).start()
            toward(fn, fn, S.b + i, 0).start()

        lag = w * (2 + jnp.where(pos == 1, 0, 1) + jnp.where(pos == 3, 1, 0))
        kf = s - lag

        @pl.when(act(kf, None))
        def _():
            i = d * n + kf
            fn = R.FN.at[d, kf]

            @pl.when(pos != 1)
            def _():
                away(fn, i, 1).wait_recv()

            @pl.when(pos == 2)
            def _():
                away(fn, i, 3).start()

            C.rc(fn, R.XH.at[d, kf], one + 4 + d, C.xp).start()
            pltpu.make_async_copy(fn, R.FH.at[d, kf], C.lsem.at[4 + d]).start()


class Chain(Ring):
    def __init__(self, sums, k0, k1, w):
        super().__init__(sums, k0, k1, w)
        self.total = k1 - k0 + 6 * w

    def half(self, s, d):
        S, w = self.S, self.w
        R, C, n, one = S.R, S.C, S.n, S.one
        pos = C.z if d == 0 else 3 - C.z
        step = 1 if d == 0 else -1
        up = ((C.z + step) * 2 + C.x, C.t)
        down = ((C.z - step) * 2 + C.x, C.t)

        def act(k, cond):
            ok = jnp.logical_and(k >= self.k0, k < self.k1)
            return ok if cond is None else jnp.logical_and(ok, cond)

        def toward(i, k):
            return C.rc(R.G.at[d, k], R.L1.at[d, k], one + 6 + d, up, S.a + i)

        def away(i, k):
            return C.rc(R.FN.at[d, k], R.FN.at[d, k], one + 8 + d, down, S.b + i)

        k = s - pos * w

        @pl.when(act(k, pos == 0))
        def _():
            toward(d * n + k, k).start()

        @pl.when(act(k, pos > 0))
        def _():
            i = d * n + k
            toward(i, k).wait_recv()
            v = (R.G[d, k].astype(F32) + R.L1[d, k].astype(F32)).astype(BF)

            @pl.when(pos < 3)
            def _():
                R.G[d, k] = v
                toward(i, k).start()

            @pl.when(pos == 3)
            def _():
                R.FN[d, k] = v

        kf = s - (6 - pos) * w

        @pl.when(act(kf, None))
        def _():
            i = d * n + kf
            fn = R.FN.at[d, kf]

            @pl.when(pos < 3)
            def _():
                away(i, kf).wait_recv()

            @pl.when(pos > 0)
            def _():
                away(i, kf).start()

            C.rc(fn, R.XH.at[d, kf], one + 4 + d, C.xp).start()
            pltpu.make_async_copy(fn, R.FH.at[d, kf], C.lsem.at[4 + d]).start()


def small_tensor(R, C):
    R.st[C.t, 0:8, :] = R.sm[...]
    R.st[C.t, 8:16, :] = R.sm2[...]
    k = C.sems(3)
    return [
        C.send(R.st.at[C.t], R.st.at[C.t], k + i, dev)
        for i, dev in enumerate((C.mate, C.yp, (C.dp, 3 - C.t)))
    ]


def small_dp(R, C, n, cps):
    for cp in cps:
        cp.wait_recv()
    tot = R.st[0] + R.st[1] + R.st[2] + R.st[3]
    sd = R.sd.at[C.dp]
    sd[0:8, :] = tot[0:8, :]
    sd[8:10, :] = tot[8:10, :]
    f = R.dproj.shape[2]

    def colsum(m):
        return rowsum(R.dproj[m].astype(F32))

    sd[10:11, 0:f] = colsum(0)
    sd[10:11, f : 2 * f] = colsum(2)
    half = R.DH.shape[2]
    for e in range(2):
        sd[11:12, e * half : (e + 1) * half] = rowsum(R.DH[e].astype(F32))
    k = C.sems(n)
    return [C.send(sd, R.sd.at[C.dp], k + o, (lax.rem(C.dp + o, n), C.t)) for o in range(1, n)]


def small_end(R, C, n, cps):
    for cp in cps:
        cp.wait_recv()
    tot = R.sd[0]
    for b in range(1, n):
        tot = tot + R.sd[b]
    R.osm[...] = tot
    for xx in range(2):
        v = R.sd[xx, 11:12, :]
        for b in range(2 + xx, n, 2):
            v = v + R.sd[b, 11:12, :]
        R.osm[11 + xx : 12 + xx, :] = v


class Refs:
    pass


LAG = 2
LAG_Q = 2
T_U, T_DA, T_DO, T_AB, T_KV, T_QB, T_QG = 3, 5, 4, 2, 4, 3, 1


def body(names, n, *refs):
    R = Refs()
    for name, ref in zip(names, refs):
        setattr(R, name, ref)
    C = Ctx(R.ssem, R.rsem, R.lsem)
    sem, count = barrier_start(C, n)
    half = R.wi.shape[2]
    off = pl.ds(al(C.x * half, half), half)
    wcp = [
        pltpu.make_async_copy(R.w_in.at[:, :, off], R.wi, C.lsem.at[2]),
        pltpu.make_async_copy(R.w_back.at[:, off, :], R.wb, C.lsem.at[3]),
    ]
    for cp in wcp:
        cp.start()
    for i, ref in enumerate((R.g1, R.b1, R.outb, R.g2, R.b2)):
        R.par[i : i + 1, :] = ref[...].astype(F32).reshape(1, ref.shape[0])
    R.par[5:7, :] = R.router[...].astype(F32)
    R.par[7:9, :] = R.backb[...].astype(F32)
    R.sm[...] = jnp.zeros_like(R.sm)
    R.sm2[...] = jnp.zeros_like(R.sm2)
    R.sd[...] = jnp.zeros_like(R.sd)
    pl.semaphore_wait(sem, count)
    wait_qkv = stage_qkv(R, C, n)
    wait_qkv()
    wait_cot = swap_cot(R, C)
    stage_attend(R, C, n)
    wait_cot()
    stage_out(R, C)
    for cp in wcp:
        cp.wait()
    over_u = Reduce8(C, R.YP, R.ly, R.sy, R.u)
    over_x = Reduce8(C, R.DXP, R.lx, R.sx, R.dx)
    stage_moe(R, C, (over_u, over_x))
    K = Kinds(half // 32, R.H2.shape[2] // 64)
    sums = Sums(R, C, K.n)
    ring = Chain(sums, 0, K.q0, LAG)
    last = Ring(sums, K.q0, K.n, LAG_Q)
    stage_moe_grads(R, C, K, ring)
    over_u.wait()
    ring.run(T_U)
    over_x.wait()
    stage_owner(R, C)
    wait_da = gather4(R, C, R.DA)
    wait_res = gather4(R, C, R.RES)
    ring.run(T_DA)
    wait_da()
    stage_out_back(R, C, n)
    wait_do = all_to_all(R, C, R.osend, R.dorecv, n)
    stage_out_grad(R, C)
    ring.run(T_DO)
    wait_do()
    C.drain()
    xo = C.send(R.A.at[:, 0:128, :], R.wi.at[:, 0:128, :], C.sems(1), C.xp)
    stage_attend_back(R, C, n, ring, xo)
    xq = stage_qkv_grad(R, C, ring)
    stage_qkv_back(R, C, lambda: ring.run(T_QB))
    wait_gin = gather4(R, C, R.GIN)
    small = small_tensor(R, C)
    for cp in xq:
        cp.wait_recv()
    add_tail(R, 2, 6)
    for r in range(8):
        last.run(1)
        ring.run(1)
        if r == 2:
            small = small_dp(R, C, n, small)
    wait_gin()
    wait_res()
    small_end(R, C, n, small)
    ring.rest()
    last.rest()
    sums.finish(K.q0)
    C.drain()


def place_body(nb, ni, fh, xh, res, gin, osm, oB, oI, oQ, oO, oR, oG, *rest):
    vec, (cf, cx, cr, cg, vB, vI, vQ, vO, vR, vG, isem, osem) = rest[:9], rest[9:]
    x = lax.rem(lax.axis_index("dp"), 2)
    n = nb + ni + 8
    half = nb * 32
    cuts = ((0, nb), (nb, ni), (nb + ni, 8))
    srcs = ((fh, cf, x), (xh, cx, 1 - x))
    ins = {}
    for j, (src, buf, h) in enumerate(srcs):
        for d in range(2):
            for c, (k0, m) in enumerate(cuts):
                cp = pltpu.make_async_copy(
                    src.at[d, pl.ds(k0, m)], buf.at[d, pl.ds(k0, m)], isem.at[j * 6 + d * 3 + c]
                )
                cp.start()
                ins[j, d, c] = cp
    rows = [pltpu.make_async_copy(a, b, isem.at[12 + i]) for i, (a, b) in enumerate(((res, cr), (gin, cg)))]
    for cp in rows:
        cp.start()
    outs = []

    def put(src, dst):
        cp = pltpu.make_async_copy(src, dst, osem.at[len(outs)])
        cp.start()
        outs.append(cp)

    for j, (src, buf, h) in enumerate(srcs):
        for d in range(2):
            ins[j, d, 0].wait()

            def back(k):
                v = buf[d, k].astype(F32)
                at = pl.ds(al(k * 32, 32), 32)
                vB[j, d, at, 0:512] = v[0:32]
                vB[j, d, at, 512:1024] = v[32:64]

            loop(nb, back)
            put(vB.at[j, d], oB.at[d, pl.ds(al(h * half, half), half), :])
            ins[j, d, 1].wait()

            def into(k):
                vI[j, d, pl.ds(al(k * 64, 64), 64), :] = buf[d, nb + k].astype(F32)

            loop(ni, into)
            put(vI.at[j, d], oI.at[d, :, pl.ds(al(h * 512, 512), 512)])
    for j, (src, buf, h) in enumerate(srcs):
        for d in range(2):
            ins[j, d, 2].wait()
            for c in range(2):
                v = buf[d, nb + ni + c].astype(F32)
                at = pl.ds(al(h * 128 + d * 64 + c * 32, 32), 32)
                vO[at, 0:512] = v[0:32]
                vO[at, 512:1024] = v[32:64]
            for c in range(6):
                v = buf[d, nb + ni + 2 + c].astype(F32)
                row = h * 512 + d * 256 + (c % 2) * 128
                vQ[c // 2, pl.ds(al(row, 64), 64), :] = v[:, 0:256]
                vQ[c // 2, pl.ds(al(row + 64, 64), 64), :] = v[:, 256:512]
    put(vO, oO)
    put(vQ, oQ)
    for cp, src, buf, out in ((rows[0], cr, vR, oR), (rows[1], cg, vG, oG)):
        cp.wait()
        for t in range(src.shape[0]):
            buf[t] = src[t].astype(F32)
        put(buf, out)
    ln1g, ln1b, qv, outb, ln2g, ln2b, rout, inb, bb = vec
    for ref, r in ((ln1g, 8), (ln1b, 9), (outb, 2), (ln2g, 0), (ln2b, 1)):
        ref[...] = osm[r : r + 1, :]
    for i in range(2):
        qv[i : i + 1, :] = osm[10:11, i * 256 : i * 256 + 256]
        rout[i : i + 1, :] = osm[3 + i : 4 + i, :]
        bb[i : i + 1, :] = osm[5 + i : 6 + i, :]
        for e in range(2):
            inb[e : e + 1, i * 512 : i * 512 + 512] = osm[11 + i : 12 + i, e * 512 : e * 512 + 512]
    for cp in outs:
        cp.wait()


def place(fh, xh, res, gin, osm, nb, ni):
    sds = jax.ShapeDtypeStruct
    vm = pl.BlockSpec(memory_space=pltpu.VMEM)
    hbm = pl.BlockSpec(memory_space=pl.ANY)
    n, half = nb + ni + 8, nb * 32
    big = [(2, 2 * half, 1024), (2, ni * 64, 1024), (3, 1024, 256), (256, 1024), res.shape, gin.shape]
    row = (1, 1024)
    small = [row, row, (2, 256), row, row, row, (2, 1024), (2, 1024), (2, 1024)]
    V = pltpu.VMEM
    return pl.pallas_call(
        functools.partial(place_body, nb, ni),
        out_shape=[sds(v, F32) for v in big + small],
        in_specs=[hbm, hbm, hbm, hbm, vm],
        out_specs=[hbm] * len(big) + [vm] * len(small),
        scratch_shapes=[
            V((2, n, 64, 512), BF),
            V((2, n, 64, 512), BF),
            V(res.shape, BF),
            V(gin.shape, BF),
            V((2, 2, half, 1024), F32),
            V((2, 2, ni * 64, 512), F32),
            V((3, 1024, 256), F32),
            V((256, 1024), F32),
            V(res.shape, F32),
            V(gin.shape, F32),
            pltpu.SemaphoreType.DMA((14,)),
            pltpu.SemaphoreType.DMA((12,)),
        ],
        compiler_params=pltpu.CompilerParams(vmem_limit_bytes=60000000),
        name="place",
    )(fh, xh, res, gin, osm)


def fast_local(args, n, nt):
    (tokens, g1, b1, w_qkv, qvb, w_out, out_b, g2, b2, router, w_in, in_b, w_back, back_b,
     routes, prefix, cot) = args
    S, span, D = tokens.shape
    rows = S * span
    F = w_qkv.shape[2]
    H = w_in.shape[2]
    half = H // 2
    total = n * span
    vm = pl.BlockSpec(memory_space=pltpu.VMEM)
    hbm = pl.BlockSpec(memory_space=pl.ANY)
    ins = [
        ("tok", tokens.reshape(rows, D), vm),
        ("g1", g1, vm),
        ("b1", b1, vm),
        ("outb", out_b, vm),
        ("g2", g2, vm),
        ("b2", b2, vm),
        ("router", router.T, vm),
        ("backb", back_b, vm),
        ("wqkv", w_qkv.transpose(1, 0, 2), vm),
        ("qvb", qvb, vm),
        ("wout", w_out, vm),
        ("routes", routes.reshape(1, rows), vm),
        ("prefix", prefix, pl.BlockSpec(memory_space=pltpu.SMEM)),
        ("cot", cot.reshape(rows, D), vm),
        ("inb", in_b, vm),
        ("w_in", w_in, hbm),
        ("w_back", w_back, hbm),
    ]
    sds = jax.ShapeDtypeStruct
    nch = half // 32 + D // 64 + 8
    outs = [
        ("RES", sds((nt, CH, D), BF), vm),
        ("GIN", sds((nt, CH, D), BF), vm),
        ("FH", sds((2, nch, 64, 512), BF), hbm),
        ("XH", sds((2, nch, 64, 512), BF), hbm),
        ("osm", sds((16, D), F32), vm),
    ]
    V = pltpu.VMEM
    scr = [
        ("h1", V((rows, D), BF)),
        ("asend", V((n, 384, 128), BF)),
        ("arecv", V((n, 384, 128), BF)),
        ("Q", V((total, 128), BF)),
        ("K", V((total, 128), BF)),
        ("V", V((total, 128), BF)),
        ("DO", V((total, 128), BF)),
        ("of", V((total, 128), F32)),
        ("dq", V((total, 128), F32)),
        ("osend", V((n, 128, 128), BF)),
        ("orecv", V((n, 128, 128), BF)),
        ("dorecv", V((n, 128, 128), BF)),
        ("otok", V((rows, F), BF)),
        ("dproj", V((3, rows, F), BF)),
        ("p4", V((3, CH, D), BF)),
        ("l4", V((3, CH, D), BF)),
        ("x1", V((CH, D), F32)),
        ("u", V((CH, D), F32)),
        ("dx", V((CH, D), F32)),
        ("cols", V((CH, 128), F32)),
        ("H2", V((8, CH, D), BF)),
        ("GG", V((8, CH, D), BF)),
        ("META", V((8, CH, 128), BF)),
        ("cx", V((rows, D), BF)),
        ("par", V((16, D), F32)),
        ("wi", V((2, D, half), BF)),
        ("wb", V((2, half, D), BF)),
        ("A", V((2, 8 * CH, half), BF)),
        ("DH", V((2, 8 * CH, half), BF)),
        ("YP", V((8, CH, D), BF)),
        ("DXP", V((8, CH, D), BF)),
        ("ly", V((7, CH, D), BF)),
        ("lx", V((7, CH, D), BF)),
        ("sy", V((3, CH, D), BF)),
        ("sx", V((3, CH, D), BF)),
        ("DA", V((nt, CH, D), BF)),
        ("G", V((2, nch, 64, 512), BF)),
        ("L1", V((2, nch, 64, 512), BF)),
        ("FN", V((2, nch, 64, 512), BF)),
        ("sm", V((8, D), F32)),
        ("sm2", V((8, D), F32)),
        ("st", V((4, 16, D), F32)),
        ("sd", V((n, 16, D), F32)),
        ("ssem", pltpu.SemaphoreType.DMA((140 + 4 * nch,))),
        ("rsem", pltpu.SemaphoreType.DMA((140 + 4 * nch,))),
        ("lsem", pltpu.SemaphoreType.DMA((16,))),
    ]
    names = [i[0] for i in ins] + [o[0] for o in outs] + [s[0] for s in scr]
    res, gin, fh, xh, osm = pl.pallas_call(
        functools.partial(body, names, n),
        out_shape=[o[1] for o in outs],
        in_specs=[i[2] for i in ins],
        out_specs=[o[2] for o in outs],
        scratch_shapes=[s[1] for s in scr],
        compiler_params=pltpu.CompilerParams(
            collective_id=0, has_side_effects=True, vmem_limit_bytes=67043328
        ),
        name="layer",
    )(*[i[1] for i in ins])
    oB, oI, oQ, oO, oR, oG, ln1g, ln1b, qv, outb, ln2g, ln2b, rout, inb, bb = place(
        fh, xh, res, gin, osm, half // 32, D // 64
    )
    return (
        oR.reshape(S, span, D),
        oG.reshape(S, span, D),
        ln1g.reshape(D),
        ln1b.reshape(D),
        oQ.transpose(1, 0, 2),
        qv,
        oO,
        outb.reshape(D),
        ln2g.reshape(D),
        ln2b.reshape(D),
        rout.T,
        oI,
        inb,
        oB,
        bb,
    )


SCALE = 0.125
EPSILON = 1e-05
MASKED = -1e30
HIGHEST = lax.Precision.HIGHEST


def layer_norm(values, norm_gain, norm_bias):
    centred = values - jnp.mean(values, axis=-1, keepdims=True)
    spread = jnp.mean(centred * centred, axis=-1, keepdims=True)
    return centred * lax.rsqrt(spread + EPSILON) * norm_gain + norm_bias


def heads_of(block, head_count):
    seq_count, row_count, feat_count = block.shape
    return block.reshape(seq_count, row_count, head_count, feat_count // head_count).transpose(
        0, 2, 1, 3
    )


def tokens_of(block):
    seq_count, head_count, row_count, head_width = block.shape
    return block.transpose(0, 2, 1, 3).reshape(seq_count, row_count, head_count * head_width)


def masked_scores(queries, key_heads, query_start, key_start, prefix):
    scores = (
        jnp.einsum("shqd,shkd->shqk", queries, key_heads, preferred_element_type=jnp.float32)
        * SCALE
    )
    query_pos = query_start + jnp.arange(queries.shape[2], dtype=jnp.int32)
    key_pos = key_start + jnp.arange(key_heads.shape[2], dtype=jnp.int32)
    visible_mask = (key_pos[None, None, :] <= query_pos[None, :, None]) | (
        key_pos[None, None, :] < prefix[:, None, None]
    )
    visible_mask = visible_mask[:, None]
    return (jnp.where(visible_mask, scores, MASKED), visible_mask)


def block_live(key_start, query_last, prefix):
    return jnp.any(key_start < prefix) | (key_start <= query_last)


def prob_grads(
    queries, key_heads, value_heads, douts, log_total, delta, query_start, key_start, prefix
):
    scores, visible_mask = masked_scores(queries, key_heads, query_start, key_start, prefix)
    probs = jnp.where(visible_mask, jnp.exp(scores - log_total[..., None]), 0.0)
    dprob = jnp.einsum("shqd,shkd->shqk", douts, value_heads, preferred_element_type=jnp.float32)
    dscore = (probs * (dprob - delta[..., None])).astype(jnp.bfloat16)
    return (probs, dscore)


def attend_fold(run_state, piece_rows, piece_start, queries, first_row, prefix):
    key_piece, value_piece = piece_rows
    head_count = queries.shape[1]
    row_count = key_piece.shape[1]
    block_width = math.gcd(row_count, 512)
    query_last = first_row + queries.shape[2] - 1

    def attend_update(block_index, state_now):
        key_start = block_index * block_width
        key_heads = heads_of(
            lax.dynamic_slice_in_dim(key_piece, block_index * block_width, block_width, 1),
            head_count,
        )
        value_heads = heads_of(
            lax.dynamic_slice_in_dim(value_piece, block_index * block_width, block_width, 1),
            head_count,
        )
        scores, visible_mask = masked_scores(queries, key_heads, first_row, key_start, prefix)
        run_max, run_sum, run_out = state_now
        new_max = jnp.maximum(run_max, jnp.max(scores, axis=-1))
        factor = jnp.exp(run_max - new_max)
        weights = jnp.where(visible_mask, jnp.exp(scores - new_max[..., None]), 0.0)
        run_sum = factor * run_sum + jnp.sum(weights, axis=-1)
        run_out = factor[..., None] * run_out + jnp.einsum(
            "shqk,shkd->shqd", weights, value_heads.astype(jnp.float32), precision=HIGHEST
        )
        return (new_max, run_sum, run_out)

    def attend_block_step(state_now, block_index):
        key_start = block_index * block_width
        is_live = block_live(key_start, query_last, prefix)
        return (
            lax.cond(
                is_live, functools.partial(attend_update, block_index), lambda unchanged: unchanged, state_now
            ),
            None,
        )

    run_state, unused = lax.scan(
        attend_block_step, run_state, jnp.arange(row_count // block_width, dtype=jnp.int32)
    )
    return run_state


def key_pass(queries, douts, log_total, delta, keys_all, values_all, first_row, prefix):
    head_count = queries.shape[1]
    total_rows = keys_all.shape[1]
    block_width = math.gcd(total_rows, 512)
    query_last = first_row + queries.shape[2] - 1

    def key_block_step(dquery, block_index):
        key_start = block_index * block_width

        def work(dquery_now):
            key_heads = heads_of(
                lax.dynamic_slice_in_dim(keys_all, key_start, block_width, 1), head_count
            )
            value_heads = heads_of(
                lax.dynamic_slice_in_dim(values_all, key_start, block_width, 1), head_count
            )
            probs, dscore = prob_grads(
                queries,
                key_heads,
                value_heads,
                douts,
                log_total,
                delta,
                first_row,
                key_start,
                prefix,
            )
            dquery_now = (
                dquery_now
                + jnp.einsum(
                    "shqk,shkd->shqd", dscore, key_heads, preferred_element_type=jnp.float32
                )
                * SCALE
            )
            return (dquery_now, ())

        def skipped(dquery_now):
            return (dquery_now, ())

        return lax.cond(block_live(key_start, query_last, prefix), work, skipped, dquery)

    dquery, key_parts = lax.scan(
        key_block_step,
        jnp.zeros(queries.shape, jnp.float32),
        jnp.arange(total_rows // block_width, dtype=jnp.int32),
    )
    return (dquery, ())


def query_fold(run_state, piece_rows, piece_start, key_heads, value_heads, first_row, prefix):
    query_piece, dout_piece, total_piece, delta_piece = piece_rows
    head_count = key_heads.shape[1]
    row_count = query_piece.shape[1]
    block_width = math.gcd(row_count, 512)

    def query_update(block_index, state_now):
        query_start = block_index * block_width
        offset = block_index * block_width
        queries = heads_of(
            lax.dynamic_slice_in_dim(query_piece, offset, block_width, 1), head_count
        )
        douts = heads_of(lax.dynamic_slice_in_dim(dout_piece, offset, block_width, 1), head_count)
        log_total = lax.dynamic_slice_in_dim(total_piece, offset, block_width, 1).transpose(0, 2, 1)
        delta = lax.dynamic_slice_in_dim(delta_piece, offset, block_width, 1).transpose(0, 2, 1)
        probs, dscore = prob_grads(
            queries, key_heads, value_heads, douts, log_total, delta, query_start, first_row, prefix
        )
        dkey_now, dvalue_now = state_now
        dkey_now = (
            dkey_now
            + jnp.einsum("shqk,shqd->shkd", dscore, queries, preferred_element_type=jnp.float32)
            * SCALE
        )
        dvalue_now = dvalue_now + jnp.einsum(
            "shqk,shqd->shkd", probs, douts.astype(jnp.float32), precision=HIGHEST
        )
        return (dkey_now, dvalue_now)

    def query_block_step(state_now, block_index):
        query_last = block_index * block_width + block_width - 1
        is_live = block_live(first_row, query_last, prefix)
        return (
            lax.cond(
                is_live, functools.partial(query_update, block_index), lambda unchanged: unchanged, state_now
            ),
            None,
        )

    run_state, unused = lax.scan(
        query_block_step, run_state, jnp.arange(row_count // block_width, dtype=jnp.int32)
    )
    return run_state


def local(
    tokens,
    ln1_gain,
    ln1_bias,
    w_qkv,
    qv_bias,
    w_out,
    out_bias,
    ln2_gain,
    ln2_bias,
    router,
    w_in,
    in_bias,
    w_back,
    back_bias,
    routes,
    prefix,
    cotangent,
):
    seq_count, span_len, model_width = tokens.shape
    tok_rows = seq_count * span_len
    local_feats = w_qkv.shape[2]
    head_count = local_feats // HEAD_DIM
    expert_count = w_in.shape[0]
    first_row = lax.axis_index("dp") * span_len
    local_shape = (seq_count, span_len, local_feats)
    source = tokens.reshape(tok_rows, model_width).astype(jnp.float32)
    normed_one, ln1_pull = jax.vjp(
        layer_norm, source, ln1_gain.astype(jnp.float32), ln1_bias.astype(jnp.float32)
    )
    hidden_one = normed_one.astype(jnp.bfloat16)
    projected = jnp.einsum("ti,icf->tcf", hidden_one, w_qkv, preferred_element_type=jnp.float32)
    bias_float = qv_bias.astype(jnp.float32)
    query_tok = (projected[:, 0] + bias_float[0]).astype(jnp.bfloat16).reshape(local_shape)
    key_tok = projected[:, 1].astype(jnp.bfloat16).reshape(local_shape)
    value_tok = (projected[:, 2] + bias_float[1]).astype(jnp.bfloat16).reshape(local_shape)
    queries = heads_of(query_tok, head_count)
    stat_shape = queries.shape[:3]
    start_state = (
        jnp.full(stat_shape, MASKED, jnp.float32),
        jnp.zeros(stat_shape, jnp.float32),
        jnp.zeros(queries.shape, jnp.float32),
    )
    fold_keys = functools.partial(attend_fold, queries=queries, first_row=first_row, prefix=prefix)
    run_max, run_sum, run_out = fold_keys(
        start_state,
        (
            lax.all_gather(key_tok, "dp", axis=1, tiled=True),
            lax.all_gather(value_tok, "dp", axis=1, tiled=True),
        ),
        jnp.int32(0),
    )
    mixed_heads = run_out / run_sum[..., None]
    log_total = run_max + jnp.log(run_sum)
    mixed_b = tokens_of(mixed_heads.astype(jnp.bfloat16)).reshape(tok_rows, local_feats)
    out_shift = out_bias.astype(jnp.float32)
    gain_two = ln2_gain.astype(jnp.float32)
    shift_two = ln2_bias.astype(jnp.float32)
    attn_part = jnp.dot(mixed_b, w_out, preferred_element_type=jnp.float32)
    attn_out = lax.psum(attn_part, "tensor") + out_shift
    residual = source + attn_out
    normed_two, ln2_pull = jax.vjp(layer_norm, residual, gain_two, shift_two)
    hidden_two = normed_two.astype(jnp.bfloat16)
    logits = jnp.dot(hidden_two, router, preferred_element_type=jnp.float32)
    chosen = routes.reshape(tok_rows)
    expert_ids = jnp.arange(expert_count, dtype=jnp.int32)
    expert_hot = (chosen[:, None] == expert_ids[None, :]).astype(jnp.int32)

    def gate_of(logit_vals):
        return jnp.sum(
            jnp.where(expert_hot == 1, jax.nn.softmax(logit_vals, axis=-1), 0.0), axis=-1
        )

    gate_value, gate_pull = jax.vjp(gate_of, logits)
    earlier = jnp.cumsum(expert_hot, axis=0, dtype=jnp.int32) - expert_hot
    slot_place = jnp.sum(earlier * expert_hot, axis=1, dtype=jnp.int32)
    slot_ids = jnp.arange(CAP, dtype=jnp.int32)
    select_mask = (expert_hot[:, :, None] == 1) & (
        slot_place[:, None, None] == slot_ids[None, None, :]
    )
    select = select_mask.astype(jnp.bfloat16)
    select_float = select_mask.astype(jnp.float32)
    dispatched = jnp.einsum(
        "tec,td->ecd", select, hidden_two, preferred_element_type=jnp.float32
    ).astype(jnp.bfloat16)
    pre_act = (
        jnp.einsum("ecd,edf->ecf", dispatched, w_in, preferred_element_type=jnp.float32)
        + in_bias.astype(jnp.float32)[:, None, :]
    )
    act_float, gelu_pull = jax.vjp(functools.partial(jax.nn.gelu, approximate=False), pre_act)
    active = act_float.astype(jnp.bfloat16)
    expert_part = jnp.einsum("ecf,efd->ecd", active, w_back, preferred_element_type=jnp.float32)
    expert_full = lax.psum(expert_part, "tensor") + back_bias.astype(jnp.float32)[:, None, :]
    combined = jnp.einsum("tec,ecd->td", select_float, expert_full, precision=HIGHEST)
    layer_rows = residual + gate_value[:, None] * combined
    grad_out = cotangent.reshape(tok_rows, model_width).astype(jnp.float32)
    dgate = jnp.sum(grad_out * combined, axis=-1)
    dlogit_b = gate_pull(dgate)[0].astype(jnp.bfloat16)
    gated_grad = (gate_value[:, None] * grad_out).astype(jnp.bfloat16)
    dexpert_b = jnp.einsum(
        "tec,td->ecd", select, gated_grad, preferred_element_type=jnp.float32
    ).astype(jnp.bfloat16)
    grad_back_bias = jnp.sum(dexpert_b, axis=1, dtype=jnp.float32)
    grad_w_back = jnp.einsum("ecf,ecd->efd", active, dexpert_b, preferred_element_type=jnp.float32)
    dactive = jnp.einsum("ecd,efd->ecf", dexpert_b, w_back, preferred_element_type=jnp.float32)
    dpre_b = gelu_pull(dactive)[0].astype(jnp.bfloat16)
    grad_in_bias = jnp.sum(dpre_b, axis=1, dtype=jnp.float32)
    grad_w_in = jnp.einsum("ecd,ecf->edf", dispatched, dpre_b, preferred_element_type=jnp.float32)
    slot_part = jnp.einsum("ecf,edf->ecd", dpre_b, w_in, preferred_element_type=jnp.float32)
    dslots = lax.psum(slot_part, "tensor")
    dnorm_two = jnp.einsum("tec,ecd->td", select_float, dslots, precision=HIGHEST) + jnp.einsum(
        "te,de->td", dlogit_b, router, preferred_element_type=jnp.float32
    )
    grad_router = jnp.einsum("td,te->de", hidden_two, dlogit_b, preferred_element_type=jnp.float32)
    dresid_norm, grad_ln2_gain, grad_ln2_bias = ln2_pull(dnorm_two)
    dresidual = grad_out + dresid_norm
    dattn_b = dresidual.astype(jnp.bfloat16)
    grad_out_bias = jnp.sum(dattn_b, axis=0, dtype=jnp.float32)
    grad_w_out = jnp.einsum("tf,td->fd", mixed_b, dattn_b, preferred_element_type=jnp.float32)
    dmixed_tok = (
        jnp.einsum("td,fd->tf", dattn_b, w_out, preferred_element_type=jnp.float32)
        .astype(jnp.bfloat16)
        .reshape(local_shape)
    )
    douts = heads_of(dmixed_tok, head_count)
    delta = jnp.sum(douts.astype(jnp.float32) * mixed_heads, axis=-1)
    keys_all, values_all = (
        lax.all_gather(key_tok, "dp", axis=1, tiled=True),
        lax.all_gather(value_tok, "dp", axis=1, tiled=True),
    )
    dquery, unused = key_pass(
        queries, douts, log_total, delta, keys_all, values_all, first_row, prefix
    )
    total_rows = log_total.transpose(0, 2, 1)
    delta_rows = delta.transpose(0, 2, 1)
    fold_rows = functools.partial(
        query_fold,
        key_heads=heads_of(key_tok, head_count),
        value_heads=heads_of(value_tok, head_count),
        first_row=first_row,
        prefix=prefix,
    )
    zero_heads = jnp.zeros(queries.shape, jnp.float32)
    dkey_heads, dvalue_heads = fold_rows(
        (zero_heads, zero_heads),
        (
            lax.all_gather(query_tok, "dp", axis=1, tiled=True),
            lax.all_gather(dmixed_tok, "dp", axis=1, tiled=True),
            lax.all_gather(total_rows.astype(jnp.bfloat16), "dp", axis=1, tiled=True).astype(
                jnp.float32
            ),
            lax.all_gather(delta_rows.astype(jnp.bfloat16), "dp", axis=1, tiled=True).astype(
                jnp.float32
            ),
        ),
        jnp.int32(0),
    )
    dkey = tokens_of(dkey_heads)
    dvalue = tokens_of(dvalue_heads)
    dquery_b = tokens_of(dquery).astype(jnp.bfloat16).reshape(tok_rows, local_feats)
    dkey_b = dkey.astype(jnp.bfloat16).reshape(tok_rows, local_feats)
    dvalue_b = dvalue.astype(jnp.bfloat16).reshape(tok_rows, local_feats)
    dproject = jnp.stack([dquery_b, dkey_b, dvalue_b], axis=1)
    grad_qv_bias = jnp.stack(
        [jnp.sum(dquery_b, axis=0, dtype=jnp.float32), jnp.sum(dvalue_b, axis=0, dtype=jnp.float32)]
    )
    grad_w_qkv = jnp.einsum("ti,tcf->icf", hidden_one, dproject, preferred_element_type=jnp.float32)
    norm_part = jnp.einsum("tcf,icf->ti", dproject, w_qkv, preferred_element_type=jnp.float32)
    dnorm_one = lax.psum(norm_part, "tensor")
    dsource_norm, grad_ln1_gain, grad_ln1_bias = ln1_pull(dnorm_one)
    input_grad = (dresidual + dsource_norm).reshape(seq_count, span_len, model_width)
    summed = lax.psum(
        (
            grad_ln1_gain,
            grad_ln1_bias,
            grad_w_qkv,
            grad_qv_bias,
            grad_w_out,
            grad_out_bias,
            grad_ln2_gain,
            grad_ln2_bias,
            grad_router,
            grad_w_in,
            grad_in_bias,
            grad_w_back,
            grad_back_bias,
        ),
        "dp",
    )
    layer_out = layer_rows.reshape(seq_count, span_len, model_width)
    return (layer_out, input_grad) + tuple(summed)


def solution(mesh):
    in_specs = (
        P(None, "dp", None),
        P(),
        P(),
        P(None, None, "tensor"),
        P(None, "tensor"),
        P("tensor", None),
        P(),
        P(),
        P(),
        P(),
        P(None, None, "tensor"),
        P(None, "tensor"),
        P(None, "tensor", None),
        P(),
        P(None, "dp", None),
        P(),
        P(None, "dp", None),
    )
    out_specs = (
        P(None, "dp", None),
        P(None, "dp", None),
        P(),
        P(),
        P(None, None, "tensor"),
        P(None, "tensor"),
        P("tensor", None),
        P(),
        P(),
        P(),
        P(),
        P(None, None, "tensor"),
        P(None, "tensor"),
        P(None, "tensor", None),
        P(),
    )
    n, nt = mesh.shape["dp"], mesh.shape["tensor"]

    def step(*args):
        tokens, w_qkv = args[0], args[3]
        heads = w_qkv.shape[2] // HEAD_DIM
        fits = (
            nt == 4
            and n == 8
            and tokens.shape[2] == 1024
            and w_qkv.shape[2] == 256
            and args[10].shape == (2, 1024, 1024)
            and n == tokens.shape[0] * heads
            and tokens.shape[0] * tokens.shape[1] == nt * CH
            and tokens.shape[1] == 256
        )
        return fast_local(args, n, nt) if fits else local(*args)

    return jax.shard_map(step, mesh=mesh, in_specs=in_specs, out_specs=out_specs, check_vma=False)
```
